32 devices in a mesh: seq: 8 (over z, x), exp: 4 (over y, core).
Axes of the slice: x: 2, y: 2, z: 4, core: 2. Of those that a mesh axis runs over, the one named last changes fastest.
Arguments:
- queries: bfloat16 [1024, 4096], P('seq', 'exp'), may hold values from -2 to 2
- keys: bfloat16 [1024, 4096], P('seq', 'exp'), may hold values from -2 to 2
- values: bfloat16 [1024, 4096], P('seq', 'exp'), may hold values from -6 to 6
- log_decay: float32 [1024, 32], P('seq', 'exp'), may hold values from -1 to 0, as said below
- residual: bfloat16 [1024, 4096], P(('seq', 'exp')), may hold values from -6 to 6
- attn_gain: float32 [4096], replicated, may hold values from 0.25 to 1.75
- moe_gain: float32 [4096], replicated, may hold values from 0.25 to 1.75
- expert_ids: int32 [1024, 2], P(('seq', 'exp')), may hold values from 0 to 3, all different within a row; in each aligned block of 32 rows (0 to 31, 32 to 63, ...) at most 24 rows name the same one
- gate_weights: float32 [1024, 2], P(('seq', 'exp')), may hold values from 0.2 to 1
- w_gate: bfloat16 [4, 9216, 4096], P('exp', 'seq'), may hold values from -0.09375 to 0.09375
- w_up: bfloat16 [4, 9216, 4096], P('exp', 'seq'), may hold values from -0.09375 to 0.09375
- w_down: bfloat16 [4, 9216, 4096], P('exp', 'seq'), may hold values from -0.0625 to 0.0625
Outputs:
- layer_out: bfloat16 [1024, 4096], P(('seq', 'exp'))
The draws below stay inside these ranges and needn't reach their ends.
Inputs may be any that keep to these rules, and one draw needn't show every extreme that they name: `expert_ids`: each token names two different experts. In each aligned block of 32 tokens (the tokens of one device) no expert is named by more than 24 tokens, a bound that some block reaches. `log_decay`: every entry is negative.
All inputs are finite; a program needn't handle non-finite values.
Results may differ from the reference program's by a relative error of at most 0.012.
Values may be sent and summed in bfloat16 or wider, within the bound.
A program may use at most 128 MiB of HBM per device.

```python
import math
import jax
import jax.numpy as jnp
import numpy as np
from jax import lax

HEAD_TOTAL = 32
HD = 128
FF = 9216
BLOCK = 128
D = 4096
EXPERTS = 4
TOK_DEV = 32
CAP = 24
TOKEN_TOTAL = 1024
N_SEQ = 8


def draw_log_decay(key, part):
    key_collection = jax.random.split(jax.random.fold_in(key, 17), 6)
    slow_share = 0.5
    slow_heads = jax.random.uniform(key_collection[0], (HEAD_TOTAL,)) < slow_share
    slow_rate = jnp.exp(jax.random.uniform(key_collection[1], (HEAD_TOTAL,), minval=math.log(0.2), maxval=math.log(1.0))) / TOKEN_TOTAL
    fast_rate = jnp.exp(jax.random.uniform(key_collection[2], (HEAD_TOTAL,), minval=math.log(1.0 / 50.0), maxval=math.log(1.0 / 30.0)))
    baseline_decay_rate = jnp.where(slow_heads, slow_rate, fast_rate)
    multiplier = jnp.exp(jax.random.uniform(key_collection[3], (TOKEN_TOTAL, HEAD_TOTAL), minval=math.log(0.5), maxval=math.log(2.0)))
    spike_rows = jax.random.uniform(key_collection[4], (TOKEN_TOTAL, 1)) < 2.0 / TOKEN_TOTAL
    spike_loss = jnp.log(jax.random.uniform(key_collection[5], (TOKEN_TOTAL, HEAD_TOTAL), minval=0.5, maxval=0.8))
    final_output = -(baseline_decay_rate[None, :] * multiplier) + jnp.where(spike_rows, spike_loss, 0.0)
    return final_output.astype(jnp.float32)


def steps_of(key, shape, pieces, smallest, largest):
    def one(axis_at, blocks):
        steps = jax.random.uniform(jax.random.fold_in(jax.random.fold_in(key, 6), axis_at), (blocks,), jnp.float32, smallest / len(pieces), largest / len(pieces))
        return jnp.repeat(jnp.exp(steps), shape[axis_at] // blocks).reshape((-1,) + (1,) * (len(shape) - axis_at - 1))

    level = one(*pieces[0])
    for cut in pieces[1:]:
        level = level * one(*cut)
    return level


def deal_out(rng, own, number, rows, amount, top, most, slope):
    ranking = jax.random.permutation(rng, amount)
    packed, ordinary = shares(amount, rows * top, most, slope, True), shares(amount, rows * top, most, slope, False)
    places = jnp.arange(amount)

    def named(tallies, rotation):
        used = int((tallies > 0).sum())
        fixed = max(1, used // 4)
        shifted = fixed + (places - fixed + rotation * (used - fixed)) % max(1, amount - fixed)
        return jnp.zeros((amount,), jnp.int32).at[ranking[jnp.where(places < fixed, places, shifted)]].set(jnp.asarray(tallies, jnp.int32))

    tallies = jnp.where(number % 4 == 0, named(packed, number // 4), named(ordinary, number - number // 4 - 1))
    mixed = jax.random.permutation(jax.random.fold_in(own, 3), amount)
    source_of, taker = mixed[0:amount // 2 * 2:2], mixed[1:amount // 2 * 2:2]
    room = jnp.minimum(tallies[source_of] - 1, most - tallies[taker]) // 2
    room = jnp.where((source_of == ranking[0]) | (taker == ranking[0]) | (tallies[taker] == 0), 0, jnp.maximum(room, 0))
    shifted = jax.random.randint(jax.random.fold_in(own, 4), (amount // 2,), 0, 1 << 20) % (room + 1)
    tallies = tallies.at[source_of].add(-shifted).at[taker].add(shifted)
    members = jnp.searchsorted(jnp.cumsum(tallies), jnp.arange(rows * top), side="right").astype(jnp.int32)
    table = members.reshape(top, rows).T
    table = table[jax.random.permutation(jax.random.fold_in(own, 1), rows)]
    rotation = jax.random.randint(jax.random.fold_in(own, 2), (rows, 1), 0, top)
    return jnp.take_along_axis(table, (jnp.arange(top)[None, :] + rotation) % top, axis=1)


def shares(count, total, most, lean, full):
    weights = [(1 << 20) // math.isqrt(grade ** lean) + 1 for grade in range(1, count + 1)]
    largest = most if full else min(most, max(-(-total // count), total * weights[0] // sum(weights)))
    least = 1 if total - largest >= count - 1 else 0
    given, surplus = [largest] + [least] * (count - 1), total - largest - least * (count - 1)
    while surplus > 0:
        free = [i for i in range(1, count) if given[i] < largest] or [i for i in range(1, count) if given[i] < most]
        pool, remaining = sum([weights[i] for i in free]), surplus
        for i in free:
            more = min(most - given[i], max(1, remaining * weights[i] // pool), surplus)
            given[i] = given[i] + more
            surplus = surplus - more
    return np.array(given)


def noise(rng, dims, deviation, reach, pieces=(), kind=jnp.bfloat16):
    entries = jax.random.normal(rng, dims, jnp.float32) * deviation
    if len(pieces) > 0:
        entries = steps_of(rng, dims, pieces, -0.22, 0.18) * entries
    return jnp.clip(entries, min=-reach, max=reach).astype(kind)


def setup_inputs(seed: int = 0) -> dict:
    seeds = jax.random.split(jax.random.key(seed), 13)
    queries = noise(seeds[0], (TOKEN_TOTAL, D), 0.15, 2.0, ((0, 8), (1, 4)))
    keys = noise(seeds[1], (TOKEN_TOTAL, D), 0.15, 2.0, ((0, 8), (1, 4)))
    values = noise(seeds[2], (TOKEN_TOTAL, D), 1.0, 6.0, ((0, 8), (1, 4)))
    log_decay = draw_log_decay(jax.random.fold_in(seeds[12], 71), 0)
    residual = noise(seeds[4], (TOKEN_TOTAL, D), 1.0, 6.0, ((0, 32),))
    attn_gain = jnp.clip(1.0 + 0.15 * jax.random.normal(seeds[5], (D,), jnp.float32), 0.25, 1.75)
    moe_gain = jnp.clip(1.0 + 0.15 * jax.random.normal(seeds[6], (D,), jnp.float32), 0.25, 1.75)
    expert_ids_keys = jax.random.split(jax.random.fold_in(seeds[7], 1), TOKEN_TOTAL // TOK_DEV)
    expert_ids_turns = jax.random.permutation(jax.random.fold_in(seeds[7], 3), TOKEN_TOTAL // TOK_DEV)
    expert_ids = jax.vmap(lambda own, number: deal_out(jax.random.fold_in(seeds[7], 2), own, number, TOK_DEV, EXPERTS, 2, CAP, 2))(expert_ids_keys, expert_ids_turns).reshape((TOKEN_TOTAL, 2))
    gate_weights = jnp.clip(0.2 + 0.8 * jax.random.uniform(seeds[8], (TOKEN_TOTAL, 2), jnp.float32) ** steps_of(seeds[8], (TOKEN_TOTAL, 2), ((0, 32),), -0.2, 0.2), 0.2, 1.0)
    w_gate = noise(seeds[9], (EXPERTS, FF, D), D ** -0.5, 0.09375, ((0, 4), (1, 8)))
    w_up = noise(seeds[10], (EXPERTS, FF, D), D ** -0.5, 0.09375, ((0, 4), (1, 8)))
    w_down = noise(seeds[11], (EXPERTS, FF, D), FF ** -0.5, 0.0625, ((0, 4), (1, 8)))
    return {"queries": queries, "keys": keys, "values": values, "log_decay": log_decay, "residual": residual, "attn_gain": attn_gain, "moe_gain": moe_gain, "expert_ids": expert_ids, "gate_weights": gate_weights, "w_gate": w_gate, "w_up": w_up, "w_down": w_down}


def attend_block(state, inputs):
    q_blk, k_blk, v_blk, decay_blk = inputs
    rows = q_blk.shape[0]
    q_heads = q_blk.reshape(rows, HEAD_TOTAL, HD).astype(jnp.float32)
    k_heads = k_blk.reshape(rows, HEAD_TOTAL, HD).astype(jnp.float32)
    v_heads = v_blk.reshape(rows, HEAD_TOTAL, HD).astype(jnp.float32)
    log_cum = jnp.cumsum(decay_blk, axis=0)
    block_total = log_cum[-1]
    scores = jnp.einsum('thd,shd->hts', q_heads, k_heads)
    gap_logs = log_cum.T[:, :, None] - log_cum.T[:, None, :]
    causal_mask = (lax.broadcasted_iota(jnp.int32, (rows, rows), 0) >= lax.broadcasted_iota(jnp.int32, (rows, rows), 1))[None, :, :]
    weights = jnp.where(causal_mask, scores * jnp.exp(jnp.where(causal_mask, gap_logs, 0.0)), 0.0).astype(jnp.bfloat16)
    intra = jnp.einsum('hts,she->the', weights.astype(jnp.float32), v_heads)
    inter = jnp.exp(log_cum)[:, :, None] * jnp.einsum('thd,hde->the', q_heads, state, precision=lax.Precision.HIGHEST)
    attn = intra + inter
    keys_weighted = (k_heads * jnp.exp(block_total[None, :] - log_cum)[:, :, None]).astype(jnp.bfloat16)
    block_state = jnp.einsum('thd,the->hde', keys_weighted.astype(jnp.float32), v_heads)
    new_state = jnp.exp(block_total)[:, None, None] * state + block_state
    normed = (attn * lax.rsqrt(lax.optimization_barrier(jnp.mean(attn * attn, axis=-1, keepdims=True)) + 1e-06)).astype(jnp.bfloat16)
    return (new_state, normed.reshape(rows, HEAD_TOTAL * HD))

def route_targets(ids_block):
    flat_ids = ids_block.reshape(-1).astype(jnp.int32)
    onehot = (flat_ids[:, None] == jnp.arange(EXPERTS, dtype=jnp.int32)[None, :]).astype(jnp.int32)
    before = jnp.cumsum(onehot, axis=0) - onehot
    slot_index = lax.optimization_barrier(jnp.sum(before * onehot, axis=1)).astype(jnp.int32)
    return (flat_ids * CAP + slot_index).astype(jnp.int32)

def reference(queries, keys, values, log_decay, residual, attn_gain, moe_gain, expert_ids, gate_weights, w_gate, w_up, w_down):
    width = HEAD_TOTAL * HD
    blocks = TOKEN_TOTAL // BLOCK
    q_all = queries.reshape(blocks, BLOCK, width)
    k_all = keys.reshape(blocks, BLOCK, width)
    v_all = values.reshape(blocks, BLOCK, width)
    d_all = log_decay.reshape(blocks, BLOCK, HEAD_TOTAL)
    start_state = jnp.zeros((HEAD_TOTAL, HD, HD), jnp.float32)
    unused, normed = lax.scan(attend_block, start_state, (q_all, k_all, v_all, d_all))
    normed = normed.reshape(TOKEN_TOTAL, width)
    hidden = (residual.astype(jnp.float32) + normed.astype(jnp.float32) * attn_gain).astype(jnp.bfloat16)
    hid32 = hidden.astype(jnp.float32)
    moe_in = (hid32 * lax.rsqrt(lax.optimization_barrier(jnp.mean(hid32 * hid32, axis=-1, keepdims=True)) + 1e-06) * moe_gain).astype(jnp.bfloat16)
    groups = TOKEN_TOTAL // TOK_DEV
    moe_groups = moe_in.reshape(groups, TOK_DEV, width)
    ids_groups = expert_ids.reshape(groups, TOK_DEV * 2)
    targets = jax.vmap(route_targets)(ids_groups)

    def fill(moe_blk, target):
        doubled = jnp.repeat(moe_blk, 2, axis=0)
        return jnp.zeros((EXPERTS * CAP, width), jnp.bfloat16).at[target].set(doubled)
    buffers = jax.vmap(fill)(moe_groups, targets).reshape(groups, EXPERTS, CAP, width)
    slice_len = FF // N_SEQ

    def one_expert(index):
        rows_in = lax.dynamic_index_in_dim(buffers, index, 1, keepdims=False).reshape(groups * CAP, width).astype(jnp.float32)
        gate_mat = lax.dynamic_index_in_dim(w_gate, index, 0, keepdims=False).astype(jnp.float32)
        up_mat = lax.dynamic_index_in_dim(w_up, index, 0, keepdims=False).astype(jnp.float32)
        down_mat = lax.dynamic_index_in_dim(w_down, index, 0, keepdims=False).astype(jnp.float32)
        gate_part = jnp.dot(rows_in, gate_mat.T, preferred_element_type=jnp.float32, precision=lax.Precision.HIGHEST)
        up_part = jnp.dot(rows_in, up_mat.T, preferred_element_type=jnp.float32, precision=lax.Precision.HIGHEST)
        active = (jax.nn.silu(gate_part) * up_part).astype(jnp.bfloat16)
        active = lax.optimization_barrier(active).astype(jnp.float32)
        act_slices = active.reshape(groups * CAP, N_SEQ, slice_len).transpose(1, 0, 2)
        down_slices = down_mat.reshape(N_SEQ, slice_len, width)

        def add_slice(total, pair):
            part = jnp.dot(pair[0], pair[1], preferred_element_type=jnp.float32, precision=lax.Precision.HIGHEST).astype(jnp.bfloat16)
            return (total + part.astype(jnp.float32), None)
        total, unused_parts = lax.scan(add_slice, jnp.zeros((groups * CAP, width), jnp.float32), (act_slices, down_slices))
        return total.astype(jnp.bfloat16).reshape(groups, CAP, width)
    expert_out = lax.map(one_expert, jnp.arange(EXPERTS, dtype=jnp.int32))
    expert_out = expert_out.transpose(1, 0, 2, 3).reshape(groups, EXPERTS * CAP, width)

    def pick_rows(table, target):
        return table[target]
    picked = jax.vmap(pick_rows)(expert_out, targets).reshape(groups, TOK_DEV, 2, width)
    gates = gate_weights.reshape(groups, TOK_DEV, 2)
    mixed = hid32.reshape(groups, TOK_DEV, width) + lax.optimization_barrier(jnp.sum(gates[:, :, :, None] * picked.astype(jnp.float32), axis=2))
    return mixed.astype(jnp.bfloat16).reshape(TOKEN_TOTAL, width)
```

```python
import functools

import jax
import jax.numpy as jnp
from jax import lax
from jax.experimental import pallas as pl
from jax.experimental.pallas import tpu as pltpu
from jax.sharding import PartitionSpec as P

MESH = pl.DeviceIdType.MESH
PARTS = 2


class Place:
    def __init__(self, n_seq, n_exp):
        s, e = lax.axis_index("seq"), lax.axis_index("exp")
        self.fold, self.n_exp = n_exp // 4, n_exp
        self.length = (n_seq // 2) * self.fold
        self.p = (s // 2) * self.fold + e // 4
        self.x, self.y, self.c = s % 2, (e // 2) % 2, e % 2

    def ids(self, p, x, y, c):
        return (p // self.fold) * 2 + x, (p % self.fold) * 4 + y * 2 + c

    def block(self, p, x, y, c):
        s, e = self.ids(p, x, y, c)
        return s * self.n_exp + e

    def dev(self, dp=0, dx=0, dy=0, dc=0):
        x = 1 - self.x if dx else self.x
        y = 1 - self.y if dy else self.y
        c = 1 - self.c if dc else self.c
        return self.ids(self.p + dp, x, y, c)

    def greet(self):
        barrier = pltpu.get_barrier_semaphore()
        for d in (dict(dx=1), dict(dy=1), dict(dc=1)):
            pl.semaphore_signal(barrier, inc=1, device_id=self.dev(**d), device_id_type=MESH)

        @pl.when(self.p > 0)
        def _():
            pl.semaphore_signal(barrier, inc=1, device_id=self.dev(dp=-1), device_id_type=MESH)

        @pl.when(self.p < self.length - 1)
        def _():
            pl.semaphore_signal(barrier, inc=1, device_id=self.dev(dp=1), device_id_type=MESH)

        ends = (self.p > 0).astype(jnp.int32) + (self.p < self.length - 1).astype(jnp.int32)
        pl.semaphore_wait(barrier, 3 + ends)

    def at(self, stage, sign, k):
        if sign == 0:
            stage(0, 0, 0)
        elif sign < 0:
            pl.when(self.p >= k)(lambda: stage(2 * k - 1, -k, -1))
        else:
            pl.when(self.p + k < self.length)(lambda: stage(2 * k, k, 1))

    def far_first(self, stage):
        def one(i, carry):
            for sign in (1, -1):
                self.at(stage, sign, self.length - 1 - i)
            return carry

        if self.length <= 8:
            for i in range(self.length - 1):
                one(i, 0)
        else:
            lax.fori_loop(0, self.length - 1, one, 0)
        self.at(stage, 0, 0)

    def near_first(self, *stages):
        depth = len(stages)

        def ring(stage, k):
            if isinstance(k, int) and k == 0:
                self.at(stage, 0, 0)
            else:
                for sign in (-1, 1):
                    self.at(stage, sign, k)

        def step(k):
            for j, stage in enumerate(stages):
                if 0 <= k - j < self.length:
                    ring(stage, k - j)

        total = self.length + depth - 1
        if self.length <= 8:
            for k in range(total):
                step(k)
            return
        for k in range(depth):
            step(k)

        def one(k, carry):
            for j, stage in enumerate(stages):
                ring(stage, k - j)
            return carry

        lax.fori_loop(depth, self.length, one, 0)
        for k in range(self.length, total):
            step(k)


def gather_kernel(n_seq, n_exp, x_ref, g_ref, out_ref, gout_ref, send, recv, loc):
    me = Place(n_seq, n_exp)
    rows, width = x_ref.shape
    grow = g_ref.shape[0]
    me.greet()

    def place(ref, off, dx, dy, dc=0):
        x = 1 - me.x if dx else me.x
        y = 1 - me.y if dy else me.y
        c = 1 - me.c if dc else me.c
        b = me.block(me.p + off, x, y, c)
        n = rows if ref is out_ref else grow
        return ref.at[pl.ds(pl.multiple_of(b * n, n), n)]

    def copies(part, kind, slot, off, dx, dy, to, own=False, half=None, dc=0):
        dst_x, dst_g = place(out_ref, off, dx, dy, dc), place(gout_ref, off, dx, dy, dc)
        src_x, src_g = (x_ref, g_ref) if own else (dst_x, dst_g)
        span = width // PARTS
        if half is None:
            cols = pl.ds(part * span, span)
        else:
            cols = pl.ds(part * span + half * (span // 2), span // 2)
        out = [
            pltpu.make_async_remote_copy(
                src_x.at[:, cols],
                dst_x.at[:, cols],
                send.at[kind, slot, part],
                recv.at[kind, slot, part],
                to,
                MESH,
            )
        ]
        if half != 1 and part == 0:
            out.append(
                pltpu.make_async_remote_copy(
                    src_g, dst_g, send.at[kind, slot, PARTS], recv.at[kind, slot, PARTS], to, MESH
                )
            )
        return out

    def start(*a, **k):
        for cp in copies(*a, **k):
            cp.start()

    def wait_recv(*a, **k):
        for cp in copies(*a, **k):
            cp.wait_recv()

    def wait_send(*a, **k):
        for cp in copies(*a, **k):
            cp.wait_send()

    left, right = dict(dp=-1), dict(dp=1)
    X, Y, C = me.dev(dx=1), me.dev(dy=1), me.dev(dc=1)

    def line_sends(off, sign, do):
        own = sign == 0
        if sign <= 0:
            pl.when(me.p + 1 < me.length)(
                lambda: do(0, 2 * (-off + 1) - 1, off, 0, 0, me.dev(**right), own=own)
            )
        if sign >= 0:
            pl.when(me.p > 0)(lambda: do(0, 2 * (off + 1), off, 0, 0, me.dev(**left), own=own))

    def stage_line(slot, off, sign, do):
        own = sign == 0
        line_sends(off, sign, do)
        do(1, slot, off, 0, 0, X, own=own)
        do(2, slot, off, 0, 0, Y, own=own)
        do(5, slot, off, 0, 0, C, own=own)

    def stage_xy_1(slot, off, do):
        do(3, slot, off, 1, 0, Y, half=0)
        do(6, slot, off, 1, 0, C)

    def stage_xy_2(slot, off, do):
        do(4, slot, off, 0, 1, X, half=1)
        do(7, slot, off, 0, 1, C)

    def stage_diag(slot, off, do):
        do(8, slot, off, 1, 1, C)

    local = [
        pltpu.make_async_copy(x_ref, place(out_ref, 0, 0, 0), loc.at[0]),
        pltpu.make_async_copy(g_ref, place(gout_ref, 0, 0, 0), loc.at[1]),
    ]
    for cp in local:
        cp.start()

    def s1(slot, off, sign):
        for part in range(PARTS):
            if sign:
                wait_recv(part, 0, slot, off, 0, 0, X)
            stage_line(slot, off, sign, functools.partial(start, part))

    def s2(slot, off, sign):
        for part in range(PARTS):
            wait_recv(part, 1, slot, off, 1, 0, X)
            stage_xy_1(slot, off, functools.partial(start, part))
            wait_recv(part, 2, slot, off, 0, 1, X)
            stage_xy_2(slot, off, functools.partial(start, part))

    def s3(slot, off, sign):
        for part in range(PARTS):
            wait_recv(part, 3, slot, off, 1, 1, X, half=0)
            wait_recv(part, 4, slot, off, 1, 1, X, half=1)
            stage_diag(slot, off, functools.partial(start, part))

    me.near_first(s1, s2, s3)

    def s4(slot, off, sign):
        for part in range(PARTS):
            done = functools.partial(wait_send, part)
            stage_line(slot, off, sign, done)
            stage_xy_1(slot, off, done)
            stage_xy_2(slot, off, done)
            stage_diag(slot, off, done)
            wait_recv(part, 5, slot, off, 0, 0, X, dc=1)
            wait_recv(part, 6, slot, off, 1, 0, X, dc=1)
            wait_recv(part, 7, slot, off, 0, 1, X, dc=1)
            wait_recv(part, 8, slot, off, 1, 1, X, dc=1)

    me.near_first(s4)
    for cp in local:
        cp.wait()


def gather_all(x, g, n_seq, n_exp):
    n = n_seq * n_exp
    length = n // 8
    anyspace = pl.BlockSpec(memory_space=pl.ANY)
    return pl.pallas_call(
        functools.partial(gather_kernel, n_seq, n_exp),
        out_shape=(
            jax.ShapeDtypeStruct((n * x.shape[0], x.shape[1]), x.dtype),
            jax.ShapeDtypeStruct((n * g.shape[0], g.shape[1]), g.dtype),
        ),
        in_specs=[anyspace, anyspace],
        out_specs=(anyspace, anyspace),
        scratch_shapes=[
            pltpu.SemaphoreType.DMA((9, 2 * length + 1, PARTS + 1)),
            pltpu.SemaphoreType.DMA((9, 2 * length + 1, PARTS + 1)),
            pltpu.SemaphoreType.DMA((2,)),
        ],
        compiler_params=pltpu.CompilerParams(collective_id=1, has_side_effects=True),
    )(x, g)


def scatter_kernel(
    n_seq, n_exp, y_ref, out_ref, acc, sib, xbuf, ybuf, dab, dbb, line, send, recv, loc
):
    me = Place(n_seq, n_exp)
    L = me.length
    rows, width = out_ref.shape
    halfw = width // 2
    me.greet()
    X, Y, C = me.dev(dx=1), me.dev(dy=1), me.dev(dc=1)

    def src(off, grp, dc):
        x = 1 - me.x if grp & 1 else me.x
        y = 1 - me.y if grp & 2 else me.y
        c = 1 - me.c if dc else me.c
        b = me.block(me.p + off, x, y, c)
        return y_ref.at[pl.ds(pl.multiple_of(b * rows, rows), rows)]

    def sib_copy(slot, off, grp):
        return pltpu.make_async_remote_copy(
            src(off, grp, 1), sib.at[grp, slot], send.at[grp, slot], recv.at[grp, slot], C, MESH
        )

    def load(slot, off, grp):
        return pltpu.make_async_copy(src(off, grp, 0), acc.at[grp, slot], loc.at[grp, slot])

    for grp in (3, 1, 2, 0):

        def go(slot, off, sign, grp=grp):
            sib_copy(slot, off, grp).start()
            load(slot, off, grp).start()

        me.far_first(go)

    f32 = jnp.float32

    def pair_sum(slot, off, grp):
        load(slot, off, grp).wait()
        sib_copy(slot, off, grp).wait_recv()
        return acc[grp, slot].astype(f32) + sib[grp, slot].astype(f32)

    def diag_a(slot):
        return pltpu.make_async_remote_copy(
            acc.at[3, slot, :, pl.ds(0, halfw)], dab.at[slot], send.at[4, slot], recv.at[4, slot], Y, MESH
        )

    def diag_b(slot):
        return pltpu.make_async_remote_copy(
            acc.at[3, slot, :, pl.ds(halfw, halfw)], dbb.at[slot], send.at[5, slot], recv.at[5, slot], X, MESH
        )

    def x_copy(slot):
        return pltpu.make_async_remote_copy(
            acc.at[1, slot], xbuf.at[slot], send.at[6, slot], recv.at[6, slot], X, MESH
        )

    def y_copy(slot):
        return pltpu.make_async_remote_copy(
            acc.at[2, slot], ybuf.at[slot], send.at[7, slot], recv.at[7, slot], Y, MESH
        )

    def line_copy(slot, sign):
        return pltpu.make_async_remote_copy(
            acc.at[0, slot],
            line.at[slot],
            send.at[8, slot],
            recv.at[8, slot],
            me.dev(dp=sign),
            MESH,
        )

    def d1(slot, off, sign):
        acc[3, slot] = pair_sum(slot, off, 3).astype(acc.dtype)
        diag_a(slot).start()
        diag_b(slot).start()

    def d2(slot, off, sign):
        sx = pair_sum(slot, off, 1)
        diag_a(slot).wait_recv()
        acc[1, slot, :, pl.ds(0, halfw)] = (sx[:, :halfw] + dab[slot].astype(f32)).astype(acc.dtype)
        acc[1, slot, :, pl.ds(halfw, halfw)] = sx[:, halfw:].astype(acc.dtype)
        x_copy(slot).start()
        sy = pair_sum(slot, off, 2)
        diag_b(slot).wait_recv()
        acc[2, slot, :, pl.ds(0, halfw)] = sy[:, :halfw].astype(acc.dtype)
        acc[2, slot, :, pl.ds(halfw, halfw)] = (sy[:, halfw:] + dbb[slot].astype(f32)).astype(acc.dtype)
        y_copy(slot).start()

    def d3(slot, off, sign):
        total = pair_sum(slot, off, 0)
        x_copy(slot).wait_recv()
        y_copy(slot).wait_recv()
        total = total + xbuf[slot].astype(f32) + ybuf[slot].astype(f32)
        if sign == 0:
            out_ref[...] = total
            if L > 1:

                @pl.when(me.p > 0)
                def _():
                    in_copy(2).wait_recv()
                    out_ref[...] += line[2].astype(f32)

                @pl.when(me.p < L - 1)
                def _():
                    in_copy(1).wait_recv()
                    out_ref[...] += line[1].astype(f32)

            return
        acc[0, slot] = total.astype(acc.dtype)
        far = slot + 2
        behind = me.p > 0 if sign > 0 else me.p < L - 1

        @pl.when(jnp.logical_and(behind, sign * off + 1 < L))
        def _():
            in_copy(far).wait_recv()
            acc[0, slot] = (acc[0, slot].astype(f32) + line[far].astype(f32)).astype(acc.dtype)

        line_copy(slot, sign).start()

    def in_copy(slot):
        return pltpu.make_async_remote_copy(
            acc.at[0, slot], line.at[slot], send.at[8, slot], recv.at[8, slot], X, MESH
        )

    me.far_first(d1)
    me.far_first(d2)
    me.far_first(d3)

    def fin(slot, off, sign):
        for grp in range(4):
            sib_copy(slot, off, grp).wait_send()
        diag_a(slot).wait_send()
        diag_b(slot).wait_send()
        x_copy(slot).wait_send()
        y_copy(slot).wait_send()
        if sign:
            line_copy(slot, sign).wait_send()

    me.far_first(fin)


def scatter_sum(part, n_seq, n_exp):
    n = n_seq * n_exp
    slots = n // 4 - 1 + 2
    rows, width = part.shape[0] // n, part.shape[1]
    bf = jnp.bfloat16
    return pl.pallas_call(
        functools.partial(scatter_kernel, n_seq, n_exp),
        out_shape=jax.ShapeDtypeStruct((rows, width), jnp.float32),
        in_specs=[pl.BlockSpec(memory_space=pl.ANY)],
        out_specs=pl.BlockSpec(memory_space=pltpu.VMEM),
        scratch_shapes=[
            pltpu.VMEM((4, slots, rows, width), bf),
            pltpu.VMEM((4, slots, rows, width), bf),
            pltpu.VMEM((slots, rows, width), bf),
            pltpu.VMEM((slots, rows, width), bf),
            pltpu.VMEM((slots, rows, width // 2), bf),
            pltpu.VMEM((slots, rows, width // 2), bf),
            pltpu.VMEM((slots, rows, width), bf),
            pltpu.SemaphoreType.DMA((9, slots)),
            pltpu.SemaphoreType.DMA((9, slots)),
            pltpu.SemaphoreType.DMA((4, slots)),
        ],
        compiler_params=pltpu.CompilerParams(
            collective_id=2, has_side_effects=True, vmem_limit_bytes=60 * 2**20
        ),
    )(part)


GPARTS = 2
HPARTS = 4


def plane_orders(length):
    visit = []
    for p in range(length):
        visit.append(sorted(range(length), key=lambda q: (abs(q - p), q)))
    lines = []
    for p in range(length):
        def ready(q):
            chain = range(0, p + 1) if q > p else range(p, length)
            return max(visit[b].index(q) for b in chain)

        low = 2 * p < length
        lines.append(sorted((q for q in range(length) if q != p), key=lambda q: (ready(q), -q if low else q)))
    return visit, lines


def pick(table, p, j):
    total = 0
    for a, row in enumerate(table):
        for b, v in enumerate(row):
            hit = jnp.logical_and(p == a, j == b).astype(jnp.int32)
            total = total + hit * v
    return total


def spans(tiles, parts):
    cuts = [(tiles * i // parts) * 128 for i in range(parts + 1)]
    return [pl.ds(a, b - a) for a, b in zip(cuts[:-1], cuts[1:])]


def when(cond, fn):
    def run():
        fn()

    pl.when(cond)(run)


def moe_kernel(
    n_seq, n_exp, x_ref, hid_ref, wg_ref, wu_ref, wd_ref, out_ref,
    xs, ys, act, sib, din, xin, yin, lin, tot, wg, wu, wd,
    gsend, grecv, bsend, brecv, ssend, srecv, loc,
):
    me = Place(n_seq, n_exp)
    L, p = me.length, me.p
    rows, width = out_ref.shape
    hidden = wg.shape[0]
    many = 8 * rows
    f32, bf = jnp.float32, jnp.bfloat16
    X, Y, C = me.dev(dx=1), me.dev(dy=1), me.dev(dc=1)
    visit, lines = plane_orders(L)
    gcols = spans(x_ref.shape[1] // 128, GPARTS)
    hcols = spans(width // 128, HPARTS)

    loads = [
        pltpu.make_async_copy(a.at[0], b, loc.at[i])
        for i, (a, b) in enumerate(((wg_ref, wg), (wu_ref, wu), (wd_ref, wd)))
    ]
    for cp in loads:
        cp.start()

    def flip(v, d):
        return 1 - v if d else v

    def row(q, dx=0, dy=0, dc=0):
        k = (flip(me.c, dc) * 2 + flip(me.x, dx)) * 2 + flip(me.y, dy)
        return pl.ds(pl.multiple_of((q * 8 + k) * rows, rows), rows)

    def srow(q, dx=0, dy=0):
        k = flip(me.x, dx) * 2 + flip(me.y, dy)
        return pl.ds(pl.multiple_of((q * 4 + k) * rows, rows), rows)

    def prow(q):
        return pl.ds(pl.multiple_of(q * rows, rows), rows)

    def gcopy(kind, q, part, r, to, skind=None):
        ref = xs.at[r, gcols[part]]
        skind = kind if skind is None else skind
        return pltpu.make_async_remote_copy(
            ref, ref, gsend.at[skind, q, part], grecv.at[kind, q, part], to, MESH
        )

    upper = GPARTS // 2

    def line_pair(q, part, do):
        pl.when(jnp.logical_and(q >= p, p > 0))(
            lambda: do(gcopy(0, q, part, row(q), me.dev(dp=-1)))
        )
        pl.when(jnp.logical_and(q <= p, p + 1 < L))(
            lambda: do(gcopy(0, q, part, row(q), me.dev(dp=1), 9))
        )

    def start(cp):
        cp.start()

    def g_line(q, part):
        pl.when(q != p)(lambda: gcopy(0, q, part, row(q), X).wait_recv())
        line_pair(q, part, start)

    def first(q, part):
        return [gcopy(1, q, part, row(q), X), gcopy(2, q, part, row(q), Y), gcopy(5, q, part, row(q), C)]

    def second_x(q, part):
        out = [gcopy(6, q, part, row(q, 1, 0), C)]
        return out if part >= upper else [gcopy(3, q, part, row(q, 1, 0), Y)] + out

    def second_y(q, part):
        out = [gcopy(7, q, part, row(q, 0, 1), C)]
        return out if part < upper else [gcopy(4, q, part, row(q, 0, 1), X)] + out

    def third(q, part):
        return [gcopy(8, q, part, row(q, 1, 1), C)]

    def g_first(q, part):
        for cp in first(q, part):
            cp.start()

    def g_second(q, part):
        gcopy(1, q, part, row(q, 1, 0), X).wait_recv()
        for cp in second_x(q, part):
            cp.start()
        gcopy(2, q, part, row(q, 0, 1), X).wait_recv()
        for cp in second_y(q, part):
            cp.start()

    def g_third(q, part):
        gcopy(3 if part < upper else 4, q, part, row(q, 1, 1), X).wait_recv()
        for cp in third(q, part):
            cp.start()

    def g_done(q):
        for part in range(GPARTS):
            gcopy(5, q, part, row(q, 0, 0, 1), X).wait_recv()
            gcopy(6, q, part, row(q, 1, 0, 1), X).wait_recv()
            gcopy(7, q, part, row(q, 0, 1, 1), X).wait_recv()
            gcopy(8, q, part, row(q, 1, 1, 1), X).wait_recv()

    def g_drain(q):
        for part in range(GPARTS):
            line_pair(q, part, lambda cp: cp.wait_send())
            for cp in first(q, part) + second_x(q, part) + second_y(q, part) + third(q, part):
                cp.wait_send()

    def sib_copy(q, h):
        r = pl.ds(pl.multiple_of((q * 2 + 1 - me.c) * 4 * rows, 4 * rows), 4 * rows)
        d = pl.ds(pl.multiple_of(q * 4 * rows, 4 * rows), 4 * rows)
        return pltpu.make_async_remote_copy(
            ys.at[r, hcols[h]], sib.at[d, hcols[h]], bsend.at[q, h], brecv.at[q, h], C, MESH
        )

    def scopy(kind, q, h, r, dst, d, to):
        return pltpu.make_async_remote_copy(
            ys.at[r, hcols[h]], dst.at[d, hcols[h]], ssend.at[kind, q, h], srecv.at[kind, q, h], to, MESH
        )

    def diag_copy(q, h):
        return scopy(0, q, h, row(q, 1, 1), din, prow(q), Y if 2 * h < HPARTS else X)

    def x_copy(q, h):
        return scopy(1, q, h, row(q, 1, 0), xin, prow(q), X)

    def y_copy(q, h):
        return scopy(2, q, h, row(q, 0, 1), yin, prow(q), Y)

    def line_copy(q, h):
        up = (q > p).astype(jnp.int32)
        last = jnp.logical_and(q < p, q == p - 1).astype(jnp.int32)
        slot = q + (L - q) * last
        return pltpu.make_async_remote_copy(
            ys.at[row(q), hcols[h]],
            lin.at[prow(slot), hcols[h]],
            ssend.at[3, q, h],
            srecv.at[3, slot, h],
            me.dev(dp=2 * up - 1),
            MESH,
        )

    def line_in(slot, h):
        return pltpu.make_async_remote_copy(
            ys.at[row(p), hcols[h]], lin.at[prow(slot), hcols[h]], ssend.at[3, p, h], srecv.at[3, slot, h], X, MESH
        )

    def pair(q, h, dx, dy):
        return ys[row(q, dx, dy), hcols[h]].astype(f32) + sib[srow(q, dx, dy), hcols[h]].astype(f32)

    def r_first(q, h):
        sib_copy(q, h).wait_recv()
        ys[row(q, 1, 1), hcols[h]] = pair(q, h, 1, 1).astype(bf)
        diag_copy(q, h).start()

    def r_second(q, h):
        sx, sy = pair(q, h, 1, 0), pair(q, h, 0, 1)
        diag_copy(q, h).wait_recv()
        more = din[prow(q), hcols[h]].astype(f32)
        if 2 * h < HPARTS:
            sx = sx + more
        else:
            sy = sy + more
        ys[row(q, 1, 0), hcols[h]] = sx.astype(bf)
        x_copy(q, h).start()
        ys[row(q, 0, 1), hcols[h]] = sy.astype(bf)
        y_copy(q, h).start()

    def r_third(q, h):
        total = pair(q, h, 0, 0)
        x_copy(q, h).wait_recv()
        y_copy(q, h).wait_recv()
        total = total + xin[prow(q), hcols[h]].astype(f32) + yin[prow(q), hcols[h]].astype(f32)
        tot[prow(q), hcols[h]] = total

    def r_line(q, h):
        behind = jnp.logical_or(jnp.logical_and(q > p, p > 0), jnp.logical_and(q < p, p < L - 1))

        @pl.when(behind)
        def _():
            line_in(q, h).wait_recv()
            ys[row(q), hcols[h]] = (tot[prow(q), hcols[h]] + lin[prow(q), hcols[h]].astype(f32)).astype(bf)

        @pl.when(jnp.logical_not(behind))
        def _():
            ys[row(q), hcols[h]] = tot[prow(q), hcols[h]].astype(bf)

        line_copy(q, h).start()

    def r_last(h):
        cols = hcols[h]

        @pl.when(p > 0)
        def _():
            line_in(p, h).wait_recv()
            tot[prow(p), cols] += lin[prow(p), cols].astype(f32)

        @pl.when(p < L - 1)
        def _():
            line_in(L, h).wait_recv()
            tot[prow(p), cols] += lin[prow(L), cols].astype(f32)

        out_ref[:, cols] = (hid_ref[:, cols].astype(f32) + tot[prow(p), cols]).astype(bf)

    at_end = jnp.logical_or(p == 0, p == L - 1)

    def r_early(q, h):
        pl.when(jnp.logical_and(at_end, q != p))(lambda: r_line(q, h))

    def r_drain(q):
        for h in range(HPARTS):
            sib_copy(q, h).wait_send()
            diag_copy(q, h).wait_send()
            x_copy(q, h).wait_send()
            y_copy(q, h).wait_send()
            pl.when(q != p)(lambda: line_copy(q, h).wait_send())

    tile = next(t for t in range(512, 0, -128) if hidden % t == 0)
    fsteps = hidden // tile

    def block_of(q):
        return pl.ds(pl.multiple_of(q * many, many), many)

    def gate_of(q):
        extra = xs[block_of(q), width : width + 128].astype(f32)
        lane = lax.broadcasted_iota(jnp.int32, extra.shape, 1)
        e = lax.axis_index("exp")
        keep = jnp.logical_or(lane == e, lane == e + 64)
        return jnp.sum(jnp.where(keep, extra, 0.0), axis=1, keepdims=True)

    nt = (((1,), (1,)), ((), ()))

    def ffn_in(q, f):
        fc = pl.ds(f * tile, tile)
        rows_in = xs[block_of(q), 0:width]
        gate = lax.dot_general(rows_in, wg[fc, :], nt, preferred_element_type=f32)
        up = lax.dot_general(rows_in, wu[fc, :], nt, preferred_element_type=f32)
        act[:, fc] = (gate / (1.0 + jnp.exp(-gate)) * up * gate_of(q)).astype(bf)

    def ffn_out(q, h):
        ys[block_of(q), hcols[h]] = jnp.dot(
            act[...], wd[:, hcols[h]], preferred_element_type=f32
        ).astype(bf)
        sib_copy(q, h).start()

    me.greet()
    xs[row(p), :] = x_ref[...]
    plane = [pick(visit, p, j) for j in range(min(3, L))]
    for part in range(GPARTS):
        g_line(plane[0], part)
        g_first(plane[0], part)
    for part in range(GPARTS):
        g_second(plane[0], part)
        if L > 1:
            g_line(plane[1], part)
            g_first(plane[1], part)
    for part in range(GPARTS):
        g_third(plane[0], part)
    if L > 2:
        for part in range(GPARTS):
            g_line(plane[2], part)
            g_first(plane[2], part)
    for cp in loads:
        cp.wait()

    def chunk(j, carry):
        q, nxt, prev = pick(visit, p, j), pick(visit, p, j + 1), pick(visit, p, j - 1)
        far = pick(visit, p, j + 3)

        def ahead(fn):
            when(j + 1 < L, fn)

        def after(fn):
            when(j > 0, fn)

        def hook(n):
            if n == 0:
                after(lambda: (r_second(prev, 0), r_second(prev, 1)))
                ahead(lambda: g_second(nxt, 0))
            if n == 1:
                after(lambda: (r_second(prev, 2), r_second(prev, 3)))
                ahead(lambda: [g_second(nxt, part) for part in range(1, GPARTS)])

                @pl.when(j + 3 < L)
                def _():
                    for part in range(GPARTS):
                        g_line(far, part)
                        g_first(far, part)

            if n == 2:
                after(lambda: (r_third(prev, 0), r_early(prev, 0), r_third(prev, 1), r_early(prev, 1)))
                ahead(lambda: [g_third(nxt, part) for part in range(GPARTS)])

        g_done(q)
        after(lambda: r_first(prev, HPARTS - 1))
        for f in range(fsteps):
            ffn_in(q, f)
            hook(f)
        for f in range(fsteps, 3):
            hook(f)
        for h in range(HPARTS):
            ffn_out(q, h)
            if h:
                r_first(q, h - 1)
            if h == 1:
                after(lambda: (r_third(prev, 2), r_early(prev, 2)))
            if h == 2:
                after(lambda: (r_third(prev, 3), r_early(prev, 3)))
        return carry

    lax.fori_loop(0, L, chunk, 0)

    final = pick(visit, p, L - 1)
    inner = jnp.logical_not(at_end)
    r_first(final, HPARTS - 1)
    for h in range(HPARTS):
        r_second(final, h)

    def one_line(i, hs):
        q = pick(lines, p, i)

        @pl.when(inner)
        def _():
            for h in hs:
                r_line(q, h)

    if L > 2:
        one_line(0, range(HPARTS))
    for h in range(HPARTS):
        r_third(final, h)
        r_early(final, h)
    for i in range(1, L - 1):
        one_line(i, range(HPARTS))
    for h in range(HPARTS):
        r_last(h)

    def drain(q, carry):
        g_drain(q)
        r_drain(q)
        return carry

    lax.fori_loop(0, L, drain, 0)


def moe_scratch(n_seq, n_exp, x_shape, w_shape):
    n, L = n_seq * n_exp, n_seq * n_exp // 8
    rows, wide = x_shape
    hidden, width = w_shape[1:]
    bf, f32 = jnp.bfloat16, jnp.float32
    return [
        ((n * rows, wide), bf),
        ((n * rows, width), bf),
        ((8 * rows, hidden), bf),
        ((n // 2 * rows, width), bf),
        ((L * rows, width), bf),
        ((L * rows, width), bf),
        ((L * rows, width), bf),
        ((L * rows + rows, width), bf),
        ((L * rows, width), f32),
        ((hidden, width), bf),
        ((hidden, width), bf),
        ((hidden, width), bf),
    ]


MOE_VMEM = 60 * 2**20


def moe_fits(n_seq, n_exp, x_shape, w_shape):
    need = sum(a * b * jnp.dtype(t).itemsize for (a, b), t in moe_scratch(n_seq, n_exp, x_shape, w_shape))
    return (
        w_shape[0] == 1
        and n_exp <= 64
        and w_shape[1] % 128 == 0
        and w_shape[2] % (128 * HPARTS) == 0
        and need + 5 * 2**20 <= MOE_VMEM
    )


def moe_layer(x, hid, w_gate, w_up, w_down, n_seq, n_exp):
    L = n_seq * n_exp // 8
    vmem = pl.BlockSpec(memory_space=pltpu.VMEM)
    anyspace = pl.BlockSpec(memory_space=pl.ANY)
    dma = pltpu.SemaphoreType.DMA
    return pl.pallas_call(
        functools.partial(moe_kernel, n_seq, n_exp),
        out_shape=jax.ShapeDtypeStruct(hid.shape, jnp.bfloat16),
        in_specs=[vmem, vmem, anyspace, anyspace, anyspace],
        out_specs=vmem,
        scratch_shapes=[
            pltpu.VMEM(s, t) for s, t in moe_scratch(n_seq, n_exp, x.shape, w_gate.shape)
        ]
        + [
            dma((10, L, GPARTS)),
            dma((10, L, GPARTS)),
            dma((L, HPARTS)),
            dma((L, HPARTS)),
            dma((4, L + 1, HPARTS)),
            dma((4, L + 1, HPARTS)),
            dma((3,)),
        ],
        compiler_params=pltpu.CompilerParams(
            collective_id=5, has_side_effects=True, vmem_limit_bytes=MOE_VMEM
        ),
    )(x, hid, w_gate, w_up, w_down)


def carry_kernel(n_seq, own_ref, own16_ref, tot_ref, out_ref, peer, ptot, cin, cout, send, recv, tsem):
    s, e = lax.axis_index("seq"), lax.axis_index("exp")
    z, odd, deep = s // 2, s % 2, n_seq // 2
    heads = own_ref.shape[0]
    pair = (z * 2 + 1 - odd, e)

    barrier = pltpu.get_barrier_semaphore()
    pl.semaphore_signal(barrier, inc=1, device_id=pair, device_id_type=MESH)

    @pl.when(z > 0)
    def _():
        pl.semaphore_signal(barrier, inc=1, device_id=(s - 2, e), device_id_type=MESH)

    @pl.when(z < deep - 1)
    def _():
        pl.semaphore_signal(barrier, inc=1, device_id=(s + 2, e), device_id_type=MESH)

    ends = (z > 0).astype(jnp.int32) + (z < deep - 1).astype(jnp.int32)
    pl.semaphore_wait(barrier, 1 + ends)

    tot_copy = pltpu.make_async_remote_copy(tot_ref, ptot, tsem.at[0], tsem.at[1], pair, MESH)

    def pair_copy(h):
        return pltpu.make_async_remote_copy(
            own16_ref.at[h], peer.at[h], send.at[0, h], recv.at[0, h], pair, MESH
        )

    def line_copy(h):
        return pltpu.make_async_remote_copy(
            cout.at[h], cin.at[h], send.at[1, h], recv.at[1, h], (s + 2, e), MESH
        )

    tot_copy.start()
    for h in range(heads):
        pair_copy(h).start()

    @pl.when(z == 0)
    def _():
        cin[...] = jnp.zeros_like(cin)

    tot_copy.wait_recv()
    mine, other = tot_ref[...], ptot[...]
    both = jnp.exp(mine + other)
    is_odd = jnp.full(mine.shape, odd, jnp.int32) == 1
    one = jnp.ones_like(mine)
    own_by = jnp.where(is_odd, one, jnp.exp(other))
    peer_by = jnp.where(is_odd, jnp.exp(mine), one)
    carry_by = jnp.where(is_odd, jnp.exp(other), one)
    peer_in = jnp.where(is_odd, one, jnp.zeros_like(mine))
    for h in range(heads):
        pair_copy(h).wait_recv()

        @pl.when(z > 0)
        def _():
            line_copy(h).wait_recv()

        near = peer[h].astype(jnp.float32)
        come = cin[h].astype(jnp.float32)

        @pl.when(z < deep - 1)
        def _():
            cout[h] = (
                both[h : h + 1] * come + own_by[h : h + 1] * own_ref[h] + peer_by[h : h + 1] * near
            ).astype(cout.dtype)
            line_copy(h).start()

        out_ref[h] = carry_by[h : h + 1] * come + peer_in[h : h + 1] * near

    tot_copy.wait_send()
    for h in range(heads):
        pair_copy(h).wait_send()

        @pl.when(z < deep - 1)
        def _():
            line_copy(h).wait_send()


def carried_in(block_total, block_state, n_seq):
    heads, dim, _ = block_state.shape
    bf = jnp.bfloat16
    tile = jnp.pad(block_total, (0, -heads % 8))
    tile = jnp.broadcast_to(tile[:, None], (tile.shape[0], dim))
    vmem = pl.BlockSpec(memory_space=pltpu.VMEM)
    return pl.pallas_call(
        functools.partial(carry_kernel, n_seq),
        out_shape=jax.ShapeDtypeStruct(block_state.shape, jnp.float32),
        in_specs=[vmem] * 3,
        out_specs=vmem,
        scratch_shapes=[
            pltpu.VMEM(block_state.shape, bf),
            pltpu.VMEM(tile.shape, jnp.float32),
            pltpu.VMEM(block_state.shape, bf),
            pltpu.VMEM(block_state.shape, bf),
            pltpu.SemaphoreType.DMA((2, heads)),
            pltpu.SemaphoreType.DMA((2, heads)),
            pltpu.SemaphoreType.DMA((2,)),
        ],
        compiler_params=pltpu.CompilerParams(collective_id=3, has_side_effects=True),
    )(block_state, block_state.astype(bf), tile)


def mix_kernel(n_exp, normed_ref, res_ref, again_ref, mgain_ref, tile_ref, hid_ref, in_ref, tok, send, recv, loc):
    s, e = lax.axis_index("seq"), lax.axis_index("exp")
    rows, width = res_ref.shape[0], normed_ref.shape[1]

    barrier = pltpu.get_barrier_semaphore()
    for k in range(1, n_exp):
        pl.semaphore_signal(
            barrier, inc=1, device_id=(s, lax.rem(e + k, n_exp)), device_id_type=MESH
        )
    pl.semaphore_wait(barrier, n_exp - 1)

    def source(peer):
        return normed_ref.at[pl.ds(pl.multiple_of(peer * rows, rows), rows)]

    own = pltpu.make_async_copy(source(e), tok.at[e], loc.at[0])

    def copy(k):
        peer = lax.rem(e + k, n_exp)
        return pltpu.make_async_remote_copy(
            source(peer), tok.at[e], send.at[k], recv.at[k], (s, peer), MESH
        )

    def arriving(k):
        sender = lax.rem(e + n_exp - k, n_exp)
        return pltpu.make_async_remote_copy(
            source(e), tok.at[sender], send.at[k], recv.at[k], (s, sender), MESH
        )

    for k in range(1, n_exp):
        copy(k).start()
    own.start()
    own.wait()
    for k in range(1, n_exp):
        arriving(k).wait_recv()
    in_ref[:, n_exp * width :] = tile_ref[...]
    square = jnp.zeros((rows, 1), jnp.float32)
    for j in range(n_exp):
        cols = pl.ds(j * width, width)
        hid = (
            res_ref[:, cols].astype(jnp.float32)
            + tok[j].astype(jnp.float32) * again_ref[:, cols]
        ).astype(jnp.bfloat16)
        hid_ref[:, cols] = hid
        wide = hid.astype(jnp.float32)
        square = square + jnp.sum(wide * wide, axis=1, keepdims=True)
    scale = lax.rsqrt(square / (n_exp * width) + 1e-06)
    for j in range(n_exp):
        cols = pl.ds(j * width, width)
        in_ref[:, cols] = (
            hid_ref[:, cols].astype(jnp.float32) * scale * mgain_ref[:, cols]
        ).astype(jnp.bfloat16)
    for k in range(1, n_exp):
        copy(k).wait_send()


def mix_tokens(normed, residual, attn_gain, moe_gain, tile, n_exp):
    vmem = pl.BlockSpec(memory_space=pltpu.VMEM)
    return pl.pallas_call(
        functools.partial(mix_kernel, n_exp),
        out_shape=(
            jax.ShapeDtypeStruct(residual.shape, jnp.bfloat16),
            jax.ShapeDtypeStruct(
                (residual.shape[0], residual.shape[1] + tile.shape[1]), jnp.bfloat16
            ),
        ),
        in_specs=[vmem] * 5,
        out_specs=(vmem, vmem),
        scratch_shapes=[
            pltpu.VMEM((n_exp, residual.shape[0], normed.shape[1]), jnp.bfloat16),
            pltpu.SemaphoreType.DMA((n_exp,)),
            pltpu.SemaphoreType.DMA((n_exp,)),
            pltpu.SemaphoreType.DMA((1,)),
        ],
        compiler_params=pltpu.CompilerParams(collective_id=4, has_side_effects=True),
    )(normed, residual, attn_gain[None, :], moe_gain[None, :], tile)


def body(
    queries,
    keys,
    values,
    log_decay,
    residual,
    attn_gain,
    moe_gain,
    expert_ids,
    gate_weights,
    w_gate,
    w_up,
    w_down,
):
    rows = queries.shape[0]
    heads = log_decay.shape[1]
    head_dim = queries.shape[1] // heads
    q_heads = queries.reshape(rows, heads, head_dim)
    k_heads = keys.reshape(rows, heads, head_dim)
    v_heads = values.reshape(rows, heads, head_dim)
    upto = (
        lax.broadcasted_iota(jnp.int32, (rows, rows), 0)
        >= lax.broadcasted_iota(jnp.int32, (rows, rows), 1)
    ).astype(jnp.float32)
    log_cum = jnp.dot(upto, log_decay, precision=lax.Precision.HIGHEST)
    block_total = log_cum[-1]
    keys_weighted = (k_heads * jnp.exp(block_total[None, :] - log_cum)[:, :, None]).astype(
        jnp.bfloat16
    )
    block_state = jnp.einsum(
        "thd,the->hde", keys_weighted, v_heads, preferred_element_type=jnp.float32
    )
    carried = carried_in(block_total, block_state, lax.axis_size("seq"))
    scores = jnp.einsum("thd,shd->hts", q_heads, k_heads, preferred_element_type=jnp.float32)
    gap_logs = log_cum.T[:, :, None] - log_cum.T[:, None, :]
    causal_mask = (
        lax.broadcasted_iota(jnp.int32, (rows, rows), 0)
        >= lax.broadcasted_iota(jnp.int32, (rows, rows), 1)
    )[None, :, :]
    weights = jnp.where(
        causal_mask, scores * jnp.exp(jnp.where(causal_mask, gap_logs, 0.0)), 0.0
    ).astype(jnp.bfloat16)
    intra = jnp.einsum("hts,she->the", weights, v_heads, preferred_element_type=jnp.float32)
    inter = jnp.exp(log_cum)[:, :, None] * jnp.einsum(
        "thd,hde->the", q_heads.astype(jnp.float32), carried, precision=lax.Precision.HIGHEST
    )
    attn = intra + inter
    normed = (attn * lax.rsqrt(jnp.mean(attn * attn, axis=-1, keepdims=True) + 1e-06)).astype(
        jnp.bfloat16
    )
    normed = normed.reshape(rows, heads * head_dim)
    n_seq, n_exp = lax.axis_size("seq"), lax.axis_size("exp")
    tok_rows, width = residual.shape
    experts = w_gate.shape[0] * n_exp
    gates = jnp.sum(
        jnp.where(
            expert_ids[:, :, None] == jnp.arange(experts, dtype=jnp.int32)[None, None, :],
            gate_weights[:, :, None],
            0.0,
        ),
        axis=1,
    )
    if experts <= 64:
        coarse = lax.reduce_precision(gates, 8, 7)
        spare = ((0, 0), (0, 64 - experts))
        tile = jnp.concatenate([jnp.pad(coarse, spare), jnp.pad(gates - coarse, spare)], axis=1)
    else:
        tile = jnp.zeros((tok_rows, 128), jnp.float32)
    hidden, moe_in = mix_tokens(
        normed, residual, attn_gain, moe_gain, tile.astype(jnp.bfloat16), n_exp
    )
    if moe_fits(n_seq, n_exp, moe_in.shape, w_gate.shape):
        return moe_layer(moe_in, hidden, w_gate, w_up, w_down, n_seq, n_exp)
    moe_in = moe_in[:, :width]
    hid32 = hidden.astype(jnp.float32)
    flat = gates.T.reshape(-1)
    pad = -flat.shape[0] % 1024
    g_tile = jnp.pad(flat, (0, pad)).reshape(-1, 128)
    everyone, g_all = gather_all(moe_in, g_tile, n_seq, n_exp)
    g_all = g_all.reshape(n_seq * n_exp, -1)[:, : experts * tok_rows]
    g_all = g_all.reshape(n_seq * n_exp, experts, tok_rows)
    mixed = None
    gate_col = lax.dynamic_slice_in_dim(
        g_all, lax.axis_index("exp") * w_gate.shape[0], w_gate.shape[0], 1
    )
    part = None
    for j in range(w_gate.shape[0]):
        gate_part = jnp.einsum("td,fd->tf", everyone, w_gate[j], preferred_element_type=jnp.float32)
        up_part = jnp.einsum("td,fd->tf", everyone, w_up[j], preferred_element_type=jnp.float32)
        active = (
            jax.nn.silu(gate_part) * up_part * gate_col[:, j, :].reshape(-1, 1)
        ).astype(jnp.bfloat16)
        one = jnp.dot(active, w_down[j], preferred_element_type=jnp.float32)
        part = one if part is None else part + one
    part = part.astype(jnp.bfloat16)
    total_rows, width = part.shape
    pieces = max(1, total_rows // 1024)
    step = width // pieces
    summed = [
        jax.jit(scatter_sum, static_argnums=(1, 2))(part[:, i * step : (i + 1) * step], n_seq, n_exp) for i in range(pieces)
    ]
    summed = summed[0] if pieces == 1 else jnp.concatenate(summed, axis=1)
    return (hid32 + summed).astype(jnp.bfloat16)


def solution(mesh):
    in_specs = (
        P("seq", "exp"),
        P("seq", "exp"),
        P("seq", "exp"),
        P("seq", "exp"),
        P(("seq", "exp"), None),
        P(),
        P(),
        P(("seq", "exp"), None),
        P(("seq", "exp"), None),
        P("exp", "seq", None),
        P("exp", "seq", None),
        P("exp", "seq", None),
    )
    out_specs = P(("seq", "exp"), None)
    return jax.shard_map(body, mesh=mesh, in_specs=in_specs, out_specs=out_specs, check_vma=False)
```

```python
import functools

import jax
import jax.numpy as jnp
from jax import lax
from jax.experimental import pallas as pl
from jax.experimental.pallas import tpu as pltpu
from jax.sharding import PartitionSpec as P

MESH = pl.DeviceIdType.MESH
PARTS = 2


class Place:
    def __init__(self, n_seq, n_exp):
        s, e = lax.axis_index("seq"), lax.axis_index("exp")
        self.fold, self.n_exp = n_exp // 4, n_exp
        self.length = (n_seq // 2) * self.fold
        self.p = (s // 2) * self.fold + e // 4
        self.x, self.y, self.c = s % 2, (e // 2) % 2, e % 2

    def ids(self, p, x, y, c):
        return (p // self.fold) * 2 + x, (p % self.fold) * 4 + y * 2 + c

    def block(self, p, x, y, c):
        s, e = self.ids(p, x, y, c)
        return s * self.n_exp + e

    def dev(self, dp=0, dx=0, dy=0, dc=0):
        x = 1 - self.x if dx else self.x
        y = 1 - self.y if dy else self.y
        c = 1 - self.c if dc else self.c
        return self.ids(self.p + dp, x, y, c)

    def greet(self, *more):
        barrier = pltpu.get_barrier_semaphore()
        for d in (dict(dx=1), dict(dy=1), dict(dc=1), *more):
            pl.semaphore_signal(barrier, inc=1, device_id=self.dev(**d), device_id_type=MESH)

        @pl.when(self.p > 0)
        def _():
            pl.semaphore_signal(barrier, inc=1, device_id=self.dev(dp=-1), device_id_type=MESH)

        @pl.when(self.p < self.length - 1)
        def _():
            pl.semaphore_signal(barrier, inc=1, device_id=self.dev(dp=1), device_id_type=MESH)

        ends = (self.p > 0).astype(jnp.int32) + (self.p < self.length - 1).astype(jnp.int32)
        pl.semaphore_wait(barrier, 3 + len(more) + ends)

    def at(self, stage, sign, k):
        if sign == 0:
            stage(0, 0, 0)
        elif sign < 0:
            pl.when(self.p >= k)(lambda: stage(2 * k - 1, -k, -1))
        else:
            pl.when(self.p + k < self.length)(lambda: stage(2 * k, k, 1))

    def far_first(self, stage):
        def one(i, carry):
            for sign in (1, -1):
                self.at(stage, sign, self.length - 1 - i)
            return carry

        if self.length <= 8:
            for i in range(self.length - 1):
                one(i, 0)
        else:
            lax.fori_loop(0, self.length - 1, one, 0)
        self.at(stage, 0, 0)

    def near_first(self, *stages):
        depth = len(stages)

        def ring(stage, k):
            if isinstance(k, int) and k == 0:
                self.at(stage, 0, 0)
            else:
                for sign in (-1, 1):
                    self.at(stage, sign, k)

        def step(k):
            for j, stage in enumerate(stages):
                if 0 <= k - j < self.length:
                    ring(stage, k - j)

        total = self.length + depth - 1
        if self.length <= 8:
            for k in range(total):
                step(k)
            return
        for k in range(depth):
            step(k)

        def one(k, carry):
            for j, stage in enumerate(stages):
                ring(stage, k - j)
            return carry

        lax.fori_loop(depth, self.length, one, 0)
        for k in range(self.length, total):
            step(k)


def gather_kernel(n_seq, n_exp, x_ref, g_ref, out_ref, gout_ref, send, recv, loc):
    me = Place(n_seq, n_exp)
    rows, width = x_ref.shape
    grow = g_ref.shape[0]
    me.greet()

    def place(ref, off, dx, dy, dc=0):
        x = 1 - me.x if dx else me.x
        y = 1 - me.y if dy else me.y
        c = 1 - me.c if dc else me.c
        b = me.block(me.p + off, x, y, c)
        n = rows if ref is out_ref else grow
        return ref.at[pl.ds(pl.multiple_of(b * n, n), n)]

    def copies(part, kind, slot, off, dx, dy, to, own=False, half=None, dc=0):
        dst_x, dst_g = place(out_ref, off, dx, dy, dc), place(gout_ref, off, dx, dy, dc)
        src_x, src_g = (x_ref, g_ref) if own else (dst_x, dst_g)
        span = width // PARTS
        if half is None:
            cols = pl.ds(part * span, span)
        else:
            cols = pl.ds(part * span + half * (span // 2), span // 2)
        out = [
            pltpu.make_async_remote_copy(
                src_x.at[:, cols],
                dst_x.at[:, cols],
                send.at[kind, slot, part],
                recv.at[kind, slot, part],
                to,
                MESH,
            )
        ]
        if half != 1 and part == 0:
            out.append(
                pltpu.make_async_remote_copy(
                    src_g, dst_g, send.at[kind, slot, PARTS], recv.at[kind, slot, PARTS], to, MESH
                )
            )
        return out

    def start(*a, **k):
        for cp in copies(*a, **k):
            cp.start()

    def wait_recv(*a, **k):
        for cp in copies(*a, **k):
            cp.wait_recv()

    def wait_send(*a, **k):
        for cp in copies(*a, **k):
            cp.wait_send()

    left, right = dict(dp=-1), dict(dp=1)
    X, Y, C = me.dev(dx=1), me.dev(dy=1), me.dev(dc=1)

    def line_sends(off, sign, do):
        own = sign == 0
        if sign <= 0:
            pl.when(me.p + 1 < me.length)(
                lambda: do(0, 2 * (-off + 1) - 1, off, 0, 0, me.dev(**right), own=own)
            )
        if sign >= 0:
            pl.when(me.p > 0)(lambda: do(0, 2 * (off + 1), off, 0, 0, me.dev(**left), own=own))

    def stage_line(slot, off, sign, do):
        own = sign == 0
        line_sends(off, sign, do)
        do(1, slot, off, 0, 0, X, own=own)
        do(2, slot, off, 0, 0, Y, own=own)
        do(5, slot, off, 0, 0, C, own=own)

    def stage_xy_1(slot, off, do):
        do(3, slot, off, 1, 0, Y, half=0)
        do(6, slot, off, 1, 0, C)

    def stage_xy_2(slot, off, do):
        do(4, slot, off, 0, 1, X, half=1)
        do(7, slot, off, 0, 1, C)

    def stage_diag(slot, off, do):
        do(8, slot, off, 1, 1, C)

    local = [
        pltpu.make_async_copy(x_ref, place(out_ref, 0, 0, 0), loc.at[0]),
        pltpu.make_async_copy(g_ref, place(gout_ref, 0, 0, 0), loc.at[1]),
    ]
    for cp in local:
        cp.start()

    def s1(slot, off, sign):
        for part in range(PARTS):
            if sign:
                wait_recv(part, 0, slot, off, 0, 0, X)
            stage_line(slot, off, sign, functools.partial(start, part))

    def s2(slot, off, sign):
        for part in range(PARTS):
            wait_recv(part, 1, slot, off, 1, 0, X)
            stage_xy_1(slot, off, functools.partial(start, part))
            wait_recv(part, 2, slot, off, 0, 1, X)
            stage_xy_2(slot, off, functools.partial(start, part))

    def s3(slot, off, sign):
        for part in range(PARTS):
            wait_recv(part, 3, slot, off, 1, 1, X, half=0)
            wait_recv(part, 4, slot, off, 1, 1, X, half=1)
            stage_diag(slot, off, functools.partial(start, part))

    me.near_first(s1, s2, s3)

    def s4(slot, off, sign):
        for part in range(PARTS):
            done = functools.partial(wait_send, part)
            stage_line(slot, off, sign, done)
            stage_xy_1(slot, off, done)
            stage_xy_2(slot, off, done)
            stage_diag(slot, off, done)
            wait_recv(part, 5, slot, off, 0, 0, X, dc=1)
            wait_recv(part, 6, slot, off, 1, 0, X, dc=1)
            wait_recv(part, 7, slot, off, 0, 1, X, dc=1)
            wait_recv(part, 8, slot, off, 1, 1, X, dc=1)

    me.near_first(s4)
    for cp in local:
        cp.wait()


def gather_all(x, g, n_seq, n_exp):
    n = n_seq * n_exp
    length = n // 8
    anyspace = pl.BlockSpec(memory_space=pl.ANY)
    return pl.pallas_call(
        functools.partial(gather_kernel, n_seq, n_exp),
        out_shape=(
            jax.ShapeDtypeStruct((n * x.shape[0], x.shape[1]), x.dtype),
            jax.ShapeDtypeStruct((n * g.shape[0], g.shape[1]), g.dtype),
        ),
        in_specs=[anyspace, anyspace],
        out_specs=(anyspace, anyspace),
        scratch_shapes=[
            pltpu.SemaphoreType.DMA((9, 2 * length + 1, PARTS + 1)),
            pltpu.SemaphoreType.DMA((9, 2 * length + 1, PARTS + 1)),
            pltpu.SemaphoreType.DMA((2,)),
        ],
        compiler_params=pltpu.CompilerParams(collective_id=1, has_side_effects=True),
    )(x, g)


def scatter_kernel(
    n_seq, n_exp, y_ref, out_ref, acc, sib, xbuf, ybuf, dab, dbb, line, send, recv, loc
):
    me = Place(n_seq, n_exp)
    L = me.length
    rows, width = out_ref.shape
    halfw = width // 2
    me.greet()
    X, Y, C = me.dev(dx=1), me.dev(dy=1), me.dev(dc=1)

    def src(off, grp, dc):
        x = 1 - me.x if grp & 1 else me.x
        y = 1 - me.y if grp & 2 else me.y
        c = 1 - me.c if dc else me.c
        b = me.block(me.p + off, x, y, c)
        return y_ref.at[pl.ds(pl.multiple_of(b * rows, rows), rows)]

    def sib_copy(slot, off, grp):
        return pltpu.make_async_remote_copy(
            src(off, grp, 1), sib.at[grp, slot], send.at[grp, slot], recv.at[grp, slot], C, MESH
        )

    def load(slot, off, grp):
        return pltpu.make_async_copy(src(off, grp, 0), acc.at[grp, slot], loc.at[grp, slot])

    for grp in (3, 1, 2, 0):

        def go(slot, off, sign, grp=grp):
            sib_copy(slot, off, grp).start()
            load(slot, off, grp).start()

        me.far_first(go)

    f32 = jnp.float32

    def pair_sum(slot, off, grp):
        load(slot, off, grp).wait()
        sib_copy(slot, off, grp).wait_recv()
        return acc[grp, slot].astype(f32) + sib[grp, slot].astype(f32)

    def diag_a(slot):
        return pltpu.make_async_remote_copy(
            acc.at[3, slot, :, pl.ds(0, halfw)], dab.at[slot], send.at[4, slot], recv.at[4, slot], Y, MESH
        )

    def diag_b(slot):
        return pltpu.make_async_remote_copy(
            acc.at[3, slot, :, pl.ds(halfw, halfw)], dbb.at[slot], send.at[5, slot], recv.at[5, slot], X, MESH
        )

    def x_copy(slot):
        return pltpu.make_async_remote_copy(
            acc.at[1, slot], xbuf.at[slot], send.at[6, slot], recv.at[6, slot], X, MESH
        )

    def y_copy(slot):
        return pltpu.make_async_remote_copy(
            acc.at[2, slot], ybuf.at[slot], send.at[7, slot], recv.at[7, slot], Y, MESH
        )

    def line_copy(slot, sign):
        return pltpu.make_async_remote_copy(
            acc.at[0, slot],
            line.at[slot],
            send.at[8, slot],
            recv.at[8, slot],
            me.dev(dp=sign),
            MESH,
        )

    def d1(slot, off, sign):
        acc[3, slot] = pair_sum(slot, off, 3).astype(acc.dtype)
        diag_a(slot).start()
        diag_b(slot).start()

    def d2(slot, off, sign):
        sx = pair_sum(slot, off, 1)
        diag_a(slot).wait_recv()
        acc[1, slot, :, pl.ds(0, halfw)] = (sx[:, :halfw] + dab[slot].astype(f32)).astype(acc.dtype)
        acc[1, slot, :, pl.ds(halfw, halfw)] = sx[:, halfw:].astype(acc.dtype)
        x_copy(slot).start()
        sy = pair_sum(slot, off, 2)
        diag_b(slot).wait_recv()
        acc[2, slot, :, pl.ds(0, halfw)] = sy[:, :halfw].astype(acc.dtype)
        acc[2, slot, :, pl.ds(halfw, halfw)] = (sy[:, halfw:] + dbb[slot].astype(f32)).astype(acc.dtype)
        y_copy(slot).start()

    def d3(slot, off, sign):
        total = pair_sum(slot, off, 0)
        x_copy(slot).wait_recv()
        y_copy(slot).wait_recv()
        total = total + xbuf[slot].astype(f32) + ybuf[slot].astype(f32)
        if sign == 0:
            out_ref[...] = total
            if L > 1:

                @pl.when(me.p > 0)
                def _():
                    in_copy(2).wait_recv()
                    out_ref[...] += line[2].astype(f32)

                @pl.when(me.p < L - 1)
                def _():
                    in_copy(1).wait_recv()
                    out_ref[...] += line[1].astype(f32)

            return
        acc[0, slot] = total.astype(acc.dtype)
        far = slot + 2
        behind = me.p > 0 if sign > 0 else me.p < L - 1

        @pl.when(jnp.logical_and(behind, sign * off + 1 < L))
        def _():
            in_copy(far).wait_recv()
            acc[0, slot] = (acc[0, slot].astype(f32) + line[far].astype(f32)).astype(acc.dtype)

        line_copy(slot, sign).start()

    def in_copy(slot):
        return pltpu.make_async_remote_copy(
            acc.at[0, slot], line.at[slot], send.at[8, slot], recv.at[8, slot], X, MESH
        )

    me.far_first(d1)
    me.far_first(d2)
    me.far_first(d3)

    def fin(slot, off, sign):
        for grp in range(4):
            sib_copy(slot, off, grp).wait_send()
        diag_a(slot).wait_send()
        diag_b(slot).wait_send()
        x_copy(slot).wait_send()
        y_copy(slot).wait_send()
        if sign:
            line_copy(slot, sign).wait_send()

    me.far_first(fin)


def scatter_sum(part, n_seq, n_exp):
    n = n_seq * n_exp
    slots = n // 4 - 1 + 2
    rows, width = part.shape[0] // n, part.shape[1]
    bf = jnp.bfloat16
    return pl.pallas_call(
        functools.partial(scatter_kernel, n_seq, n_exp),
        out_shape=jax.ShapeDtypeStruct((rows, width), jnp.float32),
        in_specs=[pl.BlockSpec(memory_space=pl.ANY)],
        out_specs=pl.BlockSpec(memory_space=pltpu.VMEM),
        scratch_shapes=[
            pltpu.VMEM((4, slots, rows, width), bf),
            pltpu.VMEM((4, slots, rows, width), bf),
            pltpu.VMEM((slots, rows, width), bf),
            pltpu.VMEM((slots, rows, width), bf),
            pltpu.VMEM((slots, rows, width // 2), bf),
            pltpu.VMEM((slots, rows, width // 2), bf),
            pltpu.VMEM((slots, rows, width), bf),
            pltpu.SemaphoreType.DMA((9, slots)),
            pltpu.SemaphoreType.DMA((9, slots)),
            pltpu.SemaphoreType.DMA((4, slots)),
        ],
        compiler_params=pltpu.CompilerParams(
            collective_id=2, has_side_effects=True, vmem_limit_bytes=60 * 2**20
        ),
    )(part)


GPARTS = 4
HPARTS = 4
PLANES = 4


def plane_orders(length):
    def depth(q):
        return min(q, length - 1 - q)

    visit = []
    for p in range(length):
        rest = [q for q in range(length) if q != p]
        near = min(rest, key=lambda q: (abs(q - p), depth(q)), default=p)
        rest = sorted((q for q in rest if q != near), key=lambda q: (depth(q), abs(q - p)))
        visit.append([p] + [near] * (length > 1) + rest)
    lines = []
    for p in range(length):
        def ready(q):
            chain = range(0, p + 1) if q > p else range(p, length)
            return max(visit[b].index(q) for b in chain)

        low = 2 * p < length
        lines.append(sorted((q for q in range(length) if q != p), key=lambda q: (ready(q), -q if low else q)))
    return visit, lines


def pick(table, p, j):
    total = 0
    for a, row in enumerate(table):
        for b, v in enumerate(row):
            hit = jnp.logical_and(p == a, j == b).astype(jnp.int32)
            total = total + hit * v
    return total


def spans(tiles, parts):
    cuts = [(tiles * i // parts) * 128 for i in range(parts + 1)]
    return [pl.ds(a, b - a) for a, b in zip(cuts[:-1], cuts[1:])]


def when(cond, fn):
    def run():
        fn()

    pl.when(cond)(run)


def attend_tokens(
    me, q_ref, k_ref, v_ref, ld_ref, res_ref, ag_ref, mg_ref, tile_ref, x_out,
    hid, work, flat, own16, peer, cin, cout, tots, tok, psend, precv, tsem, msend, mrecv,
):
    L, z = me.length, me.p
    f32, bf = jnp.float32, jnp.bfloat16
    block, heads = ld_ref.shape
    dim = q_ref.shape[1] // heads
    rows = res_ref.shape[0]
    n_exp, width = tok.shape[0], tok.shape[2]
    e = lax.axis_index("exp")
    pair = me.dev(dx=1)

    def head(h):
        return pl.ds(h * dim, dim)

    def pair_copy(h):
        return pltpu.make_async_remote_copy(
            own16.at[h], peer.at[h], psend.at[0, h], precv.at[0, h], pair, MESH
        )

    def line_copy(h):
        return pltpu.make_async_remote_copy(
            cout.at[h], cin.at[h], psend.at[1, h], precv.at[1, h], me.dev(dp=1), MESH
        )

    tot_copy = pltpu.make_async_remote_copy(tots.at[0], tots.at[1], tsem.at[0], tsem.at[1], pair, MESH)

    nt = (((1,), (1,)), ((), ()))
    tn = (((0,), (0,)), ((), ()))
    r = lax.broadcasted_iota(jnp.int32, (block, block), 0)
    c = lax.broadcasted_iota(jnp.int32, (block, block), 1)
    seen = r >= c
    decay = ld_ref[...]
    high = lax.Precision.HIGHEST
    cum = jnp.dot(seen.astype(f32), decay, precision=high, preferred_element_type=f32)
    cum_t = lax.dot_general(decay, (r <= c).astype(f32), tn, precision=high, preferred_element_type=f32)
    total = cum_t[:, block - 1 :]
    tots[0, 0:heads, :] = jnp.broadcast_to(total, (heads, dim))

    def state(h):
        kw = (k_ref[:, head(h)].astype(f32) * jnp.exp(total[h : h + 1] - cum[:, h : h + 1])).astype(bf)
        own = lax.dot_general(kw, v_ref[:, head(h)], tn, preferred_element_type=f32)
        work[:, pl.ds((heads + h) * dim, dim)] = own
        own16[h] = own.astype(bf)

    for h in range(heads):
        state(h)
    me.greet(dict(dy=1, dc=1))
    tot_copy.start()
    for h in range(heads):
        pair_copy(h).start()

    @pl.when(z == 0)
    def _():
        cin[...] = jnp.zeros_like(cin)

    for h in range(heads):
        scores = lax.dot_general(q_ref[:, head(h)], k_ref[:, head(h)], nt, preferred_element_type=f32)
        gap = cum[:, h : h + 1] - cum_t[h : h + 1, :]
        weights = jnp.where(seen, scores * jnp.exp(jnp.where(seen, gap, 0.0)), 0.0).astype(bf)
        work[:, head(h)] = jnp.dot(weights, v_ref[:, head(h)], preferred_element_type=f32)

    tot_copy.wait_recv()
    mine, other = tots[0, 0:heads, :], tots[1, 0:heads, :]
    both = jnp.exp(mine + other)
    is_odd = jnp.full(mine.shape, me.x, jnp.int32) == 1
    one = jnp.ones_like(mine)
    own_by = jnp.where(is_odd, one, jnp.exp(other))
    peer_by = jnp.where(is_odd, jnp.exp(mine), one)
    carry_by = jnp.where(is_odd, jnp.exp(other), one)
    peer_in = jnp.where(is_odd, one, jnp.zeros_like(mine))

    peers = (dict(dc=1), dict(dy=1), dict(dy=1, dc=1))
    pieces = 2
    span = width // pieces

    def mix_copy(k, i):
        to = me.dev(**peers[k])
        cols = pl.ds(i * span, span)
        src = flat.at[pl.ds(pl.multiple_of(to[1] * rows, rows), rows), cols]
        return pltpu.make_async_remote_copy(
            src, tok.at[e, :, cols], msend.at[k, i], mrecv.at[k, i], to, MESH
        )

    def mix_in(k, i):
        to = me.dev(**peers[k])
        cols = pl.ds(i * span, span)
        return pltpu.make_async_remote_copy(
            tok.at[to[1], :, cols], tok.at[to[1], :, cols], msend.at[k, i], mrecv.at[k, i], to, MESH
        )

    for h in range(heads):
        pair_copy(h).wait_recv()
        pl.when(z > 0)(lambda: line_copy(h).wait_recv())
        near = peer[h].astype(f32)
        come = cin[h].astype(f32)
        row = slice(h, h + 1)

        @pl.when(z < L - 1)
        def _():
            mix = both[row] * come + own_by[row] * work[:, pl.ds((heads + h) * dim, dim)] + peer_by[row] * near
            cout[h] = mix.astype(bf)
            line_copy(h).start()

        carried = carry_by[row] * come + peer_in[row] * near
        coarse = carried.astype(bf)
        fine = (carried - coarse.astype(f32)).astype(bf)
        query = q_ref[:, head(h)]
        inter = jnp.dot(query, coarse, preferred_element_type=f32) + jnp.dot(
            query, fine, preferred_element_type=f32
        )
        attn = work[:, head(h)] + jnp.exp(cum[:, h : h + 1]) * inter
        scale = lax.rsqrt(jnp.mean(attn * attn, axis=-1, keepdims=True) + 1e-06)
        flat[0:block, head(h)] = (attn * scale).astype(bf)
        if (h + 1) * pieces % heads == 0:
            for k in range(len(peers)):
                mix_copy(k, (h + 1) * pieces // heads - 1).start()

    tok[e] = flat[pl.ds(pl.multiple_of(e * rows, rows), rows), 0:width]
    for i in range(pieces):
        for k in range(len(peers)):
            mix_in(k, i).wait_recv()
    square = jnp.zeros((rows, 1), f32)
    for j in range(n_exp):
        cols = pl.ds(j * width, width)
        value = (res_ref[:, cols].astype(f32) + tok[j].astype(f32) * ag_ref[:, cols]).astype(bf)
        hid[:, cols] = value
        wide = value.astype(f32)
        square = square + jnp.sum(wide * wide, axis=1, keepdims=True)
    scale = lax.rsqrt(square / (n_exp * width) + 1e-06)
    for j in range(n_exp):
        cols = pl.ds(j * width, width)
        x_out[:, cols] = (hid[:, cols].astype(f32) * scale * mg_ref[:, cols]).astype(bf)
    x_out[:, n_exp * width :] = tile_ref[...]

    def finish():
        tot_copy.wait_send()
        for h in range(heads):
            pair_copy(h).wait_send()
            pl.when(z < L - 1)(lambda: line_copy(h).wait_send())
        for i in range(pieces):
            for k in range(len(peers)):
                mix_copy(k, i).wait_send()

    return finish


def moe_kernel(
    n_seq, n_exp, q_ref, k_ref, v_ref, ld_ref, res_ref, ag_ref, mg_ref, tile_ref,
    wg_ref, wu_ref, wd_ref, out_ref,
    xs, ys, act, sib, din, xin, yin, lin, tot, wg, wu, wd, hid_ref,
    own16, peer, cin, cout, tots, tok,
    gsend, grecv, bsend, brecv, ssend, srecv, loc, psend, precv, tsem, msend, mrecv,
):
    me = Place(n_seq, n_exp)
    L, p = me.length, me.p
    rows, width = out_ref.shape
    hidden = wg.shape[0]
    many = 8 * rows
    f32, bf = jnp.float32, jnp.bfloat16
    X, Y, C = me.dev(dx=1), me.dev(dy=1), me.dev(dc=1)
    visit, lines = plane_orders(L)
    gcols = spans(xs.shape[1] // 128, GPARTS)
    hcols = spans(width // 128, HPARTS)

    loads = [
        pltpu.make_async_copy(a.at[0], b, loc.at[i])
        for i, (a, b) in enumerate(((wg_ref, wg), (wu_ref, wu), (wd_ref, wd)))
    ]
    for cp in loads:
        cp.start()

    def flip(v, d):
        return 1 - v if d else v

    def row(q, dx=0, dy=0, dc=0):
        k = (flip(me.c, dc) * 2 + flip(me.x, dx)) * 2 + flip(me.y, dy)
        return pl.ds(pl.multiple_of((q * 8 + k) * rows, rows), rows)

    def srow(q, dx=0, dy=0):
        k = flip(me.x, dx) * 2 + flip(me.y, dy)
        return pl.ds(pl.multiple_of((q * 4 + k) * rows, rows), rows)

    def prow(q):
        return pl.ds(pl.multiple_of(q * rows, rows), rows)

    def gcopy(kind, q, part, r, to, skind=None):
        ref = xs.at[r, gcols[part]]
        skind = kind if skind is None else skind
        return pltpu.make_async_remote_copy(
            ref, ref, gsend.at[skind, q, part], grecv.at[kind, q, part], to, MESH
        )

    upper = GPARTS // 2

    def line_pair(q, part, do):
        pl.when(jnp.logical_and(q >= p, p > 0))(
            lambda: do(gcopy(0, q, part, row(q), me.dev(dp=-1)))
        )
        pl.when(jnp.logical_and(q <= p, p + 1 < L))(
            lambda: do(gcopy(0, q, part, row(q), me.dev(dp=1), 9))
        )

    def start(cp):
        cp.start()

    def g_line(q, part):
        pl.when(q != p)(lambda: gcopy(0, q, part, row(q), X).wait_recv())
        line_pair(q, part, start)

    def first(q, part):
        return [gcopy(2, q, part, row(q), Y), gcopy(5, q, part, row(q), C)]

    def second_x(q, part):
        out = [gcopy(6, q, part, row(q, 1, 0), C)]
        return out if part >= upper else [gcopy(3, q, part, row(q, 1, 0), Y)] + out

    def second_y(q, part):
        out = [gcopy(7, q, part, row(q, 0, 1), C)]
        return out if part < upper else [gcopy(4, q, part, row(q, 0, 1), X)] + out

    def third(q, part):
        return [gcopy(8, q, part, row(q, 1, 1), C)]

    lower, higher = range(upper), range(upper, GPARTS)

    def g_first(q, turn):
        for part in lower if turn == 0 else higher:
            gcopy(1, q, part, row(q), X).start()
        for part in higher if turn == 0 else lower:
            gcopy(2, q, part, row(q), Y).start()
        if turn == 0:
            for part in range(GPARTS):
                gcopy(5, q, part, row(q), C).start()

    def g_own(q):
        for part in lower:
            line_pair(q, part, start)
        g_first(q, 0)
        for part in lower:
            gcopy(1, q, part, row(q), X).wait_send()
        for part in higher:
            line_pair(q, part, start)
        g_first(q, 1)

    def from_x(q, part):
        gcopy(1, q, part, row(q, 1, 0), X).wait_recv()
        for cp in second_x(q, part):
            cp.start()

    def from_y(q, part):
        gcopy(2, q, part, row(q, 0, 1), X).wait_recv()
        for cp in second_y(q, part):
            cp.start()

    def g_second(q):
        for part in lower:
            from_x(q, part)
            from_y(q, part + upper)

    def g_rest(q):
        for part in lower:
            from_x(q, part + upper)
            from_y(q, part)

    def g_third(q):
        for part in range(GPARTS):
            gcopy(3 if part < upper else 4, q, part, row(q, 1, 1), X).wait_recv()
            for cp in third(q, part):
                cp.start()

    def g_ring(k, parts):
        for sign in (-1, 1):
            q = p + sign * k
            when(jnp.logical_and(q >= 0, q < L), lambda: [g_line(q, part) for part in parts])

    def g_done(q):
        for part in range(GPARTS):
            gcopy(5, q, part, row(q, 0, 0, 1), X).wait_recv()
            gcopy(6, q, part, row(q, 1, 0, 1), X).wait_recv()
            gcopy(7, q, part, row(q, 0, 1, 1), X).wait_recv()
            gcopy(8, q, part, row(q, 1, 1, 1), X).wait_recv()

    def g_drain(q):
        for part in range(GPARTS):
            line_pair(q, part, lambda cp: cp.wait_send())
            across = gcopy(1, q, part, row(q), X)
            if part < upper:
                pl.when(q != p)(lambda: across.wait_send())
            else:
                across.wait_send()
            for cp in first(q, part) + second_x(q, part) + second_y(q, part) + third(q, part):
                cp.wait_send()

    def sib_copy(q, h):
        r = pl.ds(pl.multiple_of((q * 2 + 1 - me.c) * 4 * rows, 4 * rows), 4 * rows)
        d = pl.ds(pl.multiple_of(q * 4 * rows, 4 * rows), 4 * rows)
        return pltpu.make_async_remote_copy(
            ys.at[r, hcols[h]], sib.at[d, hcols[h]], bsend.at[q, h], brecv.at[q, h], C, MESH
        )

    def scopy(kind, q, h, r, dst, d, to):
        return pltpu.make_async_remote_copy(
            ys.at[r, hcols[h]], dst.at[d, hcols[h]], ssend.at[kind, q, h], srecv.at[kind, q, h], to, MESH
        )

    def diag_copy(q, h):
        return scopy(0, q, h, row(q, 1, 1), din, prow(q), Y if 2 * h < HPARTS else X)

    def x_copy(q, h):
        return scopy(1, q, h, row(q, 1, 0), xin, prow(q), X)

    def y_copy(q, h):
        return scopy(2, q, h, row(q, 0, 1), yin, prow(q), Y)

    def line_copy(q, h):
        up = (q > p).astype(jnp.int32)
        last = jnp.logical_and(q < p, q == p - 1).astype(jnp.int32)
        slot = q + (L - q) * last
        return pltpu.make_async_remote_copy(
            ys.at[row(q), hcols[h]],
            lin.at[prow(slot), hcols[h]],
            ssend.at[3, q, h],
            srecv.at[3, slot, h],
            me.dev(dp=2 * up - 1),
            MESH,
        )

    def line_in(slot, h):
        return pltpu.make_async_remote_copy(
            ys.at[row(p), hcols[h]], lin.at[prow(slot), hcols[h]], ssend.at[3, p, h], srecv.at[3, slot, h], X, MESH
        )

    def pair(q, h, dx, dy):
        return ys[row(q, dx, dy), hcols[h]].astype(f32) + sib[srow(q, dx, dy), hcols[h]].astype(f32)

    def r_first(q, h):
        sib_copy(q, h).wait_recv()
        ys[row(q, 1, 1), hcols[h]] = pair(q, h, 1, 1).astype(bf)
        diag_copy(q, h).start()

    def r_second(q, h):
        sx, sy = pair(q, h, 1, 0), pair(q, h, 0, 1)
        diag_copy(q, h).wait_recv()
        more = din[prow(q), hcols[h]].astype(f32)
        if 2 * h < HPARTS:
            sx = sx + more
        else:
            sy = sy + more
        ys[row(q, 1, 0), hcols[h]] = sx.astype(bf)
        x_copy(q, h).start()
        ys[row(q, 0, 1), hcols[h]] = sy.astype(bf)
        y_copy(q, h).start()

    def r_third(q, h):
        total = pair(q, h, 0, 0)
        x_copy(q, h).wait_recv()
        y_copy(q, h).wait_recv()
        total = total + xin[prow(q), hcols[h]].astype(f32) + yin[prow(q), hcols[h]].astype(f32)
        tot[prow(q), hcols[h]] = total

    def r_line(q, h):
        behind = jnp.logical_or(jnp.logical_and(q > p, p > 0), jnp.logical_and(q < p, p < L - 1))

        @pl.when(behind)
        def _():
            line_in(q, h).wait_recv()
            ys[row(q), hcols[h]] = (tot[prow(q), hcols[h]] + lin[prow(q), hcols[h]].astype(f32)).astype(bf)

        @pl.when(jnp.logical_not(behind))
        def _():
            ys[row(q), hcols[h]] = tot[prow(q), hcols[h]].astype(bf)

        line_copy(q, h).start()

    def r_last(h):
        cols = hcols[h]

        @pl.when(p > 0)
        def _():
            line_in(p, h).wait_recv()
            tot[prow(p), cols] += lin[prow(p), cols].astype(f32)

        @pl.when(p < L - 1)
        def _():
            line_in(L, h).wait_recv()
            tot[prow(p), cols] += lin[prow(L), cols].astype(f32)

        out_ref[:, cols] = (hid_ref[:, cols].astype(f32) + tot[prow(p), cols]).astype(bf)

    at_end = jnp.logical_or(p == 0, p == L - 1)
    inner = jnp.logical_not(at_end)

    def r_early(q, h):
        pl.when(jnp.logical_and(at_end, q != p))(lambda: r_line(q, h))

    def r_drain(q):
        for h in range(HPARTS):
            sib_copy(q, h).wait_send()
            diag_copy(q, h).wait_send()
            x_copy(q, h).wait_send()
            y_copy(q, h).wait_send()
            pl.when(q != p)(lambda: line_copy(q, h).wait_send())

    tile = next(t for t in range(512, 0, -128) if hidden % t == 0)
    fsteps = hidden // tile

    def block_of(q):
        return pl.ds(pl.multiple_of(q * many, many), many)

    def gate_of(q):
        extra = xs[block_of(q), width : width + 128].astype(f32)
        lane = lax.broadcasted_iota(jnp.int32, extra.shape, 1)
        e = lax.axis_index("exp")
        keep = jnp.logical_or(lane == e, lane == e + 64)
        return jnp.sum(jnp.where(keep, extra, 0.0), axis=1, keepdims=True)

    nt = (((1,), (1,)), ((), ()))

    def ffn_in(q, f):
        fc = pl.ds(f * tile, tile)
        rows_in = xs[block_of(q), 0:width]
        gate = lax.dot_general(rows_in, wg[fc, :], nt, preferred_element_type=f32)
        up = lax.dot_general(rows_in, wu[fc, :], nt, preferred_element_type=f32)
        act[:, fc] = (gate / (1.0 + jnp.exp(-gate)) * up * gate_of(q)).astype(bf)

    def ffn_out(q, h):
        ys[block_of(q), hcols[h]] = jnp.dot(
            act[...], wd[:, hcols[h]], preferred_element_type=f32
        ).astype(bf)
        sib_copy(q, h).start()

    front_done = attend_tokens(
        me, q_ref, k_ref, v_ref, ld_ref, res_ref, ag_ref, mg_ref, tile_ref, xs.at[row(p)],
        hid_ref, tot, act, own16, peer, cin, cout, tots, tok, psend, precv, tsem, msend, mrecv,
    )
    second = pick(visit, p, 1)
    g_own(p)
    g_second(p)
    g_ring(1, lower)
    g_rest(p)
    g_ring(1, higher)
    g_first(second, 0)
    g_third(p)
    g_ring(2, lower)
    g_first(second, 1)
    front_done()
    for cp in loads:
        cp.wait()

    def chunk(j, carry):
        q, nxt, prev = pick(visit, p, j), pick(visit, p, j + 1), pick(visit, p, j - 1)

        def ahead(fn):
            when(j + 1 < L, fn)

        def after(fn):
            when(j > 0, fn)

        def opening(fn):
            when(j == 0, fn)

        def closing(fn):
            when(j == L - 1, fn)

        def hook(n):
            if n == 0:
                opening(lambda: g_ring(2, higher))
                after(lambda: (r_second(prev, 0), r_second(prev, 1)))
                ahead(lambda: g_second(nxt))
                opening(lambda: when(inner, lambda: g_first(pick(visit, p, 2), 0)))
            if n == 1:
                after(lambda: (r_second(prev, 2), r_second(prev, 3)))
                ahead(lambda: g_rest(nxt))
                opening(lambda: g_ring(3, range(GPARTS)))
                opening(lambda: when(at_end, lambda: g_first(pick(visit, p, 2), 0)))
                opening(lambda: g_first(pick(visit, p, 2), 1))
            if n == 2:
                opening(lambda: g_first(pick(visit, p, 3), 0))
                after(lambda: (r_third(prev, 0), r_early(prev, 0), r_third(prev, 1), r_early(prev, 1)))

        g_done(q)
        after(lambda: r_first(prev, HPARTS - 1))
        for f in range(fsteps):
            ffn_in(q, f)
            hook(f)
        for f in range(fsteps, 3):
            hook(f)
        for h in range(HPARTS):
            ffn_out(q, h)
            if h:
                r_first(q, h - 1)
            if h == 1:
                after(lambda: (r_third(prev, 2), r_early(prev, 2), r_third(prev, 3), r_early(prev, 3)))
            if h == 2:
                ahead(lambda: g_third(nxt))
            if h == 3:
                opening(lambda: g_first(pick(visit, p, 3), 1))
        return carry

    def one_line(i, h):
        when(inner, lambda: r_line(pick(lines, p, i), h))

    lax.fori_loop(0, L, chunk, 0)

    final = pick(visit, p, L - 1)
    r_first(final, HPARTS - 1)
    for h in range(HPARTS):
        r_second(final, h)
        one_line(0, h)
    for h in range(HPARTS):
        one_line(1, h)
        r_third(final, h)
        r_early(final, h)
    for h in range(HPARTS):
        one_line(2, h)
        if h:
            r_last(h - 1)
    r_last(HPARTS - 1)

    def drain(q, carry):
        g_drain(q)
        r_drain(q)
        return carry

    lax.fori_loop(0, L, drain, 0)


def moe_scratch(n_seq, n_exp, x_shape, w_shape):
    n, L = n_seq * n_exp, n_seq * n_exp // 8
    rows, wide = x_shape
    hidden, width = w_shape[1:]
    bf, f32 = jnp.bfloat16, jnp.float32
    return [
        ((n * rows, wide), bf),
        ((n * rows, width), bf),
        ((8 * rows, hidden), bf),
        ((n // 2 * rows, width), bf),
        ((L * rows, width), bf),
        ((L * rows, width), bf),
        ((L * rows, width), bf),
        ((L * rows + rows, width), bf),
        ((L * rows, width), f32),
        ((hidden, width), bf),
        ((hidden, width), bf),
        ((hidden, width), bf),
    ]


MOE_VMEM = 61 * 2**20


def moe_fits(n_seq, n_exp, rows, width, w_shape):
    need = sum(
        a * b * jnp.dtype(t).itemsize for (a, b), t in moe_scratch(n_seq, n_exp, (rows, width + 128), w_shape)
    )
    return (
        w_shape[0] == 1
        and n_exp // 4 == 1
        and n_seq * n_exp == 8 * PLANES
        and w_shape[1] % 128 == 0
        and w_shape[2] % (128 * HPARTS) == 0
        and need + 6 * 2**20 <= MOE_VMEM
    )


def whole_layer(
    queries, keys, values, log_decay, residual, attn_gain, moe_gain, tile, w_gate, w_up, w_down, n_seq, n_exp
):
    L = n_seq * n_exp // 8
    heads = log_decay.shape[1]
    part = queries.shape[1]
    dim = part // heads
    rows, width = residual.shape
    vmem = pl.BlockSpec(memory_space=pltpu.VMEM)
    anyspace = pl.BlockSpec(memory_space=pl.ANY)
    dma = pltpu.SemaphoreType.DMA
    bf = jnp.bfloat16
    states = pltpu.VMEM((heads, dim, dim), bf)
    scratch = moe_scratch(n_seq, n_exp, (rows, width + tile.shape[1]), w_gate.shape)
    return pl.pallas_call(
        functools.partial(moe_kernel, n_seq, n_exp),
        out_shape=jax.ShapeDtypeStruct(residual.shape, bf),
        in_specs=[vmem] * 8 + [anyspace] * 3,
        out_specs=vmem,
        scratch_shapes=[pltpu.VMEM(s, t) for s, t in scratch]
        + [
            pltpu.VMEM(residual.shape, bf),
            states,
            states,
            states,
            states,
            pltpu.VMEM((2, heads + -heads % 8, dim), jnp.float32),
            pltpu.VMEM((n_exp, rows, part), bf),
            dma((10, L, GPARTS)),
            dma((10, L, GPARTS)),
            dma((L, HPARTS)),
            dma((L, HPARTS)),
            dma((4, L + 1, HPARTS)),
            dma((4, L + 1, HPARTS)),
            dma((3,)),
            dma((2, heads)),
            dma((2, heads)),
            dma((2,)),
            dma((3, 2)),
            dma((3, 2)),
        ],
        compiler_params=pltpu.CompilerParams(
            collective_id=5, has_side_effects=True, vmem_limit_bytes=MOE_VMEM
        ),
    )(
        queries, keys, values, log_decay, residual, attn_gain[None, :], moe_gain[None, :], tile,
        w_gate, w_up, w_down,
    )


def carry_kernel(n_seq, own_ref, own16_ref, tot_ref, out_ref, peer, ptot, cin, cout, send, recv, tsem):
    s, e = lax.axis_index("seq"), lax.axis_index("exp")
    z, odd, deep = s // 2, s % 2, n_seq // 2
    heads = own_ref.shape[0]
    pair = (z * 2 + 1 - odd, e)

    barrier = pltpu.get_barrier_semaphore()
    pl.semaphore_signal(barrier, inc=1, device_id=pair, device_id_type=MESH)

    @pl.when(z > 0)
    def _():
        pl.semaphore_signal(barrier, inc=1, device_id=(s - 2, e), device_id_type=MESH)

    @pl.when(z < deep - 1)
    def _():
        pl.semaphore_signal(barrier, inc=1, device_id=(s + 2, e), device_id_type=MESH)

    ends = (z > 0).astype(jnp.int32) + (z < deep - 1).astype(jnp.int32)
    pl.semaphore_wait(barrier, 1 + ends)

    tot_copy = pltpu.make_async_remote_copy(tot_ref, ptot, tsem.at[0], tsem.at[1], pair, MESH)

    def pair_copy(h):
        return pltpu.make_async_remote_copy(
            own16_ref.at[h], peer.at[h], send.at[0, h], recv.at[0, h], pair, MESH
        )

    def line_copy(h):
        return pltpu.make_async_remote_copy(
            cout.at[h], cin.at[h], send.at[1, h], recv.at[1, h], (s + 2, e), MESH
        )

    tot_copy.start()
    for h in range(heads):
        pair_copy(h).start()

    @pl.when(z == 0)
    def _():
        cin[...] = jnp.zeros_like(cin)

    tot_copy.wait_recv()
    mine, other = tot_ref[...], ptot[...]
    both = jnp.exp(mine + other)
    is_odd = jnp.full(mine.shape, odd, jnp.int32) == 1
    one = jnp.ones_like(mine)
    own_by = jnp.where(is_odd, one, jnp.exp(other))
    peer_by = jnp.where(is_odd, jnp.exp(mine), one)
    carry_by = jnp.where(is_odd, jnp.exp(other), one)
    peer_in = jnp.where(is_odd, one, jnp.zeros_like(mine))
    for h in range(heads):
        pair_copy(h).wait_recv()

        @pl.when(z > 0)
        def _():
            line_copy(h).wait_recv()

        near = peer[h].astype(jnp.float32)
        come = cin[h].astype(jnp.float32)

        @pl.when(z < deep - 1)
        def _():
            cout[h] = (
                both[h : h + 1] * come + own_by[h : h + 1] * own_ref[h] + peer_by[h : h + 1] * near
            ).astype(cout.dtype)
            line_copy(h).start()

        out_ref[h] = carry_by[h : h + 1] * come + peer_in[h : h + 1] * near

    tot_copy.wait_send()
    for h in range(heads):
        pair_copy(h).wait_send()

        @pl.when(z < deep - 1)
        def _():
            line_copy(h).wait_send()


def carried_in(block_total, block_state, n_seq):
    heads, dim, _ = block_state.shape
    bf = jnp.bfloat16
    tile = jnp.pad(block_total, (0, -heads % 8))
    tile = jnp.broadcast_to(tile[:, None], (tile.shape[0], dim))
    vmem = pl.BlockSpec(memory_space=pltpu.VMEM)
    return pl.pallas_call(
        functools.partial(carry_kernel, n_seq),
        out_shape=jax.ShapeDtypeStruct(block_state.shape, jnp.float32),
        in_specs=[vmem] * 3,
        out_specs=vmem,
        scratch_shapes=[
            pltpu.VMEM(block_state.shape, bf),
            pltpu.VMEM(tile.shape, jnp.float32),
            pltpu.VMEM(block_state.shape, bf),
            pltpu.VMEM(block_state.shape, bf),
            pltpu.SemaphoreType.DMA((2, heads)),
            pltpu.SemaphoreType.DMA((2, heads)),
            pltpu.SemaphoreType.DMA((2,)),
        ],
        compiler_params=pltpu.CompilerParams(collective_id=3, has_side_effects=True),
    )(block_state, block_state.astype(bf), tile)


def mix_kernel(n_exp, normed_ref, res_ref, again_ref, mgain_ref, hid_ref, in_ref, tok, send, recv, loc):
    s, e = lax.axis_index("seq"), lax.axis_index("exp")
    rows, width = res_ref.shape[0], normed_ref.shape[1]

    barrier = pltpu.get_barrier_semaphore()
    for k in range(1, n_exp):
        pl.semaphore_signal(
            barrier, inc=1, device_id=(s, lax.rem(e + k, n_exp)), device_id_type=MESH
        )
    pl.semaphore_wait(barrier, n_exp - 1)

    def source(peer):
        return normed_ref.at[pl.ds(pl.multiple_of(peer * rows, rows), rows)]

    own = pltpu.make_async_copy(source(e), tok.at[e], loc.at[0])

    def copy(k):
        peer = lax.rem(e + k, n_exp)
        return pltpu.make_async_remote_copy(
            source(peer), tok.at[e], send.at[k], recv.at[k], (s, peer), MESH
        )

    def arriving(k):
        sender = lax.rem(e + n_exp - k, n_exp)
        return pltpu.make_async_remote_copy(
            source(e), tok.at[sender], send.at[k], recv.at[k], (s, sender), MESH
        )

    for k in range(1, n_exp):
        copy(k).start()
    own.start()
    own.wait()
    for k in range(1, n_exp):
        arriving(k).wait_recv()
    square = jnp.zeros((rows, 1), jnp.float32)
    for j in range(n_exp):
        cols = pl.ds(j * width, width)
        hid = (
            res_ref[:, cols].astype(jnp.float32)
            + tok[j].astype(jnp.float32) * again_ref[:, cols]
        ).astype(jnp.bfloat16)
        hid_ref[:, cols] = hid
        wide = hid.astype(jnp.float32)
        square = square + jnp.sum(wide * wide, axis=1, keepdims=True)
    scale = lax.rsqrt(square / (n_exp * width) + 1e-06)
    for j in range(n_exp):
        cols = pl.ds(j * width, width)
        in_ref[:, cols] = (
            hid_ref[:, cols].astype(jnp.float32) * scale * mgain_ref[:, cols]
        ).astype(jnp.bfloat16)
    for k in range(1, n_exp):
        copy(k).wait_send()


def mix_tokens(normed, residual, attn_gain, moe_gain, n_exp):
    vmem = pl.BlockSpec(memory_space=pltpu.VMEM)
    return pl.pallas_call(
        functools.partial(mix_kernel, n_exp),
        out_shape=(jax.ShapeDtypeStruct(residual.shape, jnp.bfloat16),) * 2,
        in_specs=[vmem] * 4,
        out_specs=(vmem, vmem),
        scratch_shapes=[
            pltpu.VMEM((n_exp, residual.shape[0], normed.shape[1]), jnp.bfloat16),
            pltpu.SemaphoreType.DMA((n_exp,)),
            pltpu.SemaphoreType.DMA((n_exp,)),
            pltpu.SemaphoreType.DMA((1,)),
        ],
        compiler_params=pltpu.CompilerParams(collective_id=4, has_side_effects=True),
    )(normed, residual, attn_gain[None, :], moe_gain[None, :])


def body(
    queries,
    keys,
    values,
    log_decay,
    residual,
    attn_gain,
    moe_gain,
    expert_ids,
    gate_weights,
    w_gate,
    w_up,
    w_down,
):
    n_seq, n_exp = lax.axis_size("seq"), lax.axis_size("exp")
    tok_rows, width = residual.shape
    experts = w_gate.shape[0] * n_exp
    gates = jnp.sum(
        jnp.where(
            expert_ids[:, :, None] == jnp.arange(experts, dtype=jnp.int32)[None, None, :],
            gate_weights[:, :, None],
            0.0,
        ),
        axis=1,
    )
    if moe_fits(n_seq, n_exp, tok_rows, width, w_gate.shape):
        coarse = lax.reduce_precision(gates, 8, 7)
        spare = ((0, 0), (0, 64 - experts))
        tile = jnp.concatenate([jnp.pad(coarse, spare), jnp.pad(gates - coarse, spare)], axis=1)
        return whole_layer(
            queries, keys, values, log_decay, residual, attn_gain, moe_gain,
            tile.astype(jnp.bfloat16), w_gate, w_up, w_down, n_seq, n_exp,
        )
    rows = queries.shape[0]
    heads = log_decay.shape[1]
    head_dim = queries.shape[1] // heads
    q_heads = queries.reshape(rows, heads, head_dim)
    k_heads = keys.reshape(rows, heads, head_dim)
    v_heads = values.reshape(rows, heads, head_dim)
    upto = (
        lax.broadcasted_iota(jnp.int32, (rows, rows), 0)
        >= lax.broadcasted_iota(jnp.int32, (rows, rows), 1)
    ).astype(jnp.float32)
    log_cum = jnp.dot(upto, log_decay, precision=lax.Precision.HIGHEST)
    block_total = log_cum[-1]
    keys_weighted = (k_heads * jnp.exp(block_total[None, :] - log_cum)[:, :, None]).astype(
        jnp.bfloat16
    )
    block_state = jnp.einsum(
        "thd,the->hde", keys_weighted, v_heads, preferred_element_type=jnp.float32
    )
    carried = carried_in(block_total, block_state, lax.axis_size("seq"))
    scores = jnp.einsum("thd,shd->hts", q_heads, k_heads, preferred_element_type=jnp.float32)
    gap_logs = log_cum.T[:, :, None] - log_cum.T[:, None, :]
    causal_mask = (
        lax.broadcasted_iota(jnp.int32, (rows, rows), 0)
        >= lax.broadcasted_iota(jnp.int32, (rows, rows), 1)
    )[None, :, :]
    weights = jnp.where(
        causal_mask, scores * jnp.exp(jnp.where(causal_mask, gap_logs, 0.0)), 0.0
    ).astype(jnp.bfloat16)
    intra = jnp.einsum("hts,she->the", weights, v_heads, preferred_element_type=jnp.float32)
    inter = jnp.exp(log_cum)[:, :, None] * jnp.einsum(
        "thd,hde->the", q_heads.astype(jnp.float32), carried, precision=lax.Precision.HIGHEST
    )
    attn = intra + inter
    normed = (attn * lax.rsqrt(jnp.mean(attn * attn, axis=-1, keepdims=True) + 1e-06)).astype(
        jnp.bfloat16
    )
    normed = normed.reshape(rows, heads * head_dim)
    hidden, moe_in = mix_tokens(normed, residual, attn_gain, moe_gain, n_exp)
    hid32 = hidden.astype(jnp.float32)
    flat = gates.T.reshape(-1)
    pad = -flat.shape[0] % 1024
    g_tile = jnp.pad(flat, (0, pad)).reshape(-1, 128)
    everyone, g_all = gather_all(moe_in, g_tile, n_seq, n_exp)
    g_all = g_all.reshape(n_seq * n_exp, -1)[:, : experts * tok_rows]
    g_all = g_all.reshape(n_seq * n_exp, experts, tok_rows)
    mixed = None
    gate_col = lax.dynamic_slice_in_dim(
        g_all, lax.axis_index("exp") * w_gate.shape[0], w_gate.shape[0], 1
    )
    part = None
    for j in range(w_gate.shape[0]):
        gate_part = jnp.einsum("td,fd->tf", everyone, w_gate[j], preferred_element_type=jnp.float32)
        up_part = jnp.einsum("td,fd->tf", everyone, w_up[j], preferred_element_type=jnp.float32)
        active = (
            jax.nn.silu(gate_part) * up_part * gate_col[:, j, :].reshape(-1, 1)
        ).astype(jnp.bfloat16)
        one = jnp.dot(active, w_down[j], preferred_element_type=jnp.float32)
        part = one if part is None else part + one
    part = part.astype(jnp.bfloat16)
    total_rows, width = part.shape
    pieces = max(1, total_rows // 1024)
    step = width // pieces
    summed = [
        jax.jit(scatter_sum, static_argnums=(1, 2))(part[:, i * step : (i + 1) * step], n_seq, n_exp) for i in range(pieces)
    ]
    summed = summed[0] if pieces == 1 else jnp.concatenate(summed, axis=1)
    return (hid32 + summed).astype(jnp.bfloat16)


def solution(mesh):
    in_specs = (
        P("seq", "exp"),
        P("seq", "exp"),
        P("seq", "exp"),
        P("seq", "exp"),
        P(("seq", "exp"), None),
        P(),
        P(),
        P(("seq", "exp"), None),
        P(("seq", "exp"), None),
        P("exp", "seq", None),
        P("exp", "seq", None),
        P("exp", "seq", None),
    )
    out_specs = P(("seq", "exp"), None)
    return jax.shard_map(body, mesh=mesh, in_specs=in_specs, out_specs=out_specs, check_vma=False)
```

```python
import functools

import jax
import jax.numpy as jnp
from jax import lax
from jax.experimental import pallas as pl
from jax.experimental.pallas import tpu as pltpu
from jax.sharding import PartitionSpec as P

MESH = pl.DeviceIdType.MESH
PARTS = 2


class Place:
    def __init__(self, n_seq, n_exp):
        s, e = lax.axis_index("seq"), lax.axis_index("exp")
        self.fold, self.n_exp = n_exp // 4, n_exp
        self.length = (n_seq // 2) * self.fold
        self.p = (s // 2) * self.fold + e // 4
        self.x, self.y, self.c = s % 2, (e // 2) % 2, e % 2

    def ids(self, p, x, y, c):
        return (p // self.fold) * 2 + x, (p % self.fold) * 4 + y * 2 + c

    def block(self, p, x, y, c):
        s, e = self.ids(p, x, y, c)
        return s * self.n_exp + e

    def dev(self, dp=0, dx=0, dy=0, dc=0):
        x = 1 - self.x if dx else self.x
        y = 1 - self.y if dy else self.y
        c = 1 - self.c if dc else self.c
        return self.ids(self.p + dp, x, y, c)

    def greet(self, *more):
        barrier = pltpu.get_barrier_semaphore()
        for d in (dict(dx=1), dict(dy=1), dict(dc=1), *more):
            pl.semaphore_signal(barrier, inc=1, device_id=self.dev(**d), device_id_type=MESH)

        @pl.when(self.p > 0)
        def _():
            pl.semaphore_signal(barrier, inc=1, device_id=self.dev(dp=-1), device_id_type=MESH)

        @pl.when(self.p < self.length - 1)
        def _():
            pl.semaphore_signal(barrier, inc=1, device_id=self.dev(dp=1), device_id_type=MESH)

        ends = (self.p > 0).astype(jnp.int32) + (self.p < self.length - 1).astype(jnp.int32)
        pl.semaphore_wait(barrier, 3 + len(more) + ends)

    def at(self, stage, sign, k):
        if sign == 0:
            stage(0, 0, 0)
        elif sign < 0:
            pl.when(self.p >= k)(lambda: stage(2 * k - 1, -k, -1))
        else:
            pl.when(self.p + k < self.length)(lambda: stage(2 * k, k, 1))

    def far_first(self, stage):
        def one(i, carry):
            for sign in (1, -1):
                self.at(stage, sign, self.length - 1 - i)
            return carry

        if self.length <= 8:
            for i in range(self.length - 1):
                one(i, 0)
        else:
            lax.fori_loop(0, self.length - 1, one, 0)
        self.at(stage, 0, 0)

    def near_first(self, *stages):
        depth = len(stages)

        def ring(stage, k):
            if isinstance(k, int) and k == 0:
                self.at(stage, 0, 0)
            else:
                for sign in (-1, 1):
                    self.at(stage, sign, k)

        def step(k):
            for j, stage in enumerate(stages):
                if 0 <= k - j < self.length:
                    ring(stage, k - j)

        total = self.length + depth - 1
        if self.length <= 8:
            for k in range(total):
                step(k)
            return
        for k in range(depth):
            step(k)

        def one(k, carry):
            for j, stage in enumerate(stages):
                ring(stage, k - j)
            return carry

        lax.fori_loop(depth, self.length, one, 0)
        for k in range(self.length, total):
            step(k)


def gather_kernel(n_seq, n_exp, x_ref, g_ref, out_ref, gout_ref, send, recv, loc):
    me = Place(n_seq, n_exp)
    rows, width = x_ref.shape
    grow = g_ref.shape[0]
    me.greet()

    def place(ref, off, dx, dy, dc=0):
        x = 1 - me.x if dx else me.x
        y = 1 - me.y if dy else me.y
        c = 1 - me.c if dc else me.c
        b = me.block(me.p + off, x, y, c)
        n = rows if ref is out_ref else grow
        return ref.at[pl.ds(pl.multiple_of(b * n, n), n)]

    def copies(part, kind, slot, off, dx, dy, to, own=False, half=None, dc=0):
        dst_x, dst_g = place(out_ref, off, dx, dy, dc), place(gout_ref, off, dx, dy, dc)
        src_x, src_g = (x_ref, g_ref) if own else (dst_x, dst_g)
        span = width // PARTS
        if half is None:
            cols = pl.ds(part * span, span)
        else:
            cols = pl.ds(part * span + half * (span // 2), span // 2)
        out = [
            pltpu.make_async_remote_copy(
                src_x.at[:, cols],
                dst_x.at[:, cols],
                send.at[kind, slot, part],
                recv.at[kind, slot, part],
                to,
                MESH,
            )
        ]
        if half != 1 and part == 0:
            out.append(
                pltpu.make_async_remote_copy(
                    src_g, dst_g, send.at[kind, slot, PARTS], recv.at[kind, slot, PARTS], to, MESH
                )
            )
        return out

    def start(*a, **k):
        for cp in copies(*a, **k):
            cp.start()

    def wait_recv(*a, **k):
        for cp in copies(*a, **k):
            cp.wait_recv()

    def wait_send(*a, **k):
        for cp in copies(*a, **k):
            cp.wait_send()

    left, right = dict(dp=-1), dict(dp=1)
    X, Y, C = me.dev(dx=1), me.dev(dy=1), me.dev(dc=1)

    def line_sends(off, sign, do):
        own = sign == 0
        if sign <= 0:
            pl.when(me.p + 1 < me.length)(
                lambda: do(0, 2 * (-off + 1) - 1, off, 0, 0, me.dev(**right), own=own)
            )
        if sign >= 0:
            pl.when(me.p > 0)(lambda: do(0, 2 * (off + 1), off, 0, 0, me.dev(**left), own=own))

    def stage_line(slot, off, sign, do):
        own = sign == 0
        line_sends(off, sign, do)
        do(1, slot, off, 0, 0, X, own=own)
        do(2, slot, off, 0, 0, Y, own=own)
        do(5, slot, off, 0, 0, C, own=own)

    def stage_xy_1(slot, off, do):
        do(3, slot, off, 1, 0, Y, half=0)
        do(6, slot, off, 1, 0, C)

    def stage_xy_2(slot, off, do):
        do(4, slot, off, 0, 1, X, half=1)
        do(7, slot, off, 0, 1, C)

    def stage_diag(slot, off, do):
        do(8, slot, off, 1, 1, C)

    local = [
        pltpu.make_async_copy(x_ref, place(out_ref, 0, 0, 0), loc.at[0]),
        pltpu.make_async_copy(g_ref, place(gout_ref, 0, 0, 0), loc.at[1]),
    ]
    for cp in local:
        cp.start()

    def s1(slot, off, sign):
        for part in range(PARTS):
            if sign:
                wait_recv(part, 0, slot, off, 0, 0, X)
            stage_line(slot, off, sign, functools.partial(start, part))

    def s2(slot, off, sign):
        for part in range(PARTS):
            wait_recv(part, 1, slot, off, 1, 0, X)
            stage_xy_1(slot, off, functools.partial(start, part))
            wait_recv(part, 2, slot, off, 0, 1, X)
            stage_xy_2(slot, off, functools.partial(start, part))

    def s3(slot, off, sign):
        for part in range(PARTS):
            wait_recv(part, 3, slot, off, 1, 1, X, half=0)
            wait_recv(part, 4, slot, off, 1, 1, X, half=1)
            stage_diag(slot, off, functools.partial(start, part))

    me.near_first(s1, s2, s3)

    def s4(slot, off, sign):
        for part in range(PARTS):
            done = functools.partial(wait_send, part)
            stage_line(slot, off, sign, done)
            stage_xy_1(slot, off, done)
            stage_xy_2(slot, off, done)
            stage_diag(slot, off, done)
            wait_recv(part, 5, slot, off, 0, 0, X, dc=1)
            wait_recv(part, 6, slot, off, 1, 0, X, dc=1)
            wait_recv(part, 7, slot, off, 0, 1, X, dc=1)
            wait_recv(part, 8, slot, off, 1, 1, X, dc=1)

    me.near_first(s4)
    for cp in local:
        cp.wait()


def gather_all(x, g, n_seq, n_exp):
    n = n_seq * n_exp
    length = n // 8
    anyspace = pl.BlockSpec(memory_space=pl.ANY)
    return pl.pallas_call(
        functools.partial(gather_kernel, n_seq, n_exp),
        out_shape=(
            jax.ShapeDtypeStruct((n * x.shape[0], x.shape[1]), x.dtype),
            jax.ShapeDtypeStruct((n * g.shape[0], g.shape[1]), g.dtype),
        ),
        in_specs=[anyspace, anyspace],
        out_specs=(anyspace, anyspace),
        scratch_shapes=[
            pltpu.SemaphoreType.DMA((9, 2 * length + 1, PARTS + 1)),
            pltpu.SemaphoreType.DMA((9, 2 * length + 1, PARTS + 1)),
            pltpu.SemaphoreType.DMA((2,)),
        ],
        compiler_params=pltpu.CompilerParams(collective_id=1, has_side_effects=True),
    )(x, g)


def scatter_kernel(
    n_seq, n_exp, y_ref, out_ref, acc, sib, xbuf, ybuf, dab, dbb, line, send, recv, loc
):
    me = Place(n_seq, n_exp)
    L = me.length
    rows, width = out_ref.shape
    halfw = width // 2
    me.greet()
    X, Y, C = me.dev(dx=1), me.dev(dy=1), me.dev(dc=1)

    def src(off, grp, dc):
        x = 1 - me.x if grp & 1 else me.x
        y = 1 - me.y if grp & 2 else me.y
        c = 1 - me.c if dc else me.c
        b = me.block(me.p + off, x, y, c)
        return y_ref.at[pl.ds(pl.multiple_of(b * rows, rows), rows)]

    def sib_copy(slot, off, grp):
        return pltpu.make_async_remote_copy(
            src(off, grp, 1), sib.at[grp, slot], send.at[grp, slot], recv.at[grp, slot], C, MESH
        )

    def load(slot, off, grp):
        return pltpu.make_async_copy(src(off, grp, 0), acc.at[grp, slot], loc.at[grp, slot])

    for grp in (3, 1, 2, 0):

        def go(slot, off, sign, grp=grp):
            sib_copy(slot, off, grp).start()
            load(slot, off, grp).start()

        me.far_first(go)

    f32 = jnp.float32

    def pair_sum(slot, off, grp):
        load(slot, off, grp).wait()
        sib_copy(slot, off, grp).wait_recv()
        return acc[grp, slot].astype(f32) + sib[grp, slot].astype(f32)

    def diag_a(slot):
        return pltpu.make_async_remote_copy(
            acc.at[3, slot, :, pl.ds(0, halfw)], dab.at[slot], send.at[4, slot], recv.at[4, slot], Y, MESH
        )

    def diag_b(slot):
        return pltpu.make_async_remote_copy(
            acc.at[3, slot, :, pl.ds(halfw, halfw)], dbb.at[slot], send.at[5, slot], recv.at[5, slot], X, MESH
        )

    def x_copy(slot):
        return pltpu.make_async_remote_copy(
            acc.at[1, slot], xbuf.at[slot], send.at[6, slot], recv.at[6, slot], X, MESH
        )

    def y_copy(slot):
        return pltpu.make_async_remote_copy(
            acc.at[2, slot], ybuf.at[slot], send.at[7, slot], recv.at[7, slot], Y, MESH
        )

    def line_copy(slot, sign):
        return pltpu.make_async_remote_copy(
            acc.at[0, slot],
            line.at[slot],
            send.at[8, slot],
            recv.at[8, slot],
            me.dev(dp=sign),
            MESH,
        )

    def d1(slot, off, sign):
        acc[3, slot] = pair_sum(slot, off, 3).astype(acc.dtype)
        diag_a(slot).start()
        diag_b(slot).start()

    def d2(slot, off, sign):
        sx = pair_sum(slot, off, 1)
        diag_a(slot).wait_recv()
        acc[1, slot, :, pl.ds(0, halfw)] = (sx[:, :halfw] + dab[slot].astype(f32)).astype(acc.dtype)
        acc[1, slot, :, pl.ds(halfw, halfw)] = sx[:, halfw:].astype(acc.dtype)
        x_copy(slot).start()
        sy = pair_sum(slot, off, 2)
        diag_b(slot).wait_recv()
        acc[2, slot, :, pl.ds(0, halfw)] = sy[:, :halfw].astype(acc.dtype)
        acc[2, slot, :, pl.ds(halfw, halfw)] = (sy[:, halfw:] + dbb[slot].astype(f32)).astype(acc.dtype)
        y_copy(slot).start()

    def d3(slot, off, sign):
        total = pair_sum(slot, off, 0)
        x_copy(slot).wait_recv()
        y_copy(slot).wait_recv()
        total = total + xbuf[slot].astype(f32) + ybuf[slot].astype(f32)
        if sign == 0:
            out_ref[...] = total
            if L > 1:

                @pl.when(me.p > 0)
                def _():
                    in_copy(2).wait_recv()
                    out_ref[...] += line[2].astype(f32)

                @pl.when(me.p < L - 1)
                def _():
                    in_copy(1).wait_recv()
                    out_ref[...] += line[1].astype(f32)

            return
        acc[0, slot] = total.astype(acc.dtype)
        far = slot + 2
        behind = me.p > 0 if sign > 0 else me.p < L - 1

        @pl.when(jnp.logical_and(behind, sign * off + 1 < L))
        def _():
            in_copy(far).wait_recv()
            acc[0, slot] = (acc[0, slot].astype(f32) + line[far].astype(f32)).astype(acc.dtype)

        line_copy(slot, sign).start()

    def in_copy(slot):
        return pltpu.make_async_remote_copy(
            acc.at[0, slot], line.at[slot], send.at[8, slot], recv.at[8, slot], X, MESH
        )

    me.far_first(d1)
    me.far_first(d2)
    me.far_first(d3)

    def fin(slot, off, sign):
        for grp in range(4):
            sib_copy(slot, off, grp).wait_send()
        diag_a(slot).wait_send()
        diag_b(slot).wait_send()
        x_copy(slot).wait_send()
        y_copy(slot).wait_send()
        if sign:
            line_copy(slot, sign).wait_send()

    me.far_first(fin)


def scatter_sum(part, n_seq, n_exp):
    n = n_seq * n_exp
    slots = n // 4 - 1 + 2
    rows, width = part.shape[0] // n, part.shape[1]
    bf = jnp.bfloat16
    return pl.pallas_call(
        functools.partial(scatter_kernel, n_seq, n_exp),
        out_shape=jax.ShapeDtypeStruct((rows, width), jnp.float32),
        in_specs=[pl.BlockSpec(memory_space=pl.ANY)],
        out_specs=pl.BlockSpec(memory_space=pltpu.VMEM),
        scratch_shapes=[
            pltpu.VMEM((4, slots, rows, width), bf),
            pltpu.VMEM((4, slots, rows, width), bf),
            pltpu.VMEM((slots, rows, width), bf),
            pltpu.VMEM((slots, rows, width), bf),
            pltpu.VMEM((slots, rows, width // 2), bf),
            pltpu.VMEM((slots, rows, width // 2), bf),
            pltpu.VMEM((slots, rows, width), bf),
            pltpu.SemaphoreType.DMA((9, slots)),
            pltpu.SemaphoreType.DMA((9, slots)),
            pltpu.SemaphoreType.DMA((4, slots)),
        ],
        compiler_params=pltpu.CompilerParams(
            collective_id=2, has_side_effects=True, vmem_limit_bytes=60 * 2**20
        ),
    )(part)


GPARTS = 4
HPARTS = 4
PLANES = 4


def plane_orders(length):
    def depth(q):
        return min(q, length - 1 - q)

    visit = []
    for p in range(length):
        rest = [q for q in range(length) if q != p]
        near = min(rest, key=lambda q: (abs(q - p), depth(q)), default=p)
        rest = sorted((q for q in rest if q != near), key=lambda q: (depth(q), abs(q - p)))
        visit.append([p] + [near] * (length > 1) + rest)
    lines = []
    for p in range(length):
        def ready(q):
            chain = range(0, p + 1) if q > p else range(p, length)
            return max(visit[b].index(q) for b in chain)

        low = 2 * p < length
        lines.append(sorted((q for q in range(length) if q != p), key=lambda q: (ready(q), -q if low else q)))
    return visit, lines


def pick(table, p, j):
    total = 0
    for a, row in enumerate(table):
        for b, v in enumerate(row):
            hit = jnp.logical_and(p == a, j == b).astype(jnp.int32)
            total = total + hit * v
    return total


def spans(tiles, parts):
    cuts = [(tiles * i // parts) * 128 for i in range(parts + 1)]
    return [pl.ds(a, b - a) for a, b in zip(cuts[:-1], cuts[1:])]


def when(cond, fn):
    def run():
        fn()

    pl.when(cond)(run)


def attend_tokens(
    me, q_ref, k_ref, v_ref, ld_ref, res_ref, ag_ref, mg_ref, ids_ref, gw_ref, x_out,
    hid, work, flat, own16, peer, cin, cout, tots, tok, psend, precv, tsem, msend, mrecv,
):
    L, z = me.length, me.p
    f32, bf = jnp.float32, jnp.bfloat16
    heads, block = ld_ref.shape
    dim = q_ref.shape[1] // heads
    rows = res_ref.shape[0]
    n_exp, width = tok.shape[0], tok.shape[2]
    e = lax.axis_index("exp")
    pair = me.dev(dx=1)

    def head(h):
        return pl.ds(h * dim, dim)

    def pair_copy(h):
        return pltpu.make_async_remote_copy(
            own16.at[h], peer.at[h], psend.at[0, h], precv.at[0, h], pair, MESH
        )

    def line_copy(h):
        return pltpu.make_async_remote_copy(
            cout.at[h], cin.at[h], psend.at[1, h], precv.at[1, h], me.dev(dp=1), MESH
        )

    tot_copy = pltpu.make_async_remote_copy(tots.at[0], tots.at[1], tsem.at[0], tsem.at[1], pair, MESH)

    nt = (((1,), (1,)), ((), ()))
    tn = (((0,), (0,)), ((), ()))
    r = lax.broadcasted_iota(jnp.int32, (block, block), 0)
    c = lax.broadcasted_iota(jnp.int32, (block, block), 1)
    seen = r >= c
    decay = ld_ref[...]
    high = lax.Precision.HIGHEST
    cum = lax.dot_general(seen.astype(f32), decay, nt, precision=high, preferred_element_type=f32)
    cum_t = jnp.dot(decay, (r <= c).astype(f32), precision=high, preferred_element_type=f32)
    total = cum_t[:, block - 1 :]
    tots[0, 0:heads, :] = jnp.broadcast_to(total, (heads, dim))

    def state(h):
        kw = (k_ref[:, head(h)].astype(f32) * jnp.exp(total[h : h + 1] - cum[:, h : h + 1])).astype(bf)
        own = lax.dot_general(kw, v_ref[:, head(h)], tn, preferred_element_type=f32)
        work[:, pl.ds((heads + h) * dim, dim)] = own
        own16[h] = own.astype(bf)

    for h in range(heads):
        state(h)
    me.greet(dict(dy=1, dc=1))
    tot_copy.start()
    for h in range(heads):
        pair_copy(h).start()

    @pl.when(z == 0)
    def _():
        cin[...] = jnp.zeros_like(cin)

    def f_intra(h):
        scores = lax.dot_general(q_ref[:, head(h)], k_ref[:, head(h)], nt, preferred_element_type=f32)
        gap = cum[:, h : h + 1] - cum_t[h : h + 1, :]
        weights = jnp.where(seen, scores * jnp.exp(jnp.where(seen, gap, 0.0)), 0.0).astype(bf)
        work[:, head(h)] = jnp.dot(weights, v_ref[:, head(h)], preferred_element_type=f32)

    for h in range(heads):
        f_intra(h)
    tot_copy.wait_recv()
    mine, other = tots[0, 0:heads, :], tots[1, 0:heads, :]
    both = jnp.exp(mine + other)
    is_odd = jnp.full(mine.shape, me.x, jnp.int32) == 1
    one = jnp.ones_like(mine)
    own_by = jnp.where(is_odd, one, jnp.exp(other))
    peer_by = jnp.where(is_odd, jnp.exp(mine), one)
    carry_by = jnp.where(is_odd, jnp.exp(other), one)
    peer_in = jnp.where(is_odd, one, jnp.zeros_like(mine))

    peers = (dict(dc=1), dict(dy=1), dict(dy=1, dc=1))
    pieces = 2
    span = width // pieces

    def mix_copy(k, i):
        to = me.dev(**peers[k])
        cols = pl.ds(i * span, span)
        src = flat.at[pl.ds(pl.multiple_of(to[1] * rows, rows), rows), cols]
        return pltpu.make_async_remote_copy(
            src, tok.at[e, :, cols], msend.at[k, i], mrecv.at[k, i], to, MESH
        )

    def mix_in(k, i):
        to = me.dev(**peers[k])
        cols = pl.ds(i * span, span)
        return pltpu.make_async_remote_copy(
            tok.at[to[1], :, cols], tok.at[to[1], :, cols], msend.at[k, i], mrecv.at[k, i], to, MESH
        )

    def f_chain(h):
        pair_copy(h).wait_recv()
        pl.when(z > 0)(lambda: line_copy(h).wait_recv())
        near = peer[h].astype(f32)
        come = cin[h].astype(f32)
        row = slice(h, h + 1)

        @pl.when(z < L - 1)
        def _():
            mix = both[row] * come + own_by[row] * work[:, pl.ds((heads + h) * dim, dim)] + peer_by[row] * near
            cout[h] = mix.astype(bf)
            line_copy(h).start()

    def f_head(h):
        near = peer[h].astype(f32)
        come = cin[h].astype(f32)
        row = slice(h, h + 1)
        carried = carry_by[row] * come + peer_in[row] * near
        coarse = carried.astype(bf)
        fine = (carried - coarse.astype(f32)).astype(bf)
        query = q_ref[:, head(h)]
        inter = jnp.dot(query, coarse, preferred_element_type=f32) + jnp.dot(
            query, fine, preferred_element_type=f32
        )
        attn = work[:, head(h)] + jnp.exp(cum[:, h : h + 1]) * inter
        scale = lax.rsqrt(jnp.mean(attn * attn, axis=-1, keepdims=True) + 1e-06)
        flat[0:block, head(h)] = (attn * scale).astype(bf)
        if (h + 1) * pieces % heads == 0:
            for k in range(len(peers)):
                mix_copy(k, (h + 1) * pieces // heads - 1).start()

    for h in range(heads):
        f_chain(h)
        f_head(h)

    tok[e] = flat[pl.ds(pl.multiple_of(e * rows, rows), rows), 0:width]

    def f_mix():
        for i in range(pieces):
            for k in range(len(peers)):
                mix_in(k, i).wait_recv()

    f_mix()
    square = jnp.zeros((rows, 1), f32)
    for j in range(n_exp):
        cols = pl.ds(j * width, width)
        value = (res_ref[:, cols].astype(f32) + tok[j].astype(f32) * ag_ref[:, cols]).astype(bf)
        hid[:, cols] = value
        wide = value.astype(f32)
        square = square + jnp.sum(wide * wide, axis=1, keepdims=True)
    scale = lax.rsqrt(square / (n_exp * width) + 1e-06)
    for j in range(n_exp):
        cols = pl.ds(j * width, width)
        x_out[:, cols] = (hid[:, cols].astype(f32) * scale * mg_ref[:, cols]).astype(bf)

    def column(ref):
        same = lax.broadcasted_iota(jnp.int32, (rows, rows), 0) == lax.broadcasted_iota(jnp.int32, (rows, rows), 1)
        return lax.dot_general(
            same.astype(f32), ref[...].astype(f32), nt, precision=high, preferred_element_type=f32
        )

    ids, gates = column(ids_ref).astype(jnp.int32), column(gw_ref)
    coarse = gates.astype(bf).astype(f32)
    rest = gates - coarse
    lane = lax.broadcasted_iota(jnp.int32, (rows, 128), 1)
    extra = jnp.zeros((rows, 128), f32)
    for i in range(ids_ref.shape[0]):
        who = ids[:, i : i + 1]
        extra = jnp.where(lane == who, coarse[:, i : i + 1], extra)
        extra = jnp.where(lane == who + 64, rest[:, i : i + 1], extra)
    x_out[:, n_exp * width :] = extra.astype(bf)

    def finish():
        tot_copy.wait_send()
        for h in range(heads):
            pair_copy(h).wait_send()
            pl.when(z < L - 1)(lambda: line_copy(h).wait_send())
        for i in range(pieces):
            for k in range(len(peers)):
                mix_copy(k, i).wait_send()

    return finish


def moe_kernel(
    n_seq, n_exp, q_ref, k_ref, v_ref, ld_ref, res_ref, ag_ref, mg_ref, ids_ref, gw_ref,
    wg_ref, wu_ref, wd_ref, out_ref,
    xs, ys, act, sib, din, xin, yin, lin, tot, wg, wu, wd, hid_ref,
    own16, peer, cin, cout, tots, tok,
    gsend, grecv, bsend, brecv, ssend, srecv, loc, psend, precv, tsem, msend, mrecv,
):
    me = Place(n_seq, n_exp)
    L, p = me.length, me.p
    rows, width = out_ref.shape
    hidden = wg.shape[0]
    many = 8 * rows
    f32, bf = jnp.float32, jnp.bfloat16
    X, Y, C = me.dev(dx=1), me.dev(dy=1), me.dev(dc=1)
    visit, lines = plane_orders(L)
    gcols = spans(xs.shape[1] // 128, GPARTS)
    hcols = spans(width // 128, HPARTS)

    loads = [
        pltpu.make_async_copy(a.at[0], b, loc.at[i])
        for i, (a, b) in enumerate(((wg_ref, wg), (wu_ref, wu), (wd_ref, wd)))
    ]
    for cp in loads:
        cp.start()

    def flip(v, d):
        return 1 - v if d else v

    def row(q, dx=0, dy=0, dc=0):
        k = (flip(me.c, dc) * 2 + flip(me.x, dx)) * 2 + flip(me.y, dy)
        return pl.ds(pl.multiple_of((q * 8 + k) * rows, rows), rows)

    def srow(q, dx=0, dy=0):
        k = flip(me.x, dx) * 2 + flip(me.y, dy)
        return pl.ds(pl.multiple_of((q * 4 + k) * rows, rows), rows)

    def prow(q):
        return pl.ds(pl.multiple_of(q * rows, rows), rows)

    def gcopy(kind, q, part, r, to, skind=None):
        ref = xs.at[r, gcols[part]]
        skind = kind if skind is None else skind
        return pltpu.make_async_remote_copy(
            ref, ref, gsend.at[skind, q, part], grecv.at[kind, q, part], to, MESH
        )

    upper = GPARTS // 2

    def line_pair(q, part, do):
        pl.when(jnp.logical_and(q >= p, p > 0))(
            lambda: do(gcopy(0, q, part, row(q), me.dev(dp=-1)))
        )
        pl.when(jnp.logical_and(q <= p, p + 1 < L))(
            lambda: do(gcopy(0, q, part, row(q), me.dev(dp=1), 9))
        )

    def start(cp):
        cp.start()

    def g_line(q, part):
        pl.when(q != p)(lambda: gcopy(0, q, part, row(q), X).wait_recv())
        line_pair(q, part, start)

    def first(q, part):
        return [gcopy(2, q, part, row(q), Y), gcopy(5, q, part, row(q), C)]

    def second_x(q, part):
        out = [gcopy(6, q, part, row(q, 1, 0), C)]
        return out if part >= upper else [gcopy(3, q, part, row(q, 1, 0), Y)] + out

    def second_y(q, part):
        out = [gcopy(7, q, part, row(q, 0, 1), C)]
        return out if part < upper else [gcopy(4, q, part, row(q, 0, 1), X)] + out

    def third(q, part):
        return [gcopy(8, q, part, row(q, 1, 1), C)]

    lower, higher = range(upper), range(upper, GPARTS)

    def g_first(q, turn):
        for part in lower if turn == 0 else higher:
            gcopy(1, q, part, row(q), X).start()
        for part in higher if turn == 0 else lower:
            gcopy(2, q, part, row(q), Y).start()
        if turn == 0:
            for part in range(GPARTS):
                gcopy(5, q, part, row(q), C).start()

    def g_own(q):
        for part in lower:
            line_pair(q, part, start)
        g_first(q, 0)
        for part in lower:
            gcopy(1, q, part, row(q), X).wait_send()
        for part in higher:
            line_pair(q, part, start)
        g_first(q, 1)

    def from_x(q, part):
        gcopy(1, q, part, row(q, 1, 0), X).wait_recv()
        for cp in second_x(q, part):
            cp.start()

    def from_y(q, part):
        gcopy(2, q, part, row(q, 0, 1), X).wait_recv()
        for cp in second_y(q, part):
            cp.start()

    def g_second(q):
        for part in lower:
            from_x(q, part)
            from_y(q, part + upper)

    def g_rest(q):
        for part in lower:
            from_x(q, part + upper)
            from_y(q, part)

    def g_third(q):
        for part in range(GPARTS):
            gcopy(3 if part < upper else 4, q, part, row(q, 1, 1), X).wait_recv()
            for cp in third(q, part):
                cp.start()

    def g_ring(k, parts):
        for sign in (-1, 1):
            q = p + sign * k
            when(jnp.logical_and(q >= 0, q < L), lambda: [g_line(q, part) for part in parts])

    def g_done(q):
        for part in range(GPARTS):
            gcopy(5, q, part, row(q, 0, 0, 1), X).wait_recv()
            gcopy(6, q, part, row(q, 1, 0, 1), X).wait_recv()
            gcopy(7, q, part, row(q, 0, 1, 1), X).wait_recv()
            gcopy(8, q, part, row(q, 1, 1, 1), X).wait_recv()

    def g_drain(q):
        for part in range(GPARTS):
            line_pair(q, part, lambda cp: cp.wait_send())
            across = gcopy(1, q, part, row(q), X)
            if part < upper:
                pl.when(q != p)(lambda: across.wait_send())
            else:
                across.wait_send()
            for cp in first(q, part) + second_x(q, part) + second_y(q, part) + third(q, part):
                cp.wait_send()

    def sib_copy(q, h):
        r = pl.ds(pl.multiple_of((q * 2 + 1 - me.c) * 4 * rows, 4 * rows), 4 * rows)
        d = pl.ds(pl.multiple_of(q * 4 * rows, 4 * rows), 4 * rows)
        return pltpu.make_async_remote_copy(
            ys.at[r, hcols[h]], sib.at[d, hcols[h]], bsend.at[q, h], brecv.at[q, h], C, MESH
        )

    def scopy(kind, q, h, r, dst, d, to):
        return pltpu.make_async_remote_copy(
            ys.at[r, hcols[h]], dst.at[d, hcols[h]], ssend.at[kind, q, h], srecv.at[kind, q, h], to, MESH
        )

    def diag_copy(q, h):
        return scopy(0, q, h, row(q, 1, 1), din, prow(q), Y if 2 * h < HPARTS else X)

    def x_copy(q, h):
        return scopy(1, q, h, row(q, 1, 0), xin, prow(q), X)

    def y_copy(q, h):
        return scopy(2, q, h, row(q, 0, 1), yin, prow(q), Y)

    def line_copy(q, h):
        up = (q > p).astype(jnp.int32)
        last = jnp.logical_and(q < p, q == p - 1).astype(jnp.int32)
        slot = q + (L - q) * last
        return pltpu.make_async_remote_copy(
            ys.at[row(q), hcols[h]],
            lin.at[prow(slot), hcols[h]],
            ssend.at[3, q, h],
            srecv.at[3, slot, h],
            me.dev(dp=2 * up - 1),
            MESH,
        )

    def line_in(slot, h):
        return pltpu.make_async_remote_copy(
            ys.at[row(p), hcols[h]], lin.at[prow(slot), hcols[h]], ssend.at[3, p, h], srecv.at[3, slot, h], X, MESH
        )

    def pair(q, h, dx, dy):
        return ys[row(q, dx, dy), hcols[h]].astype(f32) + sib[srow(q, dx, dy), hcols[h]].astype(f32)

    def r_first(q, h):
        sib_copy(q, h).wait_recv()
        ys[row(q, 1, 1), hcols[h]] = pair(q, h, 1, 1).astype(bf)
        diag_copy(q, h).start()

    def r_second(q, h):
        sx, sy = pair(q, h, 1, 0), pair(q, h, 0, 1)
        diag_copy(q, h).wait_recv()
        more = din[prow(q), hcols[h]].astype(f32)
        if 2 * h < HPARTS:
            sx = sx + more
        else:
            sy = sy + more
        ys[row(q, 1, 0), hcols[h]] = sx.astype(bf)
        x_copy(q, h).start()
        ys[row(q, 0, 1), hcols[h]] = sy.astype(bf)
        y_copy(q, h).start()

    def r_third(q, h):
        total = pair(q, h, 0, 0)
        x_copy(q, h).wait_recv()
        y_copy(q, h).wait_recv()
        total = total + xin[prow(q), hcols[h]].astype(f32) + yin[prow(q), hcols[h]].astype(f32)
        tot[prow(q), hcols[h]] = total

    def r_line(q, h):
        behind = jnp.logical_or(jnp.logical_and(q > p, p > 0), jnp.logical_and(q < p, p < L - 1))

        @pl.when(behind)
        def _():
            line_in(q, h).wait_recv()
            ys[row(q), hcols[h]] = (tot[prow(q), hcols[h]] + lin[prow(q), hcols[h]].astype(f32)).astype(bf)

        @pl.when(jnp.logical_not(behind))
        def _():
            ys[row(q), hcols[h]] = tot[prow(q), hcols[h]].astype(bf)

        line_copy(q, h).start()

    def r_last(h):
        cols = hcols[h]

        @pl.when(p > 0)
        def _():
            line_in(p, h).wait_recv()
            tot[prow(p), cols] += lin[prow(p), cols].astype(f32)

        @pl.when(p < L - 1)
        def _():
            line_in(L, h).wait_recv()
            tot[prow(p), cols] += lin[prow(L), cols].astype(f32)

        out_ref[:, cols] = (hid_ref[:, cols].astype(f32) + tot[prow(p), cols]).astype(bf)

    at_end = jnp.logical_or(p == 0, p == L - 1)
    inner = jnp.logical_not(at_end)

    def r_early(q, h):
        pl.when(jnp.logical_and(at_end, q != p))(lambda: r_line(q, h))

    def r_drain(q):
        for h in range(HPARTS):
            sib_copy(q, h).wait_send()
            diag_copy(q, h).wait_send()
            x_copy(q, h).wait_send()
            y_copy(q, h).wait_send()
            pl.when(q != p)(lambda: line_copy(q, h).wait_send())

    tile = next(t for t in range(512, 0, -128) if hidden % t == 0)
    fsteps = hidden // tile

    def block_of(q):
        return pl.ds(pl.multiple_of(q * many, many), many)

    def gate_of(q):
        extra = xs[block_of(q), width : width + 128].astype(f32)
        lane = lax.broadcasted_iota(jnp.int32, extra.shape, 1)
        e = lax.axis_index("exp")
        keep = jnp.logical_or(lane == e, lane == e + 64)
        return jnp.sum(jnp.where(keep, extra, 0.0), axis=1, keepdims=True)

    nt = (((1,), (1,)), ((), ()))

    def ffn_in(q, f):
        fc = pl.ds(f * tile, tile)
        rows_in = xs[block_of(q), 0:width]
        gate = lax.dot_general(rows_in, wg[fc, :], nt, preferred_element_type=f32)
        up = lax.dot_general(rows_in, wu[fc, :], nt, preferred_element_type=f32)
        act[:, fc] = (gate / (1.0 + jnp.exp(-gate)) * up * gate_of(q)).astype(bf)

    def ffn_out(q, h):
        ys[block_of(q), hcols[h]] = jnp.dot(
            act[...], wd[:, hcols[h]], preferred_element_type=f32
        ).astype(bf)
        sib_copy(q, h).start()

    front_done = attend_tokens(
        me, q_ref, k_ref, v_ref, ld_ref, res_ref, ag_ref, mg_ref, ids_ref, gw_ref, xs.at[row(p)],
        hid_ref, tot, act, own16, peer, cin, cout, tots, tok, psend, precv, tsem, msend, mrecv,
    )
    second = pick(visit, p, 1)
    g_own(p)
    g_second(p)
    g_ring(1, lower)
    g_rest(p)
    g_ring(1, higher)
    g_first(second, 0)
    g_third(p)
    g_first(second, 1)
    front_done()
    for cp in loads:
        cp.wait()

    def chunk(j, carry):
        q, nxt, prev = pick(visit, p, j), pick(visit, p, j + 1), pick(visit, p, j - 1)
        older = pick(visit, p, j - 2)
        third, fourth = pick(visit, p, 2), pick(visit, p, 3)

        def opening(*fns):
            when(j == 0, lambda: [fn() for fn in fns])

        def closing(*fns):
            when(j == L - 1, lambda: [fn() for fn in fns])

        def ahead(*fns):
            when(jnp.logical_and(j > 0, j + 1 < L), lambda: [fn() for fn in fns])

        def after(*fns):
            when(j > 0, lambda: [fn() for fn in fns])

        def later(*fns):
            when(j > 1, lambda: [fn() for fn in fns])

        def settle(at, h):
            r_third(at, h)
            r_early(at, h)

        def hook(n):
            if n == 0:
                after(lambda: r_first(prev, 2), lambda: r_first(prev, 3))
                opening(
                    lambda: g_ring(2, lower),
                    lambda: g_second(nxt),
                    lambda: g_ring(2, higher),
                    lambda: g_first(fourth, 0),
                )
            if n == 1:
                opening(lambda: g_rest(nxt), lambda: g_first(fourth, 1))
                ahead(lambda: g_second(nxt))
                later(lambda: settle(older, 0), lambda: settle(older, 1))
                after(lambda: r_second(prev, 0), lambda: r_second(prev, 1))
            if n == 2:
                ahead(lambda: g_rest(nxt))
                later(lambda: settle(older, 2), lambda: settle(older, 3))

        g_done(q)
        for f in range(fsteps):
            ffn_in(q, f)
            hook(f)
        for f in range(fsteps, 3):
            hook(f)
        for h in range(HPARTS):
            ffn_out(q, h)
            if h == 0:
                after(lambda: r_second(prev, 2))
            if h == 1:
                after(lambda: r_second(prev, 3))
                opening(lambda: g_ring(3, range(GPARTS)), lambda: g_first(third, 0))
            if h == 2:
                r_first(q, 0)
                ahead(lambda: g_third(nxt))
                opening(lambda: g_third(nxt))
                closing(lambda: settle(prev, 0))
            if h == 3:
                r_first(q, 1)
                opening(lambda: g_first(third, 1))
                closing(lambda: settle(prev, 1))
        return carry

    def one_line(i, h):
        when(inner, lambda: r_line(pick(lines, p, i), h))

    lax.fori_loop(0, L, chunk, 0)

    final, prior = pick(visit, p, L - 1), pick(visit, p, L - 2)
    r_first(final, 2)
    r_first(final, 3)
    for h in (2, 3):
        r_third(prior, h)
        r_early(prior, h)
    for h in range(HPARTS):
        r_second(final, h)
        one_line(0, h)
    for h in range(HPARTS):
        one_line(1, h)
        r_third(final, h)
        r_early(final, h)
    for h in range(HPARTS):
        one_line(2, h)
        if h:
            r_last(h - 1)
    r_last(HPARTS - 1)

    def drain(q, carry):
        g_drain(q)
        r_drain(q)
        return carry

    lax.fori_loop(0, L, drain, 0)


def moe_scratch(n_seq, n_exp, x_shape, w_shape):
    n, L = n_seq * n_exp, n_seq * n_exp // 8
    rows, wide = x_shape
    hidden, width = w_shape[1:]
    bf, f32 = jnp.bfloat16, jnp.float32
    return [
        ((n * rows, wide), bf),
        ((n * rows, width), bf),
        ((8 * rows, hidden), bf),
        ((n // 2 * rows, width), bf),
        ((L * rows, width), bf),
        ((L * rows, width), bf),
        ((L * rows, width), bf),
        ((L * rows + rows, width), bf),
        ((L * rows, width), f32),
        ((hidden, width), bf),
        ((hidden, width), bf),
        ((hidden, width), bf),
    ]


MOE_VMEM = 61 * 2**20


def moe_fits(n_seq, n_exp, rows, width, w_shape):
    need = sum(
        a * b * jnp.dtype(t).itemsize for (a, b), t in moe_scratch(n_seq, n_exp, (rows, width + 128), w_shape)
    )
    return (
        w_shape[0] == 1
        and n_exp // 4 == 1
        and n_seq * n_exp == 8 * PLANES
        and w_shape[1] % 128 == 0
        and w_shape[2] % (128 * HPARTS) == 0
        and need + 6 * 2**20 <= MOE_VMEM
    )


def whole_layer(
    queries, keys, values, log_decay, residual, attn_gain, moe_gain, expert_ids, gate_weights,
    w_gate, w_up, w_down, n_seq, n_exp,
):
    L = n_seq * n_exp // 8
    heads = log_decay.shape[1]
    part = queries.shape[1]
    dim = part // heads
    rows, width = residual.shape
    vmem = pl.BlockSpec(memory_space=pltpu.VMEM)
    anyspace = pl.BlockSpec(memory_space=pl.ANY)
    dma = pltpu.SemaphoreType.DMA
    bf = jnp.bfloat16
    states = pltpu.VMEM((heads, dim, dim), bf)
    scratch = moe_scratch(n_seq, n_exp, (rows, width + 128), w_gate.shape)
    return pl.pallas_call(
        functools.partial(moe_kernel, n_seq, n_exp),
        out_shape=jax.ShapeDtypeStruct(residual.shape, bf),
        in_specs=[vmem] * 9 + [anyspace] * 3,
        out_specs=vmem,
        scratch_shapes=[pltpu.VMEM(s, t) for s, t in scratch]
        + [
            pltpu.VMEM(residual.shape, bf),
            states,
            states,
            states,
            states,
            pltpu.VMEM((2, heads + -heads % 8, dim), jnp.float32),
            pltpu.VMEM((n_exp, rows, part), bf),
            dma((10, L, GPARTS)),
            dma((10, L, GPARTS)),
            dma((L, HPARTS)),
            dma((L, HPARTS)),
            dma((4, L + 1, HPARTS)),
            dma((4, L + 1, HPARTS)),
            dma((3,)),
            dma((2, heads)),
            dma((2, heads)),
            dma((2,)),
            dma((3, 2)),
            dma((3, 2)),
        ],
        compiler_params=pltpu.CompilerParams(
            collective_id=5, has_side_effects=True, vmem_limit_bytes=MOE_VMEM
        ),
    )(
        queries, keys, values, log_decay.T, residual, attn_gain[None, :], moe_gain[None, :],
        expert_ids.T, gate_weights.T, w_gate, w_up, w_down,
    )


def carry_kernel(n_seq, own_ref, own16_ref, tot_ref, out_ref, peer, ptot, cin, cout, send, recv, tsem):
    s, e = lax.axis_index("seq"), lax.axis_index("exp")
    z, odd, deep = s // 2, s % 2, n_seq // 2
    heads = own_ref.shape[0]
    pair = (z * 2 + 1 - odd, e)

    barrier = pltpu.get_barrier_semaphore()
    pl.semaphore_signal(barrier, inc=1, device_id=pair, device_id_type=MESH)

    @pl.when(z > 0)
    def _():
        pl.semaphore_signal(barrier, inc=1, device_id=(s - 2, e), device_id_type=MESH)

    @pl.when(z < deep - 1)
    def _():
        pl.semaphore_signal(barrier, inc=1, device_id=(s + 2, e), device_id_type=MESH)

    ends = (z > 0).astype(jnp.int32) + (z < deep - 1).astype(jnp.int32)
    pl.semaphore_wait(barrier, 1 + ends)

    tot_copy = pltpu.make_async_remote_copy(tot_ref, ptot, tsem.at[0], tsem.at[1], pair, MESH)

    def pair_copy(h):
        return pltpu.make_async_remote_copy(
            own16_ref.at[h], peer.at[h], send.at[0, h], recv.at[0, h], pair, MESH
        )

    def line_copy(h):
        return pltpu.make_async_remote_copy(
            cout.at[h], cin.at[h], send.at[1, h], recv.at[1, h], (s + 2, e), MESH
        )

    tot_copy.start()
    for h in range(heads):
        pair_copy(h).start()

    @pl.when(z == 0)
    def _():
        cin[...] = jnp.zeros_like(cin)

    tot_copy.wait_recv()
    mine, other = tot_ref[...], ptot[...]
    both = jnp.exp(mine + other)
    is_odd = jnp.full(mine.shape, odd, jnp.int32) == 1
    one = jnp.ones_like(mine)
    own_by = jnp.where(is_odd, one, jnp.exp(other))
    peer_by = jnp.where(is_odd, jnp.exp(mine), one)
    carry_by = jnp.where(is_odd, jnp.exp(other), one)
    peer_in = jnp.where(is_odd, one, jnp.zeros_like(mine))
    for h in range(heads):
        pair_copy(h).wait_recv()

        @pl.when(z > 0)
        def _():
            line_copy(h).wait_recv()

        near = peer[h].astype(jnp.float32)
        come = cin[h].astype(jnp.float32)

        @pl.when(z < deep - 1)
        def _():
            cout[h] = (
                both[h : h + 1] * come + own_by[h : h + 1] * own_ref[h] + peer_by[h : h + 1] * near
            ).astype(cout.dtype)
            line_copy(h).start()

        out_ref[h] = carry_by[h : h + 1] * come + peer_in[h : h + 1] * near

    tot_copy.wait_send()
    for h in range(heads):
        pair_copy(h).wait_send()

        @pl.when(z < deep - 1)
        def _():
            line_copy(h).wait_send()


def carried_in(block_total, block_state, n_seq):
    heads, dim, _ = block_state.shape
    bf = jnp.bfloat16
    tile = jnp.pad(block_total, (0, -heads % 8))
    tile = jnp.broadcast_to(tile[:, None], (tile.shape[0], dim))
    vmem = pl.BlockSpec(memory_space=pltpu.VMEM)
    return pl.pallas_call(
        functools.partial(carry_kernel, n_seq),
        out_shape=jax.ShapeDtypeStruct(block_state.shape, jnp.float32),
        in_specs=[vmem] * 3,
        out_specs=vmem,
        scratch_shapes=[
            pltpu.VMEM(block_state.shape, bf),
            pltpu.VMEM(tile.shape, jnp.float32),
            pltpu.VMEM(block_state.shape, bf),
            pltpu.VMEM(block_state.shape, bf),
            pltpu.SemaphoreType.DMA((2, heads)),
            pltpu.SemaphoreType.DMA((2, heads)),
            pltpu.SemaphoreType.DMA((2,)),
        ],
        compiler_params=pltpu.CompilerParams(collective_id=3, has_side_effects=True),
    )(block_state, block_state.astype(bf), tile)


def mix_kernel(n_exp, normed_ref, res_ref, again_ref, mgain_ref, hid_ref, in_ref, tok, send, recv, loc):
    s, e = lax.axis_index("seq"), lax.axis_index("exp")
    rows, width = res_ref.shape[0], normed_ref.shape[1]

    barrier = pltpu.get_barrier_semaphore()
    for k in range(1, n_exp):
        pl.semaphore_signal(
            barrier, inc=1, device_id=(s, lax.rem(e + k, n_exp)), device_id_type=MESH
        )
    pl.semaphore_wait(barrier, n_exp - 1)

    def source(peer):
        return normed_ref.at[pl.ds(pl.multiple_of(peer * rows, rows), rows)]

    own = pltpu.make_async_copy(source(e), tok.at[e], loc.at[0])

    def copy(k):
        peer = lax.rem(e + k, n_exp)
        return pltpu.make_async_remote_copy(
            source(peer), tok.at[e], send.at[k], recv.at[k], (s, peer), MESH
        )

    def arriving(k):
        sender = lax.rem(e + n_exp - k, n_exp)
        return pltpu.make_async_remote_copy(
            source(e), tok.at[sender], send.at[k], recv.at[k], (s, sender), MESH
        )

    for k in range(1, n_exp):
        copy(k).start()
    own.start()
    own.wait()
    for k in range(1, n_exp):
        arriving(k).wait_recv()
    square = jnp.zeros((rows, 1), jnp.float32)
    for j in range(n_exp):
        cols = pl.ds(j * width, width)
        hid = (
            res_ref[:, cols].astype(jnp.float32)
            + tok[j].astype(jnp.float32) * again_ref[:, cols]
        ).astype(jnp.bfloat16)
        hid_ref[:, cols] = hid
        wide = hid.astype(jnp.float32)
        square = square + jnp.sum(wide * wide, axis=1, keepdims=True)
    scale = lax.rsqrt(square / (n_exp * width) + 1e-06)
    for j in range(n_exp):
        cols = pl.ds(j * width, width)
        in_ref[:, cols] = (
            hid_ref[:, cols].astype(jnp.float32) * scale * mgain_ref[:, cols]
        ).astype(jnp.bfloat16)
    for k in range(1, n_exp):
        copy(k).wait_send()


def mix_tokens(normed, residual, attn_gain, moe_gain, n_exp):
    vmem = pl.BlockSpec(memory_space=pltpu.VMEM)
    return pl.pallas_call(
        functools.partial(mix_kernel, n_exp),
        out_shape=(jax.ShapeDtypeStruct(residual.shape, jnp.bfloat16),) * 2,
        in_specs=[vmem] * 4,
        out_specs=(vmem, vmem),
        scratch_shapes=[
            pltpu.VMEM((n_exp, residual.shape[0], normed.shape[1]), jnp.bfloat16),
            pltpu.SemaphoreType.DMA((n_exp,)),
            pltpu.SemaphoreType.DMA((n_exp,)),
            pltpu.SemaphoreType.DMA((1,)),
        ],
        compiler_params=pltpu.CompilerParams(collective_id=4, has_side_effects=True),
    )(normed, residual, attn_gain[None, :], moe_gain[None, :])


def body(
    queries,
    keys,
    values,
    log_decay,
    residual,
    attn_gain,
    moe_gain,
    expert_ids,
    gate_weights,
    w_gate,
    w_up,
    w_down,
):
    n_seq, n_exp = lax.axis_size("seq"), lax.axis_size("exp")
    if moe_fits(n_seq, n_exp, *residual.shape, w_gate.shape):
        return whole_layer(
            queries, keys, values, log_decay, residual, attn_gain, moe_gain, expert_ids, gate_weights,
            w_gate, w_up, w_down, n_seq, n_exp,
        )
    tok_rows, width = residual.shape
    experts = w_gate.shape[0] * n_exp
    gates = jnp.sum(
        jnp.where(
            expert_ids[:, :, None] == jnp.arange(experts, dtype=jnp.int32)[None, None, :],
            gate_weights[:, :, None],
            0.0,
        ),
        axis=1,
    )
    rows = queries.shape[0]
    heads = log_decay.shape[1]
    head_dim = queries.shape[1] // heads
    q_heads = queries.reshape(rows, heads, head_dim)
    k_heads = keys.reshape(rows, heads, head_dim)
    v_heads = values.reshape(rows, heads, head_dim)
    upto = (
        lax.broadcasted_iota(jnp.int32, (rows, rows), 0)
        >= lax.broadcasted_iota(jnp.int32, (rows, rows), 1)
    ).astype(jnp.float32)
    log_cum = jnp.dot(upto, log_decay, precision=lax.Precision.HIGHEST)
    block_total = log_cum[-1]
    keys_weighted = (k_heads * jnp.exp(block_total[None, :] - log_cum)[:, :, None]).astype(
        jnp.bfloat16
    )
    block_state = jnp.einsum(
        "thd,the->hde", keys_weighted, v_heads, preferred_element_type=jnp.float32
    )
    carried = carried_in(block_total, block_state, lax.axis_size("seq"))
    scores = jnp.einsum("thd,shd->hts", q_heads, k_heads, preferred_element_type=jnp.float32)
    gap_logs = log_cum.T[:, :, None] - log_cum.T[:, None, :]
    causal_mask = (
        lax.broadcasted_iota(jnp.int32, (rows, rows), 0)
        >= lax.broadcasted_iota(jnp.int32, (rows, rows), 1)
    )[None, :, :]
    weights = jnp.where(
        causal_mask, scores * jnp.exp(jnp.where(causal_mask, gap_logs, 0.0)), 0.0
    ).astype(jnp.bfloat16)
    intra = jnp.einsum("hts,she->the", weights, v_heads, preferred_element_type=jnp.float32)
    inter = jnp.exp(log_cum)[:, :, None] * jnp.einsum(
        "thd,hde->the", q_heads.astype(jnp.float32), carried, precision=lax.Precision.HIGHEST
    )
    attn = intra + inter
    normed = (attn * lax.rsqrt(jnp.mean(attn * attn, axis=-1, keepdims=True) + 1e-06)).astype(
        jnp.bfloat16
    )
    normed = normed.reshape(rows, heads * head_dim)
    hidden, moe_in = mix_tokens(normed, residual, attn_gain, moe_gain, n_exp)
    hid32 = hidden.astype(jnp.float32)
    flat = gates.T.reshape(-1)
    pad = -flat.shape[0] % 1024
    g_tile = jnp.pad(flat, (0, pad)).reshape(-1, 128)
    everyone, g_all = gather_all(moe_in, g_tile, n_seq, n_exp)
    g_all = g_all.reshape(n_seq * n_exp, -1)[:, : experts * tok_rows]
    g_all = g_all.reshape(n_seq * n_exp, experts, tok_rows)
    mixed = None
    gate_col = lax.dynamic_slice_in_dim(
        g_all, lax.axis_index("exp") * w_gate.shape[0], w_gate.shape[0], 1
    )
    part = None
    for j in range(w_gate.shape[0]):
        gate_part = jnp.einsum("td,fd->tf", everyone, w_gate[j], preferred_element_type=jnp.float32)
        up_part = jnp.einsum("td,fd->tf", everyone, w_up[j], preferred_element_type=jnp.float32)
        active = (
            jax.nn.silu(gate_part) * up_part * gate_col[:, j, :].reshape(-1, 1)
        ).astype(jnp.bfloat16)
        one = jnp.dot(active, w_down[j], preferred_element_type=jnp.float32)
        part = one if part is None else part + one
    part = part.astype(jnp.bfloat16)
    total_rows, width = part.shape
    pieces = max(1, total_rows // 1024)
    step = width // pieces
    summed = [
        jax.jit(scatter_sum, static_argnums=(1, 2))(part[:, i * step : (i + 1) * step], n_seq, n_exp) for i in range(pieces)
    ]
    summed = summed[0] if pieces == 1 else jnp.concatenate(summed, axis=1)
    return (hid32 + summed).astype(jnp.bfloat16)


def solution(mesh):
    in_specs = (
        P("seq", "exp"),
        P("seq", "exp"),
        P("seq", "exp"),
        P("seq", "exp"),
        P(("seq", "exp"), None),
        P(),
        P(),
        P(("seq", "exp"), None),
        P(("seq", "exp"), None),
        P("exp", "seq", None),
        P("exp", "seq", None),
        P("exp", "seq", None),
    )
    out_specs = P(("seq", "exp"), None)
    return jax.shard_map(body, mesh=mesh, in_specs=in_specs, out_specs=out_specs, check_vma=False)
```

```python
import functools

import jax
import jax.numpy as jnp
from jax import lax
from jax.experimental import pallas as pl
from jax.experimental.pallas import tpu as pltpu
from jax.sharding import PartitionSpec as P

MESH = pl.DeviceIdType.MESH
PARTS = 2


class Place:
    def __init__(self, n_seq, n_exp):
        s, e = lax.axis_index("seq"), lax.axis_index("exp")
        self.fold, self.n_exp = n_exp // 4, n_exp
        self.length = (n_seq // 2) * self.fold
        self.p = (s // 2) * self.fold + e // 4
        self.x, self.y, self.c = s % 2, (e // 2) % 2, e % 2

    def ids(self, p, x, y, c):
        return (p // self.fold) * 2 + x, (p % self.fold) * 4 + y * 2 + c

    def block(self, p, x, y, c):
        s, e = self.ids(p, x, y, c)
        return s * self.n_exp + e

    def dev(self, dp=0, dx=0, dy=0, dc=0):
        x = 1 - self.x if dx else self.x
        y = 1 - self.y if dy else self.y
        c = 1 - self.c if dc else self.c
        return self.ids(self.p + dp, x, y, c)

    def greet(self, *more):
        barrier = pltpu.get_barrier_semaphore()
        for d in (dict(dx=1), dict(dy=1), dict(dc=1), *more):
            pl.semaphore_signal(barrier, inc=1, device_id=self.dev(**d), device_id_type=MESH)

        @pl.when(self.p > 0)
        def _():
            pl.semaphore_signal(barrier, inc=1, device_id=self.dev(dp=-1), device_id_type=MESH)

        @pl.when(self.p < self.length - 1)
        def _():
            pl.semaphore_signal(barrier, inc=1, device_id=self.dev(dp=1), device_id_type=MESH)

        ends = (self.p > 0).astype(jnp.int32) + (self.p < self.length - 1).astype(jnp.int32)
        pl.semaphore_wait(barrier, 3 + len(more) + ends)

    def at(self, stage, sign, k):
        if sign == 0:
            stage(0, 0, 0)
        elif sign < 0:
            pl.when(self.p >= k)(lambda: stage(2 * k - 1, -k, -1))
        else:
            pl.when(self.p + k < self.length)(lambda: stage(2 * k, k, 1))

    def far_first(self, stage):
        def one(i, carry):
            for sign in (1, -1):
                self.at(stage, sign, self.length - 1 - i)
            return carry

        if self.length <= 8:
            for i in range(self.length - 1):
                one(i, 0)
        else:
            lax.fori_loop(0, self.length - 1, one, 0)
        self.at(stage, 0, 0)

    def near_first(self, *stages):
        depth = len(stages)

        def ring(stage, k):
            if isinstance(k, int) and k == 0:
                self.at(stage, 0, 0)
            else:
                for sign in (-1, 1):
                    self.at(stage, sign, k)

        def step(k):
            for j, stage in enumerate(stages):
                if 0 <= k - j < self.length:
                    ring(stage, k - j)

        total = self.length + depth - 1
        if self.length <= 8:
            for k in range(total):
                step(k)
            return
        for k in range(depth):
            step(k)

        def one(k, carry):
            for j, stage in enumerate(stages):
                ring(stage, k - j)
            return carry

        lax.fori_loop(depth, self.length, one, 0)
        for k in range(self.length, total):
            step(k)


def gather_kernel(n_seq, n_exp, x_ref, g_ref, out_ref, gout_ref, send, recv, loc):
    me = Place(n_seq, n_exp)
    rows, width = x_ref.shape
    grow = g_ref.shape[0]
    me.greet()

    def place(ref, off, dx, dy, dc=0):
        x = 1 - me.x if dx else me.x
        y = 1 - me.y if dy else me.y
        c = 1 - me.c if dc else me.c
        b = me.block(me.p + off, x, y, c)
        n = rows if ref is out_ref else grow
        return ref.at[pl.ds(pl.multiple_of(b * n, n), n)]

    def copies(part, kind, slot, off, dx, dy, to, own=False, half=None, dc=0):
        dst_x, dst_g = place(out_ref, off, dx, dy, dc), place(gout_ref, off, dx, dy, dc)
        src_x, src_g = (x_ref, g_ref) if own else (dst_x, dst_g)
        span = width // PARTS
        if half is None:
            cols = pl.ds(part * span, span)
        else:
            cols = pl.ds(part * span + half * (span // 2), span // 2)
        out = [
            pltpu.make_async_remote_copy(
                src_x.at[:, cols],
                dst_x.at[:, cols],
                send.at[kind, slot, part],
                recv.at[kind, slot, part],
                to,
                MESH,
            )
        ]
        if half != 1 and part == 0:
            out.append(
                pltpu.make_async_remote_copy(
                    src_g, dst_g, send.at[kind, slot, PARTS], recv.at[kind, slot, PARTS], to, MESH
                )
            )
        return out

    def start(*a, **k):
        for cp in copies(*a, **k):
            cp.start()

    def wait_recv(*a, **k):
        for cp in copies(*a, **k):
            cp.wait_recv()

    def wait_send(*a, **k):
        for cp in copies(*a, **k):
            cp.wait_send()

    left, right = dict(dp=-1), dict(dp=1)
    X, Y, C = me.dev(dx=1), me.dev(dy=1), me.dev(dc=1)

    def line_sends(off, sign, do):
        own = sign == 0
        if sign <= 0:
            pl.when(me.p + 1 < me.length)(
                lambda: do(0, 2 * (-off + 1) - 1, off, 0, 0, me.dev(**right), own=own)
            )
        if sign >= 0:
            pl.when(me.p > 0)(lambda: do(0, 2 * (off + 1), off, 0, 0, me.dev(**left), own=own))

    def stage_line(slot, off, sign, do):
        own = sign == 0
        line_sends(off, sign, do)
        do(1, slot, off, 0, 0, X, own=own)
        do(2, slot, off, 0, 0, Y, own=own)
        do(5, slot, off, 0, 0, C, own=own)

    def stage_xy_1(slot, off, do):
        do(3, slot, off, 1, 0, Y, half=0)
        do(6, slot, off, 1, 0, C)

    def stage_xy_2(slot, off, do):
        do(4, slot, off, 0, 1, X, half=1)
        do(7, slot, off, 0, 1, C)

    def stage_diag(slot, off, do):
        do(8, slot, off, 1, 1, C)

    local = [
        pltpu.make_async_copy(x_ref, place(out_ref, 0, 0, 0), loc.at[0]),
        pltpu.make_async_copy(g_ref, place(gout_ref, 0, 0, 0), loc.at[1]),
    ]
    for cp in local:
        cp.start()

    def s1(slot, off, sign):
        for part in range(PARTS):
            if sign:
                wait_recv(part, 0, slot, off, 0, 0, X)
            stage_line(slot, off, sign, functools.partial(start, part))

    def s2(slot, off, sign):
        for part in range(PARTS):
            wait_recv(part, 1, slot, off, 1, 0, X)
            stage_xy_1(slot, off, functools.partial(start, part))
            wait_recv(part, 2, slot, off, 0, 1, X)
            stage_xy_2(slot, off, functools.partial(start, part))

    def s3(slot, off, sign):
        for part in range(PARTS):
            wait_recv(part, 3, slot, off, 1, 1, X, half=0)
            wait_recv(part, 4, slot, off, 1, 1, X, half=1)
            stage_diag(slot, off, functools.partial(start, part))

    me.near_first(s1, s2, s3)

    def s4(slot, off, sign):
        for part in range(PARTS):
            done = functools.partial(wait_send, part)
            stage_line(slot, off, sign, done)
            stage_xy_1(slot, off, done)
            stage_xy_2(slot, off, done)
            stage_diag(slot, off, done)
            wait_recv(part, 5, slot, off, 0, 0, X, dc=1)
            wait_recv(part, 6, slot, off, 1, 0, X, dc=1)
            wait_recv(part, 7, slot, off, 0, 1, X, dc=1)
            wait_recv(part, 8, slot, off, 1, 1, X, dc=1)

    me.near_first(s4)
    for cp in local:
        cp.wait()


def gather_all(x, g, n_seq, n_exp):
    n = n_seq * n_exp
    length = n // 8
    anyspace = pl.BlockSpec(memory_space=pl.ANY)
    return pl.pallas_call(
        functools.partial(gather_kernel, n_seq, n_exp),
        out_shape=(
            jax.ShapeDtypeStruct((n * x.shape[0], x.shape[1]), x.dtype),
            jax.ShapeDtypeStruct((n * g.shape[0], g.shape[1]), g.dtype),
        ),
        in_specs=[anyspace, anyspace],
        out_specs=(anyspace, anyspace),
        scratch_shapes=[
            pltpu.SemaphoreType.DMA((9, 2 * length + 1, PARTS + 1)),
            pltpu.SemaphoreType.DMA((9, 2 * length + 1, PARTS + 1)),
            pltpu.SemaphoreType.DMA((2,)),
        ],
        compiler_params=pltpu.CompilerParams(collective_id=1, has_side_effects=True),
    )(x, g)


def scatter_kernel(
    n_seq, n_exp, y_ref, out_ref, acc, sib, xbuf, ybuf, dab, dbb, line, send, recv, loc
):
    me = Place(n_seq, n_exp)
    L = me.length
    rows, width = out_ref.shape
    halfw = width // 2
    me.greet()
    X, Y, C = me.dev(dx=1), me.dev(dy=1), me.dev(dc=1)

    def src(off, grp, dc):
        x = 1 - me.x if grp & 1 else me.x
        y = 1 - me.y if grp & 2 else me.y
        c = 1 - me.c if dc else me.c
        b = me.block(me.p + off, x, y, c)
        return y_ref.at[pl.ds(pl.multiple_of(b * rows, rows), rows)]

    def sib_copy(slot, off, grp):
        return pltpu.make_async_remote_copy(
            src(off, grp, 1), sib.at[grp, slot], send.at[grp, slot], recv.at[grp, slot], C, MESH
        )

    def load(slot, off, grp):
        return pltpu.make_async_copy(src(off, grp, 0), acc.at[grp, slot], loc.at[grp, slot])

    for grp in (3, 1, 2, 0):

        def go(slot, off, sign, grp=grp):
            sib_copy(slot, off, grp).start()
            load(slot, off, grp).start()

        me.far_first(go)

    f32 = jnp.float32

    def pair_sum(slot, off, grp):
        load(slot, off, grp).wait()
        sib_copy(slot, off, grp).wait_recv()
        return acc[grp, slot].astype(f32) + sib[grp, slot].astype(f32)

    def diag_a(slot):
        return pltpu.make_async_remote_copy(
            acc.at[3, slot, :, pl.ds(0, halfw)], dab.at[slot], send.at[4, slot], recv.at[4, slot], Y, MESH
        )

    def diag_b(slot):
        return pltpu.make_async_remote_copy(
            acc.at[3, slot, :, pl.ds(halfw, halfw)], dbb.at[slot], send.at[5, slot], recv.at[5, slot], X, MESH
        )

    def x_copy(slot):
        return pltpu.make_async_remote_copy(
            acc.at[1, slot], xbuf.at[slot], send.at[6, slot], recv.at[6, slot], X, MESH
        )

    def y_copy(slot):
        return pltpu.make_async_remote_copy(
            acc.at[2, slot], ybuf.at[slot], send.at[7, slot], recv.at[7, slot], Y, MESH
        )

    def line_copy(slot, sign):
        return pltpu.make_async_remote_copy(
            acc.at[0, slot],
            line.at[slot],
            send.at[8, slot],
            recv.at[8, slot],
            me.dev(dp=sign),
            MESH,
        )

    def d1(slot, off, sign):
        acc[3, slot] = pair_sum(slot, off, 3).astype(acc.dtype)
        diag_a(slot).start()
        diag_b(slot).start()

    def d2(slot, off, sign):
        sx = pair_sum(slot, off, 1)
        diag_a(slot).wait_recv()
        acc[1, slot, :, pl.ds(0, halfw)] = (sx[:, :halfw] + dab[slot].astype(f32)).astype(acc.dtype)
        acc[1, slot, :, pl.ds(halfw, halfw)] = sx[:, halfw:].astype(acc.dtype)
        x_copy(slot).start()
        sy = pair_sum(slot, off, 2)
        diag_b(slot).wait_recv()
        acc[2, slot, :, pl.ds(0, halfw)] = sy[:, :halfw].astype(acc.dtype)
        acc[2, slot, :, pl.ds(halfw, halfw)] = (sy[:, halfw:] + dbb[slot].astype(f32)).astype(acc.dtype)
        y_copy(slot).start()

    def d3(slot, off, sign):
        total = pair_sum(slot, off, 0)
        x_copy(slot).wait_recv()
        y_copy(slot).wait_recv()
        total = total + xbuf[slot].astype(f32) + ybuf[slot].astype(f32)
        if sign == 0:
            out_ref[...] = total
            if L > 1:

                @pl.when(me.p > 0)
                def _():
                    in_copy(2).wait_recv()
                    out_ref[...] += line[2].astype(f32)

                @pl.when(me.p < L - 1)
                def _():
                    in_copy(1).wait_recv()
                    out_ref[...] += line[1].astype(f32)

            return
        acc[0, slot] = total.astype(acc.dtype)
        far = slot + 2
        behind = me.p > 0 if sign > 0 else me.p < L - 1

        @pl.when(jnp.logical_and(behind, sign * off + 1 < L))
        def _():
            in_copy(far).wait_recv()
            acc[0, slot] = (acc[0, slot].astype(f32) + line[far].astype(f32)).astype(acc.dtype)

        line_copy(slot, sign).start()

    def in_copy(slot):
        return pltpu.make_async_remote_copy(
            acc.at[0, slot], line.at[slot], send.at[8, slot], recv.at[8, slot], X, MESH
        )

    me.far_first(d1)
    me.far_first(d2)
    me.far_first(d3)

    def fin(slot, off, sign):
        for grp in range(4):
            sib_copy(slot, off, grp).wait_send()
        diag_a(slot).wait_send()
        diag_b(slot).wait_send()
        x_copy(slot).wait_send()
        y_copy(slot).wait_send()
        if sign:
            line_copy(slot, sign).wait_send()

    me.far_first(fin)


def scatter_sum(part, n_seq, n_exp):
    n = n_seq * n_exp
    slots = n // 4 - 1 + 2
    rows, width = part.shape[0] // n, part.shape[1]
    bf = jnp.bfloat16
    return pl.pallas_call(
        functools.partial(scatter_kernel, n_seq, n_exp),
        out_shape=jax.ShapeDtypeStruct((rows, width), jnp.float32),
        in_specs=[pl.BlockSpec(memory_space=pl.ANY)],
        out_specs=pl.BlockSpec(memory_space=pltpu.VMEM),
        scratch_shapes=[
            pltpu.VMEM((4, slots, rows, width), bf),
            pltpu.VMEM((4, slots, rows, width), bf),
            pltpu.VMEM((slots, rows, width), bf),
            pltpu.VMEM((slots, rows, width), bf),
            pltpu.VMEM((slots, rows, width // 2), bf),
            pltpu.VMEM((slots, rows, width // 2), bf),
            pltpu.VMEM((slots, rows, width), bf),
            pltpu.SemaphoreType.DMA((9, slots)),
            pltpu.SemaphoreType.DMA((9, slots)),
            pltpu.SemaphoreType.DMA((4, slots)),
        ],
        compiler_params=pltpu.CompilerParams(
            collective_id=2, has_side_effects=True, vmem_limit_bytes=60 * 2**20
        ),
    )(part)


GPARTS = 4
HPARTS = 4
PLANES = 4
MPARTS = 4


def plane_orders(length):
    def depth(q):
        return min(q, length - 1 - q)

    visit = []
    for p in range(length):
        rest = [q for q in range(length) if q != p]
        near = min(rest, key=lambda q: (abs(q - p), depth(q)), default=p)
        rest = sorted((q for q in rest if q != near), key=lambda q: (depth(q), abs(q - p)))
        visit.append([p] + [near] * (length > 1) + rest)
    lines = []
    for p in range(length):
        def ready(q):
            chain = range(0, p + 1) if q > p else range(p, length)
            return max(visit[b].index(q) for b in chain)

        low = 2 * p < length
        lines.append(sorted((q for q in range(length) if q != p), key=lambda q: (ready(q), -q if low else q)))
    return visit, lines


def pick(table, p, j):
    total = 0
    for a, row in enumerate(table):
        for b, v in enumerate(row):
            hit = jnp.logical_and(p == a, j == b).astype(jnp.int32)
            total = total + hit * v
    return total


def spans(tiles, parts):
    cuts = [(tiles * i // parts) * 128 for i in range(parts + 1)]
    return [pl.ds(a, b - a) for a, b in zip(cuts[:-1], cuts[1:])]


def when(cond, fn):
    def run():
        fn()

    pl.when(cond)(run)


def attend_tokens(
    me, q_ref, k_ref, v_ref, ld_ref, res_ref, ag_ref, mg_ref, ids_ref, gw_ref, x_out,
    hid, work, flat, own16, peer, cin, cout, tots, tok, psend, precv, tsem, msend, mrecv,
):
    L, z = me.length, me.p
    f32, bf = jnp.float32, jnp.bfloat16
    heads, block = ld_ref.shape
    dim = q_ref.shape[1] // heads
    rows = res_ref.shape[0]
    n_exp, width = tok.shape[0], tok.shape[2]
    e = lax.axis_index("exp")
    pair = me.dev(dx=1)

    def head(h):
        return pl.ds(h * dim, dim)

    def pair_copy(h):
        return pltpu.make_async_remote_copy(
            own16.at[h], peer.at[h], psend.at[0], precv.at[0, h], pair, MESH
        )

    def line_copy(h):
        return pltpu.make_async_remote_copy(
            cout.at[h], cin.at[h], psend.at[1], precv.at[1, h], me.dev(dp=1), MESH
        )

    tot_copy = pltpu.make_async_remote_copy(tots.at[0], tots.at[1], tsem.at[0], tsem.at[1], pair, MESH)

    nt = (((1,), (1,)), ((), ()))
    tn = (((0,), (0,)), ((), ()))
    r = lax.broadcasted_iota(jnp.int32, (block, block), 0)
    c = lax.broadcasted_iota(jnp.int32, (block, block), 1)
    seen = r >= c
    decay = ld_ref[...]
    high = lax.Precision.HIGHEST
    cum = lax.dot_general(seen.astype(f32), decay, nt, precision=high, preferred_element_type=f32)
    cum_t = jnp.dot(decay, (r <= c).astype(f32), precision=high, preferred_element_type=f32)
    total = cum_t[:, block - 1 :]
    tots[0, 0:heads, :] = jnp.broadcast_to(total, (heads, dim))

    def state(h):
        kw = (k_ref[:, head(h)].astype(f32) * jnp.exp(total[h : h + 1] - cum[:, h : h + 1])).astype(bf)
        own = lax.dot_general(kw, v_ref[:, head(h)], tn, preferred_element_type=f32)
        work[:, pl.ds((heads + h) * dim, dim)] = own
        own16[h] = own.astype(bf)

    for h in range(heads):
        state(h)
    me.greet(dict(dy=1, dc=1))
    tot_copy.start()
    for h in range(heads):
        pair_copy(h).start()

    @pl.when(z == 0)
    def _():
        cin[...] = jnp.zeros_like(cin)

    def f_intra(h):
        scores = lax.dot_general(q_ref[:, head(h)], k_ref[:, head(h)], nt, preferred_element_type=f32)
        gap = cum[:, h : h + 1] - cum_t[h : h + 1, :]
        weights = jnp.where(seen, scores * jnp.exp(jnp.where(seen, gap, 0.0)), 0.0).astype(bf)
        work[:, head(h)] = jnp.dot(weights, v_ref[:, head(h)], preferred_element_type=f32)

    for h in range(heads):
        f_intra(h)
    tot_copy.wait_recv()
    mine, other = tots[0, 0:heads, :], tots[1, 0:heads, :]
    both = jnp.exp(mine + other)
    is_odd = jnp.full(mine.shape, me.x, jnp.int32) == 1
    one = jnp.ones_like(mine)
    own_by = jnp.where(is_odd, one, jnp.exp(other))
    peer_by = jnp.where(is_odd, jnp.exp(mine), one)
    carry_by = jnp.where(is_odd, jnp.exp(other), one)
    peer_in = jnp.where(is_odd, one, jnp.zeros_like(mine))

    peers = (dict(dc=1), dict(dy=1), dict(dy=1, dc=1))
    pieces = MPARTS
    span = width // pieces

    def mix_copy(k, i):
        to = me.dev(**peers[k])
        cols = pl.ds(i * span, span)
        src = flat.at[pl.ds(pl.multiple_of(to[1] * rows, rows), rows), cols]
        return pltpu.make_async_remote_copy(
            src, tok.at[e, :, cols], msend.at[0], mrecv.at[k, i], to, MESH
        )

    def mix_in(k, i):
        to = me.dev(**peers[k])
        cols = pl.ds(i * span, span)
        return pltpu.make_async_remote_copy(
            tok.at[to[1], :, cols], tok.at[to[1], :, cols], msend.at[0], mrecv.at[k, i], to, MESH
        )

    def f_chain(h):
        pair_copy(h).wait_recv()
        pl.when(z > 0)(lambda: line_copy(h).wait_recv())
        near = peer[h].astype(f32)
        come = cin[h].astype(f32)
        row = slice(h, h + 1)

        @pl.when(z < L - 1)
        def _():
            mix = both[row] * come + own_by[row] * work[:, pl.ds((heads + h) * dim, dim)] + peer_by[row] * near
            cout[h] = mix.astype(bf)
            line_copy(h).start()

    def f_head(h):
        near = peer[h].astype(f32)
        come = cin[h].astype(f32)
        row = slice(h, h + 1)
        carried = carry_by[row] * come + peer_in[row] * near
        coarse = carried.astype(bf)
        fine = (carried - coarse.astype(f32)).astype(bf)
        query = q_ref[:, head(h)]
        inter = jnp.dot(query, coarse, preferred_element_type=f32) + jnp.dot(
            query, fine, preferred_element_type=f32
        )
        attn = work[:, head(h)] + jnp.exp(cum[:, h : h + 1]) * inter
        scale = lax.rsqrt(jnp.mean(attn * attn, axis=-1, keepdims=True) + 1e-06)
        flat[0:block, head(h)] = (attn * scale).astype(bf)
        if (h + 1) * pieces % heads == 0:
            for k in range(len(peers)):
                mix_copy(k, (h + 1) * pieces // heads - 1).start()

    for h in range(heads):
        f_chain(h)
        f_head(h)

    tok[e] = flat[pl.ds(pl.multiple_of(e * rows, rows), rows), 0:width]

    def f_mix():
        for i in range(pieces):
            for k in range(len(peers)):
                mix_in(k, i).wait_recv()

    f_mix()
    square = jnp.zeros((rows, 1), f32)
    for j in range(n_exp):
        cols = pl.ds(j * width, width)
        value = (res_ref[:, cols].astype(f32) + tok[j].astype(f32) * ag_ref[:, cols]).astype(bf)
        hid[:, cols] = value
        wide = value.astype(f32)
        square = square + jnp.sum(wide * wide, axis=1, keepdims=True)
    scale = lax.rsqrt(square / (n_exp * width) + 1e-06)
    for j in range(n_exp):
        cols = pl.ds(j * width, width)
        x_out[:, cols] = (hid[:, cols].astype(f32) * scale * mg_ref[:, cols]).astype(bf)

    def column(ref):
        same = lax.broadcasted_iota(jnp.int32, (rows, rows), 0) == lax.broadcasted_iota(jnp.int32, (rows, rows), 1)
        return lax.dot_general(
            same.astype(f32), ref[...].astype(f32), nt, precision=high, preferred_element_type=f32
        )

    ids, gates = column(ids_ref).astype(jnp.int32), column(gw_ref)
    coarse = gates.astype(bf).astype(f32)
    rest = gates - coarse
    lane = lax.broadcasted_iota(jnp.int32, (rows, 128), 1)
    extra = jnp.zeros((rows, 128), f32)
    for i in range(ids_ref.shape[0]):
        who = ids[:, i : i + 1]
        extra = jnp.where(lane == who, coarse[:, i : i + 1], extra)
        extra = jnp.where(lane == who + 64, rest[:, i : i + 1], extra)
    x_out[:, n_exp * width :] = extra.astype(bf)

    def finish():
        def out(ref, sent):
            pltpu.make_async_remote_copy(ref, ref, sent, sent, pair, MESH).wait_send()

        tot_copy.wait_send()
        out(own16, psend.at[0])
        pl.when(z < L - 1)(lambda: out(cout, psend.at[1]))
        out(tok.at[pl.ds(0, len(peers))], msend.at[0])

    return finish


def moe_kernel(
    n_seq, n_exp, q_ref, k_ref, v_ref, ld_ref, res_ref, ag_ref, mg_ref, ids_ref, gw_ref,
    wg_ref, wu_ref, wd_ref, out_ref,
    xs, ys, act, sib, din, xin, yin, lin, tot, wg, wu, wd, hid_ref,
    own16, peer, cin, cout, tots, tok,
    gsend, lsend, grecv, crecv, brecv, ssend, srecv, loc, psend, precv, tsem, msend, mrecv,
):
    me = Place(n_seq, n_exp)
    L, p = me.length, me.p
    rows, width = out_ref.shape
    hidden = wg.shape[0]
    many = 8 * rows
    f32, bf = jnp.float32, jnp.bfloat16
    X, Y, C = me.dev(dx=1), me.dev(dy=1), me.dev(dc=1)
    visit, lines = plane_orders(L)
    gcols = spans(xs.shape[1] // 128, GPARTS)
    hcols = spans(width // 128, HPARTS)

    loads = [
        pltpu.make_async_copy(a.at[0], b, loc.at[i])
        for i, (a, b) in enumerate(((wg_ref, wg), (wu_ref, wu), (wd_ref, wd)))
    ]
    for cp in loads:
        cp.start()

    def flip(v, d):
        return 1 - v if d else v

    def row(q, dx=0, dy=0, dc=0):
        k = (flip(me.c, dc) * 2 + flip(me.x, dx)) * 2 + flip(me.y, dy)
        return pl.ds(pl.multiple_of((q * 8 + k) * rows, rows), rows)

    def srow(q, dx=0, dy=0):
        k = flip(me.x, dx) * 2 + flip(me.y, dy)
        return pl.ds(pl.multiple_of((q * 4 + k) * rows, rows), rows)

    def prow(q):
        return pl.ds(pl.multiple_of(q * rows, rows), rows)

    def gcopy(kind, q, part, r, to, sent=None):
        ref = xs.at[r, gcols[part]]
        sent = gsend.at[kind] if sent is None else sent
        got = crecv.at[q] if kind == 0 else grecv.at[kind - 1, q, part]
        return pltpu.make_async_remote_copy(ref, ref, sent, got, to, MESH)

    def bulk(ref, sent):
        return pltpu.make_async_remote_copy(ref, ref, sent, sent, X, MESH)

    upper = GPARTS // 2
    cut = gcols[upper].start
    low_cols, high_cols = pl.ds(0, cut), pl.ds(cut, xs.shape[1] - cut)

    def line_pair(q, part):
        pl.when(jnp.logical_and(q >= p, p > 0))(
            lambda: gcopy(5, q, part, row(q), me.dev(dp=-1), lsend.at[0, q]).start()
        )
        pl.when(jnp.logical_and(q <= p, p + 1 < L))(
            lambda: gcopy(5, q, part, row(q), me.dev(dp=1), lsend.at[1, q]).start()
        )

    def g_line(q, part):
        pl.when(q != p)(lambda: gcopy(5, q, part, row(q), X).wait_recv())
        line_pair(q, part)

    def second_x(q, part):
        out = [gcopy(0, q, part, row(q, 1, 0), C)]
        return out if part >= upper else [gcopy(3, q, part, row(q, 1, 0), Y)] + out

    def second_y(q, part):
        out = [gcopy(0, q, part, row(q, 0, 1), C)]
        return out if part < upper else [gcopy(4, q, part, row(q, 0, 1), X)] + out

    def third(q, part):
        return [gcopy(0, q, part, row(q, 1, 1), C)]

    lower, higher = range(upper), range(upper, GPARTS)

    def g_first(q, turn, own=False):
        for part in lower if turn == 0 else higher:
            gcopy(1, q, part, row(q), X, gsend.at[5 + turn] if own else None).start()
        for part in higher if turn == 0 else lower:
            gcopy(2, q, part, row(q), Y).start()
        if turn == 0:
            for part in range(GPARTS):
                gcopy(0, q, part, row(q), C).start()

    def g_own(q):
        for part in lower:
            line_pair(q, part)
        g_first(q, 0, True)
        bulk(xs.at[row(q), low_cols], gsend.at[5]).wait_send()
        for part in higher:
            line_pair(q, part)
        g_first(q, 1, True)

    def from_x(q, part):
        gcopy(1, q, part, row(q, 1, 0), X).wait_recv()
        for cp in second_x(q, part):
            cp.start()

    def from_y(q, part):
        gcopy(2, q, part, row(q, 0, 1), X).wait_recv()
        for cp in second_y(q, part):
            cp.start()

    def g_second(q):
        for part in lower:
            from_x(q, part)
            from_y(q, part + upper)

    def g_rest(q):
        for part in lower:
            from_x(q, part + upper)
            from_y(q, part)

    def g_third(q):
        for part in range(GPARTS):
            gcopy(3 if part < upper else 4, q, part, row(q, 1, 1), X).wait_recv()
            for cp in third(q, part):
                cp.start()

    def g_ring(k, parts):
        for sign in (-1, 1):
            q = p + sign * k
            when(jnp.logical_and(q >= 0, q < L), lambda: [g_line(q, part) for part in parts])

    def g_done(q):
        r = pl.ds(pl.multiple_of((q * 2 + 1 - me.c) * 4 * rows, 4 * rows), 4 * rows)
        pltpu.make_async_remote_copy(xs.at[r], xs.at[r], gsend.at[0], crecv.at[q], X, MESH).wait_recv()

    def g_drain():
        bulk(xs.at[pl.ds(0, L * 4 * rows)], gsend.at[0]).wait_send()
        bulk(xs.at[pl.ds(0, (L - 1) * rows)], gsend.at[1]).wait_send()
        bulk(xs.at[pl.ds(0, L * rows)], gsend.at[2]).wait_send()
        bulk(xs.at[pl.ds(0, L * rows), low_cols], gsend.at[3]).wait_send()
        bulk(xs.at[pl.ds(0, L * rows), high_cols], gsend.at[4]).wait_send()
        bulk(xs.at[row(p), high_cols], gsend.at[6]).wait_send()
        for q in range(L):
            pl.when(jnp.logical_and(q >= p, p > 0))(lambda: bulk(xs.at[row(q)], lsend.at[0, q]).wait_send())
            pl.when(jnp.logical_and(q <= p, p + 1 < L))(lambda: bulk(xs.at[row(q)], lsend.at[1, q]).wait_send())

    def sib_copy(q, h):
        r = pl.ds(pl.multiple_of((q * 2 + 1 - me.c) * 4 * rows, 4 * rows), 4 * rows)
        d = pl.ds(pl.multiple_of(q * 4 * rows, 4 * rows), 4 * rows)
        return pltpu.make_async_remote_copy(
            ys.at[r, hcols[h]], sib.at[d, hcols[h]], ssend.at[4], brecv.at[q, h], C, MESH
        )

    def scopy(kind, q, h, r, dst, d, to):
        return pltpu.make_async_remote_copy(
            ys.at[r, hcols[h]], dst.at[d, hcols[h]], ssend.at[kind], srecv.at[kind, q, h], to, MESH
        )

    def diag_copy(q, h):
        return scopy(0, q, h, row(q, 1, 1), din, prow(q), Y if 2 * h < HPARTS else X)

    def x_copy(q, h):
        return scopy(1, q, h, row(q, 1, 0), xin, prow(q), X)

    def y_copy(q, h):
        return scopy(2, q, h, row(q, 0, 1), yin, prow(q), Y)

    def line_copy(q, h):
        up = (q > p).astype(jnp.int32)
        last = jnp.logical_and(q < p, q == p - 1).astype(jnp.int32)
        slot = q + (L - q) * last
        return pltpu.make_async_remote_copy(
            ys.at[row(q), hcols[h]],
            lin.at[prow(slot), hcols[h]],
            ssend.at[3],
            srecv.at[3, slot, h],
            me.dev(dp=2 * up - 1),
            MESH,
        )

    def line_in(slot, h):
        return pltpu.make_async_remote_copy(
            ys.at[row(p), hcols[h]], lin.at[prow(slot), hcols[h]], ssend.at[3], srecv.at[3, slot, h], X, MESH
        )

    def pair(q, h, dx, dy):
        return ys[row(q, dx, dy), hcols[h]].astype(f32) + sib[srow(q, dx, dy), hcols[h]].astype(f32)

    def r_first(q, h):
        sib_copy(q, h).wait_recv()
        ys[row(q, 1, 1), hcols[h]] = pair(q, h, 1, 1).astype(bf)
        diag_copy(q, h).start()

    def r_second(q, h):
        sx, sy = pair(q, h, 1, 0), pair(q, h, 0, 1)
        diag_copy(q, h).wait_recv()
        more = din[prow(q), hcols[h]].astype(f32)
        if 2 * h < HPARTS:
            sx = sx + more
        else:
            sy = sy + more
        ys[row(q, 1, 0), hcols[h]] = sx.astype(bf)
        x_copy(q, h).start()
        ys[row(q, 0, 1), hcols[h]] = sy.astype(bf)
        y_copy(q, h).start()

    def r_third(q, h):
        total = pair(q, h, 0, 0)
        x_copy(q, h).wait_recv()
        y_copy(q, h).wait_recv()
        total = total + xin[prow(q), hcols[h]].astype(f32) + yin[prow(q), hcols[h]].astype(f32)
        tot[prow(q), hcols[h]] = total

    def r_line(q, h):
        behind = jnp.logical_or(jnp.logical_and(q > p, p > 0), jnp.logical_and(q < p, p < L - 1))

        @pl.when(behind)
        def _():
            line_in(q, h).wait_recv()
            ys[row(q), hcols[h]] = (tot[prow(q), hcols[h]] + lin[prow(q), hcols[h]].astype(f32)).astype(bf)

        @pl.when(jnp.logical_not(behind))
        def _():
            ys[row(q), hcols[h]] = tot[prow(q), hcols[h]].astype(bf)

        line_copy(q, h).start()

    def r_last(h):
        cols = hcols[h]

        @pl.when(p > 0)
        def _():
            line_in(p, h).wait_recv()
            tot[prow(p), cols] += lin[prow(p), cols].astype(f32)

        @pl.when(p < L - 1)
        def _():
            line_in(L, h).wait_recv()
            tot[prow(p), cols] += lin[prow(L), cols].astype(f32)

        out_ref[:, cols] = (hid_ref[:, cols].astype(f32) + tot[prow(p), cols]).astype(bf)

    at_end = jnp.logical_or(p == 0, p == L - 1)
    inner = jnp.logical_not(at_end)

    def r_early(q, h):
        pl.when(jnp.logical_and(at_end, q != p))(lambda: r_line(q, h))

    def r_drain():
        bulk(sib, ssend.at[4]).wait_send()
        for kind, ref in enumerate((din, xin, yin, lin.at[pl.ds(0, (L - 1) * rows)])):
            bulk(ref, ssend.at[kind]).wait_send()

    tile = next(t for t in range(512, 0, -128) if hidden % t == 0)
    fsteps = hidden // tile

    def block_of(q):
        return pl.ds(pl.multiple_of(q * many, many), many)

    def gate_of(q):
        extra = xs[block_of(q), width : width + 128].astype(f32)
        lane = lax.broadcasted_iota(jnp.int32, extra.shape, 1)
        e = lax.axis_index("exp")
        keep = jnp.logical_or(lane == e, lane == e + 64)
        return jnp.sum(jnp.where(keep, extra, 0.0), axis=1, keepdims=True)

    nt = (((1,), (1,)), ((), ()))

    def ffn_in(q, f):
        fc = pl.ds(f * tile, tile)
        rows_in = xs[block_of(q), 0:width]
        gate = lax.dot_general(rows_in, wg[fc, :], nt, preferred_element_type=f32)
        up = lax.dot_general(rows_in, wu[fc, :], nt, preferred_element_type=f32)
        act[:, fc] = (gate / (1.0 + jnp.exp(-gate)) * up * gate_of(q)).astype(bf)

    def ffn_out(q, h):
        ys[block_of(q), hcols[h]] = jnp.dot(
            act[...], wd[:, hcols[h]], preferred_element_type=f32
        ).astype(bf)
        sib_copy(q, h).start()

    front_done = attend_tokens(
        me, q_ref, k_ref, v_ref, ld_ref, res_ref, ag_ref, mg_ref, ids_ref, gw_ref, xs.at[row(p)],
        hid_ref, tot, act, own16, peer, cin, cout, tots, tok, psend, precv, tsem, msend, mrecv,
    )
    second = pick(visit, p, 1)
    g_own(p)
    g_second(p)
    g_ring(1, lower)
    g_rest(p)
    g_ring(1, higher)
    g_first(second, 0)
    g_third(p)
    g_first(second, 1)
    front_done()
    for cp in loads:
        cp.wait()

    def chunk(j, carry):
        q, nxt, prev = pick(visit, p, j), pick(visit, p, j + 1), pick(visit, p, j - 1)
        older = pick(visit, p, j - 2)
        third, fourth = pick(visit, p, 2), pick(visit, p, 3)

        def opening(*fns):
            when(j == 0, lambda: [fn() for fn in fns])

        def closing(*fns):
            when(j == L - 1, lambda: [fn() for fn in fns])

        def ahead(*fns):
            when(jnp.logical_and(j > 0, j + 1 < L), lambda: [fn() for fn in fns])

        def after(*fns):
            when(j > 0, lambda: [fn() for fn in fns])

        def later(*fns):
            when(j > 1, lambda: [fn() for fn in fns])

        def settle(at, h):
            r_third(at, h)
            r_early(at, h)

        def hook(n):
            if n == 0:
                after(lambda: r_first(prev, 2), lambda: r_first(prev, 3))
                opening(
                    lambda: g_ring(2, lower),
                    lambda: g_second(nxt),
                    lambda: g_ring(2, higher),
                    lambda: g_first(fourth, 0),
                )
            if n == 1:
                opening(lambda: g_rest(nxt), lambda: g_first(fourth, 1))
                ahead(lambda: g_second(nxt))
                later(lambda: settle(older, 0), lambda: settle(older, 1))
                after(lambda: r_second(prev, 0), lambda: r_second(prev, 1))
            if n == 2:
                ahead(lambda: g_rest(nxt))
                later(lambda: settle(older, 2), lambda: settle(older, 3))
                closing(lambda: r_second(prev, 2))

        g_done(q)
        for f in range(fsteps):
            ffn_in(q, f)
            hook(f)
        for f in range(fsteps, 3):
            hook(f)
        for h in range(HPARTS):
            ffn_out(q, h)
            if h == 0:
                ahead(lambda: r_second(prev, 2))
                closing(lambda: r_second(prev, 3))
            if h == 1:
                ahead(lambda: r_second(prev, 3))
                opening(lambda: g_ring(3, range(GPARTS)), lambda: g_first(third, 0))
                closing(lambda: settle(prev, 0))
            if h == 2:
                r_first(q, 0)
                ahead(lambda: g_third(nxt))
                opening(lambda: g_third(nxt))
                closing(lambda: settle(prev, 1))
            if h == 3:
                r_first(q, 1)
                opening(lambda: g_first(third, 1))
        return carry

    def one_line(i, h):
        when(inner, lambda: r_line(pick(lines, p, i), h))

    lax.fori_loop(0, L, chunk, 0)

    final, prior = pick(visit, p, L - 1), pick(visit, p, L - 2)
    r_first(final, 2)
    r_first(final, 3)
    for h in (2, 3):
        r_third(prior, h)
        r_early(prior, h)
    for h in range(HPARTS):
        r_second(final, h)
        one_line(0, h)
    for h in range(HPARTS):
        one_line(1, h)
        r_third(final, h)
        r_early(final, h)
    for h in range(HPARTS):
        one_line(2, h)
        if h:
            r_last(h - 1)
    r_last(HPARTS - 1)

    g_drain()
    r_drain()


def moe_scratch(n_seq, n_exp, x_shape, w_shape):
    n, L = n_seq * n_exp, n_seq * n_exp // 8
    rows, wide = x_shape
    hidden, width = w_shape[1:]
    bf, f32 = jnp.bfloat16, jnp.float32
    return [
        ((n * rows, wide), bf),
        ((n * rows, width), bf),
        ((8 * rows, hidden), bf),
        ((n // 2 * rows, width), bf),
        ((L * rows, width), bf),
        ((L * rows, width), bf),
        ((L * rows, width), bf),
        ((L * rows + rows, width), bf),
        ((L * rows, width), f32),
        ((hidden, width), bf),
        ((hidden, width), bf),
        ((hidden, width), bf),
    ]


MOE_VMEM = 61 * 2**20


def moe_fits(n_seq, n_exp, rows, width, w_shape):
    need = sum(
        a * b * jnp.dtype(t).itemsize for (a, b), t in moe_scratch(n_seq, n_exp, (rows, width + 128), w_shape)
    )
    return (
        w_shape[0] == 1
        and n_exp // 4 == 1
        and n_seq * n_exp == 8 * PLANES
        and w_shape[1] % 128 == 0
        and w_shape[2] % (128 * HPARTS) == 0
        and w_shape[2] // n_exp % (128 * MPARTS) == 0
        and need + 6 * 2**20 <= MOE_VMEM
    )


def whole_layer(
    queries, keys, values, log_decay, residual, attn_gain, moe_gain, expert_ids, gate_weights,
    w_gate, w_up, w_down, n_seq, n_exp,
):
    L = n_seq * n_exp // 8
    heads = log_decay.shape[1]
    part = queries.shape[1]
    dim = part // heads
    rows, width = residual.shape
    vmem = pl.BlockSpec(memory_space=pltpu.VMEM)
    anyspace = pl.BlockSpec(memory_space=pl.ANY)
    dma = pltpu.SemaphoreType.DMA
    bf = jnp.bfloat16
    states = pltpu.VMEM((heads, dim, dim), bf)
    scratch = moe_scratch(n_seq, n_exp, (rows, width + 128), w_gate.shape)
    return pl.pallas_call(
        functools.partial(moe_kernel, n_seq, n_exp),
        out_shape=jax.ShapeDtypeStruct(residual.shape, bf),
        in_specs=[vmem] * 9 + [anyspace] * 3,
        out_specs=vmem,
        scratch_shapes=[pltpu.VMEM(s, t) for s, t in scratch]
        + [
            pltpu.VMEM(residual.shape, bf),
            states,
            states,
            states,
            states,
            pltpu.VMEM((2, heads + -heads % 8, dim), jnp.float32),
            pltpu.VMEM((n_exp, rows, part), bf),
            dma((7,)),
            dma((2, L)),
            dma((5, L, GPARTS)),
            dma((L,)),
            dma((L, HPARTS)),
            dma((5,)),
            dma((4, L + 1, HPARTS)),
            dma((3,)),
            dma((2,)),
            dma((2, heads)),
            dma((2,)),
            dma((1,)),
            dma((3, MPARTS)),
        ],
        compiler_params=pltpu.CompilerParams(
            collective_id=5, has_side_effects=True, vmem_limit_bytes=MOE_VMEM
        ),
    )(
        queries, keys, values, log_decay.T, residual, attn_gain[None, :], moe_gain[None, :],
        expert_ids.T, gate_weights.T, w_gate, w_up, w_down,
    )


def carry_kernel(n_seq, own_ref, own16_ref, tot_ref, out_ref, peer, ptot, cin, cout, send, recv, tsem):
    s, e = lax.axis_index("seq"), lax.axis_index("exp")
    z, odd, deep = s // 2, s % 2, n_seq // 2
    heads = own_ref.shape[0]
    pair = (z * 2 + 1 - odd, e)

    barrier = pltpu.get_barrier_semaphore()
    pl.semaphore_signal(barrier, inc=1, device_id=pair, device_id_type=MESH)

    @pl.when(z > 0)
    def _():
        pl.semaphore_signal(barrier, inc=1, device_id=(s - 2, e), device_id_type=MESH)

    @pl.when(z < deep - 1)
    def _():
        pl.semaphore_signal(barrier, inc=1, device_id=(s + 2, e), device_id_type=MESH)

    ends = (z > 0).astype(jnp.int32) + (z < deep - 1).astype(jnp.int32)
    pl.semaphore_wait(barrier, 1 + ends)

    tot_copy = pltpu.make_async_remote_copy(tot_ref, ptot, tsem.at[0], tsem.at[1], pair, MESH)

    def pair_copy(h):
        return pltpu.make_async_remote_copy(
            own16_ref.at[h], peer.at[h], send.at[0, h], recv.at[0, h], pair, MESH
        )

    def line_copy(h):
        return pltpu.make_async_remote_copy(
            cout.at[h], cin.at[h], send.at[1, h], recv.at[1, h], (s + 2, e), MESH
        )

    tot_copy.start()
    for h in range(heads):
        pair_copy(h).start()

    @pl.when(z == 0)
    def _():
        cin[...] = jnp.zeros_like(cin)

    tot_copy.wait_recv()
    mine, other = tot_ref[...], ptot[...]
    both = jnp.exp(mine + other)
    is_odd = jnp.full(mine.shape, odd, jnp.int32) == 1
    one = jnp.ones_like(mine)
    own_by = jnp.where(is_odd, one, jnp.exp(other))
    peer_by = jnp.where(is_odd, jnp.exp(mine), one)
    carry_by = jnp.where(is_odd, jnp.exp(other), one)
    peer_in = jnp.where(is_odd, one, jnp.zeros_like(mine))
    for h in range(heads):
        pair_copy(h).wait_recv()

        @pl.when(z > 0)
        def _():
            line_copy(h).wait_recv()

        near = peer[h].astype(jnp.float32)
        come = cin[h].astype(jnp.float32)

        @pl.when(z < deep - 1)
        def _():
            cout[h] = (
                both[h : h + 1] * come + own_by[h : h + 1] * own_ref[h] + peer_by[h : h + 1] * near
            ).astype(cout.dtype)
            line_copy(h).start()

        out_ref[h] = carry_by[h : h + 1] * come + peer_in[h : h + 1] * near

    tot_copy.wait_send()
    for h in range(heads):
        pair_copy(h).wait_send()

        @pl.when(z < deep - 1)
        def _():
            line_copy(h).wait_send()


def carried_in(block_total, block_state, n_seq):
    heads, dim, _ = block_state.shape
    bf = jnp.bfloat16
    tile = jnp.pad(block_total, (0, -heads % 8))
    tile = jnp.broadcast_to(tile[:, None], (tile.shape[0], dim))
    vmem = pl.BlockSpec(memory_space=pltpu.VMEM)
    return pl.pallas_call(
        functools.partial(carry_kernel, n_seq),
        out_shape=jax.ShapeDtypeStruct(block_state.shape, jnp.float32),
        in_specs=[vmem] * 3,
        out_specs=vmem,
        scratch_shapes=[
            pltpu.VMEM(block_state.shape, bf),
            pltpu.VMEM(tile.shape, jnp.float32),
            pltpu.VMEM(block_state.shape, bf),
            pltpu.VMEM(block_state.shape, bf),
            pltpu.SemaphoreType.DMA((2, heads)),
            pltpu.SemaphoreType.DMA((2, heads)),
            pltpu.SemaphoreType.DMA((2,)),
        ],
        compiler_params=pltpu.CompilerParams(collective_id=3, has_side_effects=True),
    )(block_state, block_state.astype(bf), tile)


def mix_kernel(n_exp, normed_ref, res_ref, again_ref, mgain_ref, hid_ref, in_ref, tok, send, recv, loc):
    s, e = lax.axis_index("seq"), lax.axis_index("exp")
    rows, width = res_ref.shape[0], normed_ref.shape[1]

    barrier = pltpu.get_barrier_semaphore()
    for k in range(1, n_exp):
        pl.semaphore_signal(
            barrier, inc=1, device_id=(s, lax.rem(e + k, n_exp)), device_id_type=MESH
        )
    pl.semaphore_wait(barrier, n_exp - 1)

    def source(peer):
        return normed_ref.at[pl.ds(pl.multiple_of(peer * rows, rows), rows)]

    own = pltpu.make_async_copy(source(e), tok.at[e], loc.at[0])

    def copy(k):
        peer = lax.rem(e + k, n_exp)
        return pltpu.make_async_remote_copy(
            source(peer), tok.at[e], send.at[k], recv.at[k], (s, peer), MESH
        )

    def arriving(k):
        sender = lax.rem(e + n_exp - k, n_exp)
        return pltpu.make_async_remote_copy(
            source(e), tok.at[sender], send.at[k], recv.at[k], (s, sender), MESH
        )

    for k in range(1, n_exp):
        copy(k).start()
    own.start()
    own.wait()
    for k in range(1, n_exp):
        arriving(k).wait_recv()
    square = jnp.zeros((rows, 1), jnp.float32)
    for j in range(n_exp):
        cols = pl.ds(j * width, width)
        hid = (
            res_ref[:, cols].astype(jnp.float32)
            + tok[j].astype(jnp.float32) * again_ref[:, cols]
        ).astype(jnp.bfloat16)
        hid_ref[:, cols] = hid
        wide = hid.astype(jnp.float32)
        square = square + jnp.sum(wide * wide, axis=1, keepdims=True)
    scale = lax.rsqrt(square / (n_exp * width) + 1e-06)
    for j in range(n_exp):
        cols = pl.ds(j * width, width)
        in_ref[:, cols] = (
            hid_ref[:, cols].astype(jnp.float32) * scale * mgain_ref[:, cols]
        ).astype(jnp.bfloat16)
    for k in range(1, n_exp):
        copy(k).wait_send()


def mix_tokens(normed, residual, attn_gain, moe_gain, n_exp):
    vmem = pl.BlockSpec(memory_space=pltpu.VMEM)
    return pl.pallas_call(
        functools.partial(mix_kernel, n_exp),
        out_shape=(jax.ShapeDtypeStruct(residual.shape, jnp.bfloat16),) * 2,
        in_specs=[vmem] * 4,
        out_specs=(vmem, vmem),
        scratch_shapes=[
            pltpu.VMEM((n_exp, residual.shape[0], normed.shape[1]), jnp.bfloat16),
            pltpu.SemaphoreType.DMA((n_exp,)),
            pltpu.SemaphoreType.DMA((n_exp,)),
            pltpu.SemaphoreType.DMA((1,)),
        ],
        compiler_params=pltpu.CompilerParams(collective_id=4, has_side_effects=True),
    )(normed, residual, attn_gain[None, :], moe_gain[None, :])


def body(
    queries,
    keys,
    values,
    log_decay,
    residual,
    attn_gain,
    moe_gain,
    expert_ids,
    gate_weights,
    w_gate,
    w_up,
    w_down,
):
    n_seq, n_exp = lax.axis_size("seq"), lax.axis_size("exp")
    if moe_fits(n_seq, n_exp, *residual.shape, w_gate.shape):
        return whole_layer(
            queries, keys, values, log_decay, residual, attn_gain, moe_gain, expert_ids, gate_weights,
            w_gate, w_up, w_down, n_seq, n_exp,
        )
    tok_rows, width = residual.shape
    experts = w_gate.shape[0] * n_exp
    gates = jnp.sum(
        jnp.where(
            expert_ids[:, :, None] == jnp.arange(experts, dtype=jnp.int32)[None, None, :],
            gate_weights[:, :, None],
            0.0,
        ),
        axis=1,
    )
    rows = queries.shape[0]
    heads = log_decay.shape[1]
    head_dim = queries.shape[1] // heads
    q_heads = queries.reshape(rows, heads, head_dim)
    k_heads = keys.reshape(rows, heads, head_dim)
    v_heads = values.reshape(rows, heads, head_dim)
    upto = (
        lax.broadcasted_iota(jnp.int32, (rows, rows), 0)
        >= lax.broadcasted_iota(jnp.int32, (rows, rows), 1)
    ).astype(jnp.float32)
    log_cum = jnp.dot(upto, log_decay, precision=lax.Precision.HIGHEST)
    block_total = log_cum[-1]
    keys_weighted = (k_heads * jnp.exp(block_total[None, :] - log_cum)[:, :, None]).astype(
        jnp.bfloat16
    )
    block_state = jnp.einsum(
        "thd,the->hde", keys_weighted, v_heads, preferred_element_type=jnp.float32
    )
    carried = carried_in(block_total, block_state, lax.axis_size("seq"))
    scores = jnp.einsum("thd,shd->hts", q_heads, k_heads, preferred_element_type=jnp.float32)
    gap_logs = log_cum.T[:, :, None] - log_cum.T[:, None, :]
    causal_mask = (
        lax.broadcasted_iota(jnp.int32, (rows, rows), 0)
        >= lax.broadcasted_iota(jnp.int32, (rows, rows), 1)
    )[None, :, :]
    weights = jnp.where(
        causal_mask, scores * jnp.exp(jnp.where(causal_mask, gap_logs, 0.0)), 0.0
    ).astype(jnp.bfloat16)
    intra = jnp.einsum("hts,she->the", weights, v_heads, preferred_element_type=jnp.float32)
    inter = jnp.exp(log_cum)[:, :, None] * jnp.einsum(
        "thd,hde->the", q_heads.astype(jnp.float32), carried, precision=lax.Precision.HIGHEST
    )
    attn = intra + inter
    normed = (attn * lax.rsqrt(jnp.mean(attn * attn, axis=-1, keepdims=True) + 1e-06)).astype(
        jnp.bfloat16
    )
    normed = normed.reshape(rows, heads * head_dim)
    hidden, moe_in = mix_tokens(normed, residual, attn_gain, moe_gain, n_exp)
    hid32 = hidden.astype(jnp.float32)
    flat = gates.T.reshape(-1)
    pad = -flat.shape[0] % 1024
    g_tile = jnp.pad(flat, (0, pad)).reshape(-1, 128)
    everyone, g_all = gather_all(moe_in, g_tile, n_seq, n_exp)
    g_all = g_all.reshape(n_seq * n_exp, -1)[:, : experts * tok_rows]
    g_all = g_all.reshape(n_seq * n_exp, experts, tok_rows)
    mixed = None
    gate_col = lax.dynamic_slice_in_dim(
        g_all, lax.axis_index("exp") * w_gate.shape[0], w_gate.shape[0], 1
    )
    part = None
    for j in range(w_gate.shape[0]):
        gate_part = jnp.einsum("td,fd->tf", everyone, w_gate[j], preferred_element_type=jnp.float32)
        up_part = jnp.einsum("td,fd->tf", everyone, w_up[j], preferred_element_type=jnp.float32)
        active = (
            jax.nn.silu(gate_part) * up_part * gate_col[:, j, :].reshape(-1, 1)
        ).astype(jnp.bfloat16)
        one = jnp.dot(active, w_down[j], preferred_element_type=jnp.float32)
        part = one if part is None else part + one
    part = part.astype(jnp.bfloat16)
    total_rows, width = part.shape
    pieces = max(1, total_rows // 1024)
    step = width // pieces
    summed = [
        jax.jit(scatter_sum, static_argnums=(1, 2))(part[:, i * step : (i + 1) * step], n_seq, n_exp) for i in range(pieces)
    ]
    summed = summed[0] if pieces == 1 else jnp.concatenate(summed, axis=1)
    return (hid32 + summed).astype(jnp.bfloat16)


def solution(mesh):
    in_specs = (
        P("seq", "exp"),
        P("seq", "exp"),
        P("seq", "exp"),
        P("seq", "exp"),
        P(("seq", "exp"), None),
        P(),
        P(),
        P(("seq", "exp"), None),
        P(("seq", "exp"), None),
        P("exp", "seq", None),
        P("exp", "seq", None),
        P("exp", "seq", None),
    )
    out_specs = P(("seq", "exp"), None)
    return jax.shard_map(body, mesh=mesh, in_specs=in_specs, out_specs=out_specs, check_vma=False)
```

```python
import functools

import jax
import jax.numpy as jnp
from jax import lax
from jax.experimental import pallas as pl
from jax.experimental.pallas import tpu as pltpu
from jax.sharding import PartitionSpec as P

MESH = pl.DeviceIdType.MESH
PARTS = 2


class Place:
    def __init__(self, n_seq, n_exp):
        s, e = lax.axis_index("seq"), lax.axis_index("exp")
        self.fold, self.n_exp = n_exp // 4, n_exp
        self.length = (n_seq // 2) * self.fold
        self.p = (s // 2) * self.fold + e // 4
        self.x, self.y, self.c = s % 2, (e // 2) % 2, e % 2

    def ids(self, p, x, y, c):
        return (p // self.fold) * 2 + x, (p % self.fold) * 4 + y * 2 + c

    def block(self, p, x, y, c):
        s, e = self.ids(p, x, y, c)
        return s * self.n_exp + e

    def dev(self, dp=0, dx=0, dy=0, dc=0):
        x = 1 - self.x if dx else self.x
        y = 1 - self.y if dy else self.y
        c = 1 - self.c if dc else self.c
        return self.ids(self.p + dp, x, y, c)

    def greet(self, *more):
        barrier = pltpu.get_barrier_semaphore()
        for d in (dict(dx=1), dict(dy=1), dict(dc=1), *more):
            pl.semaphore_signal(barrier, inc=1, device_id=self.dev(**d), device_id_type=MESH)

        @pl.when(self.p > 0)
        def _():
            pl.semaphore_signal(barrier, inc=1, device_id=self.dev(dp=-1), device_id_type=MESH)

        @pl.when(self.p < self.length - 1)
        def _():
            pl.semaphore_signal(barrier, inc=1, device_id=self.dev(dp=1), device_id_type=MESH)

        ends = (self.p > 0).astype(jnp.int32) + (self.p < self.length - 1).astype(jnp.int32)
        pl.semaphore_wait(barrier, 3 + len(more) + ends)

    def at(self, stage, sign, k):
        if sign == 0:
            stage(0, 0, 0)
        elif sign < 0:
            pl.when(self.p >= k)(lambda: stage(2 * k - 1, -k, -1))
        else:
            pl.when(self.p + k < self.length)(lambda: stage(2 * k, k, 1))

    def far_first(self, stage):
        def one(i, carry):
            for sign in (1, -1):
                self.at(stage, sign, self.length - 1 - i)
            return carry

        if self.length <= 8:
            for i in range(self.length - 1):
                one(i, 0)
        else:
            lax.fori_loop(0, self.length - 1, one, 0)
        self.at(stage, 0, 0)

    def near_first(self, *stages):
        depth = len(stages)

        def ring(stage, k):
            if isinstance(k, int) and k == 0:
                self.at(stage, 0, 0)
            else:
                for sign in (-1, 1):
                    self.at(stage, sign, k)

        def step(k):
            for j, stage in enumerate(stages):
                if 0 <= k - j < self.length:
                    ring(stage, k - j)

        total = self.length + depth - 1
        if self.length <= 8:
            for k in range(total):
                step(k)
            return
        for k in range(depth):
            step(k)

        def one(k, carry):
            for j, stage in enumerate(stages):
                ring(stage, k - j)
            return carry

        lax.fori_loop(depth, self.length, one, 0)
        for k in range(self.length, total):
            step(k)


def gather_kernel(n_seq, n_exp, x_ref, g_ref, out_ref, gout_ref, send, recv, loc):
    me = Place(n_seq, n_exp)
    rows, width = x_ref.shape
    grow = g_ref.shape[0]
    me.greet()

    def place(ref, off, dx, dy, dc=0):
        x = 1 - me.x if dx else me.x
        y = 1 - me.y if dy else me.y
        c = 1 - me.c if dc else me.c
        b = me.block(me.p + off, x, y, c)
        n = rows if ref is out_ref else grow
        return ref.at[pl.ds(pl.multiple_of(b * n, n), n)]

    def copies(part, kind, slot, off, dx, dy, to, own=False, half=None, dc=0):
        dst_x, dst_g = place(out_ref, off, dx, dy, dc), place(gout_ref, off, dx, dy, dc)
        src_x, src_g = (x_ref, g_ref) if own else (dst_x, dst_g)
        span = width // PARTS
        if half is None:
            cols = pl.ds(part * span, span)
        else:
            cols = pl.ds(part * span + half * (span // 2), span // 2)
        out = [
            pltpu.make_async_remote_copy(
                src_x.at[:, cols],
                dst_x.at[:, cols],
                send.at[kind, slot, part],
                recv.at[kind, slot, part],
                to,
                MESH,
            )
        ]
        if half != 1 and part == 0:
            out.append(
                pltpu.make_async_remote_copy(
                    src_g, dst_g, send.at[kind, slot, PARTS], recv.at[kind, slot, PARTS], to, MESH
                )
            )
        return out

    def start(*a, **k):
        for cp in copies(*a, **k):
            cp.start()

    def wait_recv(*a, **k):
        for cp in copies(*a, **k):
            cp.wait_recv()

    def wait_send(*a, **k):
        for cp in copies(*a, **k):
            cp.wait_send()

    left, right = dict(dp=-1), dict(dp=1)
    X, Y, C = me.dev(dx=1), me.dev(dy=1), me.dev(dc=1)

    def line_sends(off, sign, do):
        own = sign == 0
        if sign <= 0:
            pl.when(me.p + 1 < me.length)(
                lambda: do(0, 2 * (-off + 1) - 1, off, 0, 0, me.dev(**right), own=own)
            )
        if sign >= 0:
            pl.when(me.p > 0)(lambda: do(0, 2 * (off + 1), off, 0, 0, me.dev(**left), own=own))

    def stage_line(slot, off, sign, do):
        own = sign == 0
        line_sends(off, sign, do)
        do(1, slot, off, 0, 0, X, own=own)
        do(2, slot, off, 0, 0, Y, own=own)
        do(5, slot, off, 0, 0, C, own=own)

    def stage_xy_1(slot, off, do):
        do(3, slot, off, 1, 0, Y, half=0)
        do(6, slot, off, 1, 0, C)

    def stage_xy_2(slot, off, do):
        do(4, slot, off, 0, 1, X, half=1)
        do(7, slot, off, 0, 1, C)

    def stage_diag(slot, off, do):
        do(8, slot, off, 1, 1, C)

    local = [
        pltpu.make_async_copy(x_ref, place(out_ref, 0, 0, 0), loc.at[0]),
        pltpu.make_async_copy(g_ref, place(gout_ref, 0, 0, 0), loc.at[1]),
    ]
    for cp in local:
        cp.start()

    def s1(slot, off, sign):
        for part in range(PARTS):
            if sign:
                wait_recv(part, 0, slot, off, 0, 0, X)
            stage_line(slot, off, sign, functools.partial(start, part))

    def s2(slot, off, sign):
        for part in range(PARTS):
            wait_recv(part, 1, slot, off, 1, 0, X)
            stage_xy_1(slot, off, functools.partial(start, part))
            wait_recv(part, 2, slot, off, 0, 1, X)
            stage_xy_2(slot, off, functools.partial(start, part))

    def s3(slot, off, sign):
        for part in range(PARTS):
            wait_recv(part, 3, slot, off, 1, 1, X, half=0)
            wait_recv(part, 4, slot, off, 1, 1, X, half=1)
            stage_diag(slot, off, functools.partial(start, part))

    me.near_first(s1, s2, s3)

    def s4(slot, off, sign):
        for part in range(PARTS):
            done = functools.partial(wait_send, part)
            stage_line(slot, off, sign, done)
            stage_xy_1(slot, off, done)
            stage_xy_2(slot, off, done)
            stage_diag(slot, off, done)
            wait_recv(part, 5, slot, off, 0, 0, X, dc=1)
            wait_recv(part, 6, slot, off, 1, 0, X, dc=1)
            wait_recv(part, 7, slot, off, 0, 1, X, dc=1)
            wait_recv(part, 8, slot, off, 1, 1, X, dc=1)

    me.near_first(s4)
    for cp in local:
        cp.wait()


def gather_all(x, g, n_seq, n_exp):
    n = n_seq * n_exp
    length = n // 8
    anyspace = pl.BlockSpec(memory_space=pl.ANY)
    return pl.pallas_call(
        functools.partial(gather_kernel, n_seq, n_exp),
        out_shape=(
            jax.ShapeDtypeStruct((n * x.shape[0], x.shape[1]), x.dtype),
            jax.ShapeDtypeStruct((n * g.shape[0], g.shape[1]), g.dtype),
        ),
        in_specs=[anyspace, anyspace],
        out_specs=(anyspace, anyspace),
        scratch_shapes=[
            pltpu.SemaphoreType.DMA((9, 2 * length + 1, PARTS + 1)),
            pltpu.SemaphoreType.DMA((9, 2 * length + 1, PARTS + 1)),
            pltpu.SemaphoreType.DMA((2,)),
        ],
        compiler_params=pltpu.CompilerParams(collective_id=1, has_side_effects=True),
    )(x, g)


def scatter_kernel(
    n_seq, n_exp, y_ref, out_ref, acc, sib, xbuf, ybuf, dab, dbb, line, send, recv, loc
):
    me = Place(n_seq, n_exp)
    L = me.length
    rows, width = out_ref.shape
    halfw = width // 2
    me.greet()
    X, Y, C = me.dev(dx=1), me.dev(dy=1), me.dev(dc=1)

    def src(off, grp, dc):
        x = 1 - me.x if grp & 1 else me.x
        y = 1 - me.y if grp & 2 else me.y
        c = 1 - me.c if dc else me.c
        b = me.block(me.p + off, x, y, c)
        return y_ref.at[pl.ds(pl.multiple_of(b * rows, rows), rows)]

    def sib_copy(slot, off, grp):
        return pltpu.make_async_remote_copy(
            src(off, grp, 1), sib.at[grp, slot], send.at[grp, slot], recv.at[grp, slot], C, MESH
        )

    def load(slot, off, grp):
        return pltpu.make_async_copy(src(off, grp, 0), acc.at[grp, slot], loc.at[grp, slot])

    for grp in (3, 1, 2, 0):

        def go(slot, off, sign, grp=grp):
            sib_copy(slot, off, grp).start()
            load(slot, off, grp).start()

        me.far_first(go)

    f32 = jnp.float32

    def pair_sum(slot, off, grp):
        load(slot, off, grp).wait()
        sib_copy(slot, off, grp).wait_recv()
        return acc[grp, slot].astype(f32) + sib[grp, slot].astype(f32)

    def diag_a(slot):
        return pltpu.make_async_remote_copy(
            acc.at[3, slot, :, pl.ds(0, halfw)], dab.at[slot], send.at[4, slot], recv.at[4, slot], Y, MESH
        )

    def diag_b(slot):
        return pltpu.make_async_remote_copy(
            acc.at[3, slot, :, pl.ds(halfw, halfw)], dbb.at[slot], send.at[5, slot], recv.at[5, slot], X, MESH
        )

    def x_copy(slot):
        return pltpu.make_async_remote_copy(
            acc.at[1, slot], xbuf.at[slot], send.at[6, slot], recv.at[6, slot], X, MESH
        )

    def y_copy(slot):
        return pltpu.make_async_remote_copy(
            acc.at[2, slot], ybuf.at[slot], send.at[7, slot], recv.at[7, slot], Y, MESH
        )

    def line_copy(slot, sign):
        return pltpu.make_async_remote_copy(
            acc.at[0, slot],
            line.at[slot],
            send.at[8, slot],
            recv.at[8, slot],
            me.dev(dp=sign),
            MESH,
        )

    def d1(slot, off, sign):
        acc[3, slot] = pair_sum(slot, off, 3).astype(acc.dtype)
        diag_a(slot).start()
        diag_b(slot).start()

    def d2(slot, off, sign):
        sx = pair_sum(slot, off, 1)
        diag_a(slot).wait_recv()
        acc[1, slot, :, pl.ds(0, halfw)] = (sx[:, :halfw] + dab[slot].astype(f32)).astype(acc.dtype)
        acc[1, slot, :, pl.ds(halfw, halfw)] = sx[:, halfw:].astype(acc.dtype)
        x_copy(slot).start()
        sy = pair_sum(slot, off, 2)
        diag_b(slot).wait_recv()
        acc[2, slot, :, pl.ds(0, halfw)] = sy[:, :halfw].astype(acc.dtype)
        acc[2, slot, :, pl.ds(halfw, halfw)] = (sy[:, halfw:] + dbb[slot].astype(f32)).astype(acc.dtype)
        y_copy(slot).start()

    def d3(slot, off, sign):
        total = pair_sum(slot, off, 0)
        x_copy(slot).wait_recv()
        y_copy(slot).wait_recv()
        total = total + xbuf[slot].astype(f32) + ybuf[slot].astype(f32)
        if sign == 0:
            out_ref[...] = total
            if L > 1:

                @pl.when(me.p > 0)
                def _():
                    in_copy(2).wait_recv()
                    out_ref[...] += line[2].astype(f32)

                @pl.when(me.p < L - 1)
                def _():
                    in_copy(1).wait_recv()
                    out_ref[...] += line[1].astype(f32)

            return
        acc[0, slot] = total.astype(acc.dtype)
        far = slot + 2
        behind = me.p > 0 if sign > 0 else me.p < L - 1

        @pl.when(jnp.logical_and(behind, sign * off + 1 < L))
        def _():
            in_copy(far).wait_recv()
            acc[0, slot] = (acc[0, slot].astype(f32) + line[far].astype(f32)).astype(acc.dtype)

        line_copy(slot, sign).start()

    def in_copy(slot):
        return pltpu.make_async_remote_copy(
            acc.at[0, slot], line.at[slot], send.at[8, slot], recv.at[8, slot], X, MESH
        )

    me.far_first(d1)
    me.far_first(d2)
    me.far_first(d3)

    def fin(slot, off, sign):
        for grp in range(4):
            sib_copy(slot, off, grp).wait_send()
        diag_a(slot).wait_send()
        diag_b(slot).wait_send()
        x_copy(slot).wait_send()
        y_copy(slot).wait_send()
        if sign:
            line_copy(slot, sign).wait_send()

    me.far_first(fin)


def scatter_sum(part, n_seq, n_exp):
    n = n_seq * n_exp
    slots = n // 4 - 1 + 2
    rows, width = part.shape[0] // n, part.shape[1]
    bf = jnp.bfloat16
    return pl.pallas_call(
        functools.partial(scatter_kernel, n_seq, n_exp),
        out_shape=jax.ShapeDtypeStruct((rows, width), jnp.float32),
        in_specs=[pl.BlockSpec(memory_space=pl.ANY)],
        out_specs=pl.BlockSpec(memory_space=pltpu.VMEM),
        scratch_shapes=[
            pltpu.VMEM((4, slots, rows, width), bf),
            pltpu.VMEM((4, slots, rows, width), bf),
            pltpu.VMEM((slots, rows, width), bf),
            pltpu.VMEM((slots, rows, width), bf),
            pltpu.VMEM((slots, rows, width // 2), bf),
            pltpu.VMEM((slots, rows, width // 2), bf),
            pltpu.VMEM((slots, rows, width), bf),
            pltpu.SemaphoreType.DMA((9, slots)),
            pltpu.SemaphoreType.DMA((9, slots)),
            pltpu.SemaphoreType.DMA((4, slots)),
        ],
        compiler_params=pltpu.CompilerParams(
            collective_id=2, has_side_effects=True, vmem_limit_bytes=60 * 2**20
        ),
    )(part)


GPARTS = 4
HPARTS = 4
PLANES = 4
MPARTS = 4


def plane_orders(length):
    def depth(q):
        return min(q, length - 1 - q)

    visit = []
    for p in range(length):
        rest = [q for q in range(length) if q != p]
        near = min(rest, key=lambda q: (abs(q - p), depth(q)), default=p)
        rest = sorted((q for q in rest if q != near), key=lambda q: (depth(q), abs(q - p)))
        visit.append([p] + [near] * (length > 1) + rest)
    lines = []
    for p in range(length):
        def ready(q):
            chain = range(0, p + 1) if q > p else range(p, length)
            return max(visit[b].index(q) for b in chain)

        low = 2 * p < length
        lines.append(sorted((q for q in range(length) if q != p), key=lambda q: (ready(q), -q if low else q)))
    return visit, lines


def pick(table, p, j):
    total = 0
    for a, row in enumerate(table):
        for b, v in enumerate(row):
            hit = jnp.logical_and(p == a, j == b).astype(jnp.int32)
            total = total + hit * v
    return total


def spans(tiles, parts):
    cuts = [(tiles * i // parts) * 128 for i in range(parts + 1)]
    return [pl.ds(a, b - a) for a, b in zip(cuts[:-1], cuts[1:])]


def when(cond, fn):
    def run():
        fn()

    pl.when(cond)(run)


def attend_tokens(
    me, q_ref, k_ref, v_ref, ld_ref, res_ref, ag_ref, mg_ref, ids_ref, gw_ref, x_out,
    hid, work, flat, own16, peer, cin, cout, tots, tok, psend, precv, tsem, msend, mrecv,
):
    L, z = me.length, me.p
    f32, bf = jnp.float32, jnp.bfloat16
    heads, block = ld_ref.shape
    dim = q_ref.shape[1] // heads
    rows = res_ref.shape[0]
    n_exp, width = tok.shape[0], tok.shape[2]
    e = lax.axis_index("exp")
    pair = me.dev(dx=1)

    def head(h):
        return pl.ds(h * dim, dim)

    def pair_copy(h):
        return pltpu.make_async_remote_copy(
            own16.at[h], peer.at[h], psend.at[0], precv.at[0, h], pair, MESH
        )

    def line_copy(h):
        return pltpu.make_async_remote_copy(
            cout.at[h], cin.at[h], psend.at[1], precv.at[1, h], me.dev(dp=1), MESH
        )

    tot_copy = pltpu.make_async_remote_copy(tots.at[0], tots.at[1], tsem.at[0], tsem.at[1], pair, MESH)

    nt = (((1,), (1,)), ((), ()))
    tn = (((0,), (0,)), ((), ()))
    r = lax.broadcasted_iota(jnp.int32, (block, block), 0)
    c = lax.broadcasted_iota(jnp.int32, (block, block), 1)
    seen = r >= c
    decay = ld_ref[...]
    high = lax.Precision.HIGHEST
    cum = lax.dot_general(seen.astype(f32), decay, nt, precision=high, preferred_element_type=f32)
    cum_t = jnp.dot(decay, (r <= c).astype(f32), precision=high, preferred_element_type=f32)
    total = cum_t[:, block - 1 :]
    tots[0, 0:heads, :] = jnp.broadcast_to(total, (heads, dim))

    def state(h):
        kw = (k_ref[:, head(h)].astype(f32) * jnp.exp(total[h : h + 1] - cum[:, h : h + 1])).astype(bf)
        own = lax.dot_general(kw, v_ref[:, head(h)], tn, preferred_element_type=f32)
        work[:, pl.ds((heads + h) * dim, dim)] = own
        own16[h] = own.astype(bf)

    for h in range(heads):
        state(h)
    me.greet(dict(dy=1, dc=1))
    tot_copy.start()
    for h in range(heads):
        pair_copy(h).start()

    @pl.when(z == 0)
    def _():
        cin[...] = jnp.zeros_like(cin)

    def f_intra(h):
        scores = lax.dot_general(q_ref[:, head(h)], k_ref[:, head(h)], nt, preferred_element_type=f32)
        gap = cum[:, h : h + 1] - cum_t[h : h + 1, :]
        weights = jnp.where(seen, scores * jnp.exp(jnp.where(seen, gap, 0.0)), 0.0).astype(bf)
        work[:, head(h)] = jnp.dot(weights, v_ref[:, head(h)], preferred_element_type=f32)

    for h in range(heads):
        f_intra(h)
    tot_copy.wait_recv()
    mine, other = tots[0, 0:heads, :], tots[1, 0:heads, :]
    both = jnp.exp(mine + other)
    is_odd = jnp.full(mine.shape, me.x, jnp.int32) == 1
    one = jnp.ones_like(mine)
    own_by = jnp.where(is_odd, one, jnp.exp(other))
    peer_by = jnp.where(is_odd, jnp.exp(mine), one)
    carry_by = jnp.where(is_odd, jnp.exp(other), one)
    peer_in = jnp.where(is_odd, one, jnp.zeros_like(mine))

    peers = (dict(dc=1), dict(dy=1), dict(dy=1, dc=1))
    pieces = MPARTS
    span = width // pieces

    def mix_copy(k, i):
        to = me.dev(**peers[k])
        cols = pl.ds(i * span, span)
        src = flat.at[pl.ds(pl.multiple_of(to[1] * rows, rows), rows), cols]
        return pltpu.make_async_remote_copy(
            src, tok.at[e, :, cols], msend.at[0], mrecv.at[k, i], to, MESH
        )

    def mix_in(k, i):
        to = me.dev(**peers[k])
        cols = pl.ds(i * span, span)
        return pltpu.make_async_remote_copy(
            tok.at[to[1], :, cols], tok.at[to[1], :, cols], msend.at[0], mrecv.at[k, i], to, MESH
        )

    def f_chain(h):
        pair_copy(h).wait_recv()
        pl.when(z > 0)(lambda: line_copy(h).wait_recv())
        near = peer[h].astype(f32)
        come = cin[h].astype(f32)
        row = slice(h, h + 1)

        @pl.when(z < L - 1)
        def _():
            mix = both[row] * come + own_by[row] * work[:, pl.ds((heads + h) * dim, dim)] + peer_by[row] * near
            cout[h] = mix.astype(bf)
            line_copy(h).start()

    def f_head(h):
        near = peer[h].astype(f32)
        come = cin[h].astype(f32)
        row = slice(h, h + 1)
        carried = carry_by[row] * come + peer_in[row] * near
        coarse = carried.astype(bf)
        fine = (carried - coarse.astype(f32)).astype(bf)
        query = q_ref[:, head(h)]
        inter = jnp.dot(query, coarse, preferred_element_type=f32) + jnp.dot(
            query, fine, preferred_element_type=f32
        )
        attn = work[:, head(h)] + jnp.exp(cum[:, h : h + 1]) * inter
        scale = lax.rsqrt(jnp.mean(attn * attn, axis=-1, keepdims=True) + 1e-06)
        flat[0:block, head(h)] = (attn * scale).astype(bf)
        if (h + 1) * pieces % heads == 0:
            for k in range(len(peers)):
                mix_copy(k, (h + 1) * pieces // heads - 1).start()

    for h in range(heads):
        f_chain(h)
        f_head(h)

    tok[e] = flat[pl.ds(pl.multiple_of(e * rows, rows), rows), 0:width]

    def f_mix():
        for i in range(pieces):
            for k in range(len(peers)):
                mix_in(k, i).wait_recv()

    f_mix()
    square = jnp.zeros((rows, 1), f32)
    for j in range(n_exp):
        cols = pl.ds(j * width, width)
        value = (res_ref[:, cols].astype(f32) + tok[j].astype(f32) * ag_ref[:, cols]).astype(bf)
        hid[:, cols] = value
        wide = value.astype(f32)
        square = square + jnp.sum(wide * wide, axis=1, keepdims=True)
    scale = lax.rsqrt(square / (n_exp * width) + 1e-06)
    for j in range(n_exp):
        cols = pl.ds(j * width, width)
        x_out[:, cols] = (hid[:, cols].astype(f32) * scale * mg_ref[:, cols]).astype(bf)

    def column(ref):
        same = lax.broadcasted_iota(jnp.int32, (rows, rows), 0) == lax.broadcasted_iota(jnp.int32, (rows, rows), 1)
        return lax.dot_general(
            same.astype(f32), ref[...].astype(f32), nt, precision=high, preferred_element_type=f32
        )

    ids, gates = column(ids_ref).astype(jnp.int32), column(gw_ref)
    coarse = gates.astype(bf).astype(f32)
    rest = gates - coarse
    lane = lax.broadcasted_iota(jnp.int32, (rows, 128), 1)
    extra = jnp.zeros((rows, 128), f32)
    for i in range(ids_ref.shape[0]):
        who = ids[:, i : i + 1]
        extra = jnp.where(lane == who, coarse[:, i : i + 1], extra)
        extra = jnp.where(lane == who + 64, rest[:, i : i + 1], extra)
    x_out[:, n_exp * width :] = extra.astype(bf)

    def finish():
        def out(ref, sent):
            pltpu.make_async_remote_copy(ref, ref, sent, sent, pair, MESH).wait_send()

        tot_copy.wait_send()
        out(own16, psend.at[0])
        pl.when(z < L - 1)(lambda: out(cout, psend.at[1]))
        out(tok.at[pl.ds(0, len(peers))], msend.at[0])

    return finish


def moe_kernel(
    n_seq, n_exp, q_ref, k_ref, v_ref, ld_ref, res_ref, ag_ref, mg_ref, ids_ref, gw_ref,
    wg_ref, wu_ref, wd_ref, out_ref,
    xs, ys, act, sib, din, xin, yin, lin, tot, wg, wu, wd, hid_ref,
    own16, peer, cin, cout, tots, tok,
    gsend, lsend, grecv, crecv, brecv, ssend, srecv, drecv, loc, psend, precv, tsem, msend, mrecv,
):
    me = Place(n_seq, n_exp)
    L, p = me.length, me.p
    rows, width = out_ref.shape
    hidden = wg.shape[0]
    many = 8 * rows
    f32, bf = jnp.float32, jnp.bfloat16
    X, Y, C = me.dev(dx=1), me.dev(dy=1), me.dev(dc=1)
    visit, lines = plane_orders(L)
    gcols = spans(xs.shape[1] // 128, GPARTS)
    hcols, dcols = spans(width // 128, HPARTS), spans(width // 128, 2 * HPARTS)

    loads = [
        pltpu.make_async_copy(a.at[0], b, loc.at[i])
        for i, (a, b) in enumerate(((wg_ref, wg), (wu_ref, wu), (wd_ref, wd)))
    ]
    for cp in loads:
        cp.start()

    def flip(v, d):
        return 1 - v if d else v

    def row(q, dx=0, dy=0, dc=0):
        k = (flip(me.c, dc) * 2 + flip(me.x, dx)) * 2 + flip(me.y, dy)
        return pl.ds(pl.multiple_of((q * 8 + k) * rows, rows), rows)

    def srow(q, dx=0, dy=0):
        k = flip(me.x, dx) * 2 + flip(me.y, dy)
        return pl.ds(pl.multiple_of((q * 4 + k) * rows, rows), rows)

    def prow(q):
        return pl.ds(pl.multiple_of(q * rows, rows), rows)

    def gcopy(kind, q, part, r, to, sent=None):
        ref = xs.at[r, gcols[part]]
        sent = gsend.at[kind] if sent is None else sent
        got = crecv.at[q] if kind == 0 else grecv.at[kind - 1, q, part]
        return pltpu.make_async_remote_copy(ref, ref, sent, got, to, MESH)

    def bulk(ref, sent):
        return pltpu.make_async_remote_copy(ref, ref, sent, sent, X, MESH)

    upper = GPARTS // 2
    cut = gcols[upper].start
    low_cols, high_cols = pl.ds(0, cut), pl.ds(cut, xs.shape[1] - cut)

    def line_pair(q, part):
        pl.when(jnp.logical_and(q >= p, p > 0))(
            lambda: gcopy(5, q, part, row(q), me.dev(dp=-1), lsend.at[0, q]).start()
        )
        pl.when(jnp.logical_and(q <= p, p + 1 < L))(
            lambda: gcopy(5, q, part, row(q), me.dev(dp=1), lsend.at[1, q]).start()
        )

    def g_line(q, part):
        pl.when(q != p)(lambda: gcopy(5, q, part, row(q), X).wait_recv())
        line_pair(q, part)

    middle = range(1, GPARTS - 1)
    mid_cols = pl.ds(gcols[1].start, gcols[-1].start - gcols[1].start)

    def second_x(q, part, own):
        out = [gcopy(0, q, part, row(q, 1, 0), C)]
        if own and part < upper:
            out.append(gcopy(3, q, part, row(q, 1, 0), Y, gsend.at[7]))
        if not own and part == 0:
            out.append(gcopy(3, q, part, row(q, 1, 0), Y))
        return out

    def second_y(q, part, own):
        out = [gcopy(0, q, part, row(q, 0, 1), C)]
        if own and part >= upper:
            out.append(gcopy(4, q, part, row(q, 0, 1), X, gsend.at[8]))
        if not own and part == GPARTS - 1:
            out.append(gcopy(4, q, part, row(q, 0, 1), X))
        return out

    def corner_out(q):
        for part in middle:
            pl.when(jnp.logical_and(q >= p, p > 0))(
                lambda: gcopy(6, q, part, row(q, 1, 1), me.dev(dp=-1), lsend.at[2, q]).start()
            )
            pl.when(jnp.logical_and(q <= p, p + 1 < L))(
                lambda: gcopy(6, q, part, row(q, 1, 1), me.dev(dp=1), lsend.at[3, q]).start()
            )

    def g_corner(k):
        for sign in (-1, 1):
            q = p + sign * k

            def arrive():
                for part in middle:
                    gcopy(6, q, part, row(q, 1, 1), X).wait_recv()
                    gcopy(0, q, part, row(q, 1, 1), C).start()
                corner_out(q)

            when(jnp.logical_and(q >= 0, q < L), arrive)

    lower, higher = range(upper), range(upper, GPARTS)

    def g_first(q, turn, own=False):
        for part in lower if turn == 0 else higher:
            gcopy(1, q, part, row(q), X, gsend.at[5 + turn] if own else None).start()
        for part in higher if turn == 0 else lower:
            gcopy(2, q, part, row(q), Y).start()
        if turn == 0:
            for part in range(GPARTS):
                gcopy(0, q, part, row(q), C).start()

    def g_own(q):
        for part in lower:
            line_pair(q, part)
        g_first(q, 0, True)
        bulk(xs.at[row(q), low_cols], gsend.at[5]).wait_send()
        for part in higher:
            line_pair(q, part)
        g_first(q, 1, True)

    def from_x(q, part, own):
        gcopy(1, q, part, row(q, 1, 0), X).wait_recv()
        for cp in second_x(q, part, own)[::-1]:
            cp.start()

    def from_y(q, part, own):
        gcopy(2, q, part, row(q, 0, 1), X).wait_recv()
        for cp in second_y(q, part, own)[::-1]:
            cp.start()

    def g_second(q, own=False):
        for part in lower:
            from_x(q, part, own)
            from_y(q, GPARTS - 1 - part, own)

    def g_rest(q, own=False):
        for part in lower:
            from_x(q, part + upper, own)
            from_y(q, part, own)

    def g_third(q, own=False):
        for part in range(GPARTS) if own else (0, GPARTS - 1):
            gcopy(3 if part < upper else 4, q, part, row(q, 1, 1), X).wait_recv()
            gcopy(0, q, part, row(q, 1, 1), C).start()
        if own:
            corner_out(q)

    def g_ring(k, parts):
        for sign in (-1, 1):
            q = p + sign * k
            when(jnp.logical_and(q >= 0, q < L), lambda: [g_line(q, part) for part in parts])

    def g_done(q):
        r = pl.ds(pl.multiple_of((q * 2 + 1 - me.c) * 4 * rows, 4 * rows), 4 * rows)
        pltpu.make_async_remote_copy(xs.at[r], xs.at[r], gsend.at[0], crecv.at[q], X, MESH).wait_recv()

    def g_drain():
        bulk(xs.at[pl.ds(0, L * 4 * rows)], gsend.at[0]).wait_send()
        bulk(xs.at[pl.ds(0, (L - 1) * rows)], gsend.at[1]).wait_send()
        bulk(xs.at[pl.ds(0, L * rows)], gsend.at[2]).wait_send()
        bulk(xs.at[pl.ds(0, (L - 1) * rows), gcols[0]], gsend.at[3]).wait_send()
        bulk(xs.at[pl.ds(0, (L - 1) * rows), gcols[-1]], gsend.at[4]).wait_send()
        bulk(xs.at[row(p), low_cols], gsend.at[7]).wait_send()
        bulk(xs.at[row(p), high_cols], gsend.at[8]).wait_send()
        bulk(xs.at[row(p), high_cols], gsend.at[6]).wait_send()
        for q in range(L):
            pl.when(jnp.logical_and(q >= p, p > 0))(lambda: bulk(xs.at[row(q)], lsend.at[0, q]).wait_send())
            pl.when(jnp.logical_and(q <= p, p + 1 < L))(lambda: bulk(xs.at[row(q)], lsend.at[1, q]).wait_send())
            mid = xs.at[row(q), mid_cols]
            pl.when(jnp.logical_and(q >= p, p > 0))(lambda: bulk(mid, lsend.at[2, q]).wait_send())
            pl.when(jnp.logical_and(q <= p, p + 1 < L))(lambda: bulk(mid, lsend.at[3, q]).wait_send())

    def sib_copy(q, h):
        r = pl.ds(pl.multiple_of((q * 2 + 1 - me.c) * 4 * rows, 4 * rows), 4 * rows)
        d = pl.ds(pl.multiple_of(q * 4 * rows, 4 * rows), 4 * rows)
        return pltpu.make_async_remote_copy(
            ys.at[r, hcols[h]], sib.at[d, hcols[h]], ssend.at[4], brecv.at[q, h], C, MESH
        )

    def scopy(kind, q, h, r, dst, d, to):
        return pltpu.make_async_remote_copy(
            ys.at[r, hcols[h]], dst.at[d, hcols[h]], ssend.at[kind], srecv.at[kind, q, h], to, MESH
        )

    def diag_copy(q, h, side):
        cols = dcols[2 * h + side]
        return pltpu.make_async_remote_copy(
            ys.at[row(q, 1, 1), cols], din.at[prow(q), cols], ssend.at[0], drecv.at[side, q, h], (Y, X)[side], MESH
        )

    def x_copy(q, h):
        return scopy(1, q, h, row(q, 1, 0), xin, prow(q), X)

    def y_copy(q, h):
        return scopy(2, q, h, row(q, 0, 1), yin, prow(q), Y)

    def line_copy(q, h):
        up = (q > p).astype(jnp.int32)
        last = jnp.logical_and(q < p, q == p - 1).astype(jnp.int32)
        slot = q + (L - q) * last
        return pltpu.make_async_remote_copy(
            ys.at[row(q), hcols[h]],
            lin.at[prow(slot), hcols[h]],
            ssend.at[3],
            srecv.at[3, slot, h],
            me.dev(dp=2 * up - 1),
            MESH,
        )

    def line_in(slot, h):
        return pltpu.make_async_remote_copy(
            ys.at[row(p), hcols[h]], lin.at[prow(slot), hcols[h]], ssend.at[3], srecv.at[3, slot, h], X, MESH
        )

    def pair(q, h, dx, dy):
        return ys[row(q, dx, dy), hcols[h]].astype(f32) + sib[srow(q, dx, dy), hcols[h]].astype(f32)

    def r_first(q, h):
        sib_copy(q, h).wait_recv()
        ys[row(q, 1, 1), hcols[h]] = pair(q, h, 1, 1).astype(bf)
        for side in range(2):
            diag_copy(q, h, side).start()

    def r_second(q, h):
        sx, sy = pair(q, h, 1, 0), pair(q, h, 0, 1)
        near, far = dcols[2 * h], dcols[2 * h + 1]
        diag_copy(q, h, 0).wait_recv()
        ys[row(q, 1, 0), near] = (sx[:, : near.size] + din[prow(q), near].astype(f32)).astype(bf)
        ys[row(q, 1, 0), far] = sx[:, near.size :].astype(bf)
        x_copy(q, h).start()
        diag_copy(q, h, 1).wait_recv()
        ys[row(q, 0, 1), near] = sy[:, : near.size].astype(bf)
        ys[row(q, 0, 1), far] = (sy[:, near.size :] + din[prow(q), far].astype(f32)).astype(bf)
        y_copy(q, h).start()

    def r_third(q, h):
        total = pair(q, h, 0, 0)
        x_copy(q, h).wait_recv()
        y_copy(q, h).wait_recv()
        total = total + xin[prow(q), hcols[h]].astype(f32) + yin[prow(q), hcols[h]].astype(f32)
        tot[prow(q), hcols[h]] = total

    def r_line(q, h):
        behind = jnp.logical_or(jnp.logical_and(q > p, p > 0), jnp.logical_and(q < p, p < L - 1))

        @pl.when(behind)
        def _():
            line_in(q, h).wait_recv()
            ys[row(q), hcols[h]] = (tot[prow(q), hcols[h]] + lin[prow(q), hcols[h]].astype(f32)).astype(bf)

        @pl.when(jnp.logical_not(behind))
        def _():
            ys[row(q), hcols[h]] = tot[prow(q), hcols[h]].astype(bf)

        line_copy(q, h).start()

    def r_last(h):
        cols = hcols[h]

        @pl.when(p > 0)
        def _():
            line_in(p, h).wait_recv()
            tot[prow(p), cols] += lin[prow(p), cols].astype(f32)

        @pl.when(p < L - 1)
        def _():
            line_in(L, h).wait_recv()
            tot[prow(p), cols] += lin[prow(L), cols].astype(f32)

        out_ref[:, cols] = (hid_ref[:, cols].astype(f32) + tot[prow(p), cols]).astype(bf)

    at_end = jnp.logical_or(p == 0, p == L - 1)
    inner = jnp.logical_not(at_end)

    def r_early(q, h):
        pl.when(jnp.logical_and(at_end, q != p))(lambda: r_line(q, h))

    def r_drain():
        bulk(sib, ssend.at[4]).wait_send()
        for kind, ref in enumerate((din, xin, yin, lin.at[pl.ds(0, (L - 1) * rows)])):
            bulk(ref, ssend.at[kind]).wait_send()

    tile = next(t for t in range(512, 0, -128) if hidden % t == 0)
    fsteps = hidden // tile

    def block_of(q):
        return pl.ds(pl.multiple_of(q * many, many), many)

    def gate_of(q):
        extra = xs[block_of(q), width : width + 128].astype(f32)
        lane = lax.broadcasted_iota(jnp.int32, extra.shape, 1)
        e = lax.axis_index("exp")
        keep = jnp.logical_or(lane == e, lane == e + 64)
        return jnp.sum(jnp.where(keep, extra, 0.0), axis=1, keepdims=True)

    nt = (((1,), (1,)), ((), ()))

    def ffn_in(q, f):
        fc = pl.ds(f * tile, tile)
        rows_in = xs[block_of(q), 0:width]
        gate = lax.dot_general(rows_in, wg[fc, :], nt, preferred_element_type=f32)
        up = lax.dot_general(rows_in, wu[fc, :], nt, preferred_element_type=f32)
        act[:, fc] = (gate / (1.0 + jnp.exp(-gate)) * up * gate_of(q)).astype(bf)

    def ffn_out(q, h):
        ys[block_of(q), hcols[h]] = jnp.dot(
            act[...], wd[:, hcols[h]], preferred_element_type=f32
        ).astype(bf)
        sib_copy(q, h).start()

    front_done = attend_tokens(
        me, q_ref, k_ref, v_ref, ld_ref, res_ref, ag_ref, mg_ref, ids_ref, gw_ref, xs.at[row(p)],
        hid_ref, tot, act, own16, peer, cin, cout, tots, tok, psend, precv, tsem, msend, mrecv,
    )
    second = pick(visit, p, 1)
    g_own(p)
    g_second(p, True)
    g_ring(1, lower)
    g_rest(p, True)
    g_ring(1, higher)
    g_first(second, 0)
    g_third(p, True)
    g_first(second, 1)
    front_done()
    for cp in loads:
        cp.wait()

    def chunk(j, carry):
        q, nxt, prev = pick(visit, p, j), pick(visit, p, j + 1), pick(visit, p, j - 1)
        older = pick(visit, p, j - 2)
        third, fourth = pick(visit, p, 2), pick(visit, p, 3)

        def opening(*fns):
            when(j == 0, lambda: [fn() for fn in fns])

        def closing(*fns):
            when(j == L - 1, lambda: [fn() for fn in fns])

        def ahead(*fns):
            when(jnp.logical_and(j > 0, j + 1 < L), lambda: [fn() for fn in fns])

        def after(*fns):
            when(j > 0, lambda: [fn() for fn in fns])

        def later(*fns):
            when(j > 1, lambda: [fn() for fn in fns])

        def settle(at, h):
            r_third(at, h)
            r_early(at, h)

        def hook(n):
            if n == 0:
                after(lambda: r_first(prev, 2), lambda: r_first(prev, 3))
                opening(
                    lambda: g_ring(2, lower),
                    lambda: g_second(nxt),
                    lambda: g_ring(2, higher),
                    lambda: g_first(fourth, 0),
                )
            if n == 1:
                opening(lambda: g_rest(nxt), lambda: g_first(fourth, 1))
                when(j == 1, lambda: g_corner(3))
                ahead(lambda: g_second(nxt))
                later(lambda: settle(older, 0), lambda: settle(older, 1))
                after(lambda: r_second(prev, 0), lambda: r_second(prev, 1))
            if n == 2:
                opening(lambda: g_corner(1))
                ahead(lambda: g_rest(nxt))
                later(lambda: settle(older, 2), lambda: settle(older, 3))
                closing(lambda: r_second(prev, 2))

        g_done(q)
        for f in range(fsteps):
            ffn_in(q, f)
            hook(f)
        for f in range(fsteps, 3):
            hook(f)
        for h in range(HPARTS):
            ffn_out(q, h)
            if h == 0:
                ahead(lambda: r_second(prev, 2))
                closing(lambda: r_second(prev, 3))
            if h == 1:
                ahead(lambda: r_second(prev, 3))
                opening(lambda: g_ring(3, range(GPARTS)), lambda: g_first(third, 0))
                closing(lambda: settle(prev, 0))
            if h == 2:
                r_first(q, 0)
                ahead(lambda: g_third(nxt))
                opening(lambda: g_third(nxt))
                closing(lambda: settle(prev, 1))
            if h == 3:
                r_first(q, 1)
                opening(lambda: g_first(third, 1), lambda: g_corner(2))
        return carry

    def one_line(i, h):
        when(inner, lambda: r_line(pick(lines, p, i), h))

    lax.fori_loop(0, L, chunk, 0)

    final, prior = pick(visit, p, L - 1), pick(visit, p, L - 2)
    r_first(final, 2)
    r_first(final, 3)
    for h in (2, 3):
        r_third(prior, h)
        r_early(prior, h)
    for h in range(HPARTS):
        r_second(final, h)
        one_line(0, h)
    for h in range(HPARTS):
        one_line(1, h)
        r_third(final, h)
        r_early(final, h)
    for h in range(HPARTS):
        one_line(2, h)
        if h:
            r_last(h - 1)
    r_last(HPARTS - 1)

    g_drain()
    r_drain()


def moe_scratch(n_seq, n_exp, x_shape, w_shape):
    n, L = n_seq * n_exp, n_seq * n_exp // 8
    rows, wide = x_shape
    hidden, width = w_shape[1:]
    bf, f32 = jnp.bfloat16, jnp.float32
    return [
        ((n * rows, wide), bf),
        ((n * rows, width), bf),
        ((8 * rows, hidden), bf),
        ((n // 2 * rows, width), bf),
        ((L * rows, width), bf),
        ((L * rows, width), bf),
        ((L * rows, width), bf),
        ((L * rows + rows, width), bf),
        ((L * rows, width), f32),
        ((hidden, width), bf),
        ((hidden, width), bf),
        ((hidden, width), bf),
    ]


MOE_VMEM = 61 * 2**20


def moe_fits(n_seq, n_exp, rows, width, w_shape):
    need = sum(
        a * b * jnp.dtype(t).itemsize for (a, b), t in moe_scratch(n_seq, n_exp, (rows, width + 128), w_shape)
    )
    return (
        w_shape[0] == 1
        and n_exp // 4 == 1
        and n_seq * n_exp == 8 * PLANES
        and w_shape[1] % 128 == 0
        and w_shape[2] % (256 * HPARTS) == 0
        and w_shape[2] // n_exp % (128 * MPARTS) == 0
        and need + 6 * 2**20 <= MOE_VMEM
    )


def whole_layer(
    queries, keys, values, log_decay, residual, attn_gain, moe_gain, expert_ids, gate_weights,
    w_gate, w_up, w_down, n_seq, n_exp,
):
    L = n_seq * n_exp // 8
    heads = log_decay.shape[1]
    part = queries.shape[1]
    dim = part // heads
    rows, width = residual.shape
    vmem = pl.BlockSpec(memory_space=pltpu.VMEM)
    anyspace = pl.BlockSpec(memory_space=pl.ANY)
    dma = pltpu.SemaphoreType.DMA
    bf = jnp.bfloat16
    states = pltpu.VMEM((heads, dim, dim), bf)
    scratch = moe_scratch(n_seq, n_exp, (rows, width + 128), w_gate.shape)
    return pl.pallas_call(
        functools.partial(moe_kernel, n_seq, n_exp),
        out_shape=jax.ShapeDtypeStruct(residual.shape, bf),
        in_specs=[vmem] * 9 + [anyspace] * 3,
        out_specs=vmem,
        scratch_shapes=[pltpu.VMEM(s, t) for s, t in scratch]
        + [
            pltpu.VMEM(residual.shape, bf),
            states,
            states,
            states,
            states,
            pltpu.VMEM((2, heads + -heads % 8, dim), jnp.float32),
            pltpu.VMEM((n_exp, rows, part), bf),
            dma((9,)),
            dma((4, L)),
            dma((6, L, GPARTS)),
            dma((L,)),
            dma((L, HPARTS)),
            dma((5,)),
            dma((4, L + 1, HPARTS)),
            dma((2, L, HPARTS)),
            dma((3,)),
            dma((2,)),
            dma((2, heads)),
            dma((2,)),
            dma((1,)),
            dma((3, MPARTS)),
        ],
        compiler_params=pltpu.CompilerParams(
            collective_id=5, has_side_effects=True, vmem_limit_bytes=MOE_VMEM
        ),
    )(
        queries, keys, values, log_decay.T, residual, attn_gain[None, :], moe_gain[None, :],
        expert_ids.T, gate_weights.T, w_gate, w_up, w_down,
    )


def carry_kernel(n_seq, own_ref, own16_ref, tot_ref, out_ref, peer, ptot, cin, cout, send, recv, tsem):
    s, e = lax.axis_index("seq"), lax.axis_index("exp")
    z, odd, deep = s // 2, s % 2, n_seq // 2
    heads = own_ref.shape[0]
    pair = (z * 2 + 1 - odd, e)

    barrier = pltpu.get_barrier_semaphore()
    pl.semaphore_signal(barrier, inc=1, device_id=pair, device_id_type=MESH)

    @pl.when(z > 0)
    def _():
        pl.semaphore_signal(barrier, inc=1, device_id=(s - 2, e), device_id_type=MESH)

    @pl.when(z < deep - 1)
    def _():
        pl.semaphore_signal(barrier, inc=1, device_id=(s + 2, e), device_id_type=MESH)

    ends = (z > 0).astype(jnp.int32) + (z < deep - 1).astype(jnp.int32)
    pl.semaphore_wait(barrier, 1 + ends)

    tot_copy = pltpu.make_async_remote_copy(tot_ref, ptot, tsem.at[0], tsem.at[1], pair, MESH)

    def pair_copy(h):
        return pltpu.make_async_remote_copy(
            own16_ref.at[h], peer.at[h], send.at[0, h], recv.at[0, h], pair, MESH
        )

    def line_copy(h):
        return pltpu.make_async_remote_copy(
            cout.at[h], cin.at[h], send.at[1, h], recv.at[1, h], (s + 2, e), MESH
        )

    tot_copy.start()
    for h in range(heads):
        pair_copy(h).start()

    @pl.when(z == 0)
    def _():
        cin[...] = jnp.zeros_like(cin)

    tot_copy.wait_recv()
    mine, other = tot_ref[...], ptot[...]
    both = jnp.exp(mine + other)
    is_odd = jnp.full(mine.shape, odd, jnp.int32) == 1
    one = jnp.ones_like(mine)
    own_by = jnp.where(is_odd, one, jnp.exp(other))
    peer_by = jnp.where(is_odd, jnp.exp(mine), one)
    carry_by = jnp.where(is_odd, jnp.exp(other), one)
    peer_in = jnp.where(is_odd, one, jnp.zeros_like(mine))
    for h in range(heads):
        pair_copy(h).wait_recv()

        @pl.when(z > 0)
        def _():
            line_copy(h).wait_recv()

        near = peer[h].astype(jnp.float32)
        come = cin[h].astype(jnp.float32)

        @pl.when(z < deep - 1)
        def _():
            cout[h] = (
                both[h : h + 1] * come + own_by[h : h + 1] * own_ref[h] + peer_by[h : h + 1] * near
            ).astype(cout.dtype)
            line_copy(h).start()

        out_ref[h] = carry_by[h : h + 1] * come + peer_in[h : h + 1] * near

    tot_copy.wait_send()
    for h in range(heads):
        pair_copy(h).wait_send()

        @pl.when(z < deep - 1)
        def _():
            line_copy(h).wait_send()


def carried_in(block_total, block_state, n_seq):
    heads, dim, _ = block_state.shape
    bf = jnp.bfloat16
    tile = jnp.pad(block_total, (0, -heads % 8))
    tile = jnp.broadcast_to(tile[:, None], (tile.shape[0], dim))
    vmem = pl.BlockSpec(memory_space=pltpu.VMEM)
    return pl.pallas_call(
        functools.partial(carry_kernel, n_seq),
        out_shape=jax.ShapeDtypeStruct(block_state.shape, jnp.float32),
        in_specs=[vmem] * 3,
        out_specs=vmem,
        scratch_shapes=[
            pltpu.VMEM(block_state.shape, bf),
            pltpu.VMEM(tile.shape, jnp.float32),
            pltpu.VMEM(block_state.shape, bf),
            pltpu.VMEM(block_state.shape, bf),
            pltpu.SemaphoreType.DMA((2, heads)),
            pltpu.SemaphoreType.DMA((2, heads)),
            pltpu.SemaphoreType.DMA((2,)),
        ],
        compiler_params=pltpu.CompilerParams(collective_id=3, has_side_effects=True),
    )(block_state, block_state.astype(bf), tile)


def mix_kernel(n_exp, normed_ref, res_ref, again_ref, mgain_ref, hid_ref, in_ref, tok, send, recv, loc):
    s, e = lax.axis_index("seq"), lax.axis_index("exp")
    rows, width = res_ref.shape[0], normed_ref.shape[1]

    barrier = pltpu.get_barrier_semaphore()
    for k in range(1, n_exp):
        pl.semaphore_signal(
            barrier, inc=1, device_id=(s, lax.rem(e + k, n_exp)), device_id_type=MESH
        )
    pl.semaphore_wait(barrier, n_exp - 1)

    def source(peer):
        return normed_ref.at[pl.ds(pl.multiple_of(peer * rows, rows), rows)]

    own = pltpu.make_async_copy(source(e), tok.at[e], loc.at[0])

    def copy(k):
        peer = lax.rem(e + k, n_exp)
        return pltpu.make_async_remote_copy(
            source(peer), tok.at[e], send.at[k], recv.at[k], (s, peer), MESH
        )

    def arriving(k):
        sender = lax.rem(e + n_exp - k, n_exp)
        return pltpu.make_async_remote_copy(
            source(e), tok.at[sender], send.at[k], recv.at[k], (s, sender), MESH
        )

    for k in range(1, n_exp):
        copy(k).start()
    own.start()
    own.wait()
    for k in range(1, n_exp):
        arriving(k).wait_recv()
    square = jnp.zeros((rows, 1), jnp.float32)
    for j in range(n_exp):
        cols = pl.ds(j * width, width)
        hid = (
            res_ref[:, cols].astype(jnp.float32)
            + tok[j].astype(jnp.float32) * again_ref[:, cols]
        ).astype(jnp.bfloat16)
        hid_ref[:, cols] = hid
        wide = hid.astype(jnp.float32)
        square = square + jnp.sum(wide * wide, axis=1, keepdims=True)
    scale = lax.rsqrt(square / (n_exp * width) + 1e-06)
    for j in range(n_exp):
        cols = pl.ds(j * width, width)
        in_ref[:, cols] = (
            hid_ref[:, cols].astype(jnp.float32) * scale * mgain_ref[:, cols]
        ).astype(jnp.bfloat16)
    for k in range(1, n_exp):
        copy(k).wait_send()


def mix_tokens(normed, residual, attn_gain, moe_gain, n_exp):
    vmem = pl.BlockSpec(memory_space=pltpu.VMEM)
    return pl.pallas_call(
        functools.partial(mix_kernel, n_exp),
        out_shape=(jax.ShapeDtypeStruct(residual.shape, jnp.bfloat16),) * 2,
        in_specs=[vmem] * 4,
        out_specs=(vmem, vmem),
        scratch_shapes=[
            pltpu.VMEM((n_exp, residual.shape[0], normed.shape[1]), jnp.bfloat16),
            pltpu.SemaphoreType.DMA((n_exp,)),
            pltpu.SemaphoreType.DMA((n_exp,)),
            pltpu.SemaphoreType.DMA((1,)),
        ],
        compiler_params=pltpu.CompilerParams(collective_id=4, has_side_effects=True),
    )(normed, residual, attn_gain[None, :], moe_gain[None, :])


def body(
    queries,
    keys,
    values,
    log_decay,
    residual,
    attn_gain,
    moe_gain,
    expert_ids,
    gate_weights,
    w_gate,
    w_up,
    w_down,
):
    n_seq, n_exp = lax.axis_size("seq"), lax.axis_size("exp")
    if moe_fits(n_seq, n_exp, *residual.shape, w_gate.shape):
        return whole_layer(
            queries, keys, values, log_decay, residual, attn_gain, moe_gain, expert_ids, gate_weights,
            w_gate, w_up, w_down, n_seq, n_exp,
        )
    tok_rows, width = residual.shape
    experts = w_gate.shape[0] * n_exp
    gates = jnp.sum(
        jnp.where(
            expert_ids[:, :, None] == jnp.arange(experts, dtype=jnp.int32)[None, None, :],
            gate_weights[:, :, None],
            0.0,
        ),
        axis=1,
    )
    rows = queries.shape[0]
    heads = log_decay.shape[1]
    head_dim = queries.shape[1] // heads
    q_heads = queries.reshape(rows, heads, head_dim)
    k_heads = keys.reshape(rows, heads, head_dim)
    v_heads = values.reshape(rows, heads, head_dim)
    upto = (
        lax.broadcasted_iota(jnp.int32, (rows, rows), 0)
        >= lax.broadcasted_iota(jnp.int32, (rows, rows), 1)
    ).astype(jnp.float32)
    log_cum = jnp.dot(upto, log_decay, precision=lax.Precision.HIGHEST)
    block_total = log_cum[-1]
    keys_weighted = (k_heads * jnp.exp(block_total[None, :] - log_cum)[:, :, None]).astype(
        jnp.bfloat16
    )
    block_state = jnp.einsum(
        "thd,the->hde", keys_weighted, v_heads, preferred_element_type=jnp.float32
    )
    carried = carried_in(block_total, block_state, lax.axis_size("seq"))
    scores = jnp.einsum("thd,shd->hts", q_heads, k_heads, preferred_element_type=jnp.float32)
    gap_logs = log_cum.T[:, :, None] - log_cum.T[:, None, :]
    causal_mask = (
        lax.broadcasted_iota(jnp.int32, (rows, rows), 0)
        >= lax.broadcasted_iota(jnp.int32, (rows, rows), 1)
    )[None, :, :]
    weights = jnp.where(
        causal_mask, scores * jnp.exp(jnp.where(causal_mask, gap_logs, 0.0)), 0.0
    ).astype(jnp.bfloat16)
    intra = jnp.einsum("hts,she->the", weights, v_heads, preferred_element_type=jnp.float32)
    inter = jnp.exp(log_cum)[:, :, None] * jnp.einsum(
        "thd,hde->the", q_heads.astype(jnp.float32), carried, precision=lax.Precision.HIGHEST
    )
    attn = intra + inter
    normed = (attn * lax.rsqrt(jnp.mean(attn * attn, axis=-1, keepdims=True) + 1e-06)).astype(
        jnp.bfloat16
    )
    normed = normed.reshape(rows, heads * head_dim)
    hidden, moe_in = mix_tokens(normed, residual, attn_gain, moe_gain, n_exp)
    hid32 = hidden.astype(jnp.float32)
    flat = gates.T.reshape(-1)
    pad = -flat.shape[0] % 1024
    g_tile = jnp.pad(flat, (0, pad)).reshape(-1, 128)
    everyone, g_all = gather_all(moe_in, g_tile, n_seq, n_exp)
    g_all = g_all.reshape(n_seq * n_exp, -1)[:, : experts * tok_rows]
    g_all = g_all.reshape(n_seq * n_exp, experts, tok_rows)
    mixed = None
    gate_col = lax.dynamic_slice_in_dim(
        g_all, lax.axis_index("exp") * w_gate.shape[0], w_gate.shape[0], 1
    )
    part = None
    for j in range(w_gate.shape[0]):
        gate_part = jnp.einsum("td,fd->tf", everyone, w_gate[j], preferred_element_type=jnp.float32)
        up_part = jnp.einsum("td,fd->tf", everyone, w_up[j], preferred_element_type=jnp.float32)
        active = (
            jax.nn.silu(gate_part) * up_part * gate_col[:, j, :].reshape(-1, 1)
        ).astype(jnp.bfloat16)
        one = jnp.dot(active, w_down[j], preferred_element_type=jnp.float32)
        part = one if part is None else part + one
    part = part.astype(jnp.bfloat16)
    total_rows, width = part.shape
    pieces = max(1, total_rows // 1024)
    step = width // pieces
    summed = [
        jax.jit(scatter_sum, static_argnums=(1, 2))(part[:, i * step : (i + 1) * step], n_seq, n_exp) for i in range(pieces)
    ]
    summed = summed[0] if pieces == 1 else jnp.concatenate(summed, axis=1)
    return (hid32 + summed).astype(jnp.bfloat16)


def solution(mesh):
    in_specs = (
        P("seq", "exp"),
        P("seq", "exp"),
        P("seq", "exp"),
        P("seq", "exp"),
        P(("seq", "exp"), None),
        P(),
        P(),
        P(("seq", "exp"), None),
        P(("seq", "exp"), None),
        P("exp", "seq", None),
        P("exp", "seq", None),
        P("exp", "seq", None),
    )
    out_specs = P(("seq", "exp"), None)
    return jax.shard_map(body, mesh=mesh, in_specs=in_specs, out_specs=out_specs, check_vma=False)
```

```python
import functools

import jax
import jax.numpy as jnp
from jax import lax
from jax.experimental import pallas as pl
from jax.experimental.pallas import tpu as pltpu
from jax.sharding import PartitionSpec as P

MESH = pl.DeviceIdType.MESH
PARTS = 2


class Place:
    def __init__(self, n_seq, n_exp):
        s, e = lax.axis_index("seq"), lax.axis_index("exp")
        self.fold, self.n_exp = n_exp // 4, n_exp
        self.length = (n_seq // 2) * self.fold
        self.p = (s // 2) * self.fold + e // 4
        self.x, self.y, self.c = s % 2, (e // 2) % 2, e % 2

    def ids(self, p, x, y, c):
        return (p // self.fold) * 2 + x, (p % self.fold) * 4 + y * 2 + c

    def block(self, p, x, y, c):
        s, e = self.ids(p, x, y, c)
        return s * self.n_exp + e

    def dev(self, dp=0, dx=0, dy=0, dc=0):
        x = 1 - self.x if dx else self.x
        y = 1 - self.y if dy else self.y
        c = 1 - self.c if dc else self.c
        return self.ids(self.p + dp, x, y, c)

    def greet(self, *more):
        barrier = pltpu.get_barrier_semaphore()
        for d in (dict(dx=1), dict(dy=1), dict(dc=1), *more):
            pl.semaphore_signal(barrier, inc=1, device_id=self.dev(**d), device_id_type=MESH)

        @pl.when(self.p > 0)
        def _():
            pl.semaphore_signal(barrier, inc=1, device_id=self.dev(dp=-1), device_id_type=MESH)

        @pl.when(self.p < self.length - 1)
        def _():
            pl.semaphore_signal(barrier, inc=1, device_id=self.dev(dp=1), device_id_type=MESH)

        ends = (self.p > 0).astype(jnp.int32) + (self.p < self.length - 1).astype(jnp.int32)
        pl.semaphore_wait(barrier, 3 + len(more) + ends)

    def at(self, stage, sign, k):
        if sign == 0:
            stage(0, 0, 0)
        elif sign < 0:
            pl.when(self.p >= k)(lambda: stage(2 * k - 1, -k, -1))
        else:
            pl.when(self.p + k < self.length)(lambda: stage(2 * k, k, 1))

    def far_first(self, stage):
        def one(i, carry):
            for sign in (1, -1):
                self.at(stage, sign, self.length - 1 - i)
            return carry

        if self.length <= 8:
            for i in range(self.length - 1):
                one(i, 0)
        else:
            lax.fori_loop(0, self.length - 1, one, 0)
        self.at(stage, 0, 0)

    def near_first(self, *stages):
        depth = len(stages)

        def ring(stage, k):
            if isinstance(k, int) and k == 0:
                self.at(stage, 0, 0)
            else:
                for sign in (-1, 1):
                    self.at(stage, sign, k)

        def step(k):
            for j, stage in enumerate(stages):
                if 0 <= k - j < self.length:
                    ring(stage, k - j)

        total = self.length + depth - 1
        if self.length <= 8:
            for k in range(total):
                step(k)
            return
        for k in range(depth):
            step(k)

        def one(k, carry):
            for j, stage in enumerate(stages):
                ring(stage, k - j)
            return carry

        lax.fori_loop(depth, self.length, one, 0)
        for k in range(self.length, total):
            step(k)


def gather_kernel(n_seq, n_exp, x_ref, g_ref, out_ref, gout_ref, send, recv, loc):
    me = Place(n_seq, n_exp)
    rows, width = x_ref.shape
    grow = g_ref.shape[0]
    me.greet()

    def place(ref, off, dx, dy, dc=0):
        x = 1 - me.x if dx else me.x
        y = 1 - me.y if dy else me.y
        c = 1 - me.c if dc else me.c
        b = me.block(me.p + off, x, y, c)
        n = rows if ref is out_ref else grow
        return ref.at[pl.ds(pl.multiple_of(b * n, n), n)]

    def copies(part, kind, slot, off, dx, dy, to, own=False, half=None, dc=0):
        dst_x, dst_g = place(out_ref, off, dx, dy, dc), place(gout_ref, off, dx, dy, dc)
        src_x, src_g = (x_ref, g_ref) if own else (dst_x, dst_g)
        span = width // PARTS
        if half is None:
            cols = pl.ds(part * span, span)
        else:
            cols = pl.ds(part * span + half * (span // 2), span // 2)
        out = [
            pltpu.make_async_remote_copy(
                src_x.at[:, cols],
                dst_x.at[:, cols],
                send.at[kind, slot, part],
                recv.at[kind, slot, part],
                to,
                MESH,
            )
        ]
        if half != 1 and part == 0:
            out.append(
                pltpu.make_async_remote_copy(
                    src_g, dst_g, send.at[kind, slot, PARTS], recv.at[kind, slot, PARTS], to, MESH
                )
            )
        return out

    def start(*a, **k):
        for cp in copies(*a, **k):
            cp.start()

    def wait_recv(*a, **k):
        for cp in copies(*a, **k):
            cp.wait_recv()

    def wait_send(*a, **k):
        for cp in copies(*a, **k):
            cp.wait_send()

    left, right = dict(dp=-1), dict(dp=1)
    X, Y, C = me.dev(dx=1), me.dev(dy=1), me.dev(dc=1)

    def line_sends(off, sign, do):
        own = sign == 0
        if sign <= 0:
            pl.when(me.p + 1 < me.length)(
                lambda: do(0, 2 * (-off + 1) - 1, off, 0, 0, me.dev(**right), own=own)
            )
        if sign >= 0:
            pl.when(me.p > 0)(lambda: do(0, 2 * (off + 1), off, 0, 0, me.dev(**left), own=own))

    def stage_line(slot, off, sign, do):
        own = sign == 0
        line_sends(off, sign, do)
        do(1, slot, off, 0, 0, X, own=own)
        do(2, slot, off, 0, 0, Y, own=own)
        do(5, slot, off, 0, 0, C, own=own)

    def stage_xy_1(slot, off, do):
        do(3, slot, off, 1, 0, Y, half=0)
        do(6, slot, off, 1, 0, C)

    def stage_xy_2(slot, off, do):
        do(4, slot, off, 0, 1, X, half=1)
        do(7, slot, off, 0, 1, C)

    def stage_diag(slot, off, do):
        do(8, slot, off, 1, 1, C)

    local = [
        pltpu.make_async_copy(x_ref, place(out_ref, 0, 0, 0), loc.at[0]),
        pltpu.make_async_copy(g_ref, place(gout_ref, 0, 0, 0), loc.at[1]),
    ]
    for cp in local:
        cp.start()

    def s1(slot, off, sign):
        for part in range(PARTS):
            if sign:
                wait_recv(part, 0, slot, off, 0, 0, X)
            stage_line(slot, off, sign, functools.partial(start, part))

    def s2(slot, off, sign):
        for part in range(PARTS):
            wait_recv(part, 1, slot, off, 1, 0, X)
            stage_xy_1(slot, off, functools.partial(start, part))
            wait_recv(part, 2, slot, off, 0, 1, X)
            stage_xy_2(slot, off, functools.partial(start, part))

    def s3(slot, off, sign):
        for part in range(PARTS):
            wait_recv(part, 3, slot, off, 1, 1, X, half=0)
            wait_recv(part, 4, slot, off, 1, 1, X, half=1)
            stage_diag(slot, off, functools.partial(start, part))

    me.near_first(s1, s2, s3)

    def s4(slot, off, sign):
        for part in range(PARTS):
            done = functools.partial(wait_send, part)
            stage_line(slot, off, sign, done)
            stage_xy_1(slot, off, done)
            stage_xy_2(slot, off, done)
            stage_diag(slot, off, done)
            wait_recv(part, 5, slot, off, 0, 0, X, dc=1)
            wait_recv(part, 6, slot, off, 1, 0, X, dc=1)
            wait_recv(part, 7, slot, off, 0, 1, X, dc=1)
            wait_recv(part, 8, slot, off, 1, 1, X, dc=1)

    me.near_first(s4)
    for cp in local:
        cp.wait()


def gather_all(x, g, n_seq, n_exp):
    n = n_seq * n_exp
    length = n // 8
    anyspace = pl.BlockSpec(memory_space=pl.ANY)
    return pl.pallas_call(
        functools.partial(gather_kernel, n_seq, n_exp),
        out_shape=(
            jax.ShapeDtypeStruct((n * x.shape[0], x.shape[1]), x.dtype),
            jax.ShapeDtypeStruct((n * g.shape[0], g.shape[1]), g.dtype),
        ),
        in_specs=[anyspace, anyspace],
        out_specs=(anyspace, anyspace),
        scratch_shapes=[
            pltpu.SemaphoreType.DMA((9, 2 * length + 1, PARTS + 1)),
            pltpu.SemaphoreType.DMA((9, 2 * length + 1, PARTS + 1)),
            pltpu.SemaphoreType.DMA((2,)),
        ],
        compiler_params=pltpu.CompilerParams(collective_id=1, has_side_effects=True),
    )(x, g)


def scatter_kernel(
    n_seq, n_exp, y_ref, out_ref, acc, sib, xbuf, ybuf, dab, dbb, line, send, recv, loc
):
    me = Place(n_seq, n_exp)
    L = me.length
    rows, width = out_ref.shape
    halfw = width // 2
    me.greet()
    X, Y, C = me.dev(dx=1), me.dev(dy=1), me.dev(dc=1)

    def src(off, grp, dc):
        x = 1 - me.x if grp & 1 else me.x
        y = 1 - me.y if grp & 2 else me.y
        c = 1 - me.c if dc else me.c
        b = me.block(me.p + off, x, y, c)
        return y_ref.at[pl.ds(pl.multiple_of(b * rows, rows), rows)]

    def sib_copy(slot, off, grp):
        return pltpu.make_async_remote_copy(
            src(off, grp, 1), sib.at[grp, slot], send.at[grp, slot], recv.at[grp, slot], C, MESH
        )

    def load(slot, off, grp):
        return pltpu.make_async_copy(src(off, grp, 0), acc.at[grp, slot], loc.at[grp, slot])

    for grp in (3, 1, 2, 0):

        def go(slot, off, sign, grp=grp):
            sib_copy(slot, off, grp).start()
            load(slot, off, grp).start()

        me.far_first(go)

    f32 = jnp.float32

    def pair_sum(slot, off, grp):
        load(slot, off, grp).wait()
        sib_copy(slot, off, grp).wait_recv()
        return acc[grp, slot].astype(f32) + sib[grp, slot].astype(f32)

    def diag_a(slot):
        return pltpu.make_async_remote_copy(
            acc.at[3, slot, :, pl.ds(0, halfw)], dab.at[slot], send.at[4, slot], recv.at[4, slot], Y, MESH
        )

    def diag_b(slot):
        return pltpu.make_async_remote_copy(
            acc.at[3, slot, :, pl.ds(halfw, halfw)], dbb.at[slot], send.at[5, slot], recv.at[5, slot], X, MESH
        )

    def x_copy(slot):
        return pltpu.make_async_remote_copy(
            acc.at[1, slot], xbuf.at[slot], send.at[6, slot], recv.at[6, slot], X, MESH
        )

    def y_copy(slot):
        return pltpu.make_async_remote_copy(
            acc.at[2, slot], ybuf.at[slot], send.at[7, slot], recv.at[7, slot], Y, MESH
        )

    def line_copy(slot, sign):
        return pltpu.make_async_remote_copy(
            acc.at[0, slot],
            line.at[slot],
            send.at[8, slot],
            recv.at[8, slot],
            me.dev(dp=sign),
            MESH,
        )

    def d1(slot, off, sign):
        acc[3, slot] = pair_sum(slot, off, 3).astype(acc.dtype)
        diag_a(slot).start()
        diag_b(slot).start()

    def d2(slot, off, sign):
        sx = pair_sum(slot, off, 1)
        diag_a(slot).wait_recv()
        acc[1, slot, :, pl.ds(0, halfw)] = (sx[:, :halfw] + dab[slot].astype(f32)).astype(acc.dtype)
        acc[1, slot, :, pl.ds(halfw, halfw)] = sx[:, halfw:].astype(acc.dtype)
        x_copy(slot).start()
        sy = pair_sum(slot, off, 2)
        diag_b(slot).wait_recv()
        acc[2, slot, :, pl.ds(0, halfw)] = sy[:, :halfw].astype(acc.dtype)
        acc[2, slot, :, pl.ds(halfw, halfw)] = (sy[:, halfw:] + dbb[slot].astype(f32)).astype(acc.dtype)
        y_copy(slot).start()

    def d3(slot, off, sign):
        total = pair_sum(slot, off, 0)
        x_copy(slot).wait_recv()
        y_copy(slot).wait_recv()
        total = total + xbuf[slot].astype(f32) + ybuf[slot].astype(f32)
        if sign == 0:
            out_ref[...] = total
            if L > 1:

                @pl.when(me.p > 0)
                def _():
                    in_copy(2).wait_recv()
                    out_ref[...] += line[2].astype(f32)

                @pl.when(me.p < L - 1)
                def _():
                    in_copy(1).wait_recv()
                    out_ref[...] += line[1].astype(f32)

            return
        acc[0, slot] = total.astype(acc.dtype)
        far = slot + 2
        behind = me.p > 0 if sign > 0 else me.p < L - 1

        @pl.when(jnp.logical_and(behind, sign * off + 1 < L))
        def _():
            in_copy(far).wait_recv()
            acc[0, slot] = (acc[0, slot].astype(f32) + line[far].astype(f32)).astype(acc.dtype)

        line_copy(slot, sign).start()

    def in_copy(slot):
        return pltpu.make_async_remote_copy(
            acc.at[0, slot], line.at[slot], send.at[8, slot], recv.at[8, slot], X, MESH
        )

    me.far_first(d1)
    me.far_first(d2)
    me.far_first(d3)

    def fin(slot, off, sign):
        for grp in range(4):
            sib_copy(slot, off, grp).wait_send()
        diag_a(slot).wait_send()
        diag_b(slot).wait_send()
        x_copy(slot).wait_send()
        y_copy(slot).wait_send()
        if sign:
            line_copy(slot, sign).wait_send()

    me.far_first(fin)


def scatter_sum(part, n_seq, n_exp):
    n = n_seq * n_exp
    slots = n // 4 - 1 + 2
    rows, width = part.shape[0] // n, part.shape[1]
    bf = jnp.bfloat16
    return pl.pallas_call(
        functools.partial(scatter_kernel, n_seq, n_exp),
        out_shape=jax.ShapeDtypeStruct((rows, width), jnp.float32),
        in_specs=[pl.BlockSpec(memory_space=pl.ANY)],
        out_specs=pl.BlockSpec(memory_space=pltpu.VMEM),
        scratch_shapes=[
            pltpu.VMEM((4, slots, rows, width), bf),
            pltpu.VMEM((4, slots, rows, width), bf),
            pltpu.VMEM((slots, rows, width), bf),
            pltpu.VMEM((slots, rows, width), bf),
            pltpu.VMEM((slots, rows, width // 2), bf),
            pltpu.VMEM((slots, rows, width // 2), bf),
            pltpu.VMEM((slots, rows, width), bf),
            pltpu.SemaphoreType.DMA((9, slots)),
            pltpu.SemaphoreType.DMA((9, slots)),
            pltpu.SemaphoreType.DMA((4, slots)),
        ],
        compiler_params=pltpu.CompilerParams(
            collective_id=2, has_side_effects=True, vmem_limit_bytes=60 * 2**20
        ),
    )(part)


GPARTS = 4
HPARTS = 4
PLANES = 4
MPARTS = 4


def plane_orders(length):
    def depth(q):
        return min(q, length - 1 - q)

    visit = []
    for p in range(length):
        rest = [q for q in range(length) if q != p]
        near = min(rest, key=lambda q: (abs(q - p), depth(q)), default=p)
        rest = sorted((q for q in rest if q != near), key=lambda q: (depth(q), abs(q - p)))
        visit.append([p] + [near] * (length > 1) + rest)
    lines = []
    for p in range(length):
        def ready(q):
            chain = range(0, p + 1) if q > p else range(p, length)
            return max(visit[b].index(q) for b in chain)

        low = 2 * p < length
        lines.append(sorted((q for q in range(length) if q != p), key=lambda q: (ready(q), -q if low else q)))
    return visit, lines


def pick(table, p, j):
    total = 0
    for a, row in enumerate(table):
        for b, v in enumerate(row):
            hit = jnp.logical_and(p == a, j == b).astype(jnp.int32)
            total = total + hit * v
    return total


def spans(tiles, parts):
    cuts = [(tiles * i // parts) * 128 for i in range(parts + 1)]
    return [pl.ds(a, b - a) for a, b in zip(cuts[:-1], cuts[1:])]


def when(cond, fn):
    def run():
        fn()

    pl.when(cond)(run)


def attend_tokens(
    me, q_ref, k_ref, v_ref, ld_ref, res_ref, ag_ref, mg_ref, ids_ref, gw_ref, x_out,
    hid, work, flat, own16, peer, cin, cout, tots, tok, psend, precv, tsem, msend, mrecv,
):
    L, z = me.length, me.p
    f32, bf = jnp.float32, jnp.bfloat16
    heads, block = ld_ref.shape
    dim = q_ref.shape[1] // heads
    rows = res_ref.shape[0]
    n_exp, width = tok.shape[0], tok.shape[2]
    e = lax.axis_index("exp")
    pair = me.dev(dx=1)

    def head(h):
        return pl.ds(h * dim, dim)

    def pair_copy(h):
        return pltpu.make_async_remote_copy(
            own16.at[h], peer.at[h], psend.at[0], precv.at[0, h], pair, MESH
        )

    def line_copy(h):
        return pltpu.make_async_remote_copy(
            cout.at[h], cin.at[h], psend.at[1], precv.at[1, h], me.dev(dp=1), MESH
        )

    tot_copy = pltpu.make_async_remote_copy(tots.at[0], tots.at[1], tsem.at[0], tsem.at[1], pair, MESH)

    nt = (((1,), (1,)), ((), ()))
    tn = (((0,), (0,)), ((), ()))
    r = lax.broadcasted_iota(jnp.int32, (block, block), 0)
    c = lax.broadcasted_iota(jnp.int32, (block, block), 1)
    seen = r >= c
    decay = ld_ref[...]
    high = lax.Precision.HIGHEST
    cum = lax.dot_general(seen.astype(f32), decay, nt, precision=high, preferred_element_type=f32)
    cum_t = jnp.dot(decay, (r <= c).astype(f32), precision=high, preferred_element_type=f32)
    total = cum_t[:, block - 1 :]
    tots[0, 0:heads, :] = jnp.broadcast_to(total, (heads, dim))

    def state(h):
        kw = (k_ref[:, head(h)].astype(f32) * jnp.exp(total[h : h + 1] - cum[:, h : h + 1])).astype(bf)
        own = lax.dot_general(kw, v_ref[:, head(h)], tn, preferred_element_type=f32)
        work[:, pl.ds((heads + h) * dim, dim)] = own
        own16[h] = own.astype(bf)

    for h in range(heads):
        state(h)
    me.greet(dict(dy=1, dc=1))
    tot_copy.start()
    for h in range(heads):
        pair_copy(h).start()

    @pl.when(z == 0)
    def _():
        cin[...] = jnp.zeros_like(cin)

    def f_intra(h):
        scores = lax.dot_general(q_ref[:, head(h)], k_ref[:, head(h)], nt, preferred_element_type=f32)
        gap = cum[:, h : h + 1] - cum_t[h : h + 1, :]
        weights = jnp.where(seen, scores * jnp.exp(jnp.where(seen, gap, 0.0)), 0.0).astype(bf)
        work[:, head(h)] = jnp.dot(weights, v_ref[:, head(h)], preferred_element_type=f32)

    for h in range(heads):
        f_intra(h)
    tot_copy.wait_recv()
    mine, other = tots[0, 0:heads, :], tots[1, 0:heads, :]
    both = jnp.exp(mine + other)
    is_odd = jnp.full(mine.shape, me.x, jnp.int32) == 1
    one = jnp.ones_like(mine)
    own_by = jnp.where(is_odd, one, jnp.exp(other))
    peer_by = jnp.where(is_odd, jnp.exp(mine), one)
    carry_by = jnp.where(is_odd, jnp.exp(other), one)
    peer_in = jnp.where(is_odd, one, jnp.zeros_like(mine))

    peers = (dict(dc=1), dict(dy=1), dict(dy=1, dc=1))
    pieces = MPARTS
    span = width // pieces

    def mix_copy(k, i):
        to = me.dev(**peers[k])
        cols = pl.ds(i * span, span)
        src = flat.at[pl.ds(pl.multiple_of(to[1] * rows, rows), rows), cols]
        return pltpu.make_async_remote_copy(
            src, tok.at[e, :, cols], msend.at[0], mrecv.at[k], to, MESH
        )

    def mix_in(k):
        to = me.dev(**peers[k])
        return pltpu.make_async_remote_copy(
            tok.at[to[1]], tok.at[to[1]], msend.at[0], mrecv.at[k], to, MESH
        )

    def f_chain(h):
        pair_copy(h).wait_recv()
        pl.when(z > 0)(lambda: line_copy(h).wait_recv())
        near = peer[h].astype(f32)
        come = cin[h].astype(f32)
        row = slice(h, h + 1)

        @pl.when(z < L - 1)
        def _():
            mix = both[row] * come + own_by[row] * work[:, pl.ds((heads + h) * dim, dim)] + peer_by[row] * near
            cout[h] = mix.astype(bf)
            line_copy(h).start()

    def f_head(h):
        near = peer[h].astype(f32)
        come = cin[h].astype(f32)
        row = slice(h, h + 1)
        carried = carry_by[row] * come + peer_in[row] * near
        coarse = carried.astype(bf)
        fine = (carried - coarse.astype(f32)).astype(bf)
        query = q_ref[:, head(h)]
        inter = jnp.dot(query, coarse, preferred_element_type=f32) + jnp.dot(
            query, fine, preferred_element_type=f32
        )
        attn = work[:, head(h)] + jnp.exp(cum[:, h : h + 1]) * inter
        scale = lax.rsqrt(jnp.mean(attn * attn, axis=-1, keepdims=True) + 1e-06)
        flat[0:block, head(h)] = (attn * scale).astype(bf)
        if (h + 1) * pieces % heads == 0:
            for k in range(len(peers)):
                mix_copy(k, (h + 1) * pieces // heads - 1).start()

    for h in range(heads):
        f_chain(h)
        f_head(h)

    tok[e] = flat[pl.ds(pl.multiple_of(e * rows, rows), rows), 0:width]

    def f_mix():
        for k in range(len(peers)):
            mix_in(k).wait_recv()

    f_mix()
    square = jnp.zeros((rows, 1), f32)
    for j in range(n_exp):
        cols = pl.ds(j * width, width)
        value = (res_ref[:, cols].astype(f32) + tok[j].astype(f32) * ag_ref[:, cols]).astype(bf)
        hid[:, cols] = value
        wide = value.astype(f32)
        square = square + jnp.sum(wide * wide, axis=1, keepdims=True)
    scale = lax.rsqrt(square / (n_exp * width) + 1e-06)
    for j in range(n_exp):
        cols = pl.ds(j * width, width)
        x_out[:, cols] = (hid[:, cols].astype(f32) * scale * mg_ref[:, cols]).astype(bf)

    def column(ref):
        same = lax.broadcasted_iota(jnp.int32, (rows, rows), 0) == lax.broadcasted_iota(jnp.int32, (rows, rows), 1)
        return lax.dot_general(
            same.astype(f32), ref[...].astype(f32), nt, precision=high, preferred_element_type=f32
        )

    ids, gates = column(ids_ref).astype(jnp.int32), column(gw_ref)
    coarse = gates.astype(bf).astype(f32)
    rest = gates - coarse
    lane = lax.broadcasted_iota(jnp.int32, (rows, 128), 1)
    extra = jnp.zeros((rows, 128), f32)
    for i in range(ids_ref.shape[0]):
        who = ids[:, i : i + 1]
        extra = jnp.where(lane == who, coarse[:, i : i + 1], extra)
        extra = jnp.where(lane == who + 64, rest[:, i : i + 1], extra)
    x_out[:, n_exp * width :] = extra.astype(bf)

    def finish():
        def out(ref, sent):
            pltpu.make_async_remote_copy(ref, ref, sent, sent, pair, MESH).wait_send()

        tot_copy.wait_send()
        out(own16, psend.at[0])
        pl.when(z < L - 1)(lambda: out(cout, psend.at[1]))
        out(tok.at[pl.ds(0, len(peers))], msend.at[0])

    return finish


def moe_kernel(
    n_seq, n_exp, q_ref, k_ref, v_ref, ld_ref, res_ref, ag_ref, mg_ref, ids_ref, gw_ref,
    wg_ref, wu_ref, wd_ref, out_ref,
    xs, ys, act, sib, din, near_in, lin, tot, wg, wu, wd, hid_ref,
    own16, peer, cin, cout, tots, tok,
    gsend, lsend, grecv, drecv, crecv, brecv, ssend, srecv, nrecv, drecv2, loc, psend, precv, tsem, msend, mrecv,
):
    me = Place(n_seq, n_exp)
    L, p = me.length, me.p
    rows, width = out_ref.shape
    hidden = wg.shape[0]
    many = 8 * rows
    f32, bf = jnp.float32, jnp.bfloat16
    X, Y, C = me.dev(dx=1), me.dev(dy=1), me.dev(dc=1)
    visit, lines = plane_orders(L)
    gcols = spans(xs.shape[1] // 128, GPARTS)
    hcols, dcols = spans(width // 128, HPARTS), spans(width // 128, 2 * HPARTS)

    loads = [
        pltpu.make_async_copy(a.at[0], b, loc.at[i])
        for i, (a, b) in enumerate(((wg_ref, wg), (wu_ref, wu), (wd_ref, wd)))
    ]
    for cp in loads:
        cp.start()

    def flip(v, d):
        return 1 - v if d else v

    def row(q, dx=0, dy=0, dc=0):
        k = (flip(me.c, dc) * 2 + flip(me.x, dx)) * 2 + flip(me.y, dy)
        return pl.ds(pl.multiple_of((q * 8 + k) * rows, rows), rows)

    def srow(q, dx=0, dy=0):
        k = flip(me.x, dx) * 2 + flip(me.y, dy)
        return pl.ds(pl.multiple_of((q * 4 + k) * rows, rows), rows)

    def prow(q):
        return pl.ds(pl.multiple_of(q * rows, rows), rows)

    cut = gcols[GPARTS // 2].start
    halves = (pl.ds(0, cut), pl.ds(cut, xs.shape[1] - cut))
    middle = pl.ds(gcols[1].start, gcols[-1].start - gcols[1].start)
    lower, higher, both = (0,), (1,), (0, 1)

    def gcopy(q, cols, r, to, sent, got):
        ref = xs.at[r, cols]
        return pltpu.make_async_remote_copy(ref, ref, sent, got, to, MESH)

    def arrive(q, cols, r, got):
        gcopy(q, cols, r, X, gsend.at[0], got).wait_recv()

    def bulk(ref, sent):
        return pltpu.make_async_remote_copy(ref, ref, sent, sent, X, MESH)

    def to_sibling(q, cols, r):
        gcopy(q, cols, r, C, gsend.at[0], crecv.at[q]).start()

    def both_ways(q, cols, r, lane, got):
        pl.when(jnp.logical_and(q >= p, p > 0))(
            lambda: gcopy(q, cols, r, me.dev(dp=-1), lsend.at[lane, q], got).start()
        )
        pl.when(jnp.logical_and(q <= p, p + 1 < L))(
            lambda: gcopy(q, cols, r, me.dev(dp=1), lsend.at[lane + 1, q], got).start()
        )

    def line_pair(q, side):
        both_ways(q, halves[side], row(q), 0, grecv.at[2, q, side])

    def corner_out(q):
        both_ways(q, middle, row(q, 1, 1), 2, drecv.at[q, 2])

    def g_first(q, turn, own=False):
        sent = gsend.at[5 + turn] if own else gsend.at[1]
        gcopy(q, halves[turn], row(q), X, sent, grecv.at[0, q, turn]).start()
        gcopy(q, halves[1 - turn], row(q), Y, gsend.at[2], grecv.at[1, q, 1 - turn]).start()
        if turn == 0:
            to_sibling(q, pl.ds(0, xs.shape[1]), row(q))

    def g_own(q):
        line_pair(q, 0)
        g_first(q, 0, True)
        bulk(xs.at[row(q), halves[0]], gsend.at[5]).wait_send()
        line_pair(q, 1)
        g_first(q, 1, True)

    def from_x(q, side, own):
        r = row(q, 1, 0)
        arrive(q, halves[side], r, grecv.at[0, q, side])
        if side == 0:
            cols, sent = (halves[0], gsend.at[7]) if own else (gcols[0], gsend.at[3])
            gcopy(q, cols, r, Y, sent, drecv.at[q, 0]).start()
        to_sibling(q, halves[side], r)

    def from_y(q, side, own):
        r = row(q, 0, 1)
        arrive(q, halves[side], r, grecv.at[1, q, side])
        if side == 1:
            cols, sent = (halves[1], gsend.at[8]) if own else (gcols[-1], gsend.at[4])
            gcopy(q, cols, r, X, sent, drecv.at[q, 1]).start()
        to_sibling(q, halves[side], r)

    def g_second(q, own=False):
        from_x(q, 0, own)
        from_y(q, 1, own)

    def g_rest(q, own=False):
        from_x(q, 1, own)
        from_y(q, 0, own)

    def g_third(q, own=False):
        r = row(q, 1, 1)
        for k, cols in enumerate(halves if own else (gcols[0], gcols[-1])):
            arrive(q, cols, r, drecv.at[q, k])
            to_sibling(q, cols, r)
        if own:
            corner_out(q)

    def g_corner(k):
        for sign in (-1, 1):
            q = p + sign * k

            def pass_on():
                arrive(q, middle, row(q, 1, 1), drecv.at[q, 2])
                corner_out(q)
                to_sibling(q, middle, row(q, 1, 1))

            when(jnp.logical_and(q >= 0, q < L), pass_on)

    def g_ring(k, sides):
        for sign in (-1, 1):
            q = p + sign * k

            def pass_on():
                for side in sides:
                    arrive(q, halves[side], row(q), grecv.at[2, q, side])
                    line_pair(q, side)

            when(jnp.logical_and(q >= 0, q < L), pass_on)

    def g_done(q):
        r = pl.ds(pl.multiple_of((q * 2 + 1 - me.c) * 4 * rows, 4 * rows), 4 * rows)
        pltpu.make_async_remote_copy(xs.at[r], xs.at[r], gsend.at[0], crecv.at[q], X, MESH).wait_recv()

    def g_drain():
        bulk(xs.at[pl.ds(0, L * 4 * rows)], gsend.at[0]).wait_send()
        bulk(xs.at[pl.ds(0, (L - 1) * rows)], gsend.at[1]).wait_send()
        bulk(xs.at[pl.ds(0, L * rows)], gsend.at[2]).wait_send()
        bulk(xs.at[pl.ds(0, (L - 1) * rows), gcols[0]], gsend.at[3]).wait_send()
        bulk(xs.at[pl.ds(0, (L - 1) * rows), gcols[-1]], gsend.at[4]).wait_send()
        bulk(xs.at[row(p), halves[0]], gsend.at[7]).wait_send()
        bulk(xs.at[row(p), halves[1]], gsend.at[8]).wait_send()
        bulk(xs.at[row(p), halves[1]], gsend.at[6]).wait_send()
        for q in range(L):
            pl.when(jnp.logical_and(q >= p, p > 0))(lambda: bulk(xs.at[row(q)], lsend.at[0, q]).wait_send())
            pl.when(jnp.logical_and(q <= p, p + 1 < L))(lambda: bulk(xs.at[row(q)], lsend.at[1, q]).wait_send())
            mid = xs.at[row(q), middle]
            pl.when(jnp.logical_and(q >= p, p > 0))(lambda: bulk(mid, lsend.at[2, q]).wait_send())
            pl.when(jnp.logical_and(q <= p, p + 1 < L))(lambda: bulk(mid, lsend.at[3, q]).wait_send())

    def sib_copy(q, h):
        r = pl.ds(pl.multiple_of((q * 2 + 1 - me.c) * 4 * rows, 4 * rows), 4 * rows)
        d = pl.ds(pl.multiple_of(q * 4 * rows, 4 * rows), 4 * rows)
        return pltpu.make_async_remote_copy(
            ys.at[r, hcols[h]], sib.at[d, hcols[h]], ssend.at[4], brecv.at[q, h], C, MESH
        )

    def plane_copy(side, q, h, r, to):
        return pltpu.make_async_remote_copy(
            ys.at[r, hcols[h]], near_in.at[prow(2 * q + side), hcols[h]], ssend.at[1 + side], nrecv.at[q, h], to, MESH
        )

    def settled(ref, got):
        pltpu.make_async_remote_copy(ref, ref, ssend.at[0], got, X, MESH).wait_recv()

    def diag_copy(q, h, side):
        cols = dcols[2 * h + side]
        return pltpu.make_async_remote_copy(
            ys.at[row(q, 1, 1), cols], din.at[prow(q), cols], ssend.at[0], drecv2.at[q, h], (Y, X)[side], MESH
        )

    def x_copy(q, h):
        return plane_copy(0, q, h, row(q, 1, 0), X)

    def y_copy(q, h):
        return plane_copy(1, q, h, row(q, 0, 1), Y)

    def line_copy(q, h):
        up = (q > p).astype(jnp.int32)
        last = jnp.logical_and(q < p, q == p - 1).astype(jnp.int32)
        slot = q + (L - q) * last
        return pltpu.make_async_remote_copy(
            ys.at[row(q), hcols[h]],
            lin.at[prow(slot), hcols[h]],
            ssend.at[3],
            srecv.at[slot, h],
            me.dev(dp=2 * up - 1),
            MESH,
        )

    def line_in(slot, h):
        return pltpu.make_async_remote_copy(
            ys.at[row(p), hcols[h]], lin.at[prow(slot), hcols[h]], ssend.at[3], srecv.at[slot, h], X, MESH
        )

    def pair(q, h, dx, dy):
        return ys[row(q, dx, dy), hcols[h]].astype(f32) + sib[srow(q, dx, dy), hcols[h]].astype(f32)

    def r_first(q, h):
        sib_copy(q, h).wait_recv()
        ys[row(q, 1, 1), hcols[h]] = pair(q, h, 1, 1).astype(bf)
        for side in range(2):
            diag_copy(q, h, side).start()

    def r_second(q, h):
        sx, sy = pair(q, h, 1, 0), pair(q, h, 0, 1)
        near, far = dcols[2 * h], dcols[2 * h + 1]
        settled(din.at[prow(q), hcols[h]], drecv2.at[q, h])
        ys[row(q, 1, 0), near] = (sx[:, : near.size] + din[prow(q), near].astype(f32)).astype(bf)
        ys[row(q, 1, 0), far] = sx[:, near.size :].astype(bf)
        x_copy(q, h).start()
        ys[row(q, 0, 1), near] = sy[:, : near.size].astype(bf)
        ys[row(q, 0, 1), far] = (sy[:, near.size :] + din[prow(q), far].astype(f32)).astype(bf)
        y_copy(q, h).start()

    def r_third(q, h):
        total = pair(q, h, 0, 0)
        settled(near_in.at[pl.ds(pl.multiple_of(2 * q * rows, rows), 2 * rows), hcols[h]], nrecv.at[q, h])
        for side in range(2):
            total = total + near_in[prow(2 * q + side), hcols[h]].astype(f32)
        tot[prow(q), hcols[h]] = total

    def r_line(q, h):
        behind = jnp.logical_or(jnp.logical_and(q > p, p > 0), jnp.logical_and(q < p, p < L - 1))

        @pl.when(behind)
        def _():
            line_in(q, h).wait_recv()
            ys[row(q), hcols[h]] = (tot[prow(q), hcols[h]] + lin[prow(q), hcols[h]].astype(f32)).astype(bf)

        @pl.when(jnp.logical_not(behind))
        def _():
            ys[row(q), hcols[h]] = tot[prow(q), hcols[h]].astype(bf)

        line_copy(q, h).start()

    def r_last(h):
        cols = hcols[h]

        @pl.when(p > 0)
        def _():
            line_in(p, h).wait_recv()
            tot[prow(p), cols] += lin[prow(p), cols].astype(f32)

        @pl.when(p < L - 1)
        def _():
            line_in(L, h).wait_recv()
            tot[prow(p), cols] += lin[prow(L), cols].astype(f32)

        out_ref[:, cols] = (hid_ref[:, cols].astype(f32) + tot[prow(p), cols]).astype(bf)

    at_end = jnp.logical_or(p == 0, p == L - 1)
    inner = jnp.logical_not(at_end)

    def r_early(q, h):
        pl.when(jnp.logical_and(at_end, q != p))(lambda: r_line(q, h))

    def r_drain():
        bulk(sib, ssend.at[4]).wait_send()
        for kind in range(3):
            bulk(din, ssend.at[kind]).wait_send()

    tile = next(t for t in range(512, 0, -128) if hidden % t == 0)
    fsteps = hidden // tile

    def block_of(q):
        return pl.ds(pl.multiple_of(q * many, many), many)

    def gate_of(q):
        extra = xs[block_of(q), width : width + 128].astype(f32)
        lane = lax.broadcasted_iota(jnp.int32, extra.shape, 1)
        e = lax.axis_index("exp")
        keep = jnp.logical_or(lane == e, lane == e + 64)
        return jnp.sum(jnp.where(keep, extra, 0.0), axis=1, keepdims=True)

    nt = (((1,), (1,)), ((), ()))

    def ffn_in(q, f):
        fc = pl.ds(f * tile, tile)
        rows_in = xs[block_of(q), 0:width]
        gate = lax.dot_general(rows_in, wg[fc, :], nt, preferred_element_type=f32)
        up = lax.dot_general(rows_in, wu[fc, :], nt, preferred_element_type=f32)
        act[:, fc] = (gate / (1.0 + jnp.exp(-gate)) * up * gate_of(q)).astype(bf)

    def ffn_out(q, h):
        ys[block_of(q), hcols[h]] = jnp.dot(
            act[...], wd[:, hcols[h]], preferred_element_type=f32
        ).astype(bf)
        sib_copy(q, h).start()

    front_done = attend_tokens(
        me, q_ref, k_ref, v_ref, ld_ref, res_ref, ag_ref, mg_ref, ids_ref, gw_ref, xs.at[row(p)],
        hid_ref, tot, act, own16, peer, cin, cout, tots, tok, psend, precv, tsem, msend, mrecv,
    )
    second = pick(visit, p, 1)
    g_own(p)
    g_second(p, True)
    g_ring(1, lower)
    g_rest(p, True)
    g_ring(1, higher)
    g_first(second, 0)
    g_third(p, True)
    g_first(second, 1)
    front_done()
    for cp in loads:
        cp.wait()

    def chunk(j, carry):
        q, nxt, prev = pick(visit, p, j), pick(visit, p, j + 1), pick(visit, p, j - 1)
        older = pick(visit, p, j - 2)
        third, fourth = pick(visit, p, 2), pick(visit, p, 3)

        def opening(*fns):
            when(j == 0, lambda: [fn() for fn in fns])

        def closing(*fns):
            when(j == L - 1, lambda: [fn() for fn in fns])

        def ahead(*fns):
            when(jnp.logical_and(j > 0, j + 1 < L), lambda: [fn() for fn in fns])

        def after(*fns):
            when(j > 0, lambda: [fn() for fn in fns])

        def later(*fns):
            when(j > 1, lambda: [fn() for fn in fns])

        def settle(at, h):
            r_third(at, h)
            r_early(at, h)

        def hook(n):
            if n == 0:
                after(lambda: r_first(prev, 2), lambda: r_first(prev, 3))
                opening(
                    lambda: g_ring(2, lower),
                    lambda: g_second(nxt),
                    lambda: g_ring(2, higher),
                    lambda: g_first(fourth, 0),
                )
            if n == 1:
                opening(lambda: g_rest(nxt), lambda: g_first(fourth, 1))
                when(j == 1, lambda: g_corner(3))
                ahead(lambda: g_second(nxt))
                later(lambda: settle(older, 0), lambda: settle(older, 1))
                after(lambda: r_second(prev, 0), lambda: r_second(prev, 1))
            if n == 2:
                opening(lambda: g_corner(1))
                ahead(lambda: g_rest(nxt))
                later(lambda: settle(older, 2), lambda: settle(older, 3))
                closing(lambda: r_second(prev, 2))

        g_done(q)
        for f in range(fsteps):
            ffn_in(q, f)
            hook(f)
        for f in range(fsteps, 3):
            hook(f)
        for h in range(HPARTS):
            ffn_out(q, h)
            if h == 0:
                ahead(lambda: r_second(prev, 2))
                closing(lambda: r_second(prev, 3))
            if h == 1:
                ahead(lambda: r_second(prev, 3))
                opening(lambda: g_ring(3, both), lambda: g_first(third, 0))
                closing(lambda: settle(prev, 0))
            if h == 2:
                r_first(q, 0)
                ahead(lambda: g_third(nxt))
                opening(lambda: g_third(nxt))
                closing(lambda: settle(prev, 1))
            if h == 3:
                r_first(q, 1)
                opening(lambda: g_first(third, 1), lambda: g_corner(2))
        return carry

    def one_line(i, h):
        when(inner, lambda: r_line(pick(lines, p, i), h))

    lax.fori_loop(0, L, chunk, 0)

    final, prior = pick(visit, p, L - 1), pick(visit, p, L - 2)
    for h in (2, 3):
        r_third(prior, h)
        r_early(prior, h)
    for h in (2, 3):
        r_first(final, h)
    for h in range(HPARTS):
        r_second(final, h)
        if h:
            one_line(0, h - 1)
    one_line(0, HPARTS - 1)
    for h in range(HPARTS):
        one_line(1, h)
        r_third(final, h)
        r_early(final, h)
    g_drain()
    for h in range(HPARTS):
        one_line(2, h)
        if h:
            r_last(h - 1)
    r_drain()
    r_last(HPARTS - 1)
    bulk(lin.at[pl.ds(0, (L - 1) * rows)], ssend.at[3]).wait_send()


def moe_scratch(n_seq, n_exp, x_shape, w_shape):
    n, L = n_seq * n_exp, n_seq * n_exp // 8
    rows, wide = x_shape
    hidden, width = w_shape[1:]
    bf, f32 = jnp.bfloat16, jnp.float32
    return [
        ((n * rows, wide), bf),
        ((n * rows, width), bf),
        ((8 * rows, hidden), bf),
        ((n // 2 * rows, width), bf),
        ((L * rows, width), bf),
        ((2 * L * rows, width), bf),
        ((L * rows + rows, width), bf),
        ((L * rows, width), f32),
        ((hidden, width), bf),
        ((hidden, width), bf),
        ((hidden, width), bf),
    ]


MOE_VMEM = 61 * 2**20


def moe_fits(n_seq, n_exp, rows, width, w_shape):
    need = sum(
        a * b * jnp.dtype(t).itemsize for (a, b), t in moe_scratch(n_seq, n_exp, (rows, width + 128), w_shape)
    )
    return (
        w_shape[0] == 1
        and n_exp // 4 == 1
        and n_seq * n_exp == 8 * PLANES
        and w_shape[1] % 128 == 0
        and w_shape[2] % (256 * HPARTS) == 0
        and w_shape[2] // n_exp % (128 * MPARTS) == 0
        and need + 6 * 2**20 <= MOE_VMEM
    )


def whole_layer(
    queries, keys, values, log_decay, residual, attn_gain, moe_gain, expert_ids, gate_weights,
    w_gate, w_up, w_down, n_seq, n_exp,
):
    L = n_seq * n_exp // 8
    heads = log_decay.shape[1]
    part = queries.shape[1]
    dim = part // heads
    rows, width = residual.shape
    vmem = pl.BlockSpec(memory_space=pltpu.VMEM)
    anyspace = pl.BlockSpec(memory_space=pl.ANY)
    dma = pltpu.SemaphoreType.DMA
    bf = jnp.bfloat16
    states = pltpu.VMEM((heads, dim, dim), bf)
    scratch = moe_scratch(n_seq, n_exp, (rows, width + 128), w_gate.shape)
    return pl.pallas_call(
        functools.partial(moe_kernel, n_seq, n_exp),
        out_shape=jax.ShapeDtypeStruct(residual.shape, bf),
        in_specs=[vmem] * 9 + [anyspace] * 3,
        out_specs=vmem,
        scratch_shapes=[pltpu.VMEM(s, t) for s, t in scratch]
        + [
            pltpu.VMEM(residual.shape, bf),
            states,
            states,
            states,
            states,
            pltpu.VMEM((2, heads + -heads % 8, dim), jnp.float32),
            pltpu.VMEM((n_exp, rows, part), bf),
            dma((9,)),
            dma((4, L)),
            dma((3, L, 2)),
            dma((L, 3)),
            dma((L,)),
            dma((L, HPARTS)),
            dma((5,)),
            dma((L + 1, HPARTS)),
            dma((L, HPARTS)),
            dma((L, HPARTS)),
            dma((3,)),
            dma((2,)),
            dma((2, heads)),
            dma((2,)),
            dma((1,)),
            dma((3,)),
        ],
        compiler_params=pltpu.CompilerParams(
            collective_id=5, has_side_effects=True, vmem_limit_bytes=MOE_VMEM
        ),
    )(
        queries, keys, values, log_decay.T, residual, attn_gain[None, :], moe_gain[None, :],
        expert_ids.T, gate_weights.T, w_gate, w_up, w_down,
    )


def carry_kernel(n_seq, own_ref, own16_ref, tot_ref, out_ref, peer, ptot, cin, cout, send, recv, tsem):
    s, e = lax.axis_index("seq"), lax.axis_index("exp")
    z, odd, deep = s // 2, s % 2, n_seq // 2
    heads = own_ref.shape[0]
    pair = (z * 2 + 1 - odd, e)

    barrier = pltpu.get_barrier_semaphore()
    pl.semaphore_signal(barrier, inc=1, device_id=pair, device_id_type=MESH)

    @pl.when(z > 0)
    def _():
        pl.semaphore_signal(barrier, inc=1, device_id=(s - 2, e), device_id_type=MESH)

    @pl.when(z < deep - 1)
    def _():
        pl.semaphore_signal(barrier, inc=1, device_id=(s + 2, e), device_id_type=MESH)

    ends = (z > 0).astype(jnp.int32) + (z < deep - 1).astype(jnp.int32)
    pl.semaphore_wait(barrier, 1 + ends)

    tot_copy = pltpu.make_async_remote_copy(tot_ref, ptot, tsem.at[0], tsem.at[1], pair, MESH)

    def pair_copy(h):
        return pltpu.make_async_remote_copy(
            own16_ref.at[h], peer.at[h], send.at[0, h], recv.at[0, h], pair, MESH
        )

    def line_copy(h):
        return pltpu.make_async_remote_copy(
            cout.at[h], cin.at[h], send.at[1, h], recv.at[1, h], (s + 2, e), MESH
        )

    tot_copy.start()
    for h in range(heads):
        pair_copy(h).start()

    @pl.when(z == 0)
    def _():
        cin[...] = jnp.zeros_like(cin)

    tot_copy.wait_recv()
    mine, other = tot_ref[...], ptot[...]
    both = jnp.exp(mine + other)
    is_odd = jnp.full(mine.shape, odd, jnp.int32) == 1
    one = jnp.ones_like(mine)
    own_by = jnp.where(is_odd, one, jnp.exp(other))
    peer_by = jnp.where(is_odd, jnp.exp(mine), one)
    carry_by = jnp.where(is_odd, jnp.exp(other), one)
    peer_in = jnp.where(is_odd, one, jnp.zeros_like(mine))
    for h in range(heads):
        pair_copy(h).wait_recv()

        @pl.when(z > 0)
        def _():
            line_copy(h).wait_recv()

        near = peer[h].astype(jnp.float32)
        come = cin[h].astype(jnp.float32)

        @pl.when(z < deep - 1)
        def _():
            cout[h] = (
                both[h : h + 1] * come + own_by[h : h + 1] * own_ref[h] + peer_by[h : h + 1] * near
            ).astype(cout.dtype)
            line_copy(h).start()

        out_ref[h] = carry_by[h : h + 1] * come + peer_in[h : h + 1] * near

    tot_copy.wait_send()
    for h in range(heads):
        pair_copy(h).wait_send()

        @pl.when(z < deep - 1)
        def _():
            line_copy(h).wait_send()


def carried_in(block_total, block_state, n_seq):
    heads, dim, _ = block_state.shape
    bf = jnp.bfloat16
    tile = jnp.pad(block_total, (0, -heads % 8))
    tile = jnp.broadcast_to(tile[:, None], (tile.shape[0], dim))
    vmem = pl.BlockSpec(memory_space=pltpu.VMEM)
    return pl.pallas_call(
        functools.partial(carry_kernel, n_seq),
        out_shape=jax.ShapeDtypeStruct(block_state.shape, jnp.float32),
        in_specs=[vmem] * 3,
        out_specs=vmem,
        scratch_shapes=[
            pltpu.VMEM(block_state.shape, bf),
            pltpu.VMEM(tile.shape, jnp.float32),
            pltpu.VMEM(block_state.shape, bf),
            pltpu.VMEM(block_state.shape, bf),
            pltpu.SemaphoreType.DMA((2, heads)),
            pltpu.SemaphoreType.DMA((2, heads)),
            pltpu.SemaphoreType.DMA((2,)),
        ],
        compiler_params=pltpu.CompilerParams(collective_id=3, has_side_effects=True),
    )(block_state, block_state.astype(bf), tile)


def mix_kernel(n_exp, normed_ref, res_ref, again_ref, mgain_ref, hid_ref, in_ref, tok, send, recv, loc):
    s, e = lax.axis_index("seq"), lax.axis_index("exp")
    rows, width = res_ref.shape[0], normed_ref.shape[1]

    barrier = pltpu.get_barrier_semaphore()
    for k in range(1, n_exp):
        pl.semaphore_signal(
            barrier, inc=1, device_id=(s, lax.rem(e + k, n_exp)), device_id_type=MESH
        )
    pl.semaphore_wait(barrier, n_exp - 1)

    def source(peer):
        return normed_ref.at[pl.ds(pl.multiple_of(peer * rows, rows), rows)]

    own = pltpu.make_async_copy(source(e), tok.at[e], loc.at[0])

    def copy(k):
        peer = lax.rem(e + k, n_exp)
        return pltpu.make_async_remote_copy(
            source(peer), tok.at[e], send.at[k], recv.at[k], (s, peer), MESH
        )

    def arriving(k):
        sender = lax.rem(e + n_exp - k, n_exp)
        return pltpu.make_async_remote_copy(
            source(e), tok.at[sender], send.at[k], recv.at[k], (s, sender), MESH
        )

    for k in range(1, n_exp):
        copy(k).start()
    own.start()
    own.wait()
    for k in range(1, n_exp):
        arriving(k).wait_recv()
    square = jnp.zeros((rows, 1), jnp.float32)
    for j in range(n_exp):
        cols = pl.ds(j * width, width)
        hid = (
            res_ref[:, cols].astype(jnp.float32)
            + tok[j].astype(jnp.float32) * again_ref[:, cols]
        ).astype(jnp.bfloat16)
        hid_ref[:, cols] = hid
        wide = hid.astype(jnp.float32)
        square = square + jnp.sum(wide * wide, axis=1, keepdims=True)
    scale = lax.rsqrt(square / (n_exp * width) + 1e-06)
    for j in range(n_exp):
        cols = pl.ds(j * width, width)
        in_ref[:, cols] = (
            hid_ref[:, cols].astype(jnp.float32) * scale * mgain_ref[:, cols]
        ).astype(jnp.bfloat16)
    for k in range(1, n_exp):
        copy(k).wait_send()


def mix_tokens(normed, residual, attn_gain, moe_gain, n_exp):
    vmem = pl.BlockSpec(memory_space=pltpu.VMEM)
    return pl.pallas_call(
        functools.partial(mix_kernel, n_exp),
        out_shape=(jax.ShapeDtypeStruct(residual.shape, jnp.bfloat16),) * 2,
        in_specs=[vmem] * 4,
        out_specs=(vmem, vmem),
        scratch_shapes=[
            pltpu.VMEM((n_exp, residual.shape[0], normed.shape[1]), jnp.bfloat16),
            pltpu.SemaphoreType.DMA((n_exp,)),
            pltpu.SemaphoreType.DMA((n_exp,)),
            pltpu.SemaphoreType.DMA((1,)),
        ],
        compiler_params=pltpu.CompilerParams(collective_id=4, has_side_effects=True),
    )(normed, residual, attn_gain[None, :], moe_gain[None, :])


def body(
    queries,
    keys,
    values,
    log_decay,
    residual,
    attn_gain,
    moe_gain,
    expert_ids,
    gate_weights,
    w_gate,
    w_up,
    w_down,
):
    n_seq, n_exp = lax.axis_size("seq"), lax.axis_size("exp")
    if moe_fits(n_seq, n_exp, *residual.shape, w_gate.shape):
        return whole_layer(
            queries, keys, values, log_decay, residual, attn_gain, moe_gain, expert_ids, gate_weights,
            w_gate, w_up, w_down, n_seq, n_exp,
        )
    tok_rows, width = residual.shape
    experts = w_gate.shape[0] * n_exp
    gates = jnp.sum(
        jnp.where(
            expert_ids[:, :, None] == jnp.arange(experts, dtype=jnp.int32)[None, None, :],
            gate_weights[:, :, None],
            0.0,
        ),
        axis=1,
    )
    rows = queries.shape[0]
    heads = log_decay.shape[1]
    head_dim = queries.shape[1] // heads
    q_heads = queries.reshape(rows, heads, head_dim)
    k_heads = keys.reshape(rows, heads, head_dim)
    v_heads = values.reshape(rows, heads, head_dim)
    upto = (
        lax.broadcasted_iota(jnp.int32, (rows, rows), 0)
        >= lax.broadcasted_iota(jnp.int32, (rows, rows), 1)
    ).astype(jnp.float32)
    log_cum = jnp.dot(upto, log_decay, precision=lax.Precision.HIGHEST)
    block_total = log_cum[-1]
    keys_weighted = (k_heads * jnp.exp(block_total[None, :] - log_cum)[:, :, None]).astype(
        jnp.bfloat16
    )
    block_state = jnp.einsum(
        "thd,the->hde", keys_weighted, v_heads, preferred_element_type=jnp.float32
    )
    carried = carried_in(block_total, block_state, lax.axis_size("seq"))
    scores = jnp.einsum("thd,shd->hts", q_heads, k_heads, preferred_element_type=jnp.float32)
    gap_logs = log_cum.T[:, :, None] - log_cum.T[:, None, :]
    causal_mask = (
        lax.broadcasted_iota(jnp.int32, (rows, rows), 0)
        >= lax.broadcasted_iota(jnp.int32, (rows, rows), 1)
    )[None, :, :]
    weights = jnp.where(
        causal_mask, scores * jnp.exp(jnp.where(causal_mask, gap_logs, 0.0)), 0.0
    ).astype(jnp.bfloat16)
    intra = jnp.einsum("hts,she->the", weights, v_heads, preferred_element_type=jnp.float32)
    inter = jnp.exp(log_cum)[:, :, None] * jnp.einsum(
        "thd,hde->the", q_heads.astype(jnp.float32), carried, precision=lax.Precision.HIGHEST
    )
    attn = intra + inter
    normed = (attn * lax.rsqrt(jnp.mean(attn * attn, axis=-1, keepdims=True) + 1e-06)).astype(
        jnp.bfloat16
    )
    normed = normed.reshape(rows, heads * head_dim)
    hidden, moe_in = mix_tokens(normed, residual, attn_gain, moe_gain, n_exp)
    hid32 = hidden.astype(jnp.float32)
    flat = gates.T.reshape(-1)
    pad = -flat.shape[0] % 1024
    g_tile = jnp.pad(flat, (0, pad)).reshape(-1, 128)
    everyone, g_all = gather_all(moe_in, g_tile, n_seq, n_exp)
    g_all = g_all.reshape(n_seq * n_exp, -1)[:, : experts * tok_rows]
    g_all = g_all.reshape(n_seq * n_exp, experts, tok_rows)
    mixed = None
    gate_col = lax.dynamic_slice_in_dim(
        g_all, lax.axis_index("exp") * w_gate.shape[0], w_gate.shape[0], 1
    )
    part = None
    for j in range(w_gate.shape[0]):
        gate_part = jnp.einsum("td,fd->tf", everyone, w_gate[j], preferred_element_type=jnp.float32)
        up_part = jnp.einsum("td,fd->tf", everyone, w_up[j], preferred_element_type=jnp.float32)
        active = (
            jax.nn.silu(gate_part) * up_part * gate_col[:, j, :].reshape(-1, 1)
        ).astype(jnp.bfloat16)
        one = jnp.dot(active, w_down[j], preferred_element_type=jnp.float32)
        part = one if part is None else part + one
    part = part.astype(jnp.bfloat16)
    total_rows, width = part.shape
    pieces = max(1, total_rows // 1024)
    step = width // pieces
    summed = [
        jax.jit(scatter_sum, static_argnums=(1, 2))(part[:, i * step : (i + 1) * step], n_seq, n_exp) for i in range(pieces)
    ]
    summed = summed[0] if pieces == 1 else jnp.concatenate(summed, axis=1)
    return (hid32 + summed).astype(jnp.bfloat16)


def solution(mesh):
    in_specs = (
        P("seq", "exp"),
        P("seq", "exp"),
        P("seq", "exp"),
        P("seq", "exp"),
        P(("seq", "exp"), None),
        P(),
        P(),
        P(("seq", "exp"), None),
        P(("seq", "exp"), None),
        P("exp", "seq", None),
        P("exp", "seq", None),
        P("exp", "seq", None),
    )
    out_specs = P(("seq", "exp"), None)
    return jax.shard_map(body, mesh=mesh, in_specs=in_specs, out_specs=out_specs, check_vma=False)
```

```python
import functools

import jax
import jax.numpy as jnp
from jax import lax
from jax.experimental import pallas as pl
from jax.experimental.pallas import tpu as pltpu
from jax.sharding import PartitionSpec as P

MESH = pl.DeviceIdType.MESH
PARTS = 2


class Place:
    def __init__(self, n_seq, n_exp):
        s, e = lax.axis_index("seq"), lax.axis_index("exp")
        self.fold, self.n_exp = n_exp // 4, n_exp
        self.length = (n_seq // 2) * self.fold
        self.p = (s // 2) * self.fold + e // 4
        self.x, self.y, self.c = s % 2, (e // 2) % 2, e % 2

    def ids(self, p, x, y, c):
        return (p // self.fold) * 2 + x, (p % self.fold) * 4 + y * 2 + c

    def block(self, p, x, y, c):
        s, e = self.ids(p, x, y, c)
        return s * self.n_exp + e

    def dev(self, dp=0, dx=0, dy=0, dc=0):
        x = 1 - self.x if dx else self.x
        y = 1 - self.y if dy else self.y
        c = 1 - self.c if dc else self.c
        return self.ids(self.p + dp, x, y, c)

    def greet(self, *more):
        barrier = pltpu.get_barrier_semaphore()
        for d in (dict(dx=1), dict(dy=1), dict(dc=1), *more):
            pl.semaphore_signal(barrier, inc=1, device_id=self.dev(**d), device_id_type=MESH)

        @pl.when(self.p > 0)
        def _():
            pl.semaphore_signal(barrier, inc=1, device_id=self.dev(dp=-1), device_id_type=MESH)

        @pl.when(self.p < self.length - 1)
        def _():
            pl.semaphore_signal(barrier, inc=1, device_id=self.dev(dp=1), device_id_type=MESH)

        ends = (self.p > 0).astype(jnp.int32) + (self.p < self.length - 1).astype(jnp.int32)
        pl.semaphore_wait(barrier, 3 + len(more) + ends)

    def at(self, stage, sign, k):
        if sign == 0:
            stage(0, 0, 0)
        elif sign < 0:
            pl.when(self.p >= k)(lambda: stage(2 * k - 1, -k, -1))
        else:
            pl.when(self.p + k < self.length)(lambda: stage(2 * k, k, 1))

    def far_first(self, stage):
        def one(i, carry):
            for sign in (1, -1):
                self.at(stage, sign, self.length - 1 - i)
            return carry

        if self.length <= 8:
            for i in range(self.length - 1):
                one(i, 0)
        else:
            lax.fori_loop(0, self.length - 1, one, 0)
        self.at(stage, 0, 0)

    def near_first(self, *stages):
        depth = len(stages)

        def ring(stage, k):
            if isinstance(k, int) and k == 0:
                self.at(stage, 0, 0)
            else:
                for sign in (-1, 1):
                    self.at(stage, sign, k)

        def step(k):
            for j, stage in enumerate(stages):
                if 0 <= k - j < self.length:
                    ring(stage, k - j)

        total = self.length + depth - 1
        if self.length <= 8:
            for k in range(total):
                step(k)
            return
        for k in range(depth):
            step(k)

        def one(k, carry):
            for j, stage in enumerate(stages):
                ring(stage, k - j)
            return carry

        lax.fori_loop(depth, self.length, one, 0)
        for k in range(self.length, total):
            step(k)


def gather_kernel(n_seq, n_exp, x_ref, g_ref, out_ref, gout_ref, send, recv, loc):
    me = Place(n_seq, n_exp)
    rows, width = x_ref.shape
    grow = g_ref.shape[0]
    me.greet()

    def place(ref, off, dx, dy, dc=0):
        x = 1 - me.x if dx else me.x
        y = 1 - me.y if dy else me.y
        c = 1 - me.c if dc else me.c
        b = me.block(me.p + off, x, y, c)
        n = rows if ref is out_ref else grow
        return ref.at[pl.ds(pl.multiple_of(b * n, n), n)]

    def copies(part, kind, slot, off, dx, dy, to, own=False, half=None, dc=0):
        dst_x, dst_g = place(out_ref, off, dx, dy, dc), place(gout_ref, off, dx, dy, dc)
        src_x, src_g = (x_ref, g_ref) if own else (dst_x, dst_g)
        span = width // PARTS
        if half is None:
            cols = pl.ds(part * span, span)
        else:
            cols = pl.ds(part * span + half * (span // 2), span // 2)
        out = [
            pltpu.make_async_remote_copy(
                src_x.at[:, cols],
                dst_x.at[:, cols],
                send.at[kind, slot, part],
                recv.at[kind, slot, part],
                to,
                MESH,
            )
        ]
        if half != 1 and part == 0:
            out.append(
                pltpu.make_async_remote_copy(
                    src_g, dst_g, send.at[kind, slot, PARTS], recv.at[kind, slot, PARTS], to, MESH
                )
            )
        return out

    def start(*a, **k):
        for cp in copies(*a, **k):
            cp.start()

    def wait_recv(*a, **k):
        for cp in copies(*a, **k):
            cp.wait_recv()

    def wait_send(*a, **k):
        for cp in copies(*a, **k):
            cp.wait_send()

    left, right = dict(dp=-1), dict(dp=1)
    X, Y, C = me.dev(dx=1), me.dev(dy=1), me.dev(dc=1)

    def line_sends(off, sign, do):
        own = sign == 0
        if sign <= 0:
            pl.when(me.p + 1 < me.length)(
                lambda: do(0, 2 * (-off + 1) - 1, off, 0, 0, me.dev(**right), own=own)
            )
        if sign >= 0:
            pl.when(me.p > 0)(lambda: do(0, 2 * (off + 1), off, 0, 0, me.dev(**left), own=own))

    def stage_line(slot, off, sign, do):
        own = sign == 0
        line_sends(off, sign, do)
        do(1, slot, off, 0, 0, X, own=own)
        do(2, slot, off, 0, 0, Y, own=own)
        do(5, slot, off, 0, 0, C, own=own)

    def stage_xy_1(slot, off, do):
        do(3, slot, off, 1, 0, Y, half=0)
        do(6, slot, off, 1, 0, C)

    def stage_xy_2(slot, off, do):
        do(4, slot, off, 0, 1, X, half=1)
        do(7, slot, off, 0, 1, C)

    def stage_diag(slot, off, do):
        do(8, slot, off, 1, 1, C)

    local = [
        pltpu.make_async_copy(x_ref, place(out_ref, 0, 0, 0), loc.at[0]),
        pltpu.make_async_copy(g_ref, place(gout_ref, 0, 0, 0), loc.at[1]),
    ]
    for cp in local:
        cp.start()

    def s1(slot, off, sign):
        for part in range(PARTS):
            if sign:
                wait_recv(part, 0, slot, off, 0, 0, X)
            stage_line(slot, off, sign, functools.partial(start, part))

    def s2(slot, off, sign):
        for part in range(PARTS):
            wait_recv(part, 1, slot, off, 1, 0, X)
            stage_xy_1(slot, off, functools.partial(start, part))
            wait_recv(part, 2, slot, off, 0, 1, X)
            stage_xy_2(slot, off, functools.partial(start, part))

    def s3(slot, off, sign):
        for part in range(PARTS):
            wait_recv(part, 3, slot, off, 1, 1, X, half=0)
            wait_recv(part, 4, slot, off, 1, 1, X, half=1)
            stage_diag(slot, off, functools.partial(start, part))

    me.near_first(s1, s2, s3)

    def s4(slot, off, sign):
        for part in range(PARTS):
            done = functools.partial(wait_send, part)
            stage_line(slot, off, sign, done)
            stage_xy_1(slot, off, done)
            stage_xy_2(slot, off, done)
            stage_diag(slot, off, done)
            wait_recv(part, 5, slot, off, 0, 0, X, dc=1)
            wait_recv(part, 6, slot, off, 1, 0, X, dc=1)
            wait_recv(part, 7, slot, off, 0, 1, X, dc=1)
            wait_recv(part, 8, slot, off, 1, 1, X, dc=1)

    me.near_first(s4)
    for cp in local:
        cp.wait()


def gather_all(x, g, n_seq, n_exp):
    n = n_seq * n_exp
    length = n // 8
    anyspace = pl.BlockSpec(memory_space=pl.ANY)
    return pl.pallas_call(
        functools.partial(gather_kernel, n_seq, n_exp),
        out_shape=(
            jax.ShapeDtypeStruct((n * x.shape[0], x.shape[1]), x.dtype),
            jax.ShapeDtypeStruct((n * g.shape[0], g.shape[1]), g.dtype),
        ),
        in_specs=[anyspace, anyspace],
        out_specs=(anyspace, anyspace),
        scratch_shapes=[
            pltpu.SemaphoreType.DMA((9, 2 * length + 1, PARTS + 1)),
            pltpu.SemaphoreType.DMA((9, 2 * length + 1, PARTS + 1)),
            pltpu.SemaphoreType.DMA((2,)),
        ],
        compiler_params=pltpu.CompilerParams(collective_id=1, has_side_effects=True),
    )(x, g)


def scatter_kernel(
    n_seq, n_exp, y_ref, out_ref, acc, sib, xbuf, ybuf, dab, dbb, line, send, recv, loc
):
    me = Place(n_seq, n_exp)
    L = me.length
    rows, width = out_ref.shape
    halfw = width // 2
    me.greet()
    X, Y, C = me.dev(dx=1), me.dev(dy=1), me.dev(dc=1)

    def src(off, grp, dc):
        x = 1 - me.x if grp & 1 else me.x
        y = 1 - me.y if grp & 2 else me.y
        c = 1 - me.c if dc else me.c
        b = me.block(me.p + off, x, y, c)
        return y_ref.at[pl.ds(pl.multiple_of(b * rows, rows), rows)]

    def sib_copy(slot, off, grp):
        return pltpu.make_async_remote_copy(
            src(off, grp, 1), sib.at[grp, slot], send.at[grp, slot], recv.at[grp, slot], C, MESH
        )

    def load(slot, off, grp):
        return pltpu.make_async_copy(src(off, grp, 0), acc.at[grp, slot], loc.at[grp, slot])

    for grp in (3, 1, 2, 0):

        def go(slot, off, sign, grp=grp):
            sib_copy(slot, off, grp).start()
            load(slot, off, grp).start()

        me.far_first(go)

    f32 = jnp.float32

    def pair_sum(slot, off, grp):
        load(slot, off, grp).wait()
        sib_copy(slot, off, grp).wait_recv()
        return acc[grp, slot].astype(f32) + sib[grp, slot].astype(f32)

    def diag_a(slot):
        return pltpu.make_async_remote_copy(
            acc.at[3, slot, :, pl.ds(0, halfw)], dab.at[slot], send.at[4, slot], recv.at[4, slot], Y, MESH
        )

    def diag_b(slot):
        return pltpu.make_async_remote_copy(
            acc.at[3, slot, :, pl.ds(halfw, halfw)], dbb.at[slot], send.at[5, slot], recv.at[5, slot], X, MESH
        )

    def x_copy(slot):
        return pltpu.make_async_remote_copy(
            acc.at[1, slot], xbuf.at[slot], send.at[6, slot], recv.at[6, slot], X, MESH
        )

    def y_copy(slot):
        return pltpu.make_async_remote_copy(
            acc.at[2, slot], ybuf.at[slot], send.at[7, slot], recv.at[7, slot], Y, MESH
        )

    def line_copy(slot, sign):
        return pltpu.make_async_remote_copy(
            acc.at[0, slot],
            line.at[slot],
            send.at[8, slot],
            recv.at[8, slot],
            me.dev(dp=sign),
            MESH,
        )

    def d1(slot, off, sign):
        acc[3, slot] = pair_sum(slot, off, 3).astype(acc.dtype)
        diag_a(slot).start()
        diag_b(slot).start()

    def d2(slot, off, sign):
        sx = pair_sum(slot, off, 1)
        diag_a(slot).wait_recv()
        acc[1, slot, :, pl.ds(0, halfw)] = (sx[:, :halfw] + dab[slot].astype(f32)).astype(acc.dtype)
        acc[1, slot, :, pl.ds(halfw, halfw)] = sx[:, halfw:].astype(acc.dtype)
        x_copy(slot).start()
        sy = pair_sum(slot, off, 2)
        diag_b(slot).wait_recv()
        acc[2, slot, :, pl.ds(0, halfw)] = sy[:, :halfw].astype(acc.dtype)
        acc[2, slot, :, pl.ds(halfw, halfw)] = (sy[:, halfw:] + dbb[slot].astype(f32)).astype(acc.dtype)
        y_copy(slot).start()

    def d3(slot, off, sign):
        total = pair_sum(slot, off, 0)
        x_copy(slot).wait_recv()
        y_copy(slot).wait_recv()
        total = total + xbuf[slot].astype(f32) + ybuf[slot].astype(f32)
        if sign == 0:
            out_ref[...] = total
            if L > 1:

                @pl.when(me.p > 0)
                def _():
                    in_copy(2).wait_recv()
                    out_ref[...] += line[2].astype(f32)

                @pl.when(me.p < L - 1)
                def _():
                    in_copy(1).wait_recv()
                    out_ref[...] += line[1].astype(f32)

            return
        acc[0, slot] = total.astype(acc.dtype)
        far = slot + 2
        behind = me.p > 0 if sign > 0 else me.p < L - 1

        @pl.when(jnp.logical_and(behind, sign * off + 1 < L))
        def _():
            in_copy(far).wait_recv()
            acc[0, slot] = (acc[0, slot].astype(f32) + line[far].astype(f32)).astype(acc.dtype)

        line_copy(slot, sign).start()

    def in_copy(slot):
        return pltpu.make_async_remote_copy(
            acc.at[0, slot], line.at[slot], send.at[8, slot], recv.at[8, slot], X, MESH
        )

    me.far_first(d1)
    me.far_first(d2)
    me.far_first(d3)

    def fin(slot, off, sign):
        for grp in range(4):
            sib_copy(slot, off, grp).wait_send()
        diag_a(slot).wait_send()
        diag_b(slot).wait_send()
        x_copy(slot).wait_send()
        y_copy(slot).wait_send()
        if sign:
            line_copy(slot, sign).wait_send()

    me.far_first(fin)


def scatter_sum(part, n_seq, n_exp):
    n = n_seq * n_exp
    slots = n // 4 - 1 + 2
    rows, width = part.shape[0] // n, part.shape[1]
    bf = jnp.bfloat16
    return pl.pallas_call(
        functools.partial(scatter_kernel, n_seq, n_exp),
        out_shape=jax.ShapeDtypeStruct((rows, width), jnp.float32),
        in_specs=[pl.BlockSpec(memory_space=pl.ANY)],
        out_specs=pl.BlockSpec(memory_space=pltpu.VMEM),
        scratch_shapes=[
            pltpu.VMEM((4, slots, rows, width), bf),
            pltpu.VMEM((4, slots, rows, width), bf),
            pltpu.VMEM((slots, rows, width), bf),
            pltpu.VMEM((slots, rows, width), bf),
            pltpu.VMEM((slots, rows, width // 2), bf),
            pltpu.VMEM((slots, rows, width // 2), bf),
            pltpu.VMEM((slots, rows, width), bf),
            pltpu.SemaphoreType.DMA((9, slots)),
            pltpu.SemaphoreType.DMA((9, slots)),
            pltpu.SemaphoreType.DMA((4, slots)),
        ],
        compiler_params=pltpu.CompilerParams(
            collective_id=2, has_side_effects=True, vmem_limit_bytes=60 * 2**20
        ),
    )(part)


GPARTS = 4
HPARTS = 4
PLANES = 4
MPARTS = 4


def plane_orders(length):
    def depth(q):
        return min(q, length - 1 - q)

    visit = []
    for p in range(length):
        rest = [q for q in range(length) if q != p]
        near = min(rest, key=lambda q: (abs(q - p), depth(q)), default=p)
        rest = sorted((q for q in rest if q != near), key=lambda q: (depth(q), abs(q - p)))
        visit.append([p] + [near] * (length > 1) + rest)
    lines = []
    for p in range(length):
        def ready(q):
            chain = range(0, p + 1) if q > p else range(p, length)
            return max(visit[b].index(q) for b in chain)

        low = 2 * p < length
        lines.append(sorted((q for q in range(length) if q != p), key=lambda q: (ready(q), -q if low else q)))
    return visit, lines


def pick(table, p, j):
    total = 0
    for a, row in enumerate(table):
        for b, v in enumerate(row):
            hit = jnp.logical_and(p == a, j == b).astype(jnp.int32)
            total = total + hit * v
    return total


def spans(tiles, parts):
    cuts = [(tiles * i // parts) * 128 for i in range(parts + 1)]
    return [pl.ds(a, b - a) for a, b in zip(cuts[:-1], cuts[1:])]


def when(cond, fn):
    def run():
        fn()

    pl.when(cond)(run)


def attend_tokens(
    me, q_ref, k_ref, v_ref, ld_ref, res_ref, ag_ref, mg_ref, ids_ref, gw_ref, x_out,
    hid, work, flat, own16, peer, cin, cout, tots, tok, psend, precv, tsem, msend, mrecv,
):
    L, z = me.length, me.p
    f32, bf = jnp.float32, jnp.bfloat16
    heads, block = ld_ref.shape
    dim = q_ref.shape[1] // heads
    rows = res_ref.shape[0]
    n_exp, width = tok.shape[0], tok.shape[2]
    e = lax.axis_index("exp")
    pair = me.dev(dx=1)

    def head(h):
        return pl.ds(h * dim, dim)

    def pair_copy(h):
        return pltpu.make_async_remote_copy(
            own16.at[h], peer.at[h], psend.at[0], precv.at[0, h], pair, MESH
        )

    def line_copy(h):
        return pltpu.make_async_remote_copy(
            cout.at[h], cin.at[h], psend.at[1], precv.at[1, h], me.dev(dp=1), MESH
        )

    tot_copy = pltpu.make_async_remote_copy(tots.at[0], tots.at[1], tsem.at[0], tsem.at[1], pair, MESH)

    nt = (((1,), (1,)), ((), ()))
    tn = (((0,), (0,)), ((), ()))
    r = lax.broadcasted_iota(jnp.int32, (block, block), 0)
    c = lax.broadcasted_iota(jnp.int32, (block, block), 1)
    seen = r >= c
    decay = ld_ref[...]
    high = lax.Precision.HIGHEST
    cum = lax.dot_general(seen.astype(f32), decay, nt, precision=high, preferred_element_type=f32)
    cum_t = jnp.dot(decay, (r <= c).astype(f32), precision=high, preferred_element_type=f32)
    total = cum_t[:, block - 1 :]
    tots[0, 0:heads, :] = jnp.broadcast_to(total, (heads, dim))

    def state(h):
        kw = (k_ref[:, head(h)].astype(f32) * jnp.exp(total[h : h + 1] - cum[:, h : h + 1])).astype(bf)
        own = lax.dot_general(kw, v_ref[:, head(h)], tn, preferred_element_type=f32)
        work[:, pl.ds((heads + h) * dim, dim)] = own
        own16[h] = own.astype(bf)

    for h in range(heads):
        state(h)
    me.greet(dict(dy=1, dc=1))
    tot_copy.start()
    for h in range(heads):
        pair_copy(h).start()

    @pl.when(z == 0)
    def _():
        cin[...] = jnp.zeros_like(cin)

    def f_intra(h):
        scores = lax.dot_general(q_ref[:, head(h)], k_ref[:, head(h)], nt, preferred_element_type=f32)
        gap = cum[:, h : h + 1] - cum_t[h : h + 1, :]
        weights = jnp.where(seen, scores * jnp.exp(jnp.where(seen, gap, 0.0)), 0.0).astype(bf)
        work[:, head(h)] = jnp.dot(weights, v_ref[:, head(h)], preferred_element_type=f32)

    for h in range(heads):
        f_intra(h)
    tot_copy.wait_recv()
    mine, other = tots[0, 0:heads, :], tots[1, 0:heads, :]
    both = jnp.exp(mine + other)
    is_odd = jnp.full(mine.shape, me.x, jnp.int32) == 1
    one = jnp.ones_like(mine)
    own_by = jnp.where(is_odd, one, jnp.exp(other))
    peer_by = jnp.where(is_odd, jnp.exp(mine), one)
    carry_by = jnp.where(is_odd, jnp.exp(other), one)
    peer_in = jnp.where(is_odd, one, jnp.zeros_like(mine))

    peers = (dict(dc=1), dict(dy=1), dict(dy=1, dc=1))
    pieces = MPARTS
    span = width // pieces

    def mix_copy(k, i):
        to = me.dev(**peers[k])
        cols = pl.ds(i * span, span)
        src = flat.at[pl.ds(pl.multiple_of(to[1] * rows, rows), rows), cols]
        return pltpu.make_async_remote_copy(
            src, tok.at[e, :, cols], msend.at[0], mrecv.at[k], to, MESH
        )

    def mix_in(k):
        to = me.dev(**peers[k])
        return pltpu.make_async_remote_copy(
            tok.at[to[1]], tok.at[to[1]], msend.at[0], mrecv.at[k], to, MESH
        )

    def f_chain(h):
        pair_copy(h).wait_recv()
        pl.when(z > 0)(lambda: line_copy(h).wait_recv())
        near = peer[h].astype(f32)
        come = cin[h].astype(f32)
        row = slice(h, h + 1)

        @pl.when(z < L - 1)
        def _():
            mix = both[row] * come + own_by[row] * work[:, pl.ds((heads + h) * dim, dim)] + peer_by[row] * near
            cout[h] = mix.astype(bf)
            line_copy(h).start()

    def f_head(h):
        near = peer[h].astype(f32)
        come = cin[h].astype(f32)
        row = slice(h, h + 1)
        carried = carry_by[row] * come + peer_in[row] * near
        coarse = carried.astype(bf)
        fine = (carried - coarse.astype(f32)).astype(bf)
        query = q_ref[:, head(h)]
        inter = jnp.dot(query, coarse, preferred_element_type=f32) + jnp.dot(
            query, fine, preferred_element_type=f32
        )
        attn = work[:, head(h)] + jnp.exp(cum[:, h : h + 1]) * inter
        scale = lax.rsqrt(jnp.mean(attn * attn, axis=-1, keepdims=True) + 1e-06)
        flat[0:block, head(h)] = (attn * scale).astype(bf)
        if (h + 1) * pieces % heads == 0:
            for k in range(len(peers)):
                mix_copy(k, (h + 1) * pieces // heads - 1).start()

    for h in range(heads):
        f_chain(h)
        f_head(h)

    tok[e] = flat[pl.ds(pl.multiple_of(e * rows, rows), rows), 0:width]

    def f_mix():
        for k in range(len(peers)):
            mix_in(k).wait_recv()

    f_mix()
    square = jnp.zeros((rows, 1), f32)
    for j in range(n_exp):
        cols = pl.ds(j * width, width)
        value = (res_ref[:, cols].astype(f32) + tok[j].astype(f32) * ag_ref[:, cols]).astype(bf)
        hid[:, cols] = value
        wide = value.astype(f32)
        square = square + jnp.sum(wide * wide, axis=1, keepdims=True)
    scale = lax.rsqrt(square / (n_exp * width) + 1e-06)
    for j in range(n_exp):
        cols = pl.ds(j * width, width)
        x_out[:, cols] = (hid[:, cols].astype(f32) * scale * mg_ref[:, cols]).astype(bf)

    def column(ref):
        same = lax.broadcasted_iota(jnp.int32, (rows, rows), 0) == lax.broadcasted_iota(jnp.int32, (rows, rows), 1)
        return lax.dot_general(
            same.astype(f32), ref[...].astype(f32), nt, precision=high, preferred_element_type=f32
        )

    ids, gates = column(ids_ref).astype(jnp.int32), column(gw_ref)
    coarse = gates.astype(bf).astype(f32)
    rest = gates - coarse
    lane = lax.broadcasted_iota(jnp.int32, (rows, 128), 1)
    extra = jnp.zeros((rows, 128), f32)
    for i in range(ids_ref.shape[0]):
        who = ids[:, i : i + 1]
        extra = jnp.where(lane == who, coarse[:, i : i + 1], extra)
        extra = jnp.where(lane == who + 64, rest[:, i : i + 1], extra)
    x_out[:, n_exp * width :] = extra.astype(bf)

    def finish():
        def out(ref, sent):
            pltpu.make_async_remote_copy(ref, ref, sent, sent, pair, MESH).wait_send()

        tot_copy.wait_send()
        out(own16, psend.at[0])
        pl.when(z < L - 1)(lambda: out(cout, psend.at[1]))
        out(tok.at[pl.ds(0, len(peers))], msend.at[0])

    return finish


def moe_kernel(
    n_seq, n_exp, q_ref, k_ref, v_ref, ld_ref, res_ref, ag_ref, mg_ref, ids_ref, gw_ref,
    wg_ref, wu_ref, wd_ref, out_ref,
    xs, ys, act, sib, din, near_in, lin, tot, wg, wu, wd, hid_ref,
    own16, peer, cin, cout, tots, tok,
    gsend, lsend, grecv, drecv, crecv, brecv, ssend, srecv, nrecv, drecv2, loc, psend, precv, tsem, msend, mrecv,
):
    me = Place(n_seq, n_exp)
    L, p = me.length, me.p
    rows, width = out_ref.shape
    hidden = wg.shape[0]
    many = 8 * rows
    f32, bf = jnp.float32, jnp.bfloat16
    X, Y, C = me.dev(dx=1), me.dev(dy=1), me.dev(dc=1)
    visit, lines = plane_orders(L)
    gcols = spans(xs.shape[1] // 128, GPARTS)
    hcols, dcols = spans(width // 128, HPARTS), spans(width // 128, 2 * HPARTS)

    loads = [
        pltpu.make_async_copy(a.at[0], b, loc.at[i])
        for i, (a, b) in enumerate(((wg_ref, wg), (wu_ref, wu), (wd_ref, wd)))
    ]
    for cp in loads:
        cp.start()

    def flip(v, d):
        return 1 - v if d else v

    def row(q, dx=0, dy=0, dc=0):
        k = (flip(me.c, dc) * 2 + flip(me.x, dx)) * 2 + flip(me.y, dy)
        return pl.ds(pl.multiple_of((q * 8 + k) * rows, rows), rows)

    def srow(q, dx=0, dy=0):
        k = flip(me.x, dx) * 2 + flip(me.y, dy)
        return pl.ds(pl.multiple_of((q * 4 + k) * rows, rows), rows)

    def prow(q):
        return pl.ds(pl.multiple_of(q * rows, rows), rows)

    cut = gcols[GPARTS // 2].start
    halves = (pl.ds(0, cut), pl.ds(cut, xs.shape[1] - cut))
    middle = pl.ds(gcols[1].start, gcols[-1].start - gcols[1].start)
    lower, higher, both = (0,), (1,), (0, 1)

    def gcopy(q, cols, r, to, sent, got):
        ref = xs.at[r, cols]
        return pltpu.make_async_remote_copy(ref, ref, sent, got, to, MESH)

    def arrive(q, cols, r, got):
        gcopy(q, cols, r, X, gsend.at[0], got).wait_recv()

    def bulk(ref, sent):
        return pltpu.make_async_remote_copy(ref, ref, sent, sent, X, MESH)

    def to_sibling(q, cols, r):
        gcopy(q, cols, r, C, gsend.at[0], crecv.at[q]).start()

    def both_ways(q, cols, r, lane, got):
        pl.when(jnp.logical_and(q >= p, p > 0))(
            lambda: gcopy(q, cols, r, me.dev(dp=-1), lsend.at[lane, q], got).start()
        )
        pl.when(jnp.logical_and(q <= p, p + 1 < L))(
            lambda: gcopy(q, cols, r, me.dev(dp=1), lsend.at[lane + 1, q], got).start()
        )

    def line_pair(q, side):
        both_ways(q, halves[side], row(q), 0, grecv.at[2, q, side])

    def corner_out(q):
        both_ways(q, middle, row(q, 1, 1), 2, drecv.at[q, 2])

    def g_first(q, turn, own=False):
        sent = gsend.at[5 + turn] if own else gsend.at[1]
        gcopy(q, halves[turn], row(q), X, sent, grecv.at[0, q, turn]).start()
        gcopy(q, halves[1 - turn], row(q), Y, gsend.at[2], grecv.at[1, q, 1 - turn]).start()
        if turn == 0:
            to_sibling(q, pl.ds(0, xs.shape[1]), row(q))

    def g_own(q):
        line_pair(q, 0)
        g_first(q, 0, True)
        line_pair(q, 1)
        g_first(q, 1, True)

    def from_x(q, side, own):
        r = row(q, 1, 0)
        arrive(q, halves[side], r, grecv.at[0, q, side])
        if side == 0:
            cols, sent = (halves[0], gsend.at[7]) if own else (gcols[0], gsend.at[3])
            gcopy(q, cols, r, Y, sent, drecv.at[q, 0]).start()
        to_sibling(q, halves[side], r)

    def from_y(q, side, own):
        r = row(q, 0, 1)
        arrive(q, halves[side], r, grecv.at[1, q, side])
        if side == 1:
            cols, sent = (halves[1], gsend.at[8]) if own else (gcols[-1], gsend.at[4])
            gcopy(q, cols, r, X, sent, drecv.at[q, 1]).start()
        to_sibling(q, halves[side], r)

    def g_second(q, own=False):
        from_x(q, 0, own)
        from_y(q, 1, own)

    def g_rest(q, own=False):
        from_x(q, 1, own)
        from_y(q, 0, own)

    def g_third(q, own=False):
        r = row(q, 1, 1)
        for k, cols in enumerate(halves if own else (gcols[0], gcols[-1])):
            arrive(q, cols, r, drecv.at[q, k])
            to_sibling(q, cols, r)
        if own:
            corner_out(q)

    def g_corner(k):
        for sign in (-1, 1):
            q = p + sign * k

            def pass_on():
                arrive(q, middle, row(q, 1, 1), drecv.at[q, 2])
                corner_out(q)
                to_sibling(q, middle, row(q, 1, 1))

            when(jnp.logical_and(q >= 0, q < L), pass_on)

    def g_ring(k, sides):
        for sign in (-1, 1):
            q = p + sign * k

            def pass_on():
                for side in sides:
                    arrive(q, halves[side], row(q), grecv.at[2, q, side])
                    line_pair(q, side)

            when(jnp.logical_and(q >= 0, q < L), pass_on)

    def g_done(q):
        r = pl.ds(pl.multiple_of((q * 2 + 1 - me.c) * 4 * rows, 4 * rows), 4 * rows)
        pltpu.make_async_remote_copy(xs.at[r], xs.at[r], gsend.at[0], crecv.at[q], X, MESH).wait_recv()

    def g_drain():
        bulk(xs.at[pl.ds(0, L * 4 * rows)], gsend.at[0]).wait_send()
        bulk(xs.at[pl.ds(0, (L - 1) * rows)], gsend.at[1]).wait_send()
        bulk(xs.at[pl.ds(0, L * rows)], gsend.at[2]).wait_send()
        bulk(xs.at[pl.ds(0, (L - 1) * rows), gcols[0]], gsend.at[3]).wait_send()
        bulk(xs.at[pl.ds(0, (L - 1) * rows), gcols[-1]], gsend.at[4]).wait_send()
        bulk(xs.at[row(p), halves[0]], gsend.at[7]).wait_send()
        bulk(xs.at[row(p), halves[1]], gsend.at[8]).wait_send()
        bulk(xs.at[row(p), halves[0]], gsend.at[5]).wait_send()
        bulk(xs.at[row(p), halves[1]], gsend.at[6]).wait_send()
        for q in range(L):
            pl.when(jnp.logical_and(q >= p, p > 0))(lambda: bulk(xs.at[row(q)], lsend.at[0, q]).wait_send())
            pl.when(jnp.logical_and(q <= p, p + 1 < L))(lambda: bulk(xs.at[row(q)], lsend.at[1, q]).wait_send())
            mid = xs.at[row(q), middle]
            pl.when(jnp.logical_and(q >= p, p > 0))(lambda: bulk(mid, lsend.at[2, q]).wait_send())
            pl.when(jnp.logical_and(q <= p, p + 1 < L))(lambda: bulk(mid, lsend.at[3, q]).wait_send())

    def sib_copy(q, h):
        r = pl.ds(pl.multiple_of((q * 2 + 1 - me.c) * 4 * rows, 4 * rows), 4 * rows)
        d = pl.ds(pl.multiple_of(q * 4 * rows, 4 * rows), 4 * rows)
        return pltpu.make_async_remote_copy(
            ys.at[r, hcols[h]], sib.at[d, hcols[h]], ssend.at[4], brecv.at[q, h], C, MESH
        )

    def plane_copy(side, q, h, r, to):
        return pltpu.make_async_remote_copy(
            ys.at[r, hcols[h]], near_in.at[prow(2 * q + side), hcols[h]], ssend.at[1 + side], nrecv.at[q, h], to, MESH
        )

    def settled(ref, got):
        pltpu.make_async_remote_copy(ref, ref, ssend.at[0], got, X, MESH).wait_recv()

    def diag_copy(q, h, side):
        cols = dcols[2 * h + side]
        return pltpu.make_async_remote_copy(
            ys.at[row(q, 1, 1), cols], din.at[prow(q), cols], ssend.at[0], drecv2.at[q, h], (Y, X)[side], MESH
        )

    def x_copy(q, h):
        return plane_copy(0, q, h, row(q, 1, 0), X)

    def y_copy(q, h):
        return plane_copy(1, q, h, row(q, 0, 1), Y)

    def line_copy(q, h):
        up = (q > p).astype(jnp.int32)
        last = jnp.logical_and(q < p, q == p - 1).astype(jnp.int32)
        slot = q + (L - q) * last
        return pltpu.make_async_remote_copy(
            ys.at[row(q), hcols[h]],
            lin.at[prow(slot), hcols[h]],
            ssend.at[3],
            srecv.at[slot, h],
            me.dev(dp=2 * up - 1),
            MESH,
        )

    def line_in(slot, h):
        return pltpu.make_async_remote_copy(
            ys.at[row(p), hcols[h]], lin.at[prow(slot), hcols[h]], ssend.at[3], srecv.at[slot, h], X, MESH
        )

    def pair(q, h, dx, dy):
        return ys[row(q, dx, dy), hcols[h]].astype(f32) + sib[srow(q, dx, dy), hcols[h]].astype(f32)

    def r_first(q, h):
        sib_copy(q, h).wait_recv()
        ys[row(q, 1, 1), hcols[h]] = pair(q, h, 1, 1).astype(bf)
        for side in range(2):
            diag_copy(q, h, side).start()

    def r_second(q, h):
        sx, sy = pair(q, h, 1, 0), pair(q, h, 0, 1)
        near, far = dcols[2 * h], dcols[2 * h + 1]
        settled(din.at[prow(q), hcols[h]], drecv2.at[q, h])
        ys[row(q, 1, 0), near] = (sx[:, : near.size] + din[prow(q), near].astype(f32)).astype(bf)
        ys[row(q, 1, 0), far] = sx[:, near.size :].astype(bf)
        x_copy(q, h).start()
        ys[row(q, 0, 1), near] = sy[:, : near.size].astype(bf)
        ys[row(q, 0, 1), far] = (sy[:, near.size :] + din[prow(q), far].astype(f32)).astype(bf)
        y_copy(q, h).start()

    def r_third(q, h):
        total = pair(q, h, 0, 0)
        settled(near_in.at[pl.ds(pl.multiple_of(2 * q * rows, rows), 2 * rows), hcols[h]], nrecv.at[q, h])
        for side in range(2):
            total = total + near_in[prow(2 * q + side), hcols[h]].astype(f32)
        tot[prow(q), hcols[h]] = total

    def r_line(q, h):
        behind = jnp.logical_or(jnp.logical_and(q > p, p > 0), jnp.logical_and(q < p, p < L - 1))

        @pl.when(behind)
        def _():
            line_in(q, h).wait_recv()
            ys[row(q), hcols[h]] = (tot[prow(q), hcols[h]] + lin[prow(q), hcols[h]].astype(f32)).astype(bf)

        @pl.when(jnp.logical_not(behind))
        def _():
            ys[row(q), hcols[h]] = tot[prow(q), hcols[h]].astype(bf)

        line_copy(q, h).start()

    def r_last(h):
        cols = hcols[h]

        @pl.when(p > 0)
        def _():
            line_in(p, h).wait_recv()
            tot[prow(p), cols] += lin[prow(p), cols].astype(f32)

        @pl.when(p < L - 1)
        def _():
            line_in(L, h).wait_recv()
            tot[prow(p), cols] += lin[prow(L), cols].astype(f32)

        out_ref[:, cols] = (hid_ref[:, cols].astype(f32) + tot[prow(p), cols]).astype(bf)

    at_end = jnp.logical_or(p == 0, p == L - 1)
    inner = jnp.logical_not(at_end)

    def r_early(q, h):
        pl.when(jnp.logical_and(at_end, q != p))(lambda: r_line(q, h))

    def r_drain():
        bulk(sib, ssend.at[4]).wait_send()
        for kind in range(3):
            bulk(din, ssend.at[kind]).wait_send()

    tile = next(t for t in range(512, 0, -128) if hidden % t == 0)
    fsteps = hidden // tile

    def block_of(q):
        return pl.ds(pl.multiple_of(q * many, many), many)

    def gate_of(q):
        extra = xs[block_of(q), width : width + 128].astype(f32)
        lane = lax.broadcasted_iota(jnp.int32, extra.shape, 1)
        e = lax.axis_index("exp")
        keep = jnp.logical_or(lane == e, lane == e + 64)
        return jnp.sum(jnp.where(keep, extra, 0.0), axis=1, keepdims=True)

    nt = (((1,), (1,)), ((), ()))

    def ffn_in(q, f):
        fc = pl.ds(f * tile, tile)
        rows_in = xs[block_of(q), 0:width]
        gate = lax.dot_general(rows_in, wg[fc, :], nt, preferred_element_type=f32)
        up = lax.dot_general(rows_in, wu[fc, :], nt, preferred_element_type=f32)
        act[:, fc] = (gate / (1.0 + jnp.exp(-gate)) * up * gate_of(q)).astype(bf)

    def ffn_out(q, h):
        ys[block_of(q), hcols[h]] = jnp.dot(
            act[...], wd[:, hcols[h]], preferred_element_type=f32
        ).astype(bf)
        sib_copy(q, h).start()

    front_done = attend_tokens(
        me, q_ref, k_ref, v_ref, ld_ref, res_ref, ag_ref, mg_ref, ids_ref, gw_ref, xs.at[row(p)],
        hid_ref, tot, act, own16, peer, cin, cout, tots, tok, psend, precv, tsem, msend, mrecv,
    )
    second = pick(visit, p, 1)
    g_own(p)
    g_second(p, True)
    g_ring(1, lower)
    g_rest(p, True)
    g_ring(1, higher)
    g_first(second, 0)
    g_third(p, True)
    g_first(second, 1)
    front_done()
    for cp in loads:
        cp.wait()

    def chunk(j, carry):
        q, nxt, prev = pick(visit, p, j), pick(visit, p, j + 1), pick(visit, p, j - 1)
        older = pick(visit, p, j - 2)
        third, fourth = pick(visit, p, 2), pick(visit, p, 3)

        def opening(*fns):
            when(j == 0, lambda: [fn() for fn in fns])

        def closing(*fns):
            when(j == L - 1, lambda: [fn() for fn in fns])

        def ahead(*fns):
            when(jnp.logical_and(j > 0, j + 1 < L), lambda: [fn() for fn in fns])

        def after(*fns):
            when(j > 0, lambda: [fn() for fn in fns])

        def later(*fns):
            when(j > 1, lambda: [fn() for fn in fns])

        def settle(at, h):
            r_third(at, h)
            r_early(at, h)

        def hook(n):
            if n == 0:
                after(lambda: r_first(prev, 2), lambda: r_first(prev, 3))
                when(j == 1, lambda: g_corner(2))
                opening(
                    lambda: g_ring(2, lower),
                    lambda: g_second(nxt),
                    lambda: g_ring(2, higher),
                    lambda: g_first(fourth, 0),
                )
            if n == 1:
                opening(lambda: g_rest(nxt), lambda: g_first(fourth, 1))
                ahead(lambda: g_second(nxt))
                later(lambda: settle(older, 0), lambda: settle(older, 1))
                after(lambda: r_second(prev, 0), lambda: r_second(prev, 1))
            if n == 2:
                opening(lambda: g_corner(1))
                ahead(lambda: g_rest(nxt))
                later(lambda: settle(older, 2), lambda: settle(older, 3))
                closing(lambda: r_second(prev, 2))

        g_done(q)
        for f in range(fsteps):
            ffn_in(q, f)
            hook(f)
        for f in range(fsteps, 3):
            hook(f)
        for h in range(HPARTS):
            ffn_out(q, h)
            if h == 0:
                ahead(lambda: r_second(prev, 2))
                closing(lambda: r_second(prev, 3))
            if h == 1:
                when(j == 1, lambda: g_corner(3))
                ahead(lambda: r_second(prev, 3))
                opening(lambda: g_ring(3, both), lambda: g_first(third, 0))
                closing(lambda: settle(prev, 0))
            if h == 2:
                r_first(q, 0)
                ahead(lambda: g_third(nxt))
                opening(lambda: g_third(nxt))
                closing(lambda: settle(prev, 1))
            if h == 3:
                r_first(q, 1)
                opening(lambda: g_first(third, 1))
        return carry

    def one_line(i, h):
        when(inner, lambda: r_line(pick(lines, p, i), h))

    lax.fori_loop(0, L, chunk, 0)

    final, prior = pick(visit, p, L - 1), pick(visit, p, L - 2)
    r_first(final, 2)
    r_third(prior, 2)
    r_early(prior, 2)
    r_first(final, 3)
    r_third(prior, 3)
    r_early(prior, 3)
    for h in range(HPARTS):
        r_second(final, h)
        if h:
            one_line(0, h - 1)
    one_line(0, HPARTS - 1)
    for h in range(HPARTS):
        one_line(1, h)
        r_third(final, h)
        r_early(final, h)
    g_drain()
    for h in range(HPARTS):
        one_line(2, h)
        if h:
            r_last(h - 1)
    r_drain()
    r_last(HPARTS - 1)
    bulk(lin.at[pl.ds(0, (L - 1) * rows)], ssend.at[3]).wait_send()


def moe_scratch(n_seq, n_exp, x_shape, w_shape):
    n, L = n_seq * n_exp, n_seq * n_exp // 8
    rows, wide = x_shape
    hidden, width = w_shape[1:]
    bf, f32 = jnp.bfloat16, jnp.float32
    return [
        ((n * rows, wide), bf),
        ((n * rows, width), bf),
        ((8 * rows, hidden), bf),
        ((n // 2 * rows, width), bf),
        ((L * rows, width), bf),
        ((2 * L * rows, width), bf),
        ((L * rows + rows, width), bf),
        ((L * rows, width), f32),
        ((hidden, width), bf),
        ((hidden, width), bf),
        ((hidden, width), bf),
    ]


MOE_VMEM = 61 * 2**20


def moe_fits(n_seq, n_exp, rows, width, w_shape):
    need = sum(
        a * b * jnp.dtype(t).itemsize for (a, b), t in moe_scratch(n_seq, n_exp, (rows, width + 128), w_shape)
    )
    return (
        w_shape[0] == 1
        and n_exp // 4 == 1
        and n_seq * n_exp == 8 * PLANES
        and w_shape[1] % 128 == 0
        and w_shape[2] % (256 * HPARTS) == 0
        and w_shape[2] // n_exp % (128 * MPARTS) == 0
        and need + 6 * 2**20 <= MOE_VMEM
    )


def whole_layer(
    queries, keys, values, log_decay, residual, attn_gain, moe_gain, expert_ids, gate_weights,
    w_gate, w_up, w_down, n_seq, n_exp,
):
    L = n_seq * n_exp // 8
    heads = log_decay.shape[1]
    part = queries.shape[1]
    dim = part // heads
    rows, width = residual.shape
    vmem = pl.BlockSpec(memory_space=pltpu.VMEM)
    anyspace = pl.BlockSpec(memory_space=pl.ANY)
    dma = pltpu.SemaphoreType.DMA
    bf = jnp.bfloat16
    states = pltpu.VMEM((heads, dim, dim), bf)
    scratch = moe_scratch(n_seq, n_exp, (rows, width + 128), w_gate.shape)
    return pl.pallas_call(
        functools.partial(moe_kernel, n_seq, n_exp),
        out_shape=jax.ShapeDtypeStruct(residual.shape, bf),
        in_specs=[vmem] * 9 + [anyspace] * 3,
        out_specs=vmem,
        scratch_shapes=[pltpu.VMEM(s, t) for s, t in scratch]
        + [
            pltpu.VMEM(residual.shape, bf),
            states,
            states,
            states,
            states,
            pltpu.VMEM((2, heads + -heads % 8, dim), jnp.float32),
            pltpu.VMEM((n_exp, rows, part), bf),
            dma((9,)),
            dma((4, L)),
            dma((3, L, 2)),
            dma((L, 3)),
            dma((L,)),
            dma((L, HPARTS)),
            dma((5,)),
            dma((L + 1, HPARTS)),
            dma((L, HPARTS)),
            dma((L, HPARTS)),
            dma((3,)),
            dma((2,)),
            dma((2, heads)),
            dma((2,)),
            dma((1,)),
            dma((3,)),
        ],
        compiler_params=pltpu.CompilerParams(
            collective_id=5, has_side_effects=True, vmem_limit_bytes=MOE_VMEM
        ),
    )(
        queries, keys, values, log_decay.T, residual, attn_gain[None, :], moe_gain[None, :],
        expert_ids.T, gate_weights.T, w_gate, w_up, w_down,
    )


def carry_kernel(n_seq, own_ref, own16_ref, tot_ref, out_ref, peer, ptot, cin, cout, send, recv, tsem):
    s, e = lax.axis_index("seq"), lax.axis_index("exp")
    z, odd, deep = s // 2, s % 2, n_seq // 2
    heads = own_ref.shape[0]
    pair = (z * 2 + 1 - odd, e)

    barrier = pltpu.get_barrier_semaphore()
    pl.semaphore_signal(barrier, inc=1, device_id=pair, device_id_type=MESH)

    @pl.when(z > 0)
    def _():
        pl.semaphore_signal(barrier, inc=1, device_id=(s - 2, e), device_id_type=MESH)

    @pl.when(z < deep - 1)
    def _():
        pl.semaphore_signal(barrier, inc=1, device_id=(s + 2, e), device_id_type=MESH)

    ends = (z > 0).astype(jnp.int32) + (z < deep - 1).astype(jnp.int32)
    pl.semaphore_wait(barrier, 1 + ends)

    tot_copy = pltpu.make_async_remote_copy(tot_ref, ptot, tsem.at[0], tsem.at[1], pair, MESH)

    def pair_copy(h):
        return pltpu.make_async_remote_copy(
            own16_ref.at[h], peer.at[h], send.at[0, h], recv.at[0, h], pair, MESH
        )

    def line_copy(h):
        return pltpu.make_async_remote_copy(
            cout.at[h], cin.at[h], send.at[1, h], recv.at[1, h], (s + 2, e), MESH
        )

    tot_copy.start()
    for h in range(heads):
        pair_copy(h).start()

    @pl.when(z == 0)
    def _():
        cin[...] = jnp.zeros_like(cin)

    tot_copy.wait_recv()
    mine, other = tot_ref[...], ptot[...]
    both = jnp.exp(mine + other)
    is_odd = jnp.full(mine.shape, odd, jnp.int32) == 1
    one = jnp.ones_like(mine)
    own_by = jnp.where(is_odd, one, jnp.exp(other))
    peer_by = jnp.where(is_odd, jnp.exp(mine), one)
    carry_by = jnp.where(is_odd, jnp.exp(other), one)
    peer_in = jnp.where(is_odd, one, jnp.zeros_like(mine))
    for h in range(heads):
        pair_copy(h).wait_recv()

        @pl.when(z > 0)
        def _():
            line_copy(h).wait_recv()

        near = peer[h].astype(jnp.float32)
        come = cin[h].astype(jnp.float32)

        @pl.when(z < deep - 1)
        def _():
            cout[h] = (
                both[h : h + 1] * come + own_by[h : h + 1] * own_ref[h] + peer_by[h : h + 1] * near
            ).astype(cout.dtype)
            line_copy(h).start()

        out_ref[h] = carry_by[h : h + 1] * come + peer_in[h : h + 1] * near

    tot_copy.wait_send()
    for h in range(heads):
        pair_copy(h).wait_send()

        @pl.when(z < deep - 1)
        def _():
            line_copy(h).wait_send()


def carried_in(block_total, block_state, n_seq):
    heads, dim, _ = block_state.shape
    bf = jnp.bfloat16
    tile = jnp.pad(block_total, (0, -heads % 8))
    tile = jnp.broadcast_to(tile[:, None], (tile.shape[0], dim))
    vmem = pl.BlockSpec(memory_space=pltpu.VMEM)
    return pl.pallas_call(
        functools.partial(carry_kernel, n_seq),
        out_shape=jax.ShapeDtypeStruct(block_state.shape, jnp.float32),
        in_specs=[vmem] * 3,
        out_specs=vmem,
        scratch_shapes=[
            pltpu.VMEM(block_state.shape, bf),
            pltpu.VMEM(tile.shape, jnp.float32),
            pltpu.VMEM(block_state.shape, bf),
            pltpu.VMEM(block_state.shape, bf),
            pltpu.SemaphoreType.DMA((2, heads)),
            pltpu.SemaphoreType.DMA((2, heads)),
            pltpu.SemaphoreType.DMA((2,)),
        ],
        compiler_params=pltpu.CompilerParams(collective_id=3, has_side_effects=True),
    )(block_state, block_state.astype(bf), tile)


def mix_kernel(n_exp, normed_ref, res_ref, again_ref, mgain_ref, hid_ref, in_ref, tok, send, recv, loc):
    s, e = lax.axis_index("seq"), lax.axis_index("exp")
    rows, width = res_ref.shape[0], normed_ref.shape[1]

    barrier = pltpu.get_barrier_semaphore()
    for k in range(1, n_exp):
        pl.semaphore_signal(
            barrier, inc=1, device_id=(s, lax.rem(e + k, n_exp)), device_id_type=MESH
        )
    pl.semaphore_wait(barrier, n_exp - 1)

    def source(peer):
        return normed_ref.at[pl.ds(pl.multiple_of(peer * rows, rows), rows)]

    own = pltpu.make_async_copy(source(e), tok.at[e], loc.at[0])

    def copy(k):
        peer = lax.rem(e + k, n_exp)
        return pltpu.make_async_remote_copy(
            source(peer), tok.at[e], send.at[k], recv.at[k], (s, peer), MESH
        )

    def arriving(k):
        sender = lax.rem(e + n_exp - k, n_exp)
        return pltpu.make_async_remote_copy(
            source(e), tok.at[sender], send.at[k], recv.at[k], (s, sender), MESH
        )

    for k in range(1, n_exp):
        copy(k).start()
    own.start()
    own.wait()
    for k in range(1, n_exp):
        arriving(k).wait_recv()
    square = jnp.zeros((rows, 1), jnp.float32)
    for j in range(n_exp):
        cols = pl.ds(j * width, width)
        hid = (
            res_ref[:, cols].astype(jnp.float32)
            + tok[j].astype(jnp.float32) * again_ref[:, cols]
        ).astype(jnp.bfloat16)
        hid_ref[:, cols] = hid
        wide = hid.astype(jnp.float32)
        square = square + jnp.sum(wide * wide, axis=1, keepdims=True)
    scale = lax.rsqrt(square / (n_exp * width) + 1e-06)
    for j in range(n_exp):
        cols = pl.ds(j * width, width)
        in_ref[:, cols] = (
            hid_ref[:, cols].astype(jnp.float32) * scale * mgain_ref[:, cols]
        ).astype(jnp.bfloat16)
    for k in range(1, n_exp):
        copy(k).wait_send()


def mix_tokens(normed, residual, attn_gain, moe_gain, n_exp):
    vmem = pl.BlockSpec(memory_space=pltpu.VMEM)
    return pl.pallas_call(
        functools.partial(mix_kernel, n_exp),
        out_shape=(jax.ShapeDtypeStruct(residual.shape, jnp.bfloat16),) * 2,
        in_specs=[vmem] * 4,
        out_specs=(vmem, vmem),
        scratch_shapes=[
            pltpu.VMEM((n_exp, residual.shape[0], normed.shape[1]), jnp.bfloat16),
            pltpu.SemaphoreType.DMA((n_exp,)),
            pltpu.SemaphoreType.DMA((n_exp,)),
            pltpu.SemaphoreType.DMA((1,)),
        ],
        compiler_params=pltpu.CompilerParams(collective_id=4, has_side_effects=True),
    )(normed, residual, attn_gain[None, :], moe_gain[None, :])


def body(
    queries,
    keys,
    values,
    log_decay,
    residual,
    attn_gain,
    moe_gain,
    expert_ids,
    gate_weights,
    w_gate,
    w_up,
    w_down,
):
    n_seq, n_exp = lax.axis_size("seq"), lax.axis_size("exp")
    if moe_fits(n_seq, n_exp, *residual.shape, w_gate.shape):
        return whole_layer(
            queries, keys, values, log_decay, residual, attn_gain, moe_gain, expert_ids, gate_weights,
            w_gate, w_up, w_down, n_seq, n_exp,
        )
    tok_rows, width = residual.shape
    experts = w_gate.shape[0] * n_exp
    gates = jnp.sum(
        jnp.where(
            expert_ids[:, :, None] == jnp.arange(experts, dtype=jnp.int32)[None, None, :],
            gate_weights[:, :, None],
            0.0,
        ),
        axis=1,
    )
    rows = queries.shape[0]
    heads = log_decay.shape[1]
    head_dim = queries.shape[1] // heads
    q_heads = queries.reshape(rows, heads, head_dim)
    k_heads = keys.reshape(rows, heads, head_dim)
    v_heads = values.reshape(rows, heads, head_dim)
    upto = (
        lax.broadcasted_iota(jnp.int32, (rows, rows), 0)
        >= lax.broadcasted_iota(jnp.int32, (rows, rows), 1)
    ).astype(jnp.float32)
    log_cum = jnp.dot(upto, log_decay, precision=lax.Precision.HIGHEST)
    block_total = log_cum[-1]
    keys_weighted = (k_heads * jnp.exp(block_total[None, :] - log_cum)[:, :, None]).astype(
        jnp.bfloat16
    )
    block_state = jnp.einsum(
        "thd,the->hde", keys_weighted, v_heads, preferred_element_type=jnp.float32
    )
    carried = carried_in(block_total, block_state, lax.axis_size("seq"))
    scores = jnp.einsum("thd,shd->hts", q_heads, k_heads, preferred_element_type=jnp.float32)
    gap_logs = log_cum.T[:, :, None] - log_cum.T[:, None, :]
    causal_mask = (
        lax.broadcasted_iota(jnp.int32, (rows, rows), 0)
        >= lax.broadcasted_iota(jnp.int32, (rows, rows), 1)
    )[None, :, :]
    weights = jnp.where(
        causal_mask, scores * jnp.exp(jnp.where(causal_mask, gap_logs, 0.0)), 0.0
    ).astype(jnp.bfloat16)
    intra = jnp.einsum("hts,she->the", weights, v_heads, preferred_element_type=jnp.float32)
    inter = jnp.exp(log_cum)[:, :, None] * jnp.einsum(
        "thd,hde->the", q_heads.astype(jnp.float32), carried, precision=lax.Precision.HIGHEST
    )
    attn = intra + inter
    normed = (attn * lax.rsqrt(jnp.mean(attn * attn, axis=-1, keepdims=True) + 1e-06)).astype(
        jnp.bfloat16
    )
    normed = normed.reshape(rows, heads * head_dim)
    hidden, moe_in = mix_tokens(normed, residual, attn_gain, moe_gain, n_exp)
    hid32 = hidden.astype(jnp.float32)
    flat = gates.T.reshape(-1)
    pad = -flat.shape[0] % 1024
    g_tile = jnp.pad(flat, (0, pad)).reshape(-1, 128)
    everyone, g_all = gather_all(moe_in, g_tile, n_seq, n_exp)
    g_all = g_all.reshape(n_seq * n_exp, -1)[:, : experts * tok_rows]
    g_all = g_all.reshape(n_seq * n_exp, experts, tok_rows)
    mixed = None
    gate_col = lax.dynamic_slice_in_dim(
        g_all, lax.axis_index("exp") * w_gate.shape[0], w_gate.shape[0], 1
    )
    part = None
    for j in range(w_gate.shape[0]):
        gate_part = jnp.einsum("td,fd->tf", everyone, w_gate[j], preferred_element_type=jnp.float32)
        up_part = jnp.einsum("td,fd->tf", everyone, w_up[j], preferred_element_type=jnp.float32)
        active = (
            jax.nn.silu(gate_part) * up_part * gate_col[:, j, :].reshape(-1, 1)
        ).astype(jnp.bfloat16)
        one = jnp.dot(active, w_down[j], preferred_element_type=jnp.float32)
        part = one if part is None else part + one
    part = part.astype(jnp.bfloat16)
    total_rows, width = part.shape
    pieces = max(1, total_rows // 1024)
    step = width // pieces
    summed = [
        jax.jit(scatter_sum, static_argnums=(1, 2))(part[:, i * step : (i + 1) * step], n_seq, n_exp) for i in range(pieces)
    ]
    summed = summed[0] if pieces == 1 else jnp.concatenate(summed, axis=1)
    return (hid32 + summed).astype(jnp.bfloat16)


def solution(mesh):
    in_specs = (
        P("seq", "exp"),
        P("seq", "exp"),
        P("seq", "exp"),
        P("seq", "exp"),
        P(("seq", "exp"), None),
        P(),
        P(),
        P(("seq", "exp"), None),
        P(("seq", "exp"), None),
        P("exp", "seq", None),
        P("exp", "seq", None),
        P("exp", "seq", None),
    )
    out_specs = P(("seq", "exp"), None)
    return jax.shard_map(body, mesh=mesh, in_specs=in_specs, out_specs=out_specs, check_vma=False)
```

```python
import functools

import jax
import jax.numpy as jnp
from jax import lax
from jax.experimental import pallas as pl
from jax.experimental.pallas import tpu as pltpu
from jax.sharding import PartitionSpec as P

MESH = pl.DeviceIdType.MESH
PARTS = 2


class Place:
    def __init__(self, n_seq, n_exp):
        s, e = lax.axis_index("seq"), lax.axis_index("exp")
        self.fold, self.n_exp = n_exp // 4, n_exp
        self.length = (n_seq // 2) * self.fold
        self.p = (s // 2) * self.fold + e // 4
        self.x, self.y, self.c = s % 2, (e // 2) % 2, e % 2

    def ids(self, p, x, y, c):
        return (p // self.fold) * 2 + x, (p % self.fold) * 4 + y * 2 + c

    def block(self, p, x, y, c):
        s, e = self.ids(p, x, y, c)
        return s * self.n_exp + e

    def dev(self, dp=0, dx=0, dy=0, dc=0):
        x = 1 - self.x if dx else self.x
        y = 1 - self.y if dy else self.y
        c = 1 - self.c if dc else self.c
        return self.ids(self.p + dp, x, y, c)

    def greet(self, *more):
        barrier = pltpu.get_barrier_semaphore()
        for d in (dict(dx=1), dict(dy=1), dict(dc=1), *more):
            pl.semaphore_signal(barrier, inc=1, device_id=self.dev(**d), device_id_type=MESH)

        @pl.when(self.p > 0)
        def _():
            pl.semaphore_signal(barrier, inc=1, device_id=self.dev(dp=-1), device_id_type=MESH)

        @pl.when(self.p < self.length - 1)
        def _():
            pl.semaphore_signal(barrier, inc=1, device_id=self.dev(dp=1), device_id_type=MESH)

        ends = (self.p > 0).astype(jnp.int32) + (self.p < self.length - 1).astype(jnp.int32)
        pl.semaphore_wait(barrier, 3 + len(more) + ends)

    def at(self, stage, sign, k):
        if sign == 0:
            stage(0, 0, 0)
        elif sign < 0:
            pl.when(self.p >= k)(lambda: stage(2 * k - 1, -k, -1))
        else:
            pl.when(self.p + k < self.length)(lambda: stage(2 * k, k, 1))

    def far_first(self, stage):
        def one(i, carry):
            for sign in (1, -1):
                self.at(stage, sign, self.length - 1 - i)
            return carry

        if self.length <= 8:
            for i in range(self.length - 1):
                one(i, 0)
        else:
            lax.fori_loop(0, self.length - 1, one, 0)
        self.at(stage, 0, 0)

    def near_first(self, *stages):
        depth = len(stages)

        def ring(stage, k):
            if isinstance(k, int) and k == 0:
                self.at(stage, 0, 0)
            else:
                for sign in (-1, 1):
                    self.at(stage, sign, k)

        def step(k):
            for j, stage in enumerate(stages):
                if 0 <= k - j < self.length:
                    ring(stage, k - j)

        total = self.length + depth - 1
        if self.length <= 8:
            for k in range(total):
                step(k)
            return
        for k in range(depth):
            step(k)

        def one(k, carry):
            for j, stage in enumerate(stages):
                ring(stage, k - j)
            return carry

        lax.fori_loop(depth, self.length, one, 0)
        for k in range(self.length, total):
            step(k)


def gather_kernel(n_seq, n_exp, x_ref, g_ref, out_ref, gout_ref, send, recv, loc):
    me = Place(n_seq, n_exp)
    rows, width = x_ref.shape
    grow = g_ref.shape[0]
    me.greet()

    def place(ref, off, dx, dy, dc=0):
        x = 1 - me.x if dx else me.x
        y = 1 - me.y if dy else me.y
        c = 1 - me.c if dc else me.c
        b = me.block(me.p + off, x, y, c)
        n = rows if ref is out_ref else grow
        return ref.at[pl.ds(pl.multiple_of(b * n, n), n)]

    def copies(part, kind, slot, off, dx, dy, to, own=False, half=None, dc=0):
        dst_x, dst_g = place(out_ref, off, dx, dy, dc), place(gout_ref, off, dx, dy, dc)
        src_x, src_g = (x_ref, g_ref) if own else (dst_x, dst_g)
        span = width // PARTS
        if half is None:
            cols = pl.ds(part * span, span)
        else:
            cols = pl.ds(part * span + half * (span // 2), span // 2)
        out = [
            pltpu.make_async_remote_copy(
                src_x.at[:, cols],
                dst_x.at[:, cols],
                send.at[kind, slot, part],
                recv.at[kind, slot, part],
                to,
                MESH,
            )
        ]
        if half != 1 and part == 0:
            out.append(
                pltpu.make_async_remote_copy(
                    src_g, dst_g, send.at[kind, slot, PARTS], recv.at[kind, slot, PARTS], to, MESH
                )
            )
        return out

    def start(*a, **k):
        for cp in copies(*a, **k):
            cp.start()

    def wait_recv(*a, **k):
        for cp in copies(*a, **k):
            cp.wait_recv()

    def wait_send(*a, **k):
        for cp in copies(*a, **k):
            cp.wait_send()

    left, right = dict(dp=-1), dict(dp=1)
    X, Y, C = me.dev(dx=1), me.dev(dy=1), me.dev(dc=1)

    def line_sends(off, sign, do):
        own = sign == 0
        if sign <= 0:
            pl.when(me.p + 1 < me.length)(
                lambda: do(0, 2 * (-off + 1) - 1, off, 0, 0, me.dev(**right), own=own)
            )
        if sign >= 0:
            pl.when(me.p > 0)(lambda: do(0, 2 * (off + 1), off, 0, 0, me.dev(**left), own=own))

    def stage_line(slot, off, sign, do):
        own = sign == 0
        line_sends(off, sign, do)
        do(1, slot, off, 0, 0, X, own=own)
        do(2, slot, off, 0, 0, Y, own=own)
        do(5, slot, off, 0, 0, C, own=own)

    def stage_xy_1(slot, off, do):
        do(3, slot, off, 1, 0, Y, half=0)
        do(6, slot, off, 1, 0, C)

    def stage_xy_2(slot, off, do):
        do(4, slot, off, 0, 1, X, half=1)
        do(7, slot, off, 0, 1, C)

    def stage_diag(slot, off, do):
        do(8, slot, off, 1, 1, C)

    local = [
        pltpu.make_async_copy(x_ref, place(out_ref, 0, 0, 0), loc.at[0]),
        pltpu.make_async_copy(g_ref, place(gout_ref, 0, 0, 0), loc.at[1]),
    ]
    for cp in local:
        cp.start()

    def s1(slot, off, sign):
        for part in range(PARTS):
            if sign:
                wait_recv(part, 0, slot, off, 0, 0, X)
            stage_line(slot, off, sign, functools.partial(start, part))

    def s2(slot, off, sign):
        for part in range(PARTS):
            wait_recv(part, 1, slot, off, 1, 0, X)
            stage_xy_1(slot, off, functools.partial(start, part))
            wait_recv(part, 2, slot, off, 0, 1, X)
            stage_xy_2(slot, off, functools.partial(start, part))

    def s3(slot, off, sign):
        for part in range(PARTS):
            wait_recv(part, 3, slot, off, 1, 1, X, half=0)
            wait_recv(part, 4, slot, off, 1, 1, X, half=1)
            stage_diag(slot, off, functools.partial(start, part))

    me.near_first(s1, s2, s3)

    def s4(slot, off, sign):
        for part in range(PARTS):
            done = functools.partial(wait_send, part)
            stage_line(slot, off, sign, done)
            stage_xy_1(slot, off, done)
            stage_xy_2(slot, off, done)
            stage_diag(slot, off, done)
            wait_recv(part, 5, slot, off, 0, 0, X, dc=1)
            wait_recv(part, 6, slot, off, 1, 0, X, dc=1)
            wait_recv(part, 7, slot, off, 0, 1, X, dc=1)
            wait_recv(part, 8, slot, off, 1, 1, X, dc=1)

    me.near_first(s4)
    for cp in local:
        cp.wait()


def gather_all(x, g, n_seq, n_exp):
    n = n_seq * n_exp
    length = n // 8
    anyspace = pl.BlockSpec(memory_space=pl.ANY)
    return pl.pallas_call(
        functools.partial(gather_kernel, n_seq, n_exp),
        out_shape=(
            jax.ShapeDtypeStruct((n * x.shape[0], x.shape[1]), x.dtype),
            jax.ShapeDtypeStruct((n * g.shape[0], g.shape[1]), g.dtype),
        ),
        in_specs=[anyspace, anyspace],
        out_specs=(anyspace, anyspace),
        scratch_shapes=[
            pltpu.SemaphoreType.DMA((9, 2 * length + 1, PARTS + 1)),
            pltpu.SemaphoreType.DMA((9, 2 * length + 1, PARTS + 1)),
            pltpu.SemaphoreType.DMA((2,)),
        ],
        compiler_params=pltpu.CompilerParams(collective_id=1, has_side_effects=True),
    )(x, g)


def scatter_kernel(
    n_seq, n_exp, y_ref, out_ref, acc, sib, xbuf, ybuf, dab, dbb, line, send, recv, loc
):
    me = Place(n_seq, n_exp)
    L = me.length
    rows, width = out_ref.shape
    halfw = width // 2
    me.greet()
    X, Y, C = me.dev(dx=1), me.dev(dy=1), me.dev(dc=1)

    def src(off, grp, dc):
        x = 1 - me.x if grp & 1 else me.x
        y = 1 - me.y if grp & 2 else me.y
        c = 1 - me.c if dc else me.c
        b = me.block(me.p + off, x, y, c)
        return y_ref.at[pl.ds(pl.multiple_of(b * rows, rows), rows)]

    def sib_copy(slot, off, grp):
        return pltpu.make_async_remote_copy(
            src(off, grp, 1), sib.at[grp, slot], send.at[grp, slot], recv.at[grp, slot], C, MESH
        )

    def load(slot, off, grp):
        return pltpu.make_async_copy(src(off, grp, 0), acc.at[grp, slot], loc.at[grp, slot])

    for grp in (3, 1, 2, 0):

        def go(slot, off, sign, grp=grp):
            sib_copy(slot, off, grp).start()
            load(slot, off, grp).start()

        me.far_first(go)

    f32 = jnp.float32

    def pair_sum(slot, off, grp):
        load(slot, off, grp).wait()
        sib_copy(slot, off, grp).wait_recv()
        return acc[grp, slot].astype(f32) + sib[grp, slot].astype(f32)

    def diag_a(slot):
        return pltpu.make_async_remote_copy(
            acc.at[3, slot, :, pl.ds(0, halfw)], dab.at[slot], send.at[4, slot], recv.at[4, slot], Y, MESH
        )

    def diag_b(slot):
        return pltpu.make_async_remote_copy(
            acc.at[3, slot, :, pl.ds(halfw, halfw)], dbb.at[slot], send.at[5, slot], recv.at[5, slot], X, MESH
        )

    def x_copy(slot):
        return pltpu.make_async_remote_copy(
            acc.at[1, slot], xbuf.at[slot], send.at[6, slot], recv.at[6, slot], X, MESH
        )

    def y_copy(slot):
        return pltpu.make_async_remote_copy(
            acc.at[2, slot], ybuf.at[slot], send.at[7, slot], recv.at[7, slot], Y, MESH
        )

    def line_copy(slot, sign):
        return pltpu.make_async_remote_copy(
            acc.at[0, slot],
            line.at[slot],
            send.at[8, slot],
            recv.at[8, slot],
            me.dev(dp=sign),
            MESH,
        )

    def d1(slot, off, sign):
        acc[3, slot] = pair_sum(slot, off, 3).astype(acc.dtype)
        diag_a(slot).start()
        diag_b(slot).start()

    def d2(slot, off, sign):
        sx = pair_sum(slot, off, 1)
        diag_a(slot).wait_recv()
        acc[1, slot, :, pl.ds(0, halfw)] = (sx[:, :halfw] + dab[slot].astype(f32)).astype(acc.dtype)
        acc[1, slot, :, pl.ds(halfw, halfw)] = sx[:, halfw:].astype(acc.dtype)
        x_copy(slot).start()
        sy = pair_sum(slot, off, 2)
        diag_b(slot).wait_recv()
        acc[2, slot, :, pl.ds(0, halfw)] = sy[:, :halfw].astype(acc.dtype)
        acc[2, slot, :, pl.ds(halfw, halfw)] = (sy[:, halfw:] + dbb[slot].astype(f32)).astype(acc.dtype)
        y_copy(slot).start()

    def d3(slot, off, sign):
        total = pair_sum(slot, off, 0)
        x_copy(slot).wait_recv()
        y_copy(slot).wait_recv()
        total = total + xbuf[slot].astype(f32) + ybuf[slot].astype(f32)
        if sign == 0:
            out_ref[...] = total
            if L > 1:

                @pl.when(me.p > 0)
                def _():
                    in_copy(2).wait_recv()
                    out_ref[...] += line[2].astype(f32)

                @pl.when(me.p < L - 1)
                def _():
                    in_copy(1).wait_recv()
                    out_ref[...] += line[1].astype(f32)

            return
        acc[0, slot] = total.astype(acc.dtype)
        far = slot + 2
        behind = me.p > 0 if sign > 0 else me.p < L - 1

        @pl.when(jnp.logical_and(behind, sign * off + 1 < L))
        def _():
            in_copy(far).wait_recv()
            acc[0, slot] = (acc[0, slot].astype(f32) + line[far].astype(f32)).astype(acc.dtype)

        line_copy(slot, sign).start()

    def in_copy(slot):
        return pltpu.make_async_remote_copy(
            acc.at[0, slot], line.at[slot], send.at[8, slot], recv.at[8, slot], X, MESH
        )

    me.far_first(d1)
    me.far_first(d2)
    me.far_first(d3)

    def fin(slot, off, sign):
        for grp in range(4):
            sib_copy(slot, off, grp).wait_send()
        diag_a(slot).wait_send()
        diag_b(slot).wait_send()
        x_copy(slot).wait_send()
        y_copy(slot).wait_send()
        if sign:
            line_copy(slot, sign).wait_send()

    me.far_first(fin)


def scatter_sum(part, n_seq, n_exp):
    n = n_seq * n_exp
    slots = n // 4 - 1 + 2
    rows, width = part.shape[0] // n, part.shape[1]
    bf = jnp.bfloat16
    return pl.pallas_call(
        functools.partial(scatter_kernel, n_seq, n_exp),
        out_shape=jax.ShapeDtypeStruct((rows, width), jnp.float32),
        in_specs=[pl.BlockSpec(memory_space=pl.ANY)],
        out_specs=pl.BlockSpec(memory_space=pltpu.VMEM),
        scratch_shapes=[
            pltpu.VMEM((4, slots, rows, width), bf),
            pltpu.VMEM((4, slots, rows, width), bf),
            pltpu.VMEM((slots, rows, width), bf),
            pltpu.VMEM((slots, rows, width), bf),
            pltpu.VMEM((slots, rows, width // 2), bf),
            pltpu.VMEM((slots, rows, width // 2), bf),
            pltpu.VMEM((slots, rows, width), bf),
            pltpu.SemaphoreType.DMA((9, slots)),
            pltpu.SemaphoreType.DMA((9, slots)),
            pltpu.SemaphoreType.DMA((4, slots)),
        ],
        compiler_params=pltpu.CompilerParams(
            collective_id=2, has_side_effects=True, vmem_limit_bytes=60 * 2**20
        ),
    )(part)


GPARTS = 4
HPARTS = 4
PLANES = 4
MPARTS = 4


def plane_orders(length):
    def depth(q):
        return min(q, length - 1 - q)

    visit = []
    for p in range(length):
        rest = [q for q in range(length) if q != p]
        near = min(rest, key=lambda q: (abs(q - p), depth(q)), default=p)
        rest = sorted((q for q in rest if q != near), key=lambda q: (depth(q), abs(q - p)))
        visit.append([p] + [near] * (length > 1) + rest)
    lines = []
    for p in range(length):
        def ready(q):
            chain = range(0, p + 1) if q > p else range(p, length)
            return max(visit[b].index(q) for b in chain)

        low = 2 * p < length
        lines.append(sorted((q for q in range(length) if q != p), key=lambda q: (ready(q), -q if low else q)))
    return visit, lines


def pick(table, p, j):
    total = 0
    for a, row in enumerate(table):
        for b, v in enumerate(row):
            hit = jnp.logical_and(p == a, j == b).astype(jnp.int32)
            total = total + hit * v
    return total


def spans(tiles, parts):
    cuts = [(tiles * i // parts) * 128 for i in range(parts + 1)]
    return [pl.ds(a, b - a) for a, b in zip(cuts[:-1], cuts[1:])]


def when(cond, fn):
    def run():
        fn()

    pl.when(cond)(run)


def attend_tokens(
    me, q_ref, k_ref, v_ref, ld_ref, res_ref, ag_ref, mg_ref, ids_ref, gw_ref, x_out,
    hid, work, flat, own16, peer, cin, cout, tots, tok, psend, precv, tsem, msend, mrecv,
):
    L, z = me.length, me.p
    f32, bf = jnp.float32, jnp.bfloat16
    heads, block = ld_ref.shape
    dim = q_ref.shape[1] // heads
    rows = res_ref.shape[0]
    n_exp, width = tok.shape[0], tok.shape[2]
    e = lax.axis_index("exp")
    pair = me.dev(dx=1)

    def head(h):
        return pl.ds(h * dim, dim)

    def pair_copy(h):
        return pltpu.make_async_remote_copy(
            own16.at[h], peer.at[h], psend.at[0], precv.at[0, h], pair, MESH
        )

    def line_copy(h):
        return pltpu.make_async_remote_copy(
            cout.at[h], cin.at[h], psend.at[1], precv.at[1, h], me.dev(dp=1), MESH
        )

    tot_copy = pltpu.make_async_remote_copy(tots.at[0], tots.at[1], tsem.at[0], tsem.at[1], pair, MESH)

    nt = (((1,), (1,)), ((), ()))
    tn = (((0,), (0,)), ((), ()))
    r = lax.broadcasted_iota(jnp.int32, (block, block), 0)
    c = lax.broadcasted_iota(jnp.int32, (block, block), 1)
    seen = r >= c
    decay = ld_ref[...]
    high = lax.Precision.HIGHEST
    cum = lax.dot_general(seen.astype(f32), decay, nt, precision=high, preferred_element_type=f32)
    cum_t = jnp.dot(decay, (r <= c).astype(f32), precision=high, preferred_element_type=f32)
    total = cum_t[:, block - 1 :]
    tots[0, 0:heads, :] = jnp.broadcast_to(total, (heads, dim))

    def state(h):
        kw = (k_ref[:, head(h)].astype(f32) * jnp.exp(total[h : h + 1] - cum[:, h : h + 1])).astype(bf)
        own = lax.dot_general(kw, v_ref[:, head(h)], tn, preferred_element_type=f32)
        work[:, pl.ds((heads + h) * dim, dim)] = own
        own16[h] = own.astype(bf)

    for h in range(heads):
        state(h)
    me.greet(dict(dy=1, dc=1))
    tot_copy.start()
    for h in range(heads):
        pair_copy(h).start()

    @pl.when(z == 0)
    def _():
        cin[...] = jnp.zeros_like(cin)

    def f_intra(h):
        scores = lax.dot_general(q_ref[:, head(h)], k_ref[:, head(h)], nt, preferred_element_type=f32)
        gap = cum[:, h : h + 1] - cum_t[h : h + 1, :]
        weights = jnp.where(seen, scores * jnp.exp(jnp.where(seen, gap, 0.0)), 0.0).astype(bf)
        work[:, head(h)] = jnp.dot(weights, v_ref[:, head(h)], preferred_element_type=f32)

    for h in range(heads):
        f_intra(h)
    tot_copy.wait_recv()
    mine, other = tots[0, 0:heads, :], tots[1, 0:heads, :]
    both = jnp.exp(mine + other)
    is_odd = jnp.full(mine.shape, me.x, jnp.int32) == 1
    one = jnp.ones_like(mine)
    own_by = jnp.where(is_odd, one, jnp.exp(other))
    peer_by = jnp.where(is_odd, jnp.exp(mine), one)
    carry_by = jnp.where(is_odd, jnp.exp(other), one)
    peer_in = jnp.where(is_odd, one, jnp.zeros_like(mine))

    peers = (dict(dc=1), dict(dy=1), dict(dy=1, dc=1))
    pieces = MPARTS
    span = width // pieces

    def mix_copy(k, i):
        to = me.dev(**peers[k])
        cols = pl.ds(i * span, span)
        src = flat.at[pl.ds(pl.multiple_of(to[1] * rows, rows), rows), cols]
        return pltpu.make_async_remote_copy(
            src, tok.at[e, :, cols], msend.at[0], mrecv.at[k], to, MESH
        )

    def mix_in(k):
        to = me.dev(**peers[k])
        return pltpu.make_async_remote_copy(
            tok.at[to[1]], tok.at[to[1]], msend.at[0], mrecv.at[k], to, MESH
        )

    def f_chain(h):
        pair_copy(h).wait_recv()
        pl.when(z > 0)(lambda: line_copy(h).wait_recv())
        near = peer[h].astype(f32)
        come = cin[h].astype(f32)
        row = slice(h, h + 1)

        @pl.when(z < L - 1)
        def _():
            mix = both[row] * come + own_by[row] * work[:, pl.ds((heads + h) * dim, dim)] + peer_by[row] * near
            cout[h] = mix.astype(bf)
            line_copy(h).start()

    def f_head(h):
        near = peer[h].astype(f32)
        come = cin[h].astype(f32)
        row = slice(h, h + 1)
        carried = carry_by[row] * come + peer_in[row] * near
        coarse = carried.astype(bf)
        fine = (carried - coarse.astype(f32)).astype(bf)
        query = q_ref[:, head(h)]
        inter = jnp.dot(query, coarse, preferred_element_type=f32) + jnp.dot(
            query, fine, preferred_element_type=f32
        )
        attn = work[:, head(h)] + jnp.exp(cum[:, h : h + 1]) * inter
        scale = lax.rsqrt(jnp.mean(attn * attn, axis=-1, keepdims=True) + 1e-06)
        flat[0:block, head(h)] = (attn * scale).astype(bf)
        if (h + 1) * pieces % heads == 0:
            for k in range(len(peers)):
                mix_copy(k, (h + 1) * pieces // heads - 1).start()

    for h in range(heads):
        f_chain(h)
        f_head(h)

    tok[e] = flat[pl.ds(pl.multiple_of(e * rows, rows), rows), 0:width]

    def f_mix():
        for k in range(len(peers)):
            mix_in(k).wait_recv()

    f_mix()
    square = jnp.zeros((rows, 1), f32)
    for j in range(n_exp):
        cols = pl.ds(j * width, width)
        value = (res_ref[:, cols].astype(f32) + tok[j].astype(f32) * ag_ref[:, cols]).astype(bf)
        hid[:, cols] = value
        wide = value.astype(f32)
        square = square + jnp.sum(wide * wide, axis=1, keepdims=True)
    scale = lax.rsqrt(square / (n_exp * width) + 1e-06)
    for j in range(n_exp):
        cols = pl.ds(j * width, width)
        x_out[:, cols] = (hid[:, cols].astype(f32) * scale * mg_ref[:, cols]).astype(bf)

    def column(ref):
        same = lax.broadcasted_iota(jnp.int32, (rows, rows), 0) == lax.broadcasted_iota(jnp.int32, (rows, rows), 1)
        return lax.dot_general(
            same.astype(f32), ref[...].astype(f32), nt, precision=high, preferred_element_type=f32
        )

    ids, gates = column(ids_ref).astype(jnp.int32), column(gw_ref)
    coarse = gates.astype(bf).astype(f32)
    rest = gates - coarse
    lane = lax.broadcasted_iota(jnp.int32, (rows, 128), 1)
    extra = jnp.zeros((rows, 128), f32)
    for i in range(ids_ref.shape[0]):
        who = ids[:, i : i + 1]
        extra = jnp.where(lane == who, coarse[:, i : i + 1], extra)
        extra = jnp.where(lane == who + 64, rest[:, i : i + 1], extra)
    x_out[:, n_exp * width :] = extra.astype(bf)

    def finish():
        def out(ref, sent):
            pltpu.make_async_remote_copy(ref, ref, sent, sent, pair, MESH).wait_send()

        tot_copy.wait_send()
        out(own16, psend.at[0])
        pl.when(z < L - 1)(lambda: out(cout, psend.at[1]))
        out(tok.at[pl.ds(0, len(peers))], msend.at[0])

    return finish


def moe_kernel(
    n_seq, n_exp, q_ref, k_ref, v_ref, ld_ref, res_ref, ag_ref, mg_ref, ids_ref, gw_ref,
    wg_ref, wu_ref, wd_ref, out_ref,
    xs, ys, act, sib, din, near_in, lin, tot, wg, wu, wd, hid_ref,
    own16, peer, cin, cout, tots, tok,
    gsend, lsend, grecv, drecv, crecv, brecv, ssend, srecv, drecv2, loc, psend, precv, tsem, msend, mrecv,
):
    me = Place(n_seq, n_exp)
    L, p = me.length, me.p
    rows, width = out_ref.shape
    hidden = wg.shape[0]
    many = 8 * rows
    f32, bf = jnp.float32, jnp.bfloat16
    X, Y, C = me.dev(dx=1), me.dev(dy=1), me.dev(dc=1)
    visit, lines = plane_orders(L)
    gcols = spans(xs.shape[1] // 128, GPARTS)
    hcols, dcols = spans(width // 128, HPARTS), spans(width // 128, 2 * HPARTS)

    loads = [
        pltpu.make_async_copy(a.at[0], b, loc.at[i])
        for i, (a, b) in enumerate(((wg_ref, wg), (wu_ref, wu), (wd_ref, wd)))
    ]
    for cp in loads:
        cp.start()

    def flip(v, d):
        return 1 - v if d else v

    def row(q, dx=0, dy=0, dc=0):
        k = (flip(me.c, dc) * 2 + flip(me.x, dx)) * 2 + flip(me.y, dy)
        return pl.ds(pl.multiple_of((q * 8 + k) * rows, rows), rows)

    def srow(q, dx=0, dy=0):
        k = flip(me.x, dx) * 2 + flip(me.y, dy)
        return pl.ds(pl.multiple_of((q * 4 + k) * rows, rows), rows)

    def prow(q):
        return pl.ds(pl.multiple_of(q * rows, rows), rows)

    cut = gcols[GPARTS // 2].start
    halves = (pl.ds(0, cut), pl.ds(cut, xs.shape[1] - cut))
    middle = pl.ds(gcols[1].start, gcols[-1].start - gcols[1].start)
    lower, higher, both = (0,), (1,), (0, 1)

    def gcopy(q, cols, r, to, sent, got):
        ref = xs.at[r, cols]
        return pltpu.make_async_remote_copy(ref, ref, sent, got, to, MESH)

    def arrive(q, cols, r, got):
        gcopy(q, cols, r, X, gsend.at[0], got).wait_recv()

    def bulk(ref, sent):
        return pltpu.make_async_remote_copy(ref, ref, sent, sent, X, MESH)

    def to_sibling(q, cols, r):
        gcopy(q, cols, r, C, gsend.at[0], crecv.at[q]).start()

    def both_ways(q, cols, r, lane, got):
        pl.when(jnp.logical_and(q >= p, p > 0))(
            lambda: gcopy(q, cols, r, me.dev(dp=-1), lsend.at[lane, q], got).start()
        )
        pl.when(jnp.logical_and(q <= p, p + 1 < L))(
            lambda: gcopy(q, cols, r, me.dev(dp=1), lsend.at[lane + 1, q], got).start()
        )

    def line_pair(q, side):
        both_ways(q, halves[side], row(q), 0, grecv.at[2, q, side])

    def corner_out(q):
        both_ways(q, middle, row(q, 1, 1), 2, drecv.at[q, 2])

    def g_first(q, turn, own=False):
        sent = gsend.at[5 + turn] if own else gsend.at[1]
        gcopy(q, halves[turn], row(q), X, sent, grecv.at[0, q, turn]).start()
        gcopy(q, halves[1 - turn], row(q), Y, gsend.at[2], grecv.at[1, q, 1 - turn]).start()
        if turn == 0:
            to_sibling(q, pl.ds(0, xs.shape[1]), row(q))

    def g_own(q):
        line_pair(q, 0)
        g_first(q, 0, True)
        line_pair(q, 1)
        g_first(q, 1, True)

    def from_x(q, side, own):
        r = row(q, 1, 0)
        arrive(q, halves[side], r, grecv.at[0, q, side])
        if side == 0:
            cols, sent = (halves[0], gsend.at[7]) if own else (gcols[0], gsend.at[3])
            gcopy(q, cols, r, Y, sent, drecv.at[q, 0]).start()
        to_sibling(q, halves[side], r)

    def from_y(q, side, own):
        r = row(q, 0, 1)
        arrive(q, halves[side], r, grecv.at[1, q, side])
        if side == 1:
            cols, sent = (halves[1], gsend.at[8]) if own else (gcols[-1], gsend.at[4])
            gcopy(q, cols, r, X, sent, drecv.at[q, 1]).start()
        to_sibling(q, halves[side], r)

    def g_second(q, own=False):
        from_x(q, 0, own)
        from_y(q, 1, own)

    def g_rest(q, own=False):
        from_x(q, 1, own)
        from_y(q, 0, own)

    def g_third(q, own=False):
        r = row(q, 1, 1)
        for k, cols in enumerate(halves if own else (gcols[0], gcols[-1])):
            arrive(q, cols, r, drecv.at[q, k])
            to_sibling(q, cols, r)
        if own:
            corner_out(q)

    def g_corner(k):
        for sign in (-1, 1):
            q = p + sign * k

            def pass_on():
                arrive(q, middle, row(q, 1, 1), drecv.at[q, 2])
                corner_out(q)
                to_sibling(q, middle, row(q, 1, 1))

            when(jnp.logical_and(q >= 0, q < L), pass_on)

    def g_ring(k, sides):
        for sign in (-1, 1):
            q = p + sign * k

            def pass_on():
                for side in sides:
                    arrive(q, halves[side], row(q), grecv.at[2, q, side])
                    line_pair(q, side)

            when(jnp.logical_and(q >= 0, q < L), pass_on)

    def g_done(q):
        r = pl.ds(pl.multiple_of((q * 2 + 1 - me.c) * 4 * rows, 4 * rows), 4 * rows)
        pltpu.make_async_remote_copy(xs.at[r], xs.at[r], gsend.at[0], crecv.at[q], X, MESH).wait_recv()

    def g_drain():
        bulk(xs.at[pl.ds(0, L * 4 * rows)], gsend.at[0]).wait_send()
        bulk(xs.at[pl.ds(0, (L - 1) * rows)], gsend.at[1]).wait_send()
        bulk(xs.at[pl.ds(0, L * rows)], gsend.at[2]).wait_send()
        bulk(xs.at[pl.ds(0, (L - 1) * rows), gcols[0]], gsend.at[3]).wait_send()
        bulk(xs.at[pl.ds(0, (L - 1) * rows), gcols[-1]], gsend.at[4]).wait_send()
        bulk(xs.at[row(p), halves[0]], gsend.at[7]).wait_send()
        bulk(xs.at[row(p), halves[1]], gsend.at[8]).wait_send()
        bulk(xs.at[row(p), halves[0]], gsend.at[5]).wait_send()
        bulk(xs.at[row(p), halves[1]], gsend.at[6]).wait_send()
        for q in range(L):
            pl.when(jnp.logical_and(q >= p, p > 0))(lambda: bulk(xs.at[row(q)], lsend.at[0, q]).wait_send())
            pl.when(jnp.logical_and(q <= p, p + 1 < L))(lambda: bulk(xs.at[row(q)], lsend.at[1, q]).wait_send())
            mid = xs.at[row(q), middle]
            pl.when(jnp.logical_and(q >= p, p > 0))(lambda: bulk(mid, lsend.at[2, q]).wait_send())
            pl.when(jnp.logical_and(q <= p, p + 1 < L))(lambda: bulk(mid, lsend.at[3, q]).wait_send())

    def sib_copy(q, h):
        r = pl.ds(pl.multiple_of((q * 2 + 1 - me.c) * 4 * rows, 4 * rows), 4 * rows)
        d = pl.ds(pl.multiple_of(q * 4 * rows, 4 * rows), 4 * rows)
        return pltpu.make_async_remote_copy(
            ys.at[r, hcols[h]], sib.at[d, hcols[h]], ssend.at[4], brecv.at[q, h], C, MESH
        )

    def plane_copy(side, q, h, r, to):
        return pltpu.make_async_remote_copy(
            ys.at[r, hcols[h]], near_in.at[prow(2 * q + side), hcols[h]], ssend.at[1 + side], brecv.at[q, h], to, MESH
        )

    def settled(ref, got):
        pltpu.make_async_remote_copy(ref, ref, ssend.at[0], got, X, MESH).wait_recv()

    def diag_copy(q, h, side):
        cols = dcols[2 * h + side]
        return pltpu.make_async_remote_copy(
            ys.at[row(q, 1, 1), cols], din.at[prow(q), cols], ssend.at[0], drecv2.at[q, h], (Y, X)[side], MESH
        )

    def x_copy(q, h):
        return plane_copy(0, q, h, row(q, 1, 0), X)

    def y_copy(q, h):
        return plane_copy(1, q, h, row(q, 0, 1), Y)

    def line_copy(q, h):
        up = (q > p).astype(jnp.int32)
        last = jnp.logical_and(q < p, q == p - 1).astype(jnp.int32)
        slot = q + (L - q) * last
        return pltpu.make_async_remote_copy(
            ys.at[row(q), hcols[h]],
            lin.at[prow(slot), hcols[h]],
            ssend.at[3],
            srecv.at[slot, h],
            me.dev(dp=2 * up - 1),
            MESH,
        )

    def line_in(slot, h):
        return pltpu.make_async_remote_copy(
            ys.at[row(p), hcols[h]], lin.at[prow(slot), hcols[h]], ssend.at[3], srecv.at[slot, h], X, MESH
        )

    def pair(q, h, dx, dy):
        return ys[row(q, dx, dy), hcols[h]].astype(f32) + sib[srow(q, dx, dy), hcols[h]].astype(f32)

    def r_first(q, h):
        sib_copy(q, h).wait_recv()
        ys[row(q, 1, 1), hcols[h]] = pair(q, h, 1, 1).astype(bf)
        for side in range(2):
            diag_copy(q, h, side).start()

    def r_second(q, h):
        sx, sy = pair(q, h, 1, 0), pair(q, h, 0, 1)
        near, far = dcols[2 * h], dcols[2 * h + 1]
        settled(din.at[prow(q), hcols[h]], drecv2.at[q, h])
        ys[row(q, 1, 0), near] = (sx[:, : near.size] + din[prow(q), near].astype(f32)).astype(bf)
        ys[row(q, 1, 0), far] = sx[:, near.size :].astype(bf)
        x_copy(q, h).start()
        ys[row(q, 0, 1), near] = sy[:, : near.size].astype(bf)
        ys[row(q, 0, 1), far] = (sy[:, near.size :] + din[prow(q), far].astype(f32)).astype(bf)
        y_copy(q, h).start()

    def r_third(q, h):
        total = pair(q, h, 0, 0)
        settled(near_in.at[pl.ds(pl.multiple_of(2 * q * rows, rows), 2 * rows), hcols[h]], brecv.at[q, h])
        for side in range(2):
            total = total + near_in[prow(2 * q + side), hcols[h]].astype(f32)
        tot[prow(q), hcols[h]] = total

    def r_line(q, h):
        behind = jnp.logical_or(jnp.logical_and(q > p, p > 0), jnp.logical_and(q < p, p < L - 1))

        @pl.when(behind)
        def _():
            line_in(q, h).wait_recv()
            ys[row(q), hcols[h]] = (tot[prow(q), hcols[h]] + lin[prow(q), hcols[h]].astype(f32)).astype(bf)

        @pl.when(jnp.logical_not(behind))
        def _():
            ys[row(q), hcols[h]] = tot[prow(q), hcols[h]].astype(bf)

        line_copy(q, h).start()

    def r_last(h):
        cols = hcols[h]

        @pl.when(p > 0)
        def _():
            line_in(p, h).wait_recv()
            tot[prow(p), cols] += lin[prow(p), cols].astype(f32)

        @pl.when(p < L - 1)
        def _():
            line_in(L, h).wait_recv()
            tot[prow(p), cols] += lin[prow(L), cols].astype(f32)

        out_ref[:, cols] = (hid_ref[:, cols].astype(f32) + tot[prow(p), cols]).astype(bf)

    at_end = jnp.logical_or(p == 0, p == L - 1)
    inner = jnp.logical_not(at_end)

    def r_early(q, h):
        pl.when(jnp.logical_and(at_end, q != p))(lambda: r_line(q, h))

    def r_drain():
        bulk(sib, ssend.at[4]).wait_send()
        for kind in range(3):
            bulk(din, ssend.at[kind]).wait_send()

    tile = next(t for t in range(512, 0, -128) if hidden % t == 0)
    fsteps = hidden // tile

    def block_of(q):
        return pl.ds(pl.multiple_of(q * many, many), many)

    def gate_of(q):
        extra = xs[block_of(q), width : width + 128].astype(f32)
        lane = lax.broadcasted_iota(jnp.int32, extra.shape, 1)
        e = lax.axis_index("exp")
        keep = jnp.logical_or(lane == e, lane == e + 64)
        return jnp.sum(jnp.where(keep, extra, 0.0), axis=1, keepdims=True)

    nt = (((1,), (1,)), ((), ()))

    def ffn_in(q, f):
        fc = pl.ds(f * tile, tile)
        rows_in = xs[block_of(q), 0:width]
        gate = lax.dot_general(rows_in, wg[fc, :], nt, preferred_element_type=f32)
        up = lax.dot_general(rows_in, wu[fc, :], nt, preferred_element_type=f32)
        act[:, fc] = (gate / (1.0 + jnp.exp(-gate)) * up * gate_of(q)).astype(bf)

    def ffn_out(q, h):
        ys[block_of(q), hcols[h]] = jnp.dot(
            act[...], wd[:, hcols[h]], preferred_element_type=f32
        ).astype(bf)
        sib_copy(q, h).start()

    front_done = attend_tokens(
        me, q_ref, k_ref, v_ref, ld_ref, res_ref, ag_ref, mg_ref, ids_ref, gw_ref, xs.at[row(p)],
        hid_ref, tot, act, own16, peer, cin, cout, tots, tok, psend, precv, tsem, msend, mrecv,
    )
    second = pick(visit, p, 1)
    g_own(p)
    g_second(p, True)
    g_ring(1, lower)
    g_rest(p, True)
    g_ring(1, higher)
    g_first(second, 0)
    g_third(p, True)
    g_first(second, 1)
    front_done()
    for cp in loads:
        cp.wait()

    def chunk(j, carry):
        q, nxt, prev = pick(visit, p, j), pick(visit, p, j + 1), pick(visit, p, j - 1)
        older = pick(visit, p, j - 2)
        third, fourth = pick(visit, p, 2), pick(visit, p, 3)

        def opening(*fns):
            when(j == 0, lambda: [fn() for fn in fns])

        def closing(*fns):
            when(j == L - 1, lambda: [fn() for fn in fns])

        def ahead(*fns):
            when(jnp.logical_and(j > 0, j + 1 < L), lambda: [fn() for fn in fns])

        def after(*fns):
            when(j > 0, lambda: [fn() for fn in fns])

        def later(*fns):
            when(j > 1, lambda: [fn() for fn in fns])

        def settle(at, h):
            r_third(at, h)
            r_early(at, h)

        def hook(n):
            if n == 0:
                after(lambda: r_first(prev, 2), lambda: r_first(prev, 3))
                when(j == 1, lambda: g_corner(2))
                opening(
                    lambda: g_ring(2, lower),
                    lambda: g_second(nxt),
                    lambda: g_ring(2, higher),
                    lambda: g_first(fourth, 0),
                )
            if n == 1:
                opening(lambda: g_rest(nxt), lambda: g_first(fourth, 1))
                ahead(lambda: g_second(nxt))
                later(lambda: settle(older, 0), lambda: settle(older, 1))
                after(lambda: r_second(prev, 0), lambda: r_second(prev, 1))
            if n == 2:
                opening(lambda: g_corner(1))
                ahead(lambda: g_rest(nxt))
                later(lambda: settle(older, 2), lambda: settle(older, 3))
                closing(lambda: r_second(prev, 2))

        g_done(q)
        for f in range(fsteps):
            ffn_in(q, f)
            hook(f)
        for f in range(fsteps, 3):
            hook(f)
        for h in range(HPARTS):
            ffn_out(q, h)
            if h == 0:
                ahead(lambda: r_second(prev, 2))
                closing(lambda: r_second(prev, 3))
            if h == 1:
                when(j == 1, lambda: g_corner(3))
                ahead(lambda: r_second(prev, 3))
                opening(lambda: g_ring(3, both), lambda: g_first(third, 0))
                closing(lambda: settle(prev, 0))
            if h == 2:
                r_first(q, 0)
                ahead(lambda: g_third(nxt))
                opening(lambda: g_third(nxt))
                closing(lambda: settle(prev, 1))
            if h == 3:
                r_first(q, 1)
                opening(lambda: g_first(third, 1))
        return carry

    def one_line(i, h):
        when(inner, lambda: r_line(pick(lines, p, i), h))

    lax.fori_loop(0, L, chunk, 0)

    final, prior = pick(visit, p, L - 1), pick(visit, p, L - 2)
    r_first(final, 2)
    r_third(prior, 2)
    r_early(prior, 2)
    r_first(final, 3)
    r_third(prior, 3)
    r_early(prior, 3)
    for h in range(HPARTS):
        r_second(final, h)
        if h:
            one_line(0, h - 1)
    one_line(0, HPARTS - 1)
    for h in range(HPARTS):
        one_line(1, h)
        r_third(final, h)
        r_early(final, h)
    g_drain()
    for h in range(HPARTS):
        one_line(2, h)
        if h:
            r_last(h - 1)
    r_drain()
    r_last(HPARTS - 1)
    bulk(lin.at[pl.ds(0, (L - 1) * rows)], ssend.at[3]).wait_send()


def moe_scratch(n_seq, n_exp, x_shape, w_shape):
    n, L = n_seq * n_exp, n_seq * n_exp // 8
    rows, wide = x_shape
    hidden, width = w_shape[1:]
    bf, f32 = jnp.bfloat16, jnp.float32
    return [
        ((n * rows, wide), bf),
        ((n * rows, width), bf),
        ((8 * rows, hidden), bf),
        ((n // 2 * rows, width), bf),
        ((L * rows, width), bf),
        ((2 * L * rows, width), bf),
        ((L * rows + rows, width), bf),
        ((L * rows, width), f32),
        ((hidden, width), bf),
        ((hidden, width), bf),
        ((hidden, width), bf),
    ]


MOE_VMEM = 61 * 2**20


def moe_fits(n_seq, n_exp, rows, width, w_shape):
    need = sum(
        a * b * jnp.dtype(t).itemsize for (a, b), t in moe_scratch(n_seq, n_exp, (rows, width + 128), w_shape)
    )
    return (
        w_shape[0] == 1
        and n_exp // 4 == 1
        and n_seq * n_exp == 8 * PLANES
        and w_shape[1] % 128 == 0
        and w_shape[2] % (256 * HPARTS) == 0
        and w_shape[2] // n_exp % (128 * MPARTS) == 0
        and need + 6 * 2**20 <= MOE_VMEM
    )


def whole_layer(
    queries, keys, values, log_decay, residual, attn_gain, moe_gain, expert_ids, gate_weights,
    w_gate, w_up, w_down, n_seq, n_exp,
):
    L = n_seq * n_exp // 8
    heads = log_decay.shape[1]
    part = queries.shape[1]
    dim = part // heads
    rows, width = residual.shape
    vmem = pl.BlockSpec(memory_space=pltpu.VMEM)
    anyspace = pl.BlockSpec(memory_space=pl.ANY)
    dma = pltpu.SemaphoreType.DMA
    bf = jnp.bfloat16
    states = pltpu.VMEM((heads, dim, dim), bf)
    scratch = moe_scratch(n_seq, n_exp, (rows, width + 128), w_gate.shape)
    return pl.pallas_call(
        functools.partial(moe_kernel, n_seq, n_exp),
        out_shape=jax.ShapeDtypeStruct(residual.shape, bf),
        in_specs=[vmem] * 9 + [anyspace] * 3,
        out_specs=vmem,
        scratch_shapes=[pltpu.VMEM(s, t) for s, t in scratch]
        + [
            pltpu.VMEM(residual.shape, bf),
            states,
            states,
            states,
            states,
            pltpu.VMEM((2, heads + -heads % 8, dim), jnp.float32),
            pltpu.VMEM((n_exp, rows, part), bf),
            dma((9,)),
            dma((4, L)),
            dma((3, L, 2)),
            dma((L, 3)),
            dma((L,)),
            dma((L, HPARTS)),
            dma((5,)),
            dma((L + 1, HPARTS)),
            dma((L, HPARTS)),
            dma((3,)),
            dma((2,)),
            dma((2, heads)),
            dma((2,)),
            dma((1,)),
            dma((3,)),
        ],
        compiler_params=pltpu.CompilerParams(
            collective_id=5, has_side_effects=True, vmem_limit_bytes=MOE_VMEM
        ),
    )(
        queries, keys, values, log_decay.T, residual, attn_gain[None, :], moe_gain[None, :],
        expert_ids.T, gate_weights.T, w_gate, w_up, w_down,
    )


def carry_kernel(n_seq, own_ref, own16_ref, tot_ref, out_ref, peer, ptot, cin, cout, send, recv, tsem):
    s, e = lax.axis_index("seq"), lax.axis_index("exp")
    z, odd, deep = s // 2, s % 2, n_seq // 2
    heads = own_ref.shape[0]
    pair = (z * 2 + 1 - odd, e)

    barrier = pltpu.get_barrier_semaphore()
    pl.semaphore_signal(barrier, inc=1, device_id=pair, device_id_type=MESH)

    @pl.when(z > 0)
    def _():
        pl.semaphore_signal(barrier, inc=1, device_id=(s - 2, e), device_id_type=MESH)

    @pl.when(z < deep - 1)
    def _():
        pl.semaphore_signal(barrier, inc=1, device_id=(s + 2, e), device_id_type=MESH)

    ends = (z > 0).astype(jnp.int32) + (z < deep - 1).astype(jnp.int32)
    pl.semaphore_wait(barrier, 1 + ends)

    tot_copy = pltpu.make_async_remote_copy(tot_ref, ptot, tsem.at[0], tsem.at[1], pair, MESH)

    def pair_copy(h):
        return pltpu.make_async_remote_copy(
            own16_ref.at[h], peer.at[h], send.at[0, h], recv.at[0, h], pair, MESH
        )

    def line_copy(h):
        return pltpu.make_async_remote_copy(
            cout.at[h], cin.at[h], send.at[1, h], recv.at[1, h], (s + 2, e), MESH
        )

    tot_copy.start()
    for h in range(heads):
        pair_copy(h).start()

    @pl.when(z == 0)
    def _():
        cin[...] = jnp.zeros_like(cin)

    tot_copy.wait_recv()
    mine, other = tot_ref[...], ptot[...]
    both = jnp.exp(mine + other)
    is_odd = jnp.full(mine.shape, odd, jnp.int32) == 1
    one = jnp.ones_like(mine)
    own_by = jnp.where(is_odd, one, jnp.exp(other))
    peer_by = jnp.where(is_odd, jnp.exp(mine), one)
    carry_by = jnp.where(is_odd, jnp.exp(other), one)
    peer_in = jnp.where(is_odd, one, jnp.zeros_like(mine))
    for h in range(heads):
        pair_copy(h).wait_recv()

        @pl.when(z > 0)
        def _():
            line_copy(h).wait_recv()

        near = peer[h].astype(jnp.float32)
        come = cin[h].astype(jnp.float32)

        @pl.when(z < deep - 1)
        def _():
            cout[h] = (
                both[h : h + 1] * come + own_by[h : h + 1] * own_ref[h] + peer_by[h : h + 1] * near
            ).astype(cout.dtype)
            line_copy(h).start()

        out_ref[h] = carry_by[h : h + 1] * come + peer_in[h : h + 1] * near

    tot_copy.wait_send()
    for h in range(heads):
        pair_copy(h).wait_send()

        @pl.when(z < deep - 1)
        def _():
            line_copy(h).wait_send()


def carried_in(block_total, block_state, n_seq):
    heads, dim, _ = block_state.shape
    bf = jnp.bfloat16
    tile = jnp.pad(block_total, (0, -heads % 8))
    tile = jnp.broadcast_to(tile[:, None], (tile.shape[0], dim))
    vmem = pl.BlockSpec(memory_space=pltpu.VMEM)
    return pl.pallas_call(
        functools.partial(carry_kernel, n_seq),
        out_shape=jax.ShapeDtypeStruct(block_state.shape, jnp.float32),
        in_specs=[vmem] * 3,
        out_specs=vmem,
        scratch_shapes=[
            pltpu.VMEM(block_state.shape, bf),
            pltpu.VMEM(tile.shape, jnp.float32),
            pltpu.VMEM(block_state.shape, bf),
            pltpu.VMEM(block_state.shape, bf),
            pltpu.SemaphoreType.DMA((2, heads)),
            pltpu.SemaphoreType.DMA((2, heads)),
            pltpu.SemaphoreType.DMA((2,)),
        ],
        compiler_params=pltpu.CompilerParams(collective_id=3, has_side_effects=True),
    )(block_state, block_state.astype(bf), tile)


def mix_kernel(n_exp, normed_ref, res_ref, again_ref, mgain_ref, hid_ref, in_ref, tok, send, recv, loc):
    s, e = lax.axis_index("seq"), lax.axis_index("exp")
    rows, width = res_ref.shape[0], normed_ref.shape[1]

    barrier = pltpu.get_barrier_semaphore()
    for k in range(1, n_exp):
        pl.semaphore_signal(
            barrier, inc=1, device_id=(s, lax.rem(e + k, n_exp)), device_id_type=MESH
        )
    pl.semaphore_wait(barrier, n_exp - 1)

    def source(peer):
        return normed_ref.at[pl.ds(pl.multiple_of(peer * rows, rows), rows)]

    own = pltpu.make_async_copy(source(e), tok.at[e], loc.at[0])

    def copy(k):
        peer = lax.rem(e + k, n_exp)
        return pltpu.make_async_remote_copy(
            source(peer), tok.at[e], send.at[k], recv.at[k], (s, peer), MESH
        )

    def arriving(k):
        sender = lax.rem(e + n_exp - k, n_exp)
        return pltpu.make_async_remote_copy(
            source(e), tok.at[sender], send.at[k], recv.at[k], (s, sender), MESH
        )

    for k in range(1, n_exp):
        copy(k).start()
    own.start()
    own.wait()
    for k in range(1, n_exp):
        arriving(k).wait_recv()
    square = jnp.zeros((rows, 1), jnp.float32)
    for j in range(n_exp):
        cols = pl.ds(j * width, width)
        hid = (
            res_ref[:, cols].astype(jnp.float32)
            + tok[j].astype(jnp.float32) * again_ref[:, cols]
        ).astype(jnp.bfloat16)
        hid_ref[:, cols] = hid
        wide = hid.astype(jnp.float32)
        square = square + jnp.sum(wide * wide, axis=1, keepdims=True)
    scale = lax.rsqrt(square / (n_exp * width) + 1e-06)
    for j in range(n_exp):
        cols = pl.ds(j * width, width)
        in_ref[:, cols] = (
            hid_ref[:, cols].astype(jnp.float32) * scale * mgain_ref[:, cols]
        ).astype(jnp.bfloat16)
    for k in range(1, n_exp):
        copy(k).wait_send()


def mix_tokens(normed, residual, attn_gain, moe_gain, n_exp):
    vmem = pl.BlockSpec(memory_space=pltpu.VMEM)
    return pl.pallas_call(
        functools.partial(mix_kernel, n_exp),
        out_shape=(jax.ShapeDtypeStruct(residual.shape, jnp.bfloat16),) * 2,
        in_specs=[vmem] * 4,
        out_specs=(vmem, vmem),
        scratch_shapes=[
            pltpu.VMEM((n_exp, residual.shape[0], normed.shape[1]), jnp.bfloat16),
            pltpu.SemaphoreType.DMA((n_exp,)),
            pltpu.SemaphoreType.DMA((n_exp,)),
            pltpu.SemaphoreType.DMA((1,)),
        ],
        compiler_params=pltpu.CompilerParams(collective_id=4, has_side_effects=True),
    )(normed, residual, attn_gain[None, :], moe_gain[None, :])


def body(
    queries,
    keys,
    values,
    log_decay,
    residual,
    attn_gain,
    moe_gain,
    expert_ids,
    gate_weights,
    w_gate,
    w_up,
    w_down,
):
    n_seq, n_exp = lax.axis_size("seq"), lax.axis_size("exp")
    if moe_fits(n_seq, n_exp, *residual.shape, w_gate.shape):
        return whole_layer(
            queries, keys, values, log_decay, residual, attn_gain, moe_gain, expert_ids, gate_weights,
            w_gate, w_up, w_down, n_seq, n_exp,
        )
    tok_rows, width = residual.shape
    experts = w_gate.shape[0] * n_exp
    gates = jnp.sum(
        jnp.where(
            expert_ids[:, :, None] == jnp.arange(experts, dtype=jnp.int32)[None, None, :],
            gate_weights[:, :, None],
            0.0,
        ),
        axis=1,
    )
    rows = queries.shape[0]
    heads = log_decay.shape[1]
    head_dim = queries.shape[1] // heads
    q_heads = queries.reshape(rows, heads, head_dim)
    k_heads = keys.reshape(rows, heads, head_dim)
    v_heads = values.reshape(rows, heads, head_dim)
    upto = (
        lax.broadcasted_iota(jnp.int32, (rows, rows), 0)
        >= lax.broadcasted_iota(jnp.int32, (rows, rows), 1)
    ).astype(jnp.float32)
    log_cum = jnp.dot(upto, log_decay, precision=lax.Precision.HIGHEST)
    block_total = log_cum[-1]
    keys_weighted = (k_heads * jnp.exp(block_total[None, :] - log_cum)[:, :, None]).astype(
        jnp.bfloat16
    )
    block_state = jnp.einsum(
        "thd,the->hde", keys_weighted, v_heads, preferred_element_type=jnp.float32
    )
    carried = carried_in(block_total, block_state, lax.axis_size("seq"))
    scores = jnp.einsum("thd,shd->hts", q_heads, k_heads, preferred_element_type=jnp.float32)
    gap_logs = log_cum.T[:, :, None] - log_cum.T[:, None, :]
    causal_mask = (
        lax.broadcasted_iota(jnp.int32, (rows, rows), 0)
        >= lax.broadcasted_iota(jnp.int32, (rows, rows), 1)
    )[None, :, :]
    weights = jnp.where(
        causal_mask, scores * jnp.exp(jnp.where(causal_mask, gap_logs, 0.0)), 0.0
    ).astype(jnp.bfloat16)
    intra = jnp.einsum("hts,she->the", weights, v_heads, preferred_element_type=jnp.float32)
    inter = jnp.exp(log_cum)[:, :, None] * jnp.einsum(
        "thd,hde->the", q_heads.astype(jnp.float32), carried, precision=lax.Precision.HIGHEST
    )
    attn = intra + inter
    normed = (attn * lax.rsqrt(jnp.mean(attn * attn, axis=-1, keepdims=True) + 1e-06)).astype(
        jnp.bfloat16
    )
    normed = normed.reshape(rows, heads * head_dim)
    hidden, moe_in = mix_tokens(normed, residual, attn_gain, moe_gain, n_exp)
    hid32 = hidden.astype(jnp.float32)
    flat = gates.T.reshape(-1)
    pad = -flat.shape[0] % 1024
    g_tile = jnp.pad(flat, (0, pad)).reshape(-1, 128)
    everyone, g_all = gather_all(moe_in, g_tile, n_seq, n_exp)
    g_all = g_all.reshape(n_seq * n_exp, -1)[:, : experts * tok_rows]
    g_all = g_all.reshape(n_seq * n_exp, experts, tok_rows)
    mixed = None
    gate_col = lax.dynamic_slice_in_dim(
        g_all, lax.axis_index("exp") * w_gate.shape[0], w_gate.shape[0], 1
    )
    part = None
    for j in range(w_gate.shape[0]):
        gate_part = jnp.einsum("td,fd->tf", everyone, w_gate[j], preferred_element_type=jnp.float32)
        up_part = jnp.einsum("td,fd->tf", everyone, w_up[j], preferred_element_type=jnp.float32)
        active = (
            jax.nn.silu(gate_part) * up_part * gate_col[:, j, :].reshape(-1, 1)
        ).astype(jnp.bfloat16)
        one = jnp.dot(active, w_down[j], preferred_element_type=jnp.float32)
        part = one if part is None else part + one
    part = part.astype(jnp.bfloat16)
    total_rows, width = part.shape
    pieces = max(1, total_rows // 1024)
    step = width // pieces
    summed = [
        jax.jit(scatter_sum, static_argnums=(1, 2))(part[:, i * step : (i + 1) * step], n_seq, n_exp) for i in range(pieces)
    ]
    summed = summed[0] if pieces == 1 else jnp.concatenate(summed, axis=1)
    return (hid32 + summed).astype(jnp.bfloat16)


def solution(mesh):
    in_specs = (
        P("seq", "exp"),
        P("seq", "exp"),
        P("seq", "exp"),
        P("seq", "exp"),
        P(("seq", "exp"), None),
        P(),
        P(),
        P(("seq", "exp"), None),
        P(("seq", "exp"), None),
        P("exp", "seq", None),
        P("exp", "seq", None),
        P("exp", "seq", None),
    )
    out_specs = P(("seq", "exp"), None)
    return jax.shard_map(body, mesh=mesh, in_specs=in_specs, out_specs=out_specs, check_vma=False)
```
